128 devices in a mesh: dp: 32 (over y_lo, z, x), tensor: 4 (over y_hi, core).
Axes of the slice: x: 4, y: 4 (y_hi: 2, y_lo: 2; y = y_hi * 2 + y_lo), z: 4, core: 2. Of those that a mesh axis runs over, the one named last changes fastest.
Arguments:
- tokens: bfloat16 [18432, 1024], P(('dp', 'tensor')), may hold values from -6 to 6
- segment: int32 [18432], replicated, may hold values from 0 to 31, as said below
- real_token: int32 [18432], replicated, may hold values from 0 to 1, as said below
- qkv_weight: bfloat16 [1, 3, 1024, 1024], P(None, None, 'dp', 'tensor'), may hold values from -0.1875 to 0.1875
- out_weight: bfloat16 [1, 1024, 1024], P(None, 'dp', 'tensor'), may hold values from -2 to 2
- up_weight: bfloat16 [1, 1024, 4, 1024], P(None, 'dp', None, 'tensor'), may hold values from -0.1875 to 0.1875
- down_weight: bfloat16 [1, 1024, 4, 1024], P(None, 'dp', None, 'tensor'), may hold values from -0.09375 to 0.09375
- unit_bias: bfloat16 [1, 6, 1024], P(None, None, 'tensor'), may hold values from -1.75 to 1.75
- norm_gain: bfloat16 [1, 2, 1024], replicated, may hold values from 0.099609375 to 1.8984375
- row_bias: bfloat16 [1, 4, 1024], replicated, may hold values from -1.75 to 1.75
- cotangent: bfloat16 [18432, 1024], P(('dp', 'tensor')), may hold values from -24 to 24
Outputs:
- block_out: bfloat16 [18432, 1024], P(('dp', 'tensor'))
- grad_tokens: bfloat16 [18432, 1024], P(('dp', 'tensor'))
- grad_qkv: float32 [1, 3, 1024, 1024], P(None, None, 'dp', 'tensor')
- grad_out: float32 [1, 1024, 1024], P(None, 'dp', 'tensor')
- grad_up: float32 [1, 1024, 4, 1024], P(None, 'dp', None, 'tensor')
- grad_down: float32 [1, 1024, 4, 1024], P(None, 'dp', None, 'tensor')
- grad_unit_bias: float32 [1, 6, 1024], P(None, None, 'tensor')
- grad_gain: float32 [1, 2, 1024], replicated
- grad_shift: float32 [1, 4, 1024], replicated
The draws below stay inside these ranges and needn't reach their ends.
Inputs may be any that keep to these rules, and one draw needn't show every extreme that they name: segment[i] is the number of the image holding token i, counted from 0 along the stream; every image is 577 consecutive tokens; padding tokens lie singly or in runs before, between and after images and have segment 31. `real_token`: 1 exactly on the tokens whose segment is under 31.
All inputs are finite; a program needn't handle non-finite values.
Results may differ from the reference program's by a relative error of at most 0.028.
Values may be sent and summed in bfloat16 or wider, within the bound.
A program may use at most 128 MiB of HBM per device.

```python
import jax
import jax.numpy as jnp
from jax import lax

D = 1024
FF = 4096
HEADS = 16
LAYERS = 1
IMG = 577
HD = 64
FF_GROUPS = 4
TOKENS = 18432
NIMG = 31
N_DP = 32


def stream_layout(key):
    base = jax.random.fold_in(key, 7)
    padding = TOKENS - NIMG * IMG
    order = jax.random.permutation(base, NIMG + padding)
    is_image = order < NIMG
    lengths = jnp.where(is_image, IMG, 1).astype(jnp.int32)
    item_ends = jnp.cumsum(lengths).astype(jnp.int32)
    places = jnp.arange(TOKENS, dtype=jnp.int32)
    item_of = jnp.searchsorted(item_ends, places, side='right').astype(jnp.int32)
    image_rank = (jnp.cumsum(is_image.astype(jnp.int32)) - 1).astype(jnp.int32)
    token_image = is_image[item_of]
    segment = jnp.where(token_image, image_rank[item_of], NIMG).astype(jnp.int32)
    return (segment, token_image.astype(jnp.int32))


def draw_segment(key, part):
    return stream_layout(key)[0]


def draw_real_token(key, part):
    return stream_layout(key)[1]


def strengthened(array, key, source, target, blocks, factor):
    owner, partner = [(jnp.arange(array.shape[position]) // (array.shape[position] // blocks)).reshape([-1 if axis == position else 1 for axis in range(array.ndim)]) for position in (source, target)]
    chosen = jax.random.permutation(key, blocks)[partner]
    strong = (owner == chosen) | (owner == (partner + blocks // 2) % blocks)
    return jnp.where(strong, factor * array, array)


def block_levels(own_key, dims, split, least, largest):
    loudness = 1.0
    for dim, shards_of in split:
        heights = jax.random.uniform(jax.random.fold_in(jax.random.fold_in(own_key, 6), dim), (shards_of,), jnp.float32, least / len(split), largest / len(split))
        loudness = loudness * jnp.repeat(jnp.exp(heights), dims[dim] // shards_of).reshape((-1,) + (1,) * (len(dims) - 1 - dim))
    return loudness


def scatter_about(key, shape, scale, most, pieces=(), kind=jnp.bfloat16):
    values = scale * jax.random.normal(key, shape, jnp.float32)
    if pieces:
        values = values * block_levels(key, shape, pieces, -0.22, 0.18)
    return jnp.clip(values, -most, most).astype(kind)


def noise_with(rng, dims, deviation, reach, split, heavy, kind=jnp.bfloat16):
    drawn = deviation * jax.random.normal(rng, dims, jnp.float32)
    if split:
        drawn = drawn * block_levels(rng, dims, split, -0.22, 0.18)
    return jnp.clip(strengthened(drawn, jax.random.fold_in(rng, 3), *heavy), -reach, reach).astype(kind)


def setup_inputs(seed: int = 0) -> dict:
    keys = jax.random.split(jax.random.key(seed), 12)
    tokens = scatter_about(keys[0], (TOKENS, D), 1.0, 6.0, ((0, 128),))
    segment = draw_segment(jax.random.fold_in(keys[11], 71), 0)
    real_token = draw_real_token(jax.random.fold_in(keys[11], 71), 0)
    qkv_weight = scatter_about(keys[3], (LAYERS, 3, D, D), D ** -0.5, 0.1875, ((2, 32), (3, 4)))
    out_weight = scatter_about(keys[4], (LAYERS, D, D), (max(D // 128, 2)) ** -0.5, 2.0, ((1, 32), (2, 4)))
    up_weight = scatter_about(keys[5], (LAYERS, D, FF_GROUPS, D), D ** -0.5, 0.1875, ((1, 32), (3, 4)))
    down_weight = scatter_about(keys[6], (LAYERS, D, FF_GROUPS, D), FF ** -0.5, 0.09375, ((1, 32), (3, 4)))
    unit_bias = scatter_about(keys[7], (LAYERS, FF_GROUPS + 2, D), 0.3, 1.75, ((2, 4),))
    norm_gain = jnp.clip(1.0 + 0.18 * jax.random.normal(keys[8], (LAYERS, 2, D), jnp.float32), 0.099609375, 1.8984375).astype(jnp.bfloat16)
    row_bias = scatter_about(keys[9], (LAYERS, 4, D), 0.3, 1.75)
    cotangent = noise_with(keys[10], (TOKENS, D), 1.0, 24.0, ((0, 128),), (0, 1, 128, 5.5))
    return {"tokens": tokens, "segment": segment, "real_token": real_token, "qkv_weight": qkv_weight, "out_weight": out_weight, "up_weight": up_weight, "down_weight": down_weight, "unit_bias": unit_bias, "norm_gain": norm_gain, "row_bias": row_bias, "cotangent": cotangent}


norm_eps = 1e-06
masked_score = -1e+30

@jax.custom_vjp
def low(v):
    return lax.optimization_barrier(v.astype(jnp.bfloat16)).astype(jnp.float32)

@jax.custom_vjp
def low_back(v):
    return v

def low_keep(v):
    return (low(v), None)

def low_pass(kept, grad):
    return (grad,)

def back_keep(v):
    return (v, None)

def back_low(kept, grad):
    return (low(grad),)
low.defvjp(low_keep, low_pass)
low_back.defvjp(back_keep, back_low)

def matmul(left_side, right_side):
    return jnp.dot(left_side, right_side, precision=lax.Precision.HIGHEST)

def matmul_trans(left_side, right_side):
    return lax.dot_general(left_side, right_side, (((1,), (1,)), ((), ())), precision=lax.Precision.HIGHEST)

def layer_norm(values, gain_row, shift_row):
    center = values - lax.optimization_barrier(jnp.mean(values, axis=-1, keepdims=True))
    spread = lax.optimization_barrier(jnp.mean(center * center, axis=-1, keepdims=True))
    return center * lax.rsqrt(spread + norm_eps) * gain_row + shift_row

def attend(queries, key_rows, value_rows, segment, real_token):
    margin = IMG - 1
    block_rows = TOKENS // N_DP
    window = block_rows + 2 * margin
    score_scale = HD ** (-0.5)
    key_pad = jnp.pad(key_rows, ((margin, margin), (0, 0)))
    value_pad = jnp.pad(value_rows, ((margin, margin), (0, 0)))
    segment_pad = jnp.pad(segment, (margin, margin), constant_values=-1)
    real_pad = jnp.pad(real_token, (margin, margin))
    place_pad = jnp.arange(TOKENS + 2 * margin, dtype=jnp.int32) - margin

    def one_block(block_index):
        block_first = (block_index * block_rows).astype(jnp.int32)
        query_block = lax.dynamic_slice_in_dim(queries, block_first, block_rows, 0).reshape(block_rows, HEADS, HD)
        key_block = lax.dynamic_slice_in_dim(key_pad, block_first, window, 0).reshape(window, HEADS, HD)
        value_block = lax.dynamic_slice_in_dim(value_pad, block_first, window, 0).reshape(window, HEADS, HD)
        segment_query = lax.dynamic_slice_in_dim(segment, block_first, block_rows, 0)
        segment_key = lax.dynamic_slice_in_dim(segment_pad, block_first, window, 0)
        real_key = lax.dynamic_slice_in_dim(real_pad, block_first, window, 0)
        place_query = block_first + jnp.arange(block_rows, dtype=jnp.int32)
        place_key = lax.dynamic_slice_in_dim(place_pad, block_first, window, 0)
        allowed = (segment_query[:, None] == segment_key[None, :]) & ((real_key[None, :] == 1) | (place_query[:, None] == place_key[None, :]))
        scores = jnp.einsum('qhd,khd->hqk', query_block, key_block, precision=lax.Precision.HIGHEST) * score_scale
        scores = jnp.where(allowed[None], low_back(scores), masked_score)
        row_top = lax.optimization_barrier(jnp.max(scores, axis=-1, keepdims=True))
        exponent = jnp.exp(scores - row_top)
        prob_low = low(exponent / lax.optimization_barrier(jnp.sum(exponent, axis=-1, keepdims=True)))
        return jnp.einsum('hqk,khd->qhd', prob_low, value_block, precision=lax.Precision.HIGHEST).reshape(block_rows, D)
    blocks_out = lax.map(jax.checkpoint(one_block), jnp.arange(N_DP, dtype=jnp.int32))
    return blocks_out.reshape(TOKENS, D)

def forward(stream, qkv_float, out_float, up_float, down_float, unit_float, gain_float, shift_float, segment, real_token):
    for layer_index in range(LAYERS):
        normed = low(layer_norm(stream, gain_float[layer_index, 0], shift_float[layer_index, 0]))
        matrices = qkv_float[layer_index]
        queries = low(low_back(matmul(normed, matrices[0]) + unit_float[layer_index, 0]))
        key_rows = low(low_back(matmul(normed, matrices[1])))
        value_rows = low(low_back(matmul(normed, matrices[2]) + unit_float[layer_index, 1]))
        attended = low(low_back(attend(queries, key_rows, value_rows, segment, real_token)))
        middle = stream + low_back(matmul_trans(attended, out_float[layer_index])) + shift_float[layer_index, 1]
        second = low(layer_norm(middle, gain_float[layer_index, 1], shift_float[layer_index, 2]))
        hidden = low_back(matmul(second, up_float[layer_index].reshape(D, FF)) + unit_float[layer_index, 2:].reshape(FF))
        active = low(jax.nn.gelu(hidden, approximate=False))
        stream = middle + low_back(matmul_trans(active, down_float[layer_index].reshape(D, FF))) + shift_float[layer_index, 3]
    return stream

def reference(tokens, segment, real_token, qkv_weight, out_weight, up_weight, down_weight, unit_bias, norm_gain, row_bias, cotangent):

    def network(stream, qkv_float, out_float, up_float, down_float, unit_float, gain_float, shift_float):
        return forward(stream, qkv_float, out_float, up_float, down_float, unit_float, gain_float, shift_float, segment, real_token)
    primals = tuple((operand.astype(jnp.float32) for operand in (tokens, qkv_weight, out_weight, up_weight, down_weight, unit_bias, norm_gain, row_bias)))
    result, pullback = jax.vjp(network, *primals)
    weighting = real_token.astype(jnp.float32)[:, None]
    gradients = pullback(cotangent.astype(jnp.float32) * weighting)
    return (result.astype(jnp.bfloat16), gradients[0].astype(jnp.bfloat16), gradients[1], gradients[2], gradients[3], gradients[4], gradients[5], gradients[6], gradients[7])
```

```python
import math

import jax
import jax.numpy as jnp
from jax import lax
from jax.sharding import PartitionSpec as P

LAYERS = 1
IMG = 577
HD = 64


norm_eps = 1e-06
masked_score = -1e30


def from_everyone(value, axis):
    devices = lax.axis_size(axis)
    return lax.all_to_all(
        jnp.broadcast_to(value[None], (devices, *value.shape)), axis, 0, 0, tiled=True
    )


def joined_along(parts, dim):
    dims = list(parts.shape[1:])
    dims[dim] *= parts.shape[0]
    return jnp.moveaxis(parts, 0, dim).reshape(dims)


def collect(value, axis, dim):
    parts = from_everyone(value, axis)
    return joined_along(parts, dim)


def split_up(value, dim, devices):
    dims = value.shape
    parts = value.reshape(*dims[:dim], devices, dims[dim] // devices, *dims[dim + 1 :])
    return jnp.moveaxis(parts, dim, 0)


def summed_on_arrival(value, axis, dim):
    devices = lax.axis_size(axis)
    parts = lax.all_to_all(split_up(value, dim, devices), axis, 0, 0, tiled=True)
    return jnp.sum(parts.astype(jnp.float32), axis=0)


def rows_first(arrays, axis, dims):
    turned = [jnp.moveaxis(a, dim, 0) for a, dim in zip(arrays, dims)]
    both = jnp.concatenate([t.reshape(len(t), -1) for t in turned], axis=1)
    filled, at, outs = (lax.all_gather(both, axis, axis=0, tiled=True), 0, [])
    for t, dim in zip(turned, dims):
        slab = filled[:, at : at + t[0].size].reshape(-1, *t.shape[1:])
        outs.append(jnp.moveaxis(slab, 0, dim))
        at += t[0].size
    return tuple(outs)


def with_halo(value, sides, width):
    for axis, dim in sides:
        devices, length = (lax.axis_size(axis), value.shape[dim])
        up = [(i, (i + 1) % devices) for i in range(devices - 1)]
        down = [(j, i) for i, j in up]
        last = lax.slice_in_dim(value, length - width, length, axis=dim)
        initial = lax.slice_in_dim(value, 0, width, axis=dim)
        before = lax.ppermute(last, axis, up)
        after = lax.ppermute(initial, axis, down)
        value = jnp.concatenate([before, value, after], axis=dim)
    return value


def from_behind(block, axis, distance):
    devices = range(lax.axis_size(axis))
    route = [(i - distance, i) for i in devices if i - distance in devices]
    return lax.ppermute(block, axis, route)


def side_by_side(arrays, axis, dim, along):
    widths = [math.prod(a.shape[along:]) for a in arrays]
    both = jnp.concatenate(
        [a.reshape(*a.shape[:along], w) for a, w in zip(arrays, widths)], axis=along
    )
    filled = lax.psum_scatter(both, axis, scatter_dimension=dim, tiled=True)
    parts = jnp.split(filled, [sum(widths[:k]) for k in range(1, len(widths))], axis=along)
    return tuple(
        (b.reshape(*filled.shape[:along], *a.shape[along:]) for a, b in zip(arrays, parts))
    )


def scatter_rows(grad):
    return lax.psum_scatter(
        grad.astype(jnp.bfloat16), "dp", scatter_dimension=0, tiled=True
    ).astype(jnp.float32)


def layer_norm(values, gain_row, shift_row):
    center = values - jnp.mean(values, axis=-1, keepdims=True)
    spread = jnp.mean(center * center, axis=-1, keepdims=True)
    return center * lax.rsqrt(spread + norm_eps) * gain_row + shift_row


def exact_gelu(values):
    return jax.nn.gelu(values, approximate=False)


def gather_forward(values):
    return collect(values, "tensor", 0)


def gather_backward(values):
    return collect(values, "tensor", 0)


def sum_forward(product, tok_rows):
    return summed_on_arrival(
        product(jnp.int32(0), tok_rows * lax.axis_size("tensor")).astype(jnp.bfloat16), "tensor", 0
    )


def sum_backward(product, tok_rows):
    return summed_on_arrival(
        product(jnp.int32(0), tok_rows * lax.axis_size("tensor")).astype(jnp.bfloat16), "tensor", 0
    )


def head_scores(query_head, key_head, allowed):
    raw = lax.dot_general(
        query_head, key_head, (((1,), (1,)), ((), ())), preferred_element_type=jnp.float32
    )
    return jnp.where(allowed, raw * HD ** (-0.5), masked_score)


def split_heads(queries, key_ext):
    heads_here = queries.shape[1] // HD
    query_heads = queries.reshape(queries.shape[0], heads_here, HD)
    key_heads = key_ext[0].reshape(key_ext.shape[1], heads_here, HD)
    value_heads = key_ext[1].reshape(key_ext.shape[1], heads_here, HD)
    return (heads_here, query_heads, key_heads, value_heads)


def merge_heads(per_head):
    return jnp.transpose(per_head, (1, 0, 2)).reshape(
        per_head.shape[1], per_head.shape[0] * per_head.shape[2]
    )


def attend_forward(queries, key_ext, allowed):
    heads_here, query_heads, key_heads, value_heads = split_heads(queries, key_ext)

    def one_head(head_index):
        query_head = lax.dynamic_index_in_dim(query_heads, head_index, 1, keepdims=False)
        key_head = lax.dynamic_index_in_dim(key_heads, head_index, 1, keepdims=False)
        value_head = lax.dynamic_index_in_dim(value_heads, head_index, 1, keepdims=False)
        scores = head_scores(query_head, key_head, allowed)
        row_top = jnp.max(scores, axis=1, keepdims=True)
        exponent = jnp.exp(scores - row_top)
        row_total = jnp.sum(exponent, axis=1, keepdims=True)
        prob_low = (exponent / row_total).astype(jnp.bfloat16)
        head_out = jnp.dot(prob_low, value_head, preferred_element_type=jnp.float32)
        return (head_out, (row_top + jnp.log(row_total))[:, 0])

    head_outs, log_norm = lax.map(one_head, jnp.arange(heads_here, dtype=jnp.int32))
    return (merge_heads(head_outs), log_norm)


def attend_backward(queries, key_ext, allowed, log_norm, grad_attended):
    heads_here, query_heads, key_heads, value_heads = split_heads(queries, key_ext)
    grad_heads = grad_attended.reshape(grad_attended.shape[0], heads_here, HD)

    def one_head(inputs):
        head_index, norm_row = inputs
        query_head = lax.dynamic_index_in_dim(query_heads, head_index, 1, keepdims=False)
        key_head = lax.dynamic_index_in_dim(key_heads, head_index, 1, keepdims=False)
        value_head = lax.dynamic_index_in_dim(value_heads, head_index, 1, keepdims=False)
        grad_head = lax.dynamic_index_in_dim(grad_heads, head_index, 1, keepdims=False)
        prob_full = jnp.exp(head_scores(query_head, key_head, allowed) - norm_row[:, None])
        prob_low = prob_full.astype(jnp.bfloat16)
        grad_value = lax.dot_general(
            prob_low, grad_head, (((0,), (0,)), ((), ())), preferred_element_type=jnp.float32
        )
        grad_prob = lax.dot_general(
            grad_head, value_head, (((1,), (1,)), ((), ())), preferred_element_type=jnp.float32
        )
        grad_score = (
            prob_full * (grad_prob - jnp.sum(prob_full * grad_prob, axis=1, keepdims=True))
        ).astype(jnp.bfloat16)
        grad_query = jnp.dot(grad_score, key_head, preferred_element_type=jnp.float32) * HD ** (
            -0.5
        )
        grad_key = lax.dot_general(
            grad_score, query_head, (((0,), (0,)), ((), ())), preferred_element_type=jnp.float32
        ) * HD ** (-0.5)
        return (grad_query, grad_key, grad_value)

    grad_queries, grad_keys, grad_values = lax.map(
        one_head, (jnp.arange(heads_here, dtype=jnp.int32), log_norm)
    )
    return (merge_heads(grad_queries), merge_heads(grad_keys), merge_heads(grad_values))


def local(
    tokens,
    segment,
    real_token,
    qkv_weight,
    out_weight,
    up_weight,
    down_weight,
    unit_bias,
    norm_gain,
    row_bias,
    cotangent,
):
    tok_rows = tokens.shape[0]
    tensor_size = lax.axis_size("tensor")
    group_rows = tok_rows * tensor_size
    margin = IMG - 1
    cols_here = qkv_weight.shape[3]
    dp_index = lax.axis_index("dp")
    tensor_index = lax.axis_index("tensor")
    group_first = dp_index * group_rows
    own_first = group_first + tensor_index * tok_rows
    segment_pad = jnp.pad(segment, (margin, margin), constant_values=-1)
    real_pad = jnp.pad(real_token, (margin, margin))
    segment_query = lax.dynamic_slice_in_dim(segment, group_first, group_rows, 0)
    segment_key = lax.dynamic_slice_in_dim(segment_pad, group_first, group_rows + 2 * margin, 0)
    real_key = lax.dynamic_slice_in_dim(real_pad, group_first, group_rows + 2 * margin, 0)
    place_query = jnp.arange(group_rows, dtype=jnp.int32)
    place_key = jnp.arange(group_rows + 2 * margin, dtype=jnp.int32) - margin
    allowed = (segment_query[:, None] == segment_key[None, :]) & (
        (real_key[None, :] == 1) | (place_query[:, None] == place_key[None, :])
    )
    own_real = lax.dynamic_slice_in_dim(real_token, own_first, tok_rows, 0).astype(jnp.float32)
    stream = tokens.astype(jnp.float32)
    layer_index = 0
    qkv_rows = lax.all_gather(
        jnp.moveaxis(qkv_weight[layer_index], 1, 0), "dp", axis=0, tiled=True
    )
    qkv_full = jnp.moveaxis(qkv_rows, 0, 1)
    out_full = lax.all_gather(out_weight[layer_index], "dp", axis=0, tiled=True)
    up_full = lax.all_gather(up_weight[layer_index], "dp", axis=0, tiled=True)
    down_full = lax.all_gather(down_weight[layer_index], "dp", axis=0, tiled=True)
    gathered = (qkv_full, out_full, up_full, down_full)
    gain_now = norm_gain[layer_index].astype(jnp.float32)
    shift_now = row_bias[layer_index].astype(jnp.float32)
    bias_now = unit_bias[layer_index].astype(jnp.float32)
    normed_full = gather_forward(layer_norm(stream, gain_now[0], shift_now[0]).astype(jnp.bfloat16))
    projected = jnp.einsum("gd,sde->sge", normed_full, qkv_full, preferred_element_type=jnp.float32)
    queries = (projected[0] + bias_now[0]).astype(jnp.bfloat16)
    key_value = jnp.stack([projected[1], projected[2] + bias_now[1]]).astype(jnp.bfloat16)
    key_ext = with_halo(key_value, (("dp", 1),), margin)
    attended, log_norm = attend_forward(queries, key_ext, allowed)
    attended = attended.astype(jnp.bfloat16)

    def attention_term(first_row, row_count):
        return lax.dot_general(
            attended, out_full, (((1,), (1,)), ((), ())), preferred_element_type=jnp.float32
        )

    middle = stream + sum_forward(attention_term, tok_rows) + shift_now[1]
    second_full = gather_forward(layer_norm(middle, gain_now[1], shift_now[2]).astype(jnp.bfloat16))
    hidden = (
        jnp.einsum("gd,dre->gre", second_full, up_full, preferred_element_type=jnp.float32)
        + bias_now[2:][None]
    )
    active = exact_gelu(hidden).astype(jnp.bfloat16)

    def feed_term(first_row, row_count):
        return jnp.einsum("gre,ore->go", active, down_full, preferred_element_type=jnp.float32)

    kept_weights = gathered
    records = [
        (
            stream,
            middle,
            normed_full,
            second_full,
            queries,
            key_ext,
            log_norm,
            attended,
            hidden,
            active,
            kept_weights,
        )
    ]
    stream = middle + sum_forward(feed_term, tok_rows) + shift_now[3]
    gradient = cotangent.astype(jnp.float32) * own_real[:, None]
    local_qkv = [None] * LAYERS
    local_out = [None] * LAYERS
    local_up = [None] * LAYERS
    local_down = [None] * LAYERS
    unit_grads = [None] * LAYERS
    gain_grads = [None] * LAYERS
    shift_grads = [None] * LAYERS
    for layer_index in reversed(range(LAYERS)):
        (
            stream_in,
            middle,
            normed_full,
            second_full,
            queries,
            key_ext,
            log_norm,
            attended,
            hidden,
            active,
            kept_weights,
        ) = records[layer_index]
        qkv_full, out_full, up_full, down_full = kept_weights
        gain_now = norm_gain[layer_index].astype(jnp.float32)
        shift_now = row_bias[layer_index].astype(jnp.float32)
        shift_three = jnp.sum(gradient, axis=0)
        grad_mlp = gather_backward(gradient.astype(jnp.bfloat16))
        down_grad = scatter_rows(
            jnp.einsum("go,gre->ore", grad_mlp, active, preferred_element_type=jnp.float32)
        )
        grad_active = jnp.einsum(
            "go,ore->gre", grad_mlp, down_full, preferred_element_type=jnp.float32
        )
        gelu_again, gelu_pull = jax.vjp(exact_gelu, hidden)
        grad_hidden = gelu_pull(grad_active)[0].astype(jnp.bfloat16)
        up_bias_grad = jnp.sum(grad_hidden.astype(jnp.float32), axis=0)
        up_grad = scatter_rows(
            jnp.einsum("gd,gre->dre", second_full, grad_hidden, preferred_element_type=jnp.float32)
        )

        def second_term(first_row, row_count):
            return jnp.einsum(
                "gre,dre->gd", grad_hidden, up_full, preferred_element_type=jnp.float32
            )

        grad_second = sum_backward(second_term, tok_rows)
        second_again, second_pull = jax.vjp(layer_norm, middle, gain_now[1], shift_now[2])
        grad_mid_norm, gain_one, shift_two = second_pull(grad_second)
        grad_middle = gradient + grad_mid_norm
        shift_one = jnp.sum(grad_middle, axis=0)
        grad_proj = gather_backward(grad_middle.astype(jnp.bfloat16))
        out_grad = scatter_rows(
            lax.dot_general(
                grad_proj, attended, (((0,), (0,)), ((), ())), preferred_element_type=jnp.float32
            )
        )
        grad_attended = jnp.dot(grad_proj, out_full, preferred_element_type=jnp.float32).astype(
            jnp.bfloat16
        )
        grad_query, grad_key_ext, grad_value_ext = attend_backward(
            queries, key_ext, allowed, log_norm, grad_attended
        )
        grad_pair_ext = jnp.stack([grad_key_ext, grad_value_ext])
        from_next = from_behind(grad_pair_ext[:, :margin].astype(jnp.bfloat16), "dp", -1).astype(
            jnp.float32
        )
        from_prev = from_behind(
            grad_pair_ext[:, margin + group_rows :].astype(jnp.bfloat16), "dp", 1
        ).astype(jnp.float32)
        grad_pair = grad_pair_ext[:, margin : margin + group_rows]
        grad_pair = (
            grad_pair.at[:, group_rows - margin :].add(from_next).at[:, :margin].add(from_prev)
        )
        grad_triple = jnp.concatenate(
            [grad_query.astype(jnp.bfloat16)[None], grad_pair.astype(jnp.bfloat16)], axis=0
        )
        qkv_grad = jnp.moveaxis(
            scatter_rows(
                jnp.einsum(
                    "gd,sge->dse", normed_full, grad_triple, preferred_element_type=jnp.float32
                )
            ),
            0,
            1,
        )
        triple_sums = jnp.sum(grad_triple.astype(jnp.float32), axis=1)

        def first_term(first_row, row_count):
            return jnp.einsum(
                "sge,sde->gd", grad_triple, qkv_full, preferred_element_type=jnp.float32
            )

        grad_first = sum_backward(first_term, tok_rows)
        first_again, first_pull = jax.vjp(layer_norm, stream_in, gain_now[0], shift_now[0])
        grad_in_norm, gain_zero, shift_zero = first_pull(grad_first)
        gradient = grad_middle + grad_in_norm
        unit_grads[layer_index] = jnp.concatenate(
            [triple_sums[0][None], triple_sums[2][None], up_bias_grad], axis=0
        )
        gain_grads[layer_index] = jnp.stack([gain_zero, gain_one])
        shift_grads[layer_index] = jnp.stack([shift_zero, shift_one, shift_two, shift_three])
        local_qkv[layer_index] = qkv_grad
        local_out[layer_index] = out_grad
        local_up[layer_index] = up_grad
        local_down[layer_index] = down_grad
    grad_qkv = jnp.stack(local_qkv).astype(jnp.float32)
    grad_out = jnp.stack(local_out).astype(jnp.float32)
    grad_up = jnp.stack(local_up).astype(jnp.float32)
    grad_down = jnp.stack(local_down).astype(jnp.float32)
    unit_local = jnp.stack(unit_grads)
    unit_wide = jnp.zeros((LAYERS, unit_local.shape[1], cols_here * tensor_size), jnp.float32)
    unit_wide = lax.dynamic_update_slice_in_dim(unit_wide, unit_local, tensor_index * cols_here, 2)
    small = jnp.concatenate(
        [jnp.stack(gain_grads), jnp.stack(shift_grads), unit_wide], axis=1
    )
    small_total = lax.psum(small, ("dp", "tensor"))
    gain_total = small_total[:, :2]
    shift_total = small_total[:, 2:6]
    unit_total = small_total[:, 6:]
    unit_mine = lax.dynamic_slice_in_dim(unit_total, tensor_index * cols_here, cols_here, 2)
    return (
        stream.astype(jnp.bfloat16),
        gradient.astype(jnp.bfloat16),
        grad_qkv,
        grad_out,
        grad_up,
        grad_down,
        unit_mine,
        gain_total,
        shift_total,
    )


def solution(mesh):
    placed = (
        P(("dp", "tensor"), None),
        P(),
        P(),
        P(None, None, "dp", "tensor"),
        P(None, "dp", "tensor"),
        P(None, "dp", None, "tensor"),
        P(None, "dp", None, "tensor"),
        P(None, None, "tensor"),
        P(),
        P(),
        P(("dp", "tensor"), None),
    )
    return jax.shard_map(
        local,
        mesh=mesh,
        in_specs=placed,
        out_specs=(
            P(("dp", "tensor"), None),
            P(("dp", "tensor"), None),
            P(None, None, "dp", "tensor"),
            P(None, "dp", "tensor"),
            P(None, "dp", None, "tensor"),
            P(None, "dp", None, "tensor"),
            P(None, None, "tensor"),
            P(),
            P(),
        ),
        check_vma=False,
    )
```

```python
import math

import jax
import jax.numpy as jnp
from jax import lax
from jax.sharding import PartitionSpec as P

LAYERS = 1
IMG = 577
HD = 64


norm_eps = 1e-06
masked_score = -1e30


def from_everyone(value, axis):
    devices = lax.axis_size(axis)
    return lax.all_to_all(
        jnp.broadcast_to(value[None], (devices, *value.shape)), axis, 0, 0, tiled=True
    )


def joined_along(parts, dim):
    dims = list(parts.shape[1:])
    dims[dim] *= parts.shape[0]
    return jnp.moveaxis(parts, 0, dim).reshape(dims)


def collect(value, axis, dim):
    parts = from_everyone(value, axis)
    return joined_along(parts, dim)


def split_up(value, dim, devices):
    dims = value.shape
    parts = value.reshape(*dims[:dim], devices, dims[dim] // devices, *dims[dim + 1 :])
    return jnp.moveaxis(parts, dim, 0)


def summed_on_arrival(value, axis, dim):
    devices = lax.axis_size(axis)
    parts = lax.all_to_all(split_up(value, dim, devices), axis, 0, 0, tiled=True)
    return jnp.sum(parts.astype(jnp.float32), axis=0)


def rows_first(arrays, axis, dims):
    turned = [jnp.moveaxis(a, dim, 0) for a, dim in zip(arrays, dims)]
    both = jnp.concatenate([t.reshape(len(t), -1) for t in turned], axis=1)
    filled, at, outs = (lax.all_gather(both, axis, axis=0, tiled=True), 0, [])
    for t, dim in zip(turned, dims):
        slab = filled[:, at : at + t[0].size].reshape(-1, *t.shape[1:])
        outs.append(jnp.moveaxis(slab, 0, dim))
        at += t[0].size
    return tuple(outs)


def with_halo(value, sides, width):
    for axis, dim in sides:
        devices, length = (lax.axis_size(axis), value.shape[dim])
        up = [(i, (i + 1) % devices) for i in range(devices - 1)]
        down = [(j, i) for i, j in up]
        last = lax.slice_in_dim(value, length - width, length, axis=dim)
        initial = lax.slice_in_dim(value, 0, width, axis=dim)
        before = lax.ppermute(last, axis, up)
        after = lax.ppermute(initial, axis, down)
        value = jnp.concatenate([before, value, after], axis=dim)
    return value


def from_behind(block, axis, distance):
    devices = range(lax.axis_size(axis))
    route = [(i - distance, i) for i in devices if i - distance in devices]
    return lax.ppermute(block, axis, route)


def side_by_side(arrays, axis, dim, along):
    widths = [math.prod(a.shape[along:]) for a in arrays]
    both = jnp.concatenate(
        [a.reshape(*a.shape[:along], w) for a, w in zip(arrays, widths)], axis=along
    )
    filled = lax.psum_scatter(both, axis, scatter_dimension=dim, tiled=True)
    parts = jnp.split(filled, [sum(widths[:k]) for k in range(1, len(widths))], axis=along)
    return tuple(
        (b.reshape(*filled.shape[:along], *a.shape[along:]) for a, b in zip(arrays, parts))
    )


def scatter_rows(grad):
    return summed_on_arrival(grad.astype(jnp.bfloat16), "dp", 0)


def layer_norm(values, gain_row, shift_row):
    center = values - jnp.mean(values, axis=-1, keepdims=True)
    spread = jnp.mean(center * center, axis=-1, keepdims=True)
    return center * lax.rsqrt(spread + norm_eps) * gain_row + shift_row


def exact_gelu(values):
    return jax.nn.gelu(values, approximate=False)


def gather_forward(values):
    return collect(values, "tensor", 0)


def gather_backward(values):
    return collect(values, "tensor", 0)


def sum_forward(product, tok_rows):
    return summed_on_arrival(
        product(jnp.int32(0), tok_rows * lax.axis_size("tensor")).astype(jnp.bfloat16), "tensor", 0
    )


def sum_backward(product, tok_rows):
    return summed_on_arrival(
        product(jnp.int32(0), tok_rows * lax.axis_size("tensor")).astype(jnp.bfloat16), "tensor", 0
    )


def head_scores(query_head, key_head, allowed):
    raw = lax.dot_general(
        query_head, key_head, (((1,), (1,)), ((), ())), preferred_element_type=jnp.float32
    )
    return jnp.where(allowed, raw * HD ** (-0.5), masked_score)


def split_heads(queries, key_ext):
    heads_here = queries.shape[1] // HD
    query_heads = queries.reshape(queries.shape[0], heads_here, HD)
    key_heads = key_ext[0].reshape(key_ext.shape[1], heads_here, HD)
    value_heads = key_ext[1].reshape(key_ext.shape[1], heads_here, HD)
    return (heads_here, query_heads, key_heads, value_heads)


def merge_heads(per_head):
    return jnp.transpose(per_head, (1, 0, 2)).reshape(
        per_head.shape[1], per_head.shape[0] * per_head.shape[2]
    )


def attend_forward(queries, key_ext, allowed):
    heads_here, query_heads, key_heads, value_heads = split_heads(queries, key_ext)

    def one_head(head_index):
        query_head = lax.dynamic_index_in_dim(query_heads, head_index, 1, keepdims=False)
        key_head = lax.dynamic_index_in_dim(key_heads, head_index, 1, keepdims=False)
        value_head = lax.dynamic_index_in_dim(value_heads, head_index, 1, keepdims=False)
        scores = head_scores(query_head, key_head, allowed)
        row_top = jnp.max(scores, axis=1, keepdims=True)
        exponent = jnp.exp(scores - row_top)
        row_total = jnp.sum(exponent, axis=1, keepdims=True)
        prob_low = (exponent / row_total).astype(jnp.bfloat16)
        head_out = jnp.dot(prob_low, value_head, preferred_element_type=jnp.float32)
        return (head_out, (row_top + jnp.log(row_total))[:, 0])

    head_outs, log_norm = lax.map(one_head, jnp.arange(heads_here, dtype=jnp.int32))
    return (merge_heads(head_outs), log_norm)


def attend_backward(queries, key_ext, allowed, log_norm, grad_attended):
    heads_here, query_heads, key_heads, value_heads = split_heads(queries, key_ext)
    grad_heads = grad_attended.reshape(grad_attended.shape[0], heads_here, HD)

    def one_head(inputs):
        head_index, norm_row = inputs
        query_head = lax.dynamic_index_in_dim(query_heads, head_index, 1, keepdims=False)
        key_head = lax.dynamic_index_in_dim(key_heads, head_index, 1, keepdims=False)
        value_head = lax.dynamic_index_in_dim(value_heads, head_index, 1, keepdims=False)
        grad_head = lax.dynamic_index_in_dim(grad_heads, head_index, 1, keepdims=False)
        prob_full = jnp.exp(head_scores(query_head, key_head, allowed) - norm_row[:, None])
        prob_low = prob_full.astype(jnp.bfloat16)
        grad_value = lax.dot_general(
            prob_low, grad_head, (((0,), (0,)), ((), ())), preferred_element_type=jnp.float32
        )
        grad_prob = lax.dot_general(
            grad_head, value_head, (((1,), (1,)), ((), ())), preferred_element_type=jnp.float32
        )
        grad_score = (
            prob_full * (grad_prob - jnp.sum(prob_full * grad_prob, axis=1, keepdims=True))
        ).astype(jnp.bfloat16)
        grad_query = jnp.dot(grad_score, key_head, preferred_element_type=jnp.float32) * HD ** (
            -0.5
        )
        grad_key = lax.dot_general(
            grad_score, query_head, (((0,), (0,)), ((), ())), preferred_element_type=jnp.float32
        ) * HD ** (-0.5)
        return (grad_query, grad_key, grad_value)

    grad_queries, grad_keys, grad_values = lax.map(
        one_head, (jnp.arange(heads_here, dtype=jnp.int32), log_norm)
    )
    return (merge_heads(grad_queries), merge_heads(grad_keys), merge_heads(grad_values))


def local(
    tokens,
    segment,
    real_token,
    qkv_weight,
    out_weight,
    up_weight,
    down_weight,
    unit_bias,
    norm_gain,
    row_bias,
    cotangent,
):
    tok_rows = tokens.shape[0]
    tensor_size = lax.axis_size("tensor")
    group_rows = tok_rows * tensor_size
    margin = IMG - 1
    cols_here = qkv_weight.shape[3]
    dp_index = lax.axis_index("dp")
    tensor_index = lax.axis_index("tensor")
    group_first = dp_index * group_rows
    own_first = group_first + tensor_index * tok_rows
    segment_pad = jnp.pad(segment, (margin, margin), constant_values=-1)
    real_pad = jnp.pad(real_token, (margin, margin))
    segment_query = lax.dynamic_slice_in_dim(segment, group_first, group_rows, 0)
    segment_key = lax.dynamic_slice_in_dim(segment_pad, group_first, group_rows + 2 * margin, 0)
    real_key = lax.dynamic_slice_in_dim(real_pad, group_first, group_rows + 2 * margin, 0)
    place_query = jnp.arange(group_rows, dtype=jnp.int32)
    place_key = jnp.arange(group_rows + 2 * margin, dtype=jnp.int32) - margin
    allowed = (segment_query[:, None] == segment_key[None, :]) & (
        (real_key[None, :] == 1) | (place_query[:, None] == place_key[None, :])
    )
    own_real = lax.dynamic_slice_in_dim(real_token, own_first, tok_rows, 0).astype(jnp.float32)
    stream = tokens.astype(jnp.float32)
    layer_index = 0
    qkv_full = jnp.moveaxis(collect(jnp.moveaxis(qkv_weight[layer_index], 1, 0), "dp", 0), 0, 1)
    out_full = collect(out_weight[layer_index], "dp", 0)
    up_full = collect(up_weight[layer_index], "dp", 0)
    down_full = collect(down_weight[layer_index], "dp", 0)
    gathered = (qkv_full, out_full, up_full, down_full)
    gain_now = norm_gain[layer_index].astype(jnp.float32)
    shift_now = row_bias[layer_index].astype(jnp.float32)
    bias_now = unit_bias[layer_index].astype(jnp.float32)
    normed_full = gather_forward(layer_norm(stream, gain_now[0], shift_now[0]).astype(jnp.bfloat16))
    projected = jnp.einsum("gd,sde->sge", normed_full, qkv_full, preferred_element_type=jnp.float32)
    queries = (projected[0] + bias_now[0]).astype(jnp.bfloat16)
    key_value = jnp.stack([projected[1], projected[2] + bias_now[1]]).astype(jnp.bfloat16)
    key_ext = with_halo(key_value, (("dp", 1),), margin)
    attended, log_norm = attend_forward(queries, key_ext, allowed)
    attended = attended.astype(jnp.bfloat16)

    def attention_term(first_row, row_count):
        return lax.dot_general(
            attended, out_full, (((1,), (1,)), ((), ())), preferred_element_type=jnp.float32
        )

    middle = stream + sum_forward(attention_term, tok_rows) + shift_now[1]
    second_full = gather_forward(layer_norm(middle, gain_now[1], shift_now[2]).astype(jnp.bfloat16))
    hidden = (
        jnp.einsum("gd,dre->gre", second_full, up_full, preferred_element_type=jnp.float32)
        + bias_now[2:][None]
    )
    active = exact_gelu(hidden).astype(jnp.bfloat16)

    def feed_term(first_row, row_count):
        return jnp.einsum("gre,ore->go", active, down_full, preferred_element_type=jnp.float32)

    kept_weights = gathered
    records = [
        (
            stream,
            middle,
            normed_full,
            second_full,
            queries,
            key_ext,
            log_norm,
            attended,
            hidden,
            active,
            kept_weights,
        )
    ]
    stream = middle + sum_forward(feed_term, tok_rows) + shift_now[3]
    gradient = cotangent.astype(jnp.float32) * own_real[:, None]
    local_qkv = [None] * LAYERS
    local_out = [None] * LAYERS
    local_up = [None] * LAYERS
    local_down = [None] * LAYERS
    unit_grads = [None] * LAYERS
    gain_grads = [None] * LAYERS
    shift_grads = [None] * LAYERS
    for layer_index in reversed(range(LAYERS)):
        (
            stream_in,
            middle,
            normed_full,
            second_full,
            queries,
            key_ext,
            log_norm,
            attended,
            hidden,
            active,
            kept_weights,
        ) = records[layer_index]
        qkv_full, out_full, up_full, down_full = kept_weights
        gain_now = norm_gain[layer_index].astype(jnp.float32)
        shift_now = row_bias[layer_index].astype(jnp.float32)
        shift_three = jnp.sum(gradient, axis=0)
        grad_mlp = gather_backward(gradient.astype(jnp.bfloat16))
        down_grad = scatter_rows(
            jnp.einsum("go,gre->ore", grad_mlp, active, preferred_element_type=jnp.float32)
        )
        grad_active = jnp.einsum(
            "go,ore->gre", grad_mlp, down_full, preferred_element_type=jnp.float32
        )
        gelu_again, gelu_pull = jax.vjp(exact_gelu, hidden)
        grad_hidden = gelu_pull(grad_active)[0].astype(jnp.bfloat16)
        up_bias_grad = jnp.sum(grad_hidden.astype(jnp.float32), axis=0)
        up_grad = scatter_rows(
            jnp.einsum("gd,gre->dre", second_full, grad_hidden, preferred_element_type=jnp.float32)
        )

        def second_term(first_row, row_count):
            return jnp.einsum(
                "gre,dre->gd", grad_hidden, up_full, preferred_element_type=jnp.float32
            )

        grad_second = sum_backward(second_term, tok_rows)
        second_again, second_pull = jax.vjp(layer_norm, middle, gain_now[1], shift_now[2])
        grad_mid_norm, gain_one, shift_two = second_pull(grad_second)
        grad_middle = gradient + grad_mid_norm
        shift_one = jnp.sum(grad_middle, axis=0)
        grad_proj = gather_backward(grad_middle.astype(jnp.bfloat16))
        out_grad = scatter_rows(
            lax.dot_general(
                grad_proj, attended, (((0,), (0,)), ((), ())), preferred_element_type=jnp.float32
            )
        )
        grad_attended = jnp.dot(grad_proj, out_full, preferred_element_type=jnp.float32).astype(
            jnp.bfloat16
        )
        grad_query, grad_key_ext, grad_value_ext = attend_backward(
            queries, key_ext, allowed, log_norm, grad_attended
        )
        grad_pair_ext = jnp.stack([grad_key_ext, grad_value_ext])
        from_next = from_behind(grad_pair_ext[:, :margin].astype(jnp.bfloat16), "dp", -1).astype(
            jnp.float32
        )
        from_prev = from_behind(
            grad_pair_ext[:, margin + group_rows :].astype(jnp.bfloat16), "dp", 1
        ).astype(jnp.float32)
        grad_pair = grad_pair_ext[:, margin : margin + group_rows]
        grad_pair = (
            grad_pair.at[:, group_rows - margin :].add(from_next).at[:, :margin].add(from_prev)
        )
        grad_triple = jnp.concatenate(
            [grad_query.astype(jnp.bfloat16)[None], grad_pair.astype(jnp.bfloat16)], axis=0
        )
        qkv_grad = jnp.moveaxis(
            scatter_rows(
                jnp.einsum(
                    "gd,sge->dse", normed_full, grad_triple, preferred_element_type=jnp.float32
                )
            ),
            0,
            1,
        )
        triple_sums = jnp.sum(grad_triple.astype(jnp.float32), axis=1)

        def first_term(first_row, row_count):
            return jnp.einsum(
                "sge,sde->gd", grad_triple, qkv_full, preferred_element_type=jnp.float32
            )

        grad_first = sum_backward(first_term, tok_rows)
        first_again, first_pull = jax.vjp(layer_norm, stream_in, gain_now[0], shift_now[0])
        grad_in_norm, gain_zero, shift_zero = first_pull(grad_first)
        gradient = grad_middle + grad_in_norm
        unit_grads[layer_index] = jnp.concatenate(
            [triple_sums[0][None], triple_sums[2][None], up_bias_grad], axis=0
        )
        gain_grads[layer_index] = jnp.stack([gain_zero, gain_one])
        shift_grads[layer_index] = jnp.stack([shift_zero, shift_one, shift_two, shift_three])
        local_qkv[layer_index] = qkv_grad
        local_out[layer_index] = out_grad
        local_up[layer_index] = up_grad
        local_down[layer_index] = down_grad
    grad_qkv = jnp.stack(local_qkv).astype(jnp.float32)
    grad_out = jnp.stack(local_out).astype(jnp.float32)
    grad_up = jnp.stack(local_up).astype(jnp.float32)
    grad_down = jnp.stack(local_down).astype(jnp.float32)
    unit_local = jnp.stack(unit_grads)
    unit_wide = jnp.zeros((LAYERS, unit_local.shape[1], cols_here * tensor_size), jnp.float32)
    unit_wide = lax.dynamic_update_slice_in_dim(unit_wide, unit_local, tensor_index * cols_here, 2)
    small = jnp.concatenate(
        [jnp.stack(gain_grads), jnp.stack(shift_grads), unit_wide], axis=1
    )
    small_total = jnp.sum(from_everyone(small, "dp"), axis=0)
    small_total = jnp.sum(from_everyone(small_total, "tensor"), axis=0)
    gain_total = small_total[:, :2]
    shift_total = small_total[:, 2:6]
    unit_total = small_total[:, 6:]
    unit_mine = lax.dynamic_slice_in_dim(unit_total, tensor_index * cols_here, cols_here, 2)
    return (
        stream.astype(jnp.bfloat16),
        gradient.astype(jnp.bfloat16),
        grad_qkv,
        grad_out,
        grad_up,
        grad_down,
        unit_mine,
        gain_total,
        shift_total,
    )


def solution(mesh):
    placed = (
        P(("dp", "tensor"), None),
        P(),
        P(),
        P(None, None, "dp", "tensor"),
        P(None, "dp", "tensor"),
        P(None, "dp", None, "tensor"),
        P(None, "dp", None, "tensor"),
        P(None, None, "tensor"),
        P(),
        P(),
        P(("dp", "tensor"), None),
    )
    return jax.shard_map(
        local,
        mesh=mesh,
        in_specs=placed,
        out_specs=(
            P(("dp", "tensor"), None),
            P(("dp", "tensor"), None),
            P(None, None, "dp", "tensor"),
            P(None, "dp", "tensor"),
            P(None, "dp", None, "tensor"),
            P(None, "dp", None, "tensor"),
            P(None, None, "tensor"),
            P(),
            P(),
        ),
        check_vma=False,
    )
```

```python
import math

import jax
import jax.numpy as jnp
from jax import lax
from jax.sharding import PartitionSpec as P

LAYERS = 1
IMG = 577
HD = 64


norm_eps = 1e-06
masked_score = -1e30


def from_everyone(value, axis):
    devices = lax.axis_size(axis)
    return lax.all_to_all(
        jnp.broadcast_to(value[None], (devices, *value.shape)), axis, 0, 0, tiled=True
    )


def joined_along(parts, dim):
    dims = list(parts.shape[1:])
    dims[dim] *= parts.shape[0]
    return jnp.moveaxis(parts, 0, dim).reshape(dims)


def collect(value, axis, dim):
    parts = from_everyone(value, axis)
    return joined_along(parts, dim)


def split_up(value, dim, devices):
    dims = value.shape
    parts = value.reshape(*dims[:dim], devices, dims[dim] // devices, *dims[dim + 1 :])
    return jnp.moveaxis(parts, dim, 0)


def summed_on_arrival(value, axis, dim):
    devices = lax.axis_size(axis)
    parts = lax.all_to_all(split_up(value, dim, devices), axis, 0, 0, tiled=True)
    return jnp.sum(parts.astype(jnp.float32), axis=0)


def rows_first(arrays, axis, dims):
    turned = [jnp.moveaxis(a, dim, 0) for a, dim in zip(arrays, dims)]
    both = jnp.concatenate([t.reshape(len(t), -1) for t in turned], axis=1)
    filled, at, outs = (lax.all_gather(both, axis, axis=0, tiled=True), 0, [])
    for t, dim in zip(turned, dims):
        slab = filled[:, at : at + t[0].size].reshape(-1, *t.shape[1:])
        outs.append(jnp.moveaxis(slab, 0, dim))
        at += t[0].size
    return tuple(outs)


def with_halo(value, sides, width):
    for axis, dim in sides:
        devices, length = (lax.axis_size(axis), value.shape[dim])
        up = [(i, (i + 1) % devices) for i in range(devices - 1)]
        down = [(j, i) for i, j in up]
        last = lax.slice_in_dim(value, length - width, length, axis=dim)
        initial = lax.slice_in_dim(value, 0, width, axis=dim)
        before = lax.ppermute(last, axis, up)
        after = lax.ppermute(initial, axis, down)
        value = jnp.concatenate([before, value, after], axis=dim)
    return value


def from_behind(block, axis, distance):
    devices = range(lax.axis_size(axis))
    route = [(i - distance, i) for i in devices if i - distance in devices]
    return lax.ppermute(block, axis, route)


def side_by_side(arrays, axis, dim, along):
    widths = [math.prod(a.shape[along:]) for a in arrays]
    both = jnp.concatenate(
        [a.reshape(*a.shape[:along], w) for a, w in zip(arrays, widths)], axis=along
    )
    filled = lax.psum_scatter(both, axis, scatter_dimension=dim, tiled=True)
    parts = jnp.split(filled, [sum(widths[:k]) for k in range(1, len(widths))], axis=along)
    return tuple(
        (b.reshape(*filled.shape[:along], *a.shape[along:]) for a, b in zip(arrays, parts))
    )


def scatter_rows(grad):
    return summed_on_arrival(grad.astype(jnp.bfloat16), "dp", 0)


def layer_norm(values, gain_row, shift_row):
    center = values - jnp.mean(values, axis=-1, keepdims=True)
    spread = jnp.mean(center * center, axis=-1, keepdims=True)
    return center * lax.rsqrt(spread + norm_eps) * gain_row + shift_row


def exact_gelu(values):
    return jax.nn.gelu(values, approximate=False)


def gather_forward(values):
    return collect(values, "tensor", 0)


def gather_backward(values):
    return collect(values, "tensor", 0)


def sum_forward(product, tok_rows):
    return summed_on_arrival(
        product(jnp.int32(0), tok_rows * lax.axis_size("tensor")).astype(jnp.bfloat16), "tensor", 0
    )


def sum_backward(product, tok_rows):
    return summed_on_arrival(
        product(jnp.int32(0), tok_rows * lax.axis_size("tensor")).astype(jnp.bfloat16), "tensor", 0
    )


def head_scores(query_head, key_head, allowed):
    raw = lax.dot_general(
        query_head, key_head, (((1,), (1,)), ((), ())), preferred_element_type=jnp.float32
    )
    return jnp.where(allowed, raw * HD ** (-0.5), masked_score)


def split_heads(queries, key_ext):
    heads_here = queries.shape[1] // HD
    query_heads = queries.reshape(queries.shape[0], heads_here, HD)
    key_heads = key_ext[0].reshape(key_ext.shape[1], heads_here, HD)
    value_heads = key_ext[1].reshape(key_ext.shape[1], heads_here, HD)
    return (heads_here, query_heads, key_heads, value_heads)


def merge_heads(per_head):
    return jnp.transpose(per_head, (1, 0, 2)).reshape(
        per_head.shape[1], per_head.shape[0] * per_head.shape[2]
    )


def attend_forward(queries, key_ext, allowed):
    heads_here, query_heads, key_heads, value_heads = split_heads(queries, key_ext)

    def one_head(head_index):
        query_head = lax.dynamic_index_in_dim(query_heads, head_index, 1, keepdims=False)
        key_head = lax.dynamic_index_in_dim(key_heads, head_index, 1, keepdims=False)
        value_head = lax.dynamic_index_in_dim(value_heads, head_index, 1, keepdims=False)
        scores = head_scores(query_head, key_head, allowed)
        row_top = jnp.max(scores, axis=1, keepdims=True)
        exponent = jnp.exp(scores - row_top)
        row_total = jnp.sum(exponent, axis=1, keepdims=True)
        prob_low = (exponent / row_total).astype(jnp.bfloat16)
        head_out = jnp.dot(prob_low, value_head, preferred_element_type=jnp.float32)
        return (head_out, (row_top + jnp.log(row_total))[:, 0])

    head_outs, log_norm = lax.map(one_head, jnp.arange(heads_here, dtype=jnp.int32))
    return (merge_heads(head_outs), log_norm)


def attend_backward(queries, key_ext, allowed, log_norm, grad_attended):
    heads_here, query_heads, key_heads, value_heads = split_heads(queries, key_ext)
    grad_heads = grad_attended.reshape(grad_attended.shape[0], heads_here, HD)

    def one_head(inputs):
        head_index, norm_row = inputs
        query_head = lax.dynamic_index_in_dim(query_heads, head_index, 1, keepdims=False)
        key_head = lax.dynamic_index_in_dim(key_heads, head_index, 1, keepdims=False)
        value_head = lax.dynamic_index_in_dim(value_heads, head_index, 1, keepdims=False)
        grad_head = lax.dynamic_index_in_dim(grad_heads, head_index, 1, keepdims=False)
        prob_full = jnp.exp(head_scores(query_head, key_head, allowed) - norm_row[:, None])
        prob_low = prob_full.astype(jnp.bfloat16)
        grad_value = lax.dot_general(
            prob_low, grad_head, (((0,), (0,)), ((), ())), preferred_element_type=jnp.float32
        )
        grad_prob = lax.dot_general(
            grad_head, value_head, (((1,), (1,)), ((), ())), preferred_element_type=jnp.float32
        )
        grad_score = (
            prob_full * (grad_prob - jnp.sum(prob_full * grad_prob, axis=1, keepdims=True))
        ).astype(jnp.bfloat16)
        grad_query = jnp.dot(grad_score, key_head, preferred_element_type=jnp.float32) * HD ** (
            -0.5
        )
        grad_key = lax.dot_general(
            grad_score, query_head, (((0,), (0,)), ((), ())), preferred_element_type=jnp.float32
        ) * HD ** (-0.5)
        return (grad_query, grad_key, grad_value)

    grad_queries, grad_keys, grad_values = lax.map(
        one_head, (jnp.arange(heads_here, dtype=jnp.int32), log_norm)
    )
    return (merge_heads(grad_queries), merge_heads(grad_keys), merge_heads(grad_values))


def local(
    tokens,
    segment,
    real_token,
    qkv_weight,
    out_weight,
    up_weight,
    down_weight,
    unit_bias,
    norm_gain,
    row_bias,
    cotangent,
):
    tok_rows = tokens.shape[0]
    tensor_size = lax.axis_size("tensor")
    group_rows = tok_rows * tensor_size
    margin = IMG - 1
    cols_here = qkv_weight.shape[3]
    dp_index = lax.axis_index("dp")
    tensor_index = lax.axis_index("tensor")
    group_first = dp_index * group_rows
    own_first = group_first + tensor_index * tok_rows
    segment_pad = jnp.pad(segment, (margin, margin), constant_values=-1)
    real_pad = jnp.pad(real_token, (margin, margin))
    segment_query = lax.dynamic_slice_in_dim(segment, group_first, group_rows, 0)
    segment_key = lax.dynamic_slice_in_dim(segment_pad, group_first, group_rows + 2 * margin, 0)
    real_key = lax.dynamic_slice_in_dim(real_pad, group_first, group_rows + 2 * margin, 0)
    place_query = jnp.arange(group_rows, dtype=jnp.int32)
    place_key = jnp.arange(group_rows + 2 * margin, dtype=jnp.int32) - margin
    allowed = (segment_query[:, None] == segment_key[None, :]) & (
        (real_key[None, :] == 1) | (place_query[:, None] == place_key[None, :])
    )
    own_real = lax.dynamic_slice_in_dim(real_token, own_first, tok_rows, 0).astype(jnp.float32)
    stream = tokens.astype(jnp.float32)
    layer_index = 0
    d_here = qkv_weight.shape[2]
    attn_rows = collect(
        jnp.concatenate(
            [
                jnp.moveaxis(qkv_weight[layer_index], 1, 0).reshape(d_here, 3 * cols_here),
                out_weight[layer_index],
            ],
            axis=1,
        ),
        "dp",
        0,
    )
    qkv_full = jnp.moveaxis(attn_rows[:, : 3 * cols_here].reshape(-1, 3, cols_here), 0, 1)
    out_full = attn_rows[:, 3 * cols_here :]
    ff_here = up_weight.shape[2] * cols_here
    ff_rows = collect(
        jnp.concatenate(
            [
                up_weight[layer_index].reshape(d_here, ff_here),
                down_weight[layer_index].reshape(d_here, ff_here),
            ],
            axis=1,
        ),
        "dp",
        0,
    )
    up_full = ff_rows[:, :ff_here].reshape(-1, up_weight.shape[2], cols_here)
    down_full = ff_rows[:, ff_here:].reshape(-1, up_weight.shape[2], cols_here)
    gathered = (qkv_full, out_full, up_full, down_full)
    gain_now = norm_gain[layer_index].astype(jnp.float32)
    shift_now = row_bias[layer_index].astype(jnp.float32)
    bias_now = unit_bias[layer_index].astype(jnp.float32)
    normed_full = gather_forward(layer_norm(stream, gain_now[0], shift_now[0]).astype(jnp.bfloat16))
    projected = jnp.einsum("gd,sde->sge", normed_full, qkv_full, preferred_element_type=jnp.float32)
    queries = (projected[0] + bias_now[0]).astype(jnp.bfloat16)
    key_value = jnp.stack([projected[1], projected[2] + bias_now[1]]).astype(jnp.bfloat16)
    key_ext = with_halo(key_value, (("dp", 1),), margin)
    attended, log_norm = attend_forward(queries, key_ext, allowed)
    attended = attended.astype(jnp.bfloat16)

    def attention_term(first_row, row_count):
        return lax.dot_general(
            attended, out_full, (((1,), (1,)), ((), ())), preferred_element_type=jnp.float32
        )

    middle = stream + sum_forward(attention_term, tok_rows) + shift_now[1]
    second_full = gather_forward(layer_norm(middle, gain_now[1], shift_now[2]).astype(jnp.bfloat16))
    hidden = (
        jnp.einsum("gd,dre->gre", second_full, up_full, preferred_element_type=jnp.float32)
        + bias_now[2:][None]
    )
    active = exact_gelu(hidden).astype(jnp.bfloat16)

    def feed_term(first_row, row_count):
        return jnp.einsum("gre,ore->go", active, down_full, preferred_element_type=jnp.float32)

    kept_weights = gathered
    records = [
        (
            stream,
            middle,
            normed_full,
            second_full,
            queries,
            key_ext,
            log_norm,
            attended,
            hidden,
            active,
            kept_weights,
        )
    ]
    stream = middle + sum_forward(feed_term, tok_rows) + shift_now[3]
    gradient = cotangent.astype(jnp.float32) * own_real[:, None]
    local_qkv = [None] * LAYERS
    local_out = [None] * LAYERS
    local_up = [None] * LAYERS
    local_down = [None] * LAYERS
    unit_grads = [None] * LAYERS
    gain_grads = [None] * LAYERS
    shift_grads = [None] * LAYERS
    for layer_index in reversed(range(LAYERS)):
        (
            stream_in,
            middle,
            normed_full,
            second_full,
            queries,
            key_ext,
            log_norm,
            attended,
            hidden,
            active,
            kept_weights,
        ) = records[layer_index]
        qkv_full, out_full, up_full, down_full = kept_weights
        gain_now = norm_gain[layer_index].astype(jnp.float32)
        shift_now = row_bias[layer_index].astype(jnp.float32)
        shift_three = jnp.sum(gradient, axis=0)
        grad_mlp = gather_backward(gradient.astype(jnp.bfloat16))
        down_local = jnp.einsum("go,gre->ore", grad_mlp, active, preferred_element_type=jnp.float32)
        grad_active = jnp.einsum(
            "go,ore->gre", grad_mlp, down_full, preferred_element_type=jnp.float32
        )
        gelu_again, gelu_pull = jax.vjp(exact_gelu, hidden)
        grad_hidden = gelu_pull(grad_active)[0].astype(jnp.bfloat16)
        up_bias_grad = jnp.sum(grad_hidden.astype(jnp.float32), axis=0)
        up_local = jnp.einsum(
            "gd,gre->dre", second_full, grad_hidden, preferred_element_type=jnp.float32
        )

        def second_term(first_row, row_count):
            return jnp.einsum(
                "gre,dre->gd", grad_hidden, up_full, preferred_element_type=jnp.float32
            )

        grad_second = sum_backward(second_term, tok_rows)
        second_again, second_pull = jax.vjp(layer_norm, middle, gain_now[1], shift_now[2])
        grad_mid_norm, gain_one, shift_two = second_pull(grad_second)
        grad_middle = gradient + grad_mid_norm
        shift_one = jnp.sum(grad_middle, axis=0)
        grad_proj = gather_backward(grad_middle.astype(jnp.bfloat16))
        out_local = lax.dot_general(
            grad_proj, attended, (((0,), (0,)), ((), ())), preferred_element_type=jnp.float32
        )
        rows_here = out_local.shape[0]
        ff_width = down_local.shape[1] * down_local.shape[2]
        packed = scatter_rows(
            jnp.concatenate(
                [
                    down_local.reshape(rows_here, ff_width),
                    up_local.reshape(rows_here, ff_width),
                    out_local,
                ],
                axis=1,
            )
        )
        down_grad = packed[:, :ff_width].reshape(-1, *down_local.shape[1:])
        up_grad = packed[:, ff_width : 2 * ff_width].reshape(-1, *up_local.shape[1:])
        out_grad = packed[:, 2 * ff_width :]
        grad_attended = jnp.dot(grad_proj, out_full, preferred_element_type=jnp.float32).astype(
            jnp.bfloat16
        )
        grad_query, grad_key_ext, grad_value_ext = attend_backward(
            queries, key_ext, allowed, log_norm, grad_attended
        )
        grad_pair_ext = jnp.stack([grad_key_ext, grad_value_ext])
        from_next = from_behind(grad_pair_ext[:, :margin].astype(jnp.bfloat16), "dp", -1).astype(
            jnp.float32
        )
        from_prev = from_behind(
            grad_pair_ext[:, margin + group_rows :].astype(jnp.bfloat16), "dp", 1
        ).astype(jnp.float32)
        grad_pair = grad_pair_ext[:, margin : margin + group_rows]
        grad_pair = (
            grad_pair.at[:, group_rows - margin :].add(from_next).at[:, :margin].add(from_prev)
        )
        grad_triple = jnp.concatenate(
            [grad_query.astype(jnp.bfloat16)[None], grad_pair.astype(jnp.bfloat16)], axis=0
        )
        qkv_grad = jnp.moveaxis(
            scatter_rows(
                jnp.einsum(
                    "gd,sge->dse", normed_full, grad_triple, preferred_element_type=jnp.float32
                )
            ),
            0,
            1,
        )
        triple_sums = jnp.sum(grad_triple.astype(jnp.float32), axis=1)

        def first_term(first_row, row_count):
            return jnp.einsum(
                "sge,sde->gd", grad_triple, qkv_full, preferred_element_type=jnp.float32
            )

        grad_first = sum_backward(first_term, tok_rows)
        first_again, first_pull = jax.vjp(layer_norm, stream_in, gain_now[0], shift_now[0])
        grad_in_norm, gain_zero, shift_zero = first_pull(grad_first)
        gradient = grad_middle + grad_in_norm
        unit_grads[layer_index] = jnp.concatenate(
            [triple_sums[0][None], triple_sums[2][None], up_bias_grad], axis=0
        )
        gain_grads[layer_index] = jnp.stack([gain_zero, gain_one])
        shift_grads[layer_index] = jnp.stack([shift_zero, shift_one, shift_two, shift_three])
        local_qkv[layer_index] = qkv_grad
        local_out[layer_index] = out_grad
        local_up[layer_index] = up_grad
        local_down[layer_index] = down_grad
    grad_qkv = jnp.stack(local_qkv).astype(jnp.float32)
    grad_out = jnp.stack(local_out).astype(jnp.float32)
    grad_up = jnp.stack(local_up).astype(jnp.float32)
    grad_down = jnp.stack(local_down).astype(jnp.float32)
    unit_local = jnp.stack(unit_grads)
    unit_wide = jnp.zeros((LAYERS, unit_local.shape[1], cols_here * tensor_size), jnp.float32)
    unit_wide = lax.dynamic_update_slice_in_dim(unit_wide, unit_local, tensor_index * cols_here, 2)
    small = jnp.concatenate(
        [jnp.stack(gain_grads), jnp.stack(shift_grads), unit_wide], axis=1
    )
    small_total = jnp.sum(from_everyone(small, "dp"), axis=0)
    small_total = jnp.sum(from_everyone(small_total, "tensor"), axis=0)
    gain_total = small_total[:, :2]
    shift_total = small_total[:, 2:6]
    unit_total = small_total[:, 6:]
    unit_mine = lax.dynamic_slice_in_dim(unit_total, tensor_index * cols_here, cols_here, 2)
    return (
        stream.astype(jnp.bfloat16),
        gradient.astype(jnp.bfloat16),
        grad_qkv,
        grad_out,
        grad_up,
        grad_down,
        unit_mine,
        gain_total,
        shift_total,
    )


def solution(mesh):
    placed = (
        P(("dp", "tensor"), None),
        P(),
        P(),
        P(None, None, "dp", "tensor"),
        P(None, "dp", "tensor"),
        P(None, "dp", None, "tensor"),
        P(None, "dp", None, "tensor"),
        P(None, None, "tensor"),
        P(),
        P(),
        P(("dp", "tensor"), None),
    )
    return jax.shard_map(
        local,
        mesh=mesh,
        in_specs=placed,
        out_specs=(
            P(("dp", "tensor"), None),
            P(("dp", "tensor"), None),
            P(None, None, "dp", "tensor"),
            P(None, "dp", "tensor"),
            P(None, "dp", None, "tensor"),
            P(None, "dp", None, "tensor"),
            P(None, None, "tensor"),
            P(),
            P(),
        ),
        check_vma=False,
    )
```

```python
import functools
import math

import jax
import jax.numpy as jnp
from jax import lax
from jax.experimental import pallas as pl
from jax.experimental.pallas import tpu as pltpu
from jax.sharding import PartitionSpec as P

MESH = pl.DeviceIdType.MESH

LAYERS = 1
IMG = 577
HD = 64


norm_eps = 1e-06
masked_score = -1e30


def from_everyone(value, axis):
    devices = lax.axis_size(axis)
    return lax.all_to_all(
        jnp.broadcast_to(value[None], (devices, *value.shape)), axis, 0, 0, tiled=True
    )


def joined_along(parts, dim):
    dims = list(parts.shape[1:])
    dims[dim] *= parts.shape[0]
    return jnp.moveaxis(parts, 0, dim).reshape(dims)


def collect(value, axis, dim):
    parts = from_everyone(value, axis)
    return joined_along(parts, dim)


def split_up(value, dim, devices):
    dims = value.shape
    parts = value.reshape(*dims[:dim], devices, dims[dim] // devices, *dims[dim + 1 :])
    return jnp.moveaxis(parts, dim, 0)


def summed_on_arrival(value, axis, dim):
    devices = lax.axis_size(axis)
    parts = lax.all_to_all(split_up(value, dim, devices), axis, 0, 0, tiled=True)
    return jnp.sum(parts.astype(jnp.float32), axis=0)


def rows_first(arrays, axis, dims):
    turned = [jnp.moveaxis(a, dim, 0) for a, dim in zip(arrays, dims)]
    both = jnp.concatenate([t.reshape(len(t), -1) for t in turned], axis=1)
    filled, at, outs = (lax.all_gather(both, axis, axis=0, tiled=True), 0, [])
    for t, dim in zip(turned, dims):
        slab = filled[:, at : at + t[0].size].reshape(-1, *t.shape[1:])
        outs.append(jnp.moveaxis(slab, 0, dim))
        at += t[0].size
    return tuple(outs)


def with_halo(value, sides, width):
    for axis, dim in sides:
        devices, length = (lax.axis_size(axis), value.shape[dim])
        up = [(i, (i + 1) % devices) for i in range(devices - 1)]
        down = [(j, i) for i, j in up]
        last = lax.slice_in_dim(value, length - width, length, axis=dim)
        initial = lax.slice_in_dim(value, 0, width, axis=dim)
        before = lax.ppermute(last, axis, up)
        after = lax.ppermute(initial, axis, down)
        value = jnp.concatenate([before, value, after], axis=dim)
    return value


def from_behind(block, axis, distance):
    devices = range(lax.axis_size(axis))
    route = [(i - distance, i) for i in devices if i - distance in devices]
    return lax.ppermute(block, axis, route)


def side_by_side(arrays, axis, dim, along):
    widths = [math.prod(a.shape[along:]) for a in arrays]
    both = jnp.concatenate(
        [a.reshape(*a.shape[:along], w) for a, w in zip(arrays, widths)], axis=along
    )
    filled = lax.psum_scatter(both, axis, scatter_dimension=dim, tiled=True)
    parts = jnp.split(filled, [sum(widths[:k]) for k in range(1, len(widths))], axis=along)
    return tuple(
        (b.reshape(*filled.shape[:along], *a.shape[along:]) for a, b in zip(arrays, parts))
    )


def scatter_rows(grad):
    return summed_on_arrival(grad.astype(jnp.bfloat16), "dp", 0)


def layer_norm(values, gain_row, shift_row):
    center = values - jnp.mean(values, axis=-1, keepdims=True)
    spread = jnp.mean(center * center, axis=-1, keepdims=True)
    return center * lax.rsqrt(spread + norm_eps) * gain_row + shift_row


def exact_gelu(values):
    return jax.nn.gelu(values, approximate=False)


def _gather_kernel(devices, x_ref, out_ref, send_sem, recv_sem):
    me = lax.axis_index("tensor")
    dp = lax.axis_index("dp")
    barrier = pltpu.get_barrier_semaphore()
    for step in range(1, devices):
        pl.semaphore_signal(
            barrier, inc=1, device_id=(dp, lax.rem(me + step, devices)), device_id_type=MESH
        )
    pl.semaphore_wait(barrier, devices - 1)
    copies = []
    for step in range(1, devices):
        copy = pltpu.make_async_remote_copy(
            src_ref=x_ref,
            dst_ref=out_ref.at[me],
            send_sem=send_sem.at[step - 1],
            recv_sem=recv_sem.at[step - 1],
            device_id=(dp, lax.rem(me + step, devices)),
            device_id_type=MESH,
        )
        copy.start()
        copies.append(copy)
    out_ref[me] = x_ref[...]
    for copy in copies:
        copy.wait()


def gather_rows(values):
    devices = lax.axis_size("tensor")
    rows, width = values.shape
    parts = pl.pallas_call(
        functools.partial(_gather_kernel, devices),
        out_shape=jax.ShapeDtypeStruct((devices, rows, width), values.dtype),
        in_specs=[pl.BlockSpec(memory_space=pltpu.VMEM)],
        out_specs=pl.BlockSpec(memory_space=pltpu.VMEM),
        scratch_shapes=[
            pltpu.SemaphoreType.DMA((devices - 1,)),
            pltpu.SemaphoreType.DMA((devices - 1,)),
        ],
        compiler_params=pltpu.CompilerParams(collective_id=0, has_side_effects=True),
    )(values)
    return parts.reshape(devices * rows, width)


def gather_forward(values):
    return gather_rows(values)


def gather_backward(values):
    return gather_rows(values)


def sum_forward(product, tok_rows):
    return summed_on_arrival(
        product(jnp.int32(0), tok_rows * lax.axis_size("tensor")).astype(jnp.bfloat16), "tensor", 0
    )


def sum_backward(product, tok_rows):
    return summed_on_arrival(
        product(jnp.int32(0), tok_rows * lax.axis_size("tensor")).astype(jnp.bfloat16), "tensor", 0
    )


def head_scores(query_head, key_head, allowed):
    raw = lax.dot_general(
        query_head, key_head, (((1,), (1,)), ((), ())), preferred_element_type=jnp.float32
    )
    return jnp.where(allowed, raw * HD ** (-0.5), masked_score)


def split_heads(queries, key_ext):
    heads_here = queries.shape[1] // HD
    query_heads = queries.reshape(queries.shape[0], heads_here, HD)
    key_heads = key_ext[0].reshape(key_ext.shape[1], heads_here, HD)
    value_heads = key_ext[1].reshape(key_ext.shape[1], heads_here, HD)
    return (heads_here, query_heads, key_heads, value_heads)


def merge_heads(per_head):
    return jnp.transpose(per_head, (1, 0, 2)).reshape(
        per_head.shape[1], per_head.shape[0] * per_head.shape[2]
    )


def attend_forward(queries, key_ext, allowed):
    heads_here, query_heads, key_heads, value_heads = split_heads(queries, key_ext)

    def one_head(head_index):
        query_head = lax.dynamic_index_in_dim(query_heads, head_index, 1, keepdims=False)
        key_head = lax.dynamic_index_in_dim(key_heads, head_index, 1, keepdims=False)
        value_head = lax.dynamic_index_in_dim(value_heads, head_index, 1, keepdims=False)
        scores = head_scores(query_head, key_head, allowed)
        row_top = jnp.max(scores, axis=1, keepdims=True)
        exponent = jnp.exp(scores - row_top)
        row_total = jnp.sum(exponent, axis=1, keepdims=True)
        prob_low = (exponent / row_total).astype(jnp.bfloat16)
        head_out = jnp.dot(prob_low, value_head, preferred_element_type=jnp.float32)
        return (head_out, (row_top + jnp.log(row_total))[:, 0])

    head_outs, log_norm = lax.map(one_head, jnp.arange(heads_here, dtype=jnp.int32))
    return (merge_heads(head_outs), log_norm)


def attend_backward(queries, key_ext, allowed, log_norm, grad_attended):
    heads_here, query_heads, key_heads, value_heads = split_heads(queries, key_ext)
    grad_heads = grad_attended.reshape(grad_attended.shape[0], heads_here, HD)

    def one_head(inputs):
        head_index, norm_row = inputs
        query_head = lax.dynamic_index_in_dim(query_heads, head_index, 1, keepdims=False)
        key_head = lax.dynamic_index_in_dim(key_heads, head_index, 1, keepdims=False)
        value_head = lax.dynamic_index_in_dim(value_heads, head_index, 1, keepdims=False)
        grad_head = lax.dynamic_index_in_dim(grad_heads, head_index, 1, keepdims=False)
        prob_full = jnp.exp(head_scores(query_head, key_head, allowed) - norm_row[:, None])
        prob_low = prob_full.astype(jnp.bfloat16)
        grad_value = lax.dot_general(
            prob_low, grad_head, (((0,), (0,)), ((), ())), preferred_element_type=jnp.float32
        )
        grad_prob = lax.dot_general(
            grad_head, value_head, (((1,), (1,)), ((), ())), preferred_element_type=jnp.float32
        )
        grad_score = (
            prob_full * (grad_prob - jnp.sum(prob_full * grad_prob, axis=1, keepdims=True))
        ).astype(jnp.bfloat16)
        grad_query = jnp.dot(grad_score, key_head, preferred_element_type=jnp.float32) * HD ** (
            -0.5
        )
        grad_key = lax.dot_general(
            grad_score, query_head, (((0,), (0,)), ((), ())), preferred_element_type=jnp.float32
        ) * HD ** (-0.5)
        return (grad_query, grad_key, grad_value)

    grad_queries, grad_keys, grad_values = lax.map(
        one_head, (jnp.arange(heads_here, dtype=jnp.int32), log_norm)
    )
    return (merge_heads(grad_queries), merge_heads(grad_keys), merge_heads(grad_values))


def local(
    tokens,
    segment,
    real_token,
    qkv_weight,
    out_weight,
    up_weight,
    down_weight,
    unit_bias,
    norm_gain,
    row_bias,
    cotangent,
):
    tok_rows = tokens.shape[0]
    tensor_size = lax.axis_size("tensor")
    group_rows = tok_rows * tensor_size
    margin = IMG - 1
    cols_here = qkv_weight.shape[3]
    dp_index = lax.axis_index("dp")
    tensor_index = lax.axis_index("tensor")
    group_first = dp_index * group_rows
    own_first = group_first + tensor_index * tok_rows
    segment_pad = jnp.pad(segment, (margin, margin), constant_values=-1)
    real_pad = jnp.pad(real_token, (margin, margin))
    segment_query = lax.dynamic_slice_in_dim(segment, group_first, group_rows, 0)
    segment_key = lax.dynamic_slice_in_dim(segment_pad, group_first, group_rows + 2 * margin, 0)
    real_key = lax.dynamic_slice_in_dim(real_pad, group_first, group_rows + 2 * margin, 0)
    place_query = jnp.arange(group_rows, dtype=jnp.int32)
    place_key = jnp.arange(group_rows + 2 * margin, dtype=jnp.int32) - margin
    allowed = (segment_query[:, None] == segment_key[None, :]) & (
        (real_key[None, :] == 1) | (place_query[:, None] == place_key[None, :])
    )
    own_real = lax.dynamic_slice_in_dim(real_token, own_first, tok_rows, 0).astype(jnp.float32)
    stream = tokens.astype(jnp.float32)
    layer_index = 0
    qkv_full = jnp.moveaxis(collect(jnp.moveaxis(qkv_weight[layer_index], 1, 0), "dp", 0), 0, 1)
    out_full = collect(out_weight[layer_index], "dp", 0)
    up_full = collect(up_weight[layer_index], "dp", 0)
    down_full = collect(down_weight[layer_index], "dp", 0)
    gathered = (qkv_full, out_full, up_full, down_full)
    gain_now = norm_gain[layer_index].astype(jnp.float32)
    shift_now = row_bias[layer_index].astype(jnp.float32)
    bias_now = unit_bias[layer_index].astype(jnp.float32)
    normed_full = gather_forward(layer_norm(stream, gain_now[0], shift_now[0]).astype(jnp.bfloat16))
    projected = jnp.einsum("gd,sde->sge", normed_full, qkv_full, preferred_element_type=jnp.float32)
    queries = (projected[0] + bias_now[0]).astype(jnp.bfloat16)
    key_value = jnp.stack([projected[1], projected[2] + bias_now[1]]).astype(jnp.bfloat16)
    key_ext = with_halo(key_value, (("dp", 1),), margin)
    attended, log_norm = attend_forward(queries, key_ext, allowed)
    attended = attended.astype(jnp.bfloat16)

    def attention_term(first_row, row_count):
        return lax.dot_general(
            attended, out_full, (((1,), (1,)), ((), ())), preferred_element_type=jnp.float32
        )

    middle = stream + sum_forward(attention_term, tok_rows) + shift_now[1]
    second_full = gather_forward(layer_norm(middle, gain_now[1], shift_now[2]).astype(jnp.bfloat16))
    hidden = (
        jnp.einsum("gd,dre->gre", second_full, up_full, preferred_element_type=jnp.float32)
        + bias_now[2:][None]
    )
    active = exact_gelu(hidden).astype(jnp.bfloat16)

    def feed_term(first_row, row_count):
        return jnp.einsum("gre,ore->go", active, down_full, preferred_element_type=jnp.float32)

    kept_weights = gathered
    records = [
        (
            stream,
            middle,
            normed_full,
            second_full,
            queries,
            key_ext,
            log_norm,
            attended,
            hidden,
            active,
            kept_weights,
        )
    ]
    stream = middle + sum_forward(feed_term, tok_rows) + shift_now[3]
    gradient = cotangent.astype(jnp.float32) * own_real[:, None]
    local_qkv = [None] * LAYERS
    local_out = [None] * LAYERS
    local_up = [None] * LAYERS
    local_down = [None] * LAYERS
    unit_grads = [None] * LAYERS
    gain_grads = [None] * LAYERS
    shift_grads = [None] * LAYERS
    for layer_index in reversed(range(LAYERS)):
        (
            stream_in,
            middle,
            normed_full,
            second_full,
            queries,
            key_ext,
            log_norm,
            attended,
            hidden,
            active,
            kept_weights,
        ) = records[layer_index]
        qkv_full, out_full, up_full, down_full = kept_weights
        gain_now = norm_gain[layer_index].astype(jnp.float32)
        shift_now = row_bias[layer_index].astype(jnp.float32)
        shift_three = jnp.sum(gradient, axis=0)
        grad_mlp = gather_backward(gradient.astype(jnp.bfloat16))
        down_grad = scatter_rows(
            jnp.einsum("go,gre->ore", grad_mlp, active, preferred_element_type=jnp.float32)
        )
        grad_active = jnp.einsum(
            "go,ore->gre", grad_mlp, down_full, preferred_element_type=jnp.float32
        )
        gelu_again, gelu_pull = jax.vjp(exact_gelu, hidden)
        grad_hidden = gelu_pull(grad_active)[0].astype(jnp.bfloat16)
        up_bias_grad = jnp.sum(grad_hidden.astype(jnp.float32), axis=0)
        up_grad = scatter_rows(
            jnp.einsum("gd,gre->dre", second_full, grad_hidden, preferred_element_type=jnp.float32)
        )

        def second_term(first_row, row_count):
            return jnp.einsum(
                "gre,dre->gd", grad_hidden, up_full, preferred_element_type=jnp.float32
            )

        grad_second = sum_backward(second_term, tok_rows)
        second_again, second_pull = jax.vjp(layer_norm, middle, gain_now[1], shift_now[2])
        grad_mid_norm, gain_one, shift_two = second_pull(grad_second)
        grad_middle = gradient + grad_mid_norm
        shift_one = jnp.sum(grad_middle, axis=0)
        grad_proj = gather_backward(grad_middle.astype(jnp.bfloat16))
        out_grad = scatter_rows(
            lax.dot_general(
                grad_proj, attended, (((0,), (0,)), ((), ())), preferred_element_type=jnp.float32
            )
        )
        grad_attended = jnp.dot(grad_proj, out_full, preferred_element_type=jnp.float32).astype(
            jnp.bfloat16
        )
        grad_query, grad_key_ext, grad_value_ext = attend_backward(
            queries, key_ext, allowed, log_norm, grad_attended
        )
        grad_pair_ext = jnp.stack([grad_key_ext, grad_value_ext])
        from_next = from_behind(grad_pair_ext[:, :margin].astype(jnp.bfloat16), "dp", -1).astype(
            jnp.float32
        )
        from_prev = from_behind(
            grad_pair_ext[:, margin + group_rows :].astype(jnp.bfloat16), "dp", 1
        ).astype(jnp.float32)
        grad_pair = grad_pair_ext[:, margin : margin + group_rows]
        grad_pair = (
            grad_pair.at[:, group_rows - margin :].add(from_next).at[:, :margin].add(from_prev)
        )
        grad_triple = jnp.concatenate(
            [grad_query.astype(jnp.bfloat16)[None], grad_pair.astype(jnp.bfloat16)], axis=0
        )
        qkv_grad = jnp.moveaxis(
            scatter_rows(
                jnp.einsum(
                    "gd,sge->dse", normed_full, grad_triple, preferred_element_type=jnp.float32
                )
            ),
            0,
            1,
        )
        triple_sums = jnp.sum(grad_triple.astype(jnp.float32), axis=1)

        def first_term(first_row, row_count):
            return jnp.einsum(
                "sge,sde->gd", grad_triple, qkv_full, preferred_element_type=jnp.float32
            )

        grad_first = sum_backward(first_term, tok_rows)
        first_again, first_pull = jax.vjp(layer_norm, stream_in, gain_now[0], shift_now[0])
        grad_in_norm, gain_zero, shift_zero = first_pull(grad_first)
        gradient = grad_middle + grad_in_norm
        unit_grads[layer_index] = jnp.concatenate(
            [triple_sums[0][None], triple_sums[2][None], up_bias_grad], axis=0
        )
        gain_grads[layer_index] = jnp.stack([gain_zero, gain_one])
        shift_grads[layer_index] = jnp.stack([shift_zero, shift_one, shift_two, shift_three])
        local_qkv[layer_index] = qkv_grad
        local_out[layer_index] = out_grad
        local_up[layer_index] = up_grad
        local_down[layer_index] = down_grad
    grad_qkv = jnp.stack(local_qkv).astype(jnp.float32)
    grad_out = jnp.stack(local_out).astype(jnp.float32)
    grad_up = jnp.stack(local_up).astype(jnp.float32)
    grad_down = jnp.stack(local_down).astype(jnp.float32)
    unit_local = jnp.stack(unit_grads)
    unit_wide = jnp.zeros((LAYERS, unit_local.shape[1], cols_here * tensor_size), jnp.float32)
    unit_wide = lax.dynamic_update_slice_in_dim(unit_wide, unit_local, tensor_index * cols_here, 2)
    small = jnp.concatenate(
        [jnp.stack(gain_grads), jnp.stack(shift_grads), unit_wide], axis=1
    )
    small_total = jnp.sum(from_everyone(small, "dp"), axis=0)
    small_total = jnp.sum(from_everyone(small_total, "tensor"), axis=0)
    gain_total = small_total[:, :2]
    shift_total = small_total[:, 2:6]
    unit_total = small_total[:, 6:]
    unit_mine = lax.dynamic_slice_in_dim(unit_total, tensor_index * cols_here, cols_here, 2)
    return (
        stream.astype(jnp.bfloat16),
        gradient.astype(jnp.bfloat16),
        grad_qkv,
        grad_out,
        grad_up,
        grad_down,
        unit_mine,
        gain_total,
        shift_total,
    )


def solution(mesh):
    placed = (
        P(("dp", "tensor"), None),
        P(),
        P(),
        P(None, None, "dp", "tensor"),
        P(None, "dp", "tensor"),
        P(None, "dp", None, "tensor"),
        P(None, "dp", None, "tensor"),
        P(None, None, "tensor"),
        P(),
        P(),
        P(("dp", "tensor"), None),
    )
    return jax.shard_map(
        local,
        mesh=mesh,
        in_specs=placed,
        out_specs=(
            P(("dp", "tensor"), None),
            P(("dp", "tensor"), None),
            P(None, None, "dp", "tensor"),
            P(None, "dp", "tensor"),
            P(None, "dp", None, "tensor"),
            P(None, "dp", None, "tensor"),
            P(None, None, "tensor"),
            P(),
            P(),
        ),
        check_vma=False,
    )
```

```python
import functools
import math

import jax
import jax.numpy as jnp
from jax import lax
from jax.experimental import pallas as pl
from jax.experimental.pallas import tpu as pltpu
from jax.sharding import PartitionSpec as P

MESH = pl.DeviceIdType.MESH

LAYERS = 1
IMG = 577
HD = 64


norm_eps = 1e-06
masked_score = -1e30


def from_everyone(value, axis):
    devices = lax.axis_size(axis)
    return lax.all_to_all(
        jnp.broadcast_to(value[None], (devices, *value.shape)), axis, 0, 0, tiled=True
    )


def joined_along(parts, dim):
    dims = list(parts.shape[1:])
    dims[dim] *= parts.shape[0]
    return jnp.moveaxis(parts, 0, dim).reshape(dims)


def collect(value, axis, dim):
    parts = from_everyone(value, axis)
    return joined_along(parts, dim)


def split_up(value, dim, devices):
    dims = value.shape
    parts = value.reshape(*dims[:dim], devices, dims[dim] // devices, *dims[dim + 1 :])
    return jnp.moveaxis(parts, dim, 0)


def summed_on_arrival(value, axis, dim):
    devices = lax.axis_size(axis)
    parts = lax.all_to_all(split_up(value, dim, devices), axis, 0, 0, tiled=True)
    return jnp.sum(parts.astype(jnp.float32), axis=0)


def rows_first(arrays, axis, dims):
    turned = [jnp.moveaxis(a, dim, 0) for a, dim in zip(arrays, dims)]
    both = jnp.concatenate([t.reshape(len(t), -1) for t in turned], axis=1)
    filled, at, outs = (lax.all_gather(both, axis, axis=0, tiled=True), 0, [])
    for t, dim in zip(turned, dims):
        slab = filled[:, at : at + t[0].size].reshape(-1, *t.shape[1:])
        outs.append(jnp.moveaxis(slab, 0, dim))
        at += t[0].size
    return tuple(outs)


def with_halo(value, sides, width):
    for axis, dim in sides:
        devices, length = (lax.axis_size(axis), value.shape[dim])
        up = [(i, (i + 1) % devices) for i in range(devices - 1)]
        down = [(j, i) for i, j in up]
        last = lax.slice_in_dim(value, length - width, length, axis=dim)
        initial = lax.slice_in_dim(value, 0, width, axis=dim)
        before = lax.ppermute(last, axis, up)
        after = lax.ppermute(initial, axis, down)
        value = jnp.concatenate([before, value, after], axis=dim)
    return value


def from_behind(block, axis, distance):
    devices = range(lax.axis_size(axis))
    route = [(i - distance, i) for i in devices if i - distance in devices]
    return lax.ppermute(block, axis, route)


def side_by_side(arrays, axis, dim, along):
    widths = [math.prod(a.shape[along:]) for a in arrays]
    both = jnp.concatenate(
        [a.reshape(*a.shape[:along], w) for a, w in zip(arrays, widths)], axis=along
    )
    filled = lax.psum_scatter(both, axis, scatter_dimension=dim, tiled=True)
    parts = jnp.split(filled, [sum(widths[:k]) for k in range(1, len(widths))], axis=along)
    return tuple(
        (b.reshape(*filled.shape[:along], *a.shape[along:]) for a, b in zip(arrays, parts))
    )


def scatter_rows(grad):
    return summed_on_arrival(grad.astype(jnp.bfloat16), "dp", 0)


def layer_norm(values, gain_row, shift_row):
    center = values - jnp.mean(values, axis=-1, keepdims=True)
    spread = jnp.mean(center * center, axis=-1, keepdims=True)
    return center * lax.rsqrt(spread + norm_eps) * gain_row + shift_row


def exact_gelu(values):
    return jax.nn.gelu(values, approximate=False)


def _gather_kernel(devices, x_ref, out_ref, send_sem, recv_sem):
    me = lax.axis_index("tensor")
    dp = lax.axis_index("dp")
    barrier = pltpu.get_barrier_semaphore()
    for step in range(1, devices):
        pl.semaphore_signal(
            barrier, inc=1, device_id=(dp, lax.rem(me + step, devices)), device_id_type=MESH
        )
    pl.semaphore_wait(barrier, devices - 1)
    copies = []
    for step in range(1, devices):
        copy = pltpu.make_async_remote_copy(
            src_ref=x_ref,
            dst_ref=out_ref.at[me],
            send_sem=send_sem.at[step - 1],
            recv_sem=recv_sem.at[step - 1],
            device_id=(dp, lax.rem(me + step, devices)),
            device_id_type=MESH,
        )
        copy.start()
        copies.append(copy)
    out_ref[me] = x_ref[...]
    for copy in copies:
        copy.wait()


def gather_rows(values):
    devices = lax.axis_size("tensor")
    rows, width = values.shape
    parts = pl.pallas_call(
        functools.partial(_gather_kernel, devices),
        out_shape=jax.ShapeDtypeStruct((devices, rows, width), values.dtype),
        in_specs=[pl.BlockSpec(memory_space=pltpu.VMEM)],
        out_specs=pl.BlockSpec(memory_space=pltpu.VMEM),
        scratch_shapes=[
            pltpu.SemaphoreType.DMA((devices - 1,)),
            pltpu.SemaphoreType.DMA((devices - 1,)),
        ],
        compiler_params=pltpu.CompilerParams(collective_id=0, has_side_effects=True),
    )(values)
    return parts.reshape(devices * rows, width)


def _exchange_kernel(devices, x_ref, out_ref, send_sem, recv_sem):
    me = lax.axis_index("tensor")
    dp = lax.axis_index("dp")
    barrier = pltpu.get_barrier_semaphore()
    for step in range(1, devices):
        pl.semaphore_signal(
            barrier, inc=1, device_id=(dp, lax.rem(me + step, devices)), device_id_type=MESH
        )
    pl.semaphore_wait(barrier, devices - 1)
    copies = []
    for step in range(1, devices):
        peer = lax.rem(me + step, devices)
        copy = pltpu.make_async_remote_copy(
            src_ref=x_ref.at[peer],
            dst_ref=out_ref.at[me],
            send_sem=send_sem.at[step - 1],
            recv_sem=recv_sem.at[step - 1],
            device_id=(dp, peer),
            device_id_type=MESH,
        )
        copy.start()
        copies.append(copy)
    out_ref[me] = x_ref[me]
    for copy in copies:
        copy.wait()


def exchange_rows(parts):
    devices = parts.shape[0]
    return pl.pallas_call(
        functools.partial(_exchange_kernel, devices),
        out_shape=jax.ShapeDtypeStruct(parts.shape, parts.dtype),
        in_specs=[pl.BlockSpec(memory_space=pltpu.VMEM)],
        out_specs=pl.BlockSpec(memory_space=pltpu.VMEM),
        scratch_shapes=[
            pltpu.SemaphoreType.DMA((devices - 1,)),
            pltpu.SemaphoreType.DMA((devices - 1,)),
        ],
        compiler_params=pltpu.CompilerParams(collective_id=1, has_side_effects=True),
    )(parts)


def summed_over_tensor(value):
    devices = lax.axis_size("tensor")
    parts = exchange_rows(split_up(value, 0, devices))
    return jnp.sum(parts.astype(jnp.float32), axis=0)


def gather_forward(values):
    return gather_rows(values)


def gather_backward(values):
    return gather_rows(values)


def sum_forward(product, tok_rows):
    return summed_over_tensor(
        product(jnp.int32(0), tok_rows * lax.axis_size("tensor")).astype(jnp.bfloat16)
    )


def sum_backward(product, tok_rows):
    return summed_over_tensor(
        product(jnp.int32(0), tok_rows * lax.axis_size("tensor")).astype(jnp.bfloat16)
    )


def head_scores(query_head, key_head, allowed):
    raw = lax.dot_general(
        query_head, key_head, (((1,), (1,)), ((), ())), preferred_element_type=jnp.float32
    )
    return jnp.where(allowed, raw * HD ** (-0.5), masked_score)


def split_heads(queries, key_ext):
    heads_here = queries.shape[1] // HD
    query_heads = queries.reshape(queries.shape[0], heads_here, HD)
    key_heads = key_ext[0].reshape(key_ext.shape[1], heads_here, HD)
    value_heads = key_ext[1].reshape(key_ext.shape[1], heads_here, HD)
    return (heads_here, query_heads, key_heads, value_heads)


def merge_heads(per_head):
    return jnp.transpose(per_head, (1, 0, 2)).reshape(
        per_head.shape[1], per_head.shape[0] * per_head.shape[2]
    )


def attend_forward(queries, key_ext, allowed):
    heads_here, query_heads, key_heads, value_heads = split_heads(queries, key_ext)

    def one_head(head_index):
        query_head = lax.dynamic_index_in_dim(query_heads, head_index, 1, keepdims=False)
        key_head = lax.dynamic_index_in_dim(key_heads, head_index, 1, keepdims=False)
        value_head = lax.dynamic_index_in_dim(value_heads, head_index, 1, keepdims=False)
        scores = head_scores(query_head, key_head, allowed)
        row_top = jnp.max(scores, axis=1, keepdims=True)
        exponent = jnp.exp(scores - row_top)
        row_total = jnp.sum(exponent, axis=1, keepdims=True)
        prob_low = (exponent / row_total).astype(jnp.bfloat16)
        head_out = jnp.dot(prob_low, value_head, preferred_element_type=jnp.float32)
        return (head_out, (row_top + jnp.log(row_total))[:, 0])

    head_outs, log_norm = lax.map(one_head, jnp.arange(heads_here, dtype=jnp.int32))
    return (merge_heads(head_outs), log_norm)


def attend_backward(queries, key_ext, allowed, log_norm, grad_attended):
    heads_here, query_heads, key_heads, value_heads = split_heads(queries, key_ext)
    grad_heads = grad_attended.reshape(grad_attended.shape[0], heads_here, HD)

    def one_head(inputs):
        head_index, norm_row = inputs
        query_head = lax.dynamic_index_in_dim(query_heads, head_index, 1, keepdims=False)
        key_head = lax.dynamic_index_in_dim(key_heads, head_index, 1, keepdims=False)
        value_head = lax.dynamic_index_in_dim(value_heads, head_index, 1, keepdims=False)
        grad_head = lax.dynamic_index_in_dim(grad_heads, head_index, 1, keepdims=False)
        prob_full = jnp.exp(head_scores(query_head, key_head, allowed) - norm_row[:, None])
        prob_low = prob_full.astype(jnp.bfloat16)
        grad_value = lax.dot_general(
            prob_low, grad_head, (((0,), (0,)), ((), ())), preferred_element_type=jnp.float32
        )
        grad_prob = lax.dot_general(
            grad_head, value_head, (((1,), (1,)), ((), ())), preferred_element_type=jnp.float32
        )
        grad_score = (
            prob_full * (grad_prob - jnp.sum(prob_full * grad_prob, axis=1, keepdims=True))
        ).astype(jnp.bfloat16)
        grad_query = jnp.dot(grad_score, key_head, preferred_element_type=jnp.float32) * HD ** (
            -0.5
        )
        grad_key = lax.dot_general(
            grad_score, query_head, (((0,), (0,)), ((), ())), preferred_element_type=jnp.float32
        ) * HD ** (-0.5)
        return (grad_query, grad_key, grad_value)

    grad_queries, grad_keys, grad_values = lax.map(
        one_head, (jnp.arange(heads_here, dtype=jnp.int32), log_norm)
    )
    return (merge_heads(grad_queries), merge_heads(grad_keys), merge_heads(grad_values))


def local(
    tokens,
    segment,
    real_token,
    qkv_weight,
    out_weight,
    up_weight,
    down_weight,
    unit_bias,
    norm_gain,
    row_bias,
    cotangent,
):
    tok_rows = tokens.shape[0]
    tensor_size = lax.axis_size("tensor")
    group_rows = tok_rows * tensor_size
    margin = IMG - 1
    cols_here = qkv_weight.shape[3]
    dp_index = lax.axis_index("dp")
    tensor_index = lax.axis_index("tensor")
    group_first = dp_index * group_rows
    own_first = group_first + tensor_index * tok_rows
    segment_pad = jnp.pad(segment, (margin, margin), constant_values=-1)
    real_pad = jnp.pad(real_token, (margin, margin))
    segment_query = lax.dynamic_slice_in_dim(segment, group_first, group_rows, 0)
    segment_key = lax.dynamic_slice_in_dim(segment_pad, group_first, group_rows + 2 * margin, 0)
    real_key = lax.dynamic_slice_in_dim(real_pad, group_first, group_rows + 2 * margin, 0)
    place_query = jnp.arange(group_rows, dtype=jnp.int32)
    place_key = jnp.arange(group_rows + 2 * margin, dtype=jnp.int32) - margin
    allowed = (segment_query[:, None] == segment_key[None, :]) & (
        (real_key[None, :] == 1) | (place_query[:, None] == place_key[None, :])
    )
    own_real = lax.dynamic_slice_in_dim(real_token, own_first, tok_rows, 0).astype(jnp.float32)
    stream = tokens.astype(jnp.float32)
    layer_index = 0
    qkv_full = jnp.moveaxis(collect(jnp.moveaxis(qkv_weight[layer_index], 1, 0), "dp", 0), 0, 1)
    out_full = collect(out_weight[layer_index], "dp", 0)
    up_full = collect(up_weight[layer_index], "dp", 0)
    down_full = collect(down_weight[layer_index], "dp", 0)
    gathered = (qkv_full, out_full, up_full, down_full)
    gain_now = norm_gain[layer_index].astype(jnp.float32)
    shift_now = row_bias[layer_index].astype(jnp.float32)
    bias_now = unit_bias[layer_index].astype(jnp.float32)
    normed_full = gather_forward(layer_norm(stream, gain_now[0], shift_now[0]).astype(jnp.bfloat16))
    projected = jnp.einsum("gd,sde->sge", normed_full, qkv_full, preferred_element_type=jnp.float32)
    queries = (projected[0] + bias_now[0]).astype(jnp.bfloat16)
    key_value = jnp.stack([projected[1], projected[2] + bias_now[1]]).astype(jnp.bfloat16)
    key_ext = with_halo(key_value, (("dp", 1),), margin)
    attended, log_norm = attend_forward(queries, key_ext, allowed)
    attended = attended.astype(jnp.bfloat16)

    def attention_term(first_row, row_count):
        return lax.dot_general(
            attended, out_full, (((1,), (1,)), ((), ())), preferred_element_type=jnp.float32
        )

    middle = stream + sum_forward(attention_term, tok_rows) + shift_now[1]
    second_full = gather_forward(layer_norm(middle, gain_now[1], shift_now[2]).astype(jnp.bfloat16))
    hidden = (
        jnp.einsum("gd,dre->gre", second_full, up_full, preferred_element_type=jnp.float32)
        + bias_now[2:][None]
    )
    active = exact_gelu(hidden).astype(jnp.bfloat16)

    def feed_term(first_row, row_count):
        return jnp.einsum("gre,ore->go", active, down_full, preferred_element_type=jnp.float32)

    kept_weights = gathered
    records = [
        (
            stream,
            middle,
            normed_full,
            second_full,
            queries,
            key_ext,
            log_norm,
            attended,
            hidden,
            active,
            kept_weights,
        )
    ]
    stream = middle + sum_forward(feed_term, tok_rows) + shift_now[3]
    gradient = cotangent.astype(jnp.float32) * own_real[:, None]
    local_qkv = [None] * LAYERS
    local_out = [None] * LAYERS
    local_up = [None] * LAYERS
    local_down = [None] * LAYERS
    unit_grads = [None] * LAYERS
    gain_grads = [None] * LAYERS
    shift_grads = [None] * LAYERS
    for layer_index in reversed(range(LAYERS)):
        (
            stream_in,
            middle,
            normed_full,
            second_full,
            queries,
            key_ext,
            log_norm,
            attended,
            hidden,
            active,
            kept_weights,
        ) = records[layer_index]
        qkv_full, out_full, up_full, down_full = kept_weights
        gain_now = norm_gain[layer_index].astype(jnp.float32)
        shift_now = row_bias[layer_index].astype(jnp.float32)
        shift_three = jnp.sum(gradient, axis=0)
        grad_mlp = gather_backward(gradient.astype(jnp.bfloat16))
        down_grad = scatter_rows(
            jnp.einsum("go,gre->ore", grad_mlp, active, preferred_element_type=jnp.float32)
        )
        grad_active = jnp.einsum(
            "go,ore->gre", grad_mlp, down_full, preferred_element_type=jnp.float32
        )
        gelu_again, gelu_pull = jax.vjp(exact_gelu, hidden)
        grad_hidden = gelu_pull(grad_active)[0].astype(jnp.bfloat16)
        up_bias_grad = jnp.sum(grad_hidden.astype(jnp.float32), axis=0)
        up_grad = scatter_rows(
            jnp.einsum("gd,gre->dre", second_full, grad_hidden, preferred_element_type=jnp.float32)
        )

        def second_term(first_row, row_count):
            return jnp.einsum(
                "gre,dre->gd", grad_hidden, up_full, preferred_element_type=jnp.float32
            )

        grad_second = sum_backward(second_term, tok_rows)
        second_again, second_pull = jax.vjp(layer_norm, middle, gain_now[1], shift_now[2])
        grad_mid_norm, gain_one, shift_two = second_pull(grad_second)
        grad_middle = gradient + grad_mid_norm
        shift_one = jnp.sum(grad_middle, axis=0)
        grad_proj = gather_backward(grad_middle.astype(jnp.bfloat16))
        out_grad = scatter_rows(
            lax.dot_general(
                grad_proj, attended, (((0,), (0,)), ((), ())), preferred_element_type=jnp.float32
            )
        )
        grad_attended = jnp.dot(grad_proj, out_full, preferred_element_type=jnp.float32).astype(
            jnp.bfloat16
        )
        grad_query, grad_key_ext, grad_value_ext = attend_backward(
            queries, key_ext, allowed, log_norm, grad_attended
        )
        grad_pair_ext = jnp.stack([grad_key_ext, grad_value_ext])
        from_next = from_behind(grad_pair_ext[:, :margin].astype(jnp.bfloat16), "dp", -1).astype(
            jnp.float32
        )
        from_prev = from_behind(
            grad_pair_ext[:, margin + group_rows :].astype(jnp.bfloat16), "dp", 1
        ).astype(jnp.float32)
        grad_pair = grad_pair_ext[:, margin : margin + group_rows]
        grad_pair = (
            grad_pair.at[:, group_rows - margin :].add(from_next).at[:, :margin].add(from_prev)
        )
        grad_triple = jnp.concatenate(
            [grad_query.astype(jnp.bfloat16)[None], grad_pair.astype(jnp.bfloat16)], axis=0
        )
        qkv_grad = jnp.moveaxis(
            scatter_rows(
                jnp.einsum(
                    "gd,sge->dse", normed_full, grad_triple, preferred_element_type=jnp.float32
                )
            ),
            0,
            1,
        )
        triple_sums = jnp.sum(grad_triple.astype(jnp.float32), axis=1)

        def first_term(first_row, row_count):
            return jnp.einsum(
                "sge,sde->gd", grad_triple, qkv_full, preferred_element_type=jnp.float32
            )

        grad_first = sum_backward(first_term, tok_rows)
        first_again, first_pull = jax.vjp(layer_norm, stream_in, gain_now[0], shift_now[0])
        grad_in_norm, gain_zero, shift_zero = first_pull(grad_first)
        gradient = grad_middle + grad_in_norm
        unit_grads[layer_index] = jnp.concatenate(
            [triple_sums[0][None], triple_sums[2][None], up_bias_grad], axis=0
        )
        gain_grads[layer_index] = jnp.stack([gain_zero, gain_one])
        shift_grads[layer_index] = jnp.stack([shift_zero, shift_one, shift_two, shift_three])
        local_qkv[layer_index] = qkv_grad
        local_out[layer_index] = out_grad
        local_up[layer_index] = up_grad
        local_down[layer_index] = down_grad
    grad_qkv = jnp.stack(local_qkv).astype(jnp.float32)
    grad_out = jnp.stack(local_out).astype(jnp.float32)
    grad_up = jnp.stack(local_up).astype(jnp.float32)
    grad_down = jnp.stack(local_down).astype(jnp.float32)
    unit_local = jnp.stack(unit_grads)
    unit_wide = jnp.zeros((LAYERS, unit_local.shape[1], cols_here * tensor_size), jnp.float32)
    unit_wide = lax.dynamic_update_slice_in_dim(unit_wide, unit_local, tensor_index * cols_here, 2)
    small = jnp.concatenate(
        [jnp.stack(gain_grads), jnp.stack(shift_grads), unit_wide], axis=1
    )
    small_total = jnp.sum(from_everyone(small, "dp"), axis=0)
    small_total = jnp.sum(from_everyone(small_total, "tensor"), axis=0)
    gain_total = small_total[:, :2]
    shift_total = small_total[:, 2:6]
    unit_total = small_total[:, 6:]
    unit_mine = lax.dynamic_slice_in_dim(unit_total, tensor_index * cols_here, cols_here, 2)
    return (
        stream.astype(jnp.bfloat16),
        gradient.astype(jnp.bfloat16),
        grad_qkv,
        grad_out,
        grad_up,
        grad_down,
        unit_mine,
        gain_total,
        shift_total,
    )


def solution(mesh):
    placed = (
        P(("dp", "tensor"), None),
        P(),
        P(),
        P(None, None, "dp", "tensor"),
        P(None, "dp", "tensor"),
        P(None, "dp", None, "tensor"),
        P(None, "dp", None, "tensor"),
        P(None, None, "tensor"),
        P(),
        P(),
        P(("dp", "tensor"), None),
    )
    return jax.shard_map(
        local,
        mesh=mesh,
        in_specs=placed,
        out_specs=(
            P(("dp", "tensor"), None),
            P(("dp", "tensor"), None),
            P(None, None, "dp", "tensor"),
            P(None, "dp", "tensor"),
            P(None, "dp", None, "tensor"),
            P(None, "dp", None, "tensor"),
            P(None, None, "tensor"),
            P(),
            P(),
        ),
        check_vma=False,
    )
```

```python
import functools
import math

import jax
import jax.numpy as jnp
from jax import lax
from jax.experimental import pallas as pl
from jax.experimental.pallas import tpu as pltpu
from jax.sharding import PartitionSpec as P

MESH = pl.DeviceIdType.MESH

LAYERS = 1
IMG = 577
HD = 64


norm_eps = 1e-06
masked_score = -1e30


def from_everyone(value, axis):
    devices = lax.axis_size(axis)
    return lax.all_to_all(
        jnp.broadcast_to(value[None], (devices, *value.shape)), axis, 0, 0, tiled=True
    )


def joined_along(parts, dim):
    dims = list(parts.shape[1:])
    dims[dim] *= parts.shape[0]
    return jnp.moveaxis(parts, 0, dim).reshape(dims)


def collect(value, axis, dim):
    parts = from_everyone(value, axis)
    return joined_along(parts, dim)


def split_up(value, dim, devices):
    dims = value.shape
    parts = value.reshape(*dims[:dim], devices, dims[dim] // devices, *dims[dim + 1 :])
    return jnp.moveaxis(parts, dim, 0)


def summed_on_arrival(value, axis, dim):
    devices = lax.axis_size(axis)
    parts = lax.all_to_all(split_up(value, dim, devices), axis, 0, 0, tiled=True)
    return jnp.sum(parts.astype(jnp.float32), axis=0)


def rows_first(arrays, axis, dims):
    turned = [jnp.moveaxis(a, dim, 0) for a, dim in zip(arrays, dims)]
    both = jnp.concatenate([t.reshape(len(t), -1) for t in turned], axis=1)
    filled, at, outs = (lax.all_gather(both, axis, axis=0, tiled=True), 0, [])
    for t, dim in zip(turned, dims):
        slab = filled[:, at : at + t[0].size].reshape(-1, *t.shape[1:])
        outs.append(jnp.moveaxis(slab, 0, dim))
        at += t[0].size
    return tuple(outs)


def with_halo(value, sides, width):
    for axis, dim in sides:
        devices, length = (lax.axis_size(axis), value.shape[dim])
        up = [(i, (i + 1) % devices) for i in range(devices - 1)]
        down = [(j, i) for i, j in up]
        last = lax.slice_in_dim(value, length - width, length, axis=dim)
        initial = lax.slice_in_dim(value, 0, width, axis=dim)
        before = lax.ppermute(last, axis, up)
        after = lax.ppermute(initial, axis, down)
        value = jnp.concatenate([before, value, after], axis=dim)
    return value


def from_behind(block, axis, distance):
    devices = range(lax.axis_size(axis))
    route = [(i - distance, i) for i in devices if i - distance in devices]
    return lax.ppermute(block, axis, route)


def side_by_side(arrays, axis, dim, along):
    widths = [math.prod(a.shape[along:]) for a in arrays]
    both = jnp.concatenate(
        [a.reshape(*a.shape[:along], w) for a, w in zip(arrays, widths)], axis=along
    )
    filled = lax.psum_scatter(both, axis, scatter_dimension=dim, tiled=True)
    parts = jnp.split(filled, [sum(widths[:k]) for k in range(1, len(widths))], axis=along)
    return tuple(
        (b.reshape(*filled.shape[:along], *a.shape[along:]) for a, b in zip(arrays, parts))
    )


def scatter_rows(grad):
    return summed_on_arrival(grad.astype(jnp.bfloat16), "dp", 0)


def layer_norm(values, gain_row, shift_row):
    center = values - jnp.mean(values, axis=-1, keepdims=True)
    spread = jnp.mean(center * center, axis=-1, keepdims=True)
    return center * lax.rsqrt(spread + norm_eps) * gain_row + shift_row


def exact_gelu(values):
    return jax.nn.gelu(values, approximate=False)


def _gather_kernel(devices, x_ref, out_ref, send_sem, recv_sem):
    me = lax.axis_index("tensor")
    dp = lax.axis_index("dp")
    barrier = pltpu.get_barrier_semaphore()
    for step in range(1, devices):
        pl.semaphore_signal(
            barrier, inc=1, device_id=(dp, lax.rem(me + step, devices)), device_id_type=MESH
        )
    pl.semaphore_wait(barrier, devices - 1)
    copies = []
    for step in range(1, devices):
        copy = pltpu.make_async_remote_copy(
            src_ref=x_ref,
            dst_ref=out_ref.at[me],
            send_sem=send_sem.at[step - 1],
            recv_sem=recv_sem.at[step - 1],
            device_id=(dp, lax.rem(me + step, devices)),
            device_id_type=MESH,
        )
        copy.start()
        copies.append(copy)
    out_ref[me] = x_ref[...]
    for copy in copies:
        copy.wait()


def gather_rows(values):
    devices = lax.axis_size("tensor")
    rows, width = values.shape
    parts = pl.pallas_call(
        functools.partial(_gather_kernel, devices),
        out_shape=jax.ShapeDtypeStruct((devices, rows, width), values.dtype),
        in_specs=[pl.BlockSpec(memory_space=pltpu.VMEM)],
        out_specs=pl.BlockSpec(memory_space=pltpu.VMEM),
        scratch_shapes=[
            pltpu.SemaphoreType.DMA((devices - 1,)),
            pltpu.SemaphoreType.DMA((devices - 1,)),
        ],
        compiler_params=pltpu.CompilerParams(collective_id=0, has_side_effects=True),
    )(values)
    return parts.reshape(devices * rows, width)


def _exchange_kernel(devices, x_ref, out_ref, send_sem, recv_sem):
    me = lax.axis_index("tensor")
    dp = lax.axis_index("dp")
    barrier = pltpu.get_barrier_semaphore()
    for step in range(1, devices):
        pl.semaphore_signal(
            barrier, inc=1, device_id=(dp, lax.rem(me + step, devices)), device_id_type=MESH
        )
    pl.semaphore_wait(barrier, devices - 1)
    copies = []
    for step in range(1, devices):
        peer = lax.rem(me + step, devices)
        copy = pltpu.make_async_remote_copy(
            src_ref=x_ref.at[peer],
            dst_ref=out_ref.at[me],
            send_sem=send_sem.at[step - 1],
            recv_sem=recv_sem.at[step - 1],
            device_id=(dp, peer),
            device_id_type=MESH,
        )
        copy.start()
        copies.append(copy)
    out_ref[me] = x_ref[me]
    for copy in copies:
        copy.wait()


def exchange_rows(parts):
    devices = parts.shape[0]
    return pl.pallas_call(
        functools.partial(_exchange_kernel, devices),
        out_shape=jax.ShapeDtypeStruct(parts.shape, parts.dtype),
        in_specs=[pl.BlockSpec(memory_space=pltpu.VMEM)],
        out_specs=pl.BlockSpec(memory_space=pltpu.VMEM),
        scratch_shapes=[
            pltpu.SemaphoreType.DMA((devices - 1,)),
            pltpu.SemaphoreType.DMA((devices - 1,)),
        ],
        compiler_params=pltpu.CompilerParams(collective_id=1, has_side_effects=True),
    )(parts)


def summed_over_tensor(value):
    devices = lax.axis_size("tensor")
    parts = exchange_rows(split_up(value, 0, devices))
    return jnp.sum(parts.astype(jnp.float32), axis=0)


def gather_forward(values):
    return gather_rows(values)


def gather_backward(values):
    return gather_rows(values)


def sum_forward(product, tok_rows):
    return summed_over_tensor(
        product(jnp.int32(0), tok_rows * lax.axis_size("tensor")).astype(jnp.bfloat16)
    )


def sum_backward(product, tok_rows):
    return summed_over_tensor(
        product(jnp.int32(0), tok_rows * lax.axis_size("tensor")).astype(jnp.bfloat16)
    )


def head_scores(query_head, key_head, allowed):
    raw = lax.dot_general(
        query_head, key_head, (((1,), (1,)), ((), ())), preferred_element_type=jnp.float32
    )
    return jnp.where(allowed, raw * HD ** (-0.5), masked_score)


def split_heads(queries, key_ext):
    heads_here = queries.shape[1] // HD
    query_heads = queries.reshape(queries.shape[0], heads_here, HD)
    key_heads = key_ext[0].reshape(key_ext.shape[1], heads_here, HD)
    value_heads = key_ext[1].reshape(key_ext.shape[1], heads_here, HD)
    return (heads_here, query_heads, key_heads, value_heads)


def merge_heads(per_head):
    return jnp.transpose(per_head, (1, 0, 2)).reshape(
        per_head.shape[1], per_head.shape[0] * per_head.shape[2]
    )


def attend_forward(queries, key_ext, allowed):
    heads_here, query_heads, key_heads, value_heads = split_heads(queries, key_ext)

    def one_head(head_index):
        query_head = lax.dynamic_index_in_dim(query_heads, head_index, 1, keepdims=False)
        key_head = lax.dynamic_index_in_dim(key_heads, head_index, 1, keepdims=False)
        value_head = lax.dynamic_index_in_dim(value_heads, head_index, 1, keepdims=False)
        scores = head_scores(query_head, key_head, allowed)
        row_top = jnp.max(scores, axis=1, keepdims=True)
        exponent = jnp.exp(scores - row_top)
        row_total = jnp.sum(exponent, axis=1, keepdims=True)
        prob_low = (exponent / row_total).astype(jnp.bfloat16)
        head_out = jnp.dot(prob_low, value_head, preferred_element_type=jnp.float32)
        return (head_out, (row_top + jnp.log(row_total))[:, 0])

    head_outs, log_norm = lax.map(one_head, jnp.arange(heads_here, dtype=jnp.int32))
    return (merge_heads(head_outs), log_norm)


def attend_backward(queries, key_ext, allowed, log_norm, grad_attended):
    heads_here, query_heads, key_heads, value_heads = split_heads(queries, key_ext)
    grad_heads = grad_attended.reshape(grad_attended.shape[0], heads_here, HD)

    def one_head(inputs):
        head_index, norm_row = inputs
        query_head = lax.dynamic_index_in_dim(query_heads, head_index, 1, keepdims=False)
        key_head = lax.dynamic_index_in_dim(key_heads, head_index, 1, keepdims=False)
        value_head = lax.dynamic_index_in_dim(value_heads, head_index, 1, keepdims=False)
        grad_head = lax.dynamic_index_in_dim(grad_heads, head_index, 1, keepdims=False)
        prob_full = jnp.exp(head_scores(query_head, key_head, allowed) - norm_row[:, None])
        prob_low = prob_full.astype(jnp.bfloat16)
        grad_value = lax.dot_general(
            prob_low, grad_head, (((0,), (0,)), ((), ())), preferred_element_type=jnp.float32
        )
        grad_prob = lax.dot_general(
            grad_head, value_head, (((1,), (1,)), ((), ())), preferred_element_type=jnp.float32
        )
        grad_score = (
            prob_full * (grad_prob - jnp.sum(prob_full * grad_prob, axis=1, keepdims=True))
        ).astype(jnp.bfloat16)
        grad_query = jnp.dot(grad_score, key_head, preferred_element_type=jnp.float32) * HD ** (
            -0.5
        )
        grad_key = lax.dot_general(
            grad_score, query_head, (((0,), (0,)), ((), ())), preferred_element_type=jnp.float32
        ) * HD ** (-0.5)
        return (grad_query, grad_key, grad_value)

    grad_queries, grad_keys, grad_values = lax.map(
        one_head, (jnp.arange(heads_here, dtype=jnp.int32), log_norm)
    )
    return (merge_heads(grad_queries), merge_heads(grad_keys), merge_heads(grad_values))


def local(
    tokens,
    segment,
    real_token,
    qkv_weight,
    out_weight,
    up_weight,
    down_weight,
    unit_bias,
    norm_gain,
    row_bias,
    cotangent,
):
    tok_rows = tokens.shape[0]
    tensor_size = lax.axis_size("tensor")
    group_rows = tok_rows * tensor_size
    margin = IMG - 1
    cols_here = qkv_weight.shape[3]
    dp_index = lax.axis_index("dp")
    tensor_index = lax.axis_index("tensor")
    group_first = dp_index * group_rows
    own_first = group_first + tensor_index * tok_rows
    segment_pad = jnp.pad(segment, (margin, margin), constant_values=-1)
    real_pad = jnp.pad(real_token, (margin, margin))
    segment_query = lax.dynamic_slice_in_dim(segment, group_first, group_rows, 0)
    segment_key = lax.dynamic_slice_in_dim(segment_pad, group_first, group_rows + 2 * margin, 0)
    real_key = lax.dynamic_slice_in_dim(real_pad, group_first, group_rows + 2 * margin, 0)
    place_query = jnp.arange(group_rows, dtype=jnp.int32)
    place_key = jnp.arange(group_rows + 2 * margin, dtype=jnp.int32) - margin
    allowed = (segment_query[:, None] == segment_key[None, :]) & (
        (real_key[None, :] == 1) | (place_query[:, None] == place_key[None, :])
    )
    own_real = lax.dynamic_slice_in_dim(real_token, own_first, tok_rows, 0).astype(jnp.float32)
    stream = tokens.astype(jnp.float32)
    layer_index = 0
    d_here = qkv_weight.shape[2]
    attn_rows = collect(
        jnp.concatenate(
            [
                jnp.moveaxis(qkv_weight[layer_index], 1, 0).reshape(d_here, 3 * cols_here),
                out_weight[layer_index],
            ],
            axis=1,
        ),
        "dp",
        0,
    )
    qkv_full = jnp.moveaxis(attn_rows[:, : 3 * cols_here].reshape(-1, 3, cols_here), 0, 1)
    out_full = attn_rows[:, 3 * cols_here :]
    up_full = collect(up_weight[layer_index], "dp", 0)
    down_full = collect(down_weight[layer_index], "dp", 0)
    gathered = (qkv_full, out_full, up_full, down_full)
    gain_now = norm_gain[layer_index].astype(jnp.float32)
    shift_now = row_bias[layer_index].astype(jnp.float32)
    bias_now = unit_bias[layer_index].astype(jnp.float32)
    normed_full = gather_forward(layer_norm(stream, gain_now[0], shift_now[0]).astype(jnp.bfloat16))
    projected = jnp.einsum("gd,sde->sge", normed_full, qkv_full, preferred_element_type=jnp.float32)
    queries = (projected[0] + bias_now[0]).astype(jnp.bfloat16)
    key_value = jnp.stack([projected[1], projected[2] + bias_now[1]]).astype(jnp.bfloat16)
    key_ext = with_halo(key_value, (("dp", 1),), margin)
    attended, log_norm = attend_forward(queries, key_ext, allowed)
    attended = attended.astype(jnp.bfloat16)

    def attention_term(first_row, row_count):
        return lax.dot_general(
            attended, out_full, (((1,), (1,)), ((), ())), preferred_element_type=jnp.float32
        )

    middle = stream + sum_forward(attention_term, tok_rows) + shift_now[1]
    second_full = gather_forward(layer_norm(middle, gain_now[1], shift_now[2]).astype(jnp.bfloat16))
    hidden = (
        jnp.einsum("gd,dre->gre", second_full, up_full, preferred_element_type=jnp.float32)
        + bias_now[2:][None]
    )
    active = exact_gelu(hidden).astype(jnp.bfloat16)

    def feed_term(first_row, row_count):
        return jnp.einsum("gre,ore->go", active, down_full, preferred_element_type=jnp.float32)

    kept_weights = gathered
    records = [
        (
            stream,
            middle,
            normed_full,
            second_full,
            queries,
            key_ext,
            log_norm,
            attended,
            hidden,
            active,
            kept_weights,
        )
    ]
    stream = middle + sum_forward(feed_term, tok_rows) + shift_now[3]
    gradient = cotangent.astype(jnp.float32) * own_real[:, None]
    local_qkv = [None] * LAYERS
    local_out = [None] * LAYERS
    local_up = [None] * LAYERS
    local_down = [None] * LAYERS
    unit_grads = [None] * LAYERS
    gain_grads = [None] * LAYERS
    shift_grads = [None] * LAYERS
    for layer_index in reversed(range(LAYERS)):
        (
            stream_in,
            middle,
            normed_full,
            second_full,
            queries,
            key_ext,
            log_norm,
            attended,
            hidden,
            active,
            kept_weights,
        ) = records[layer_index]
        qkv_full, out_full, up_full, down_full = kept_weights
        gain_now = norm_gain[layer_index].astype(jnp.float32)
        shift_now = row_bias[layer_index].astype(jnp.float32)
        shift_three = jnp.sum(gradient, axis=0)
        grad_mlp = gather_backward(gradient.astype(jnp.bfloat16))
        down_grad = scatter_rows(
            jnp.einsum("go,gre->ore", grad_mlp, active, preferred_element_type=jnp.float32)
        )
        grad_active = jnp.einsum(
            "go,ore->gre", grad_mlp, down_full, preferred_element_type=jnp.float32
        )
        gelu_again, gelu_pull = jax.vjp(exact_gelu, hidden)
        grad_hidden = gelu_pull(grad_active)[0].astype(jnp.bfloat16)
        up_bias_grad = jnp.sum(grad_hidden.astype(jnp.float32), axis=0)
        up_grad = scatter_rows(
            jnp.einsum("gd,gre->dre", second_full, grad_hidden, preferred_element_type=jnp.float32)
        )

        def second_term(first_row, row_count):
            return jnp.einsum(
                "gre,dre->gd", grad_hidden, up_full, preferred_element_type=jnp.float32
            )

        grad_second = sum_backward(second_term, tok_rows)
        second_again, second_pull = jax.vjp(layer_norm, middle, gain_now[1], shift_now[2])
        grad_mid_norm, gain_one, shift_two = second_pull(grad_second)
        grad_middle = gradient + grad_mid_norm
        shift_one = jnp.sum(grad_middle, axis=0)
        grad_proj = gather_backward(grad_middle.astype(jnp.bfloat16))
        out_grad = scatter_rows(
            lax.dot_general(
                grad_proj, attended, (((0,), (0,)), ((), ())), preferred_element_type=jnp.float32
            )
        )
        grad_attended = jnp.dot(grad_proj, out_full, preferred_element_type=jnp.float32).astype(
            jnp.bfloat16
        )
        grad_query, grad_key_ext, grad_value_ext = attend_backward(
            queries, key_ext, allowed, log_norm, grad_attended
        )
        grad_pair_ext = jnp.stack([grad_key_ext, grad_value_ext])
        from_next = from_behind(grad_pair_ext[:, :margin].astype(jnp.bfloat16), "dp", -1).astype(
            jnp.float32
        )
        from_prev = from_behind(
            grad_pair_ext[:, margin + group_rows :].astype(jnp.bfloat16), "dp", 1
        ).astype(jnp.float32)
        grad_pair = grad_pair_ext[:, margin : margin + group_rows]
        grad_pair = (
            grad_pair.at[:, group_rows - margin :].add(from_next).at[:, :margin].add(from_prev)
        )
        grad_triple = jnp.concatenate(
            [grad_query.astype(jnp.bfloat16)[None], grad_pair.astype(jnp.bfloat16)], axis=0
        )
        qkv_grad = jnp.moveaxis(
            scatter_rows(
                jnp.einsum(
                    "gd,sge->dse", normed_full, grad_triple, preferred_element_type=jnp.float32
                )
            ),
            0,
            1,
        )
        triple_sums = jnp.sum(grad_triple.astype(jnp.float32), axis=1)

        def first_term(first_row, row_count):
            return jnp.einsum(
                "sge,sde->gd", grad_triple, qkv_full, preferred_element_type=jnp.float32
            )

        grad_first = sum_backward(first_term, tok_rows)
        first_again, first_pull = jax.vjp(layer_norm, stream_in, gain_now[0], shift_now[0])
        grad_in_norm, gain_zero, shift_zero = first_pull(grad_first)
        gradient = grad_middle + grad_in_norm
        unit_grads[layer_index] = jnp.concatenate(
            [triple_sums[0][None], triple_sums[2][None], up_bias_grad], axis=0
        )
        gain_grads[layer_index] = jnp.stack([gain_zero, gain_one])
        shift_grads[layer_index] = jnp.stack([shift_zero, shift_one, shift_two, shift_three])
        local_qkv[layer_index] = qkv_grad
        local_out[layer_index] = out_grad
        local_up[layer_index] = up_grad
        local_down[layer_index] = down_grad
    grad_qkv = jnp.stack(local_qkv).astype(jnp.float32)
    grad_out = jnp.stack(local_out).astype(jnp.float32)
    grad_up = jnp.stack(local_up).astype(jnp.float32)
    grad_down = jnp.stack(local_down).astype(jnp.float32)
    unit_local = jnp.stack(unit_grads)
    unit_wide = jnp.zeros((LAYERS, unit_local.shape[1], cols_here * tensor_size), jnp.float32)
    unit_wide = lax.dynamic_update_slice_in_dim(unit_wide, unit_local, tensor_index * cols_here, 2)
    small = jnp.concatenate(
        [jnp.stack(gain_grads), jnp.stack(shift_grads), unit_wide], axis=1
    )
    dp_size = lax.axis_size("dp")
    small_flat = small.reshape(dp_size, -1)
    small_part = jnp.sum(lax.all_to_all(small_flat, "dp", 0, 0, tiled=True), axis=0)
    small_part = jnp.sum(from_everyone(small_part, "tensor"), axis=0)
    small_total = collect(small_part[None], "dp", 0).reshape(small.shape)
    gain_total = small_total[:, :2]
    shift_total = small_total[:, 2:6]
    unit_total = small_total[:, 6:]
    unit_mine = lax.dynamic_slice_in_dim(unit_total, tensor_index * cols_here, cols_here, 2)
    return (
        stream.astype(jnp.bfloat16),
        gradient.astype(jnp.bfloat16),
        grad_qkv,
        grad_out,
        grad_up,
        grad_down,
        unit_mine,
        gain_total,
        shift_total,
    )


def solution(mesh):
    placed = (
        P(("dp", "tensor"), None),
        P(),
        P(),
        P(None, None, "dp", "tensor"),
        P(None, "dp", "tensor"),
        P(None, "dp", None, "tensor"),
        P(None, "dp", None, "tensor"),
        P(None, None, "tensor"),
        P(),
        P(),
        P(("dp", "tensor"), None),
    )
    return jax.shard_map(
        local,
        mesh=mesh,
        in_specs=placed,
        out_specs=(
            P(("dp", "tensor"), None),
            P(("dp", "tensor"), None),
            P(None, None, "dp", "tensor"),
            P(None, "dp", "tensor"),
            P(None, "dp", None, "tensor"),
            P(None, "dp", None, "tensor"),
            P(None, None, "tensor"),
            P(),
            P(),
        ),
        check_vma=False,
    )
```

```python
import functools
import math

import jax
import jax.numpy as jnp
from jax import lax
from jax.experimental import pallas as pl
from jax.experimental.pallas import tpu as pltpu
from jax.sharding import PartitionSpec as P

MESH = pl.DeviceIdType.MESH

LAYERS = 1
IMG = 577
HD = 64


norm_eps = 1e-06
masked_score = -1e30


def from_everyone(value, axis):
    devices = lax.axis_size(axis)
    return lax.all_to_all(
        jnp.broadcast_to(value[None], (devices, *value.shape)), axis, 0, 0, tiled=True
    )


def joined_along(parts, dim):
    dims = list(parts.shape[1:])
    dims[dim] *= parts.shape[0]
    return jnp.moveaxis(parts, 0, dim).reshape(dims)


def collect(value, axis, dim):
    parts = from_everyone(value, axis)
    return joined_along(parts, dim)


def split_up(value, dim, devices):
    dims = value.shape
    parts = value.reshape(*dims[:dim], devices, dims[dim] // devices, *dims[dim + 1 :])
    return jnp.moveaxis(parts, dim, 0)


def summed_on_arrival(value, axis, dim):
    devices = lax.axis_size(axis)
    parts = lax.all_to_all(split_up(value, dim, devices), axis, 0, 0, tiled=True)
    return jnp.sum(parts.astype(jnp.float32), axis=0)


def rows_first(arrays, axis, dims):
    turned = [jnp.moveaxis(a, dim, 0) for a, dim in zip(arrays, dims)]
    both = jnp.concatenate([t.reshape(len(t), -1) for t in turned], axis=1)
    filled, at, outs = (lax.all_gather(both, axis, axis=0, tiled=True), 0, [])
    for t, dim in zip(turned, dims):
        slab = filled[:, at : at + t[0].size].reshape(-1, *t.shape[1:])
        outs.append(jnp.moveaxis(slab, 0, dim))
        at += t[0].size
    return tuple(outs)


def with_halo(value, sides, width):
    for axis, dim in sides:
        devices, length = (lax.axis_size(axis), value.shape[dim])
        up = [(i, (i + 1) % devices) for i in range(devices - 1)]
        down = [(j, i) for i, j in up]
        last = lax.slice_in_dim(value, length - width, length, axis=dim)
        initial = lax.slice_in_dim(value, 0, width, axis=dim)
        before = lax.ppermute(last, axis, up)
        after = lax.ppermute(initial, axis, down)
        value = jnp.concatenate([before, value, after], axis=dim)
    return value


def from_behind(block, axis, distance):
    devices = range(lax.axis_size(axis))
    route = [(i - distance, i) for i in devices if i - distance in devices]
    return lax.ppermute(block, axis, route)


def side_by_side(arrays, axis, dim, along):
    widths = [math.prod(a.shape[along:]) for a in arrays]
    both = jnp.concatenate(
        [a.reshape(*a.shape[:along], w) for a, w in zip(arrays, widths)], axis=along
    )
    filled = lax.psum_scatter(both, axis, scatter_dimension=dim, tiled=True)
    parts = jnp.split(filled, [sum(widths[:k]) for k in range(1, len(widths))], axis=along)
    return tuple(
        (b.reshape(*filled.shape[:along], *a.shape[along:]) for a, b in zip(arrays, parts))
    )


def scatter_rows(grad):
    return summed_on_arrival(grad.astype(jnp.bfloat16), "dp", 0)


def layer_norm(values, gain_row, shift_row):
    center = values - jnp.mean(values, axis=-1, keepdims=True)
    spread = jnp.mean(center * center, axis=-1, keepdims=True)
    return center * lax.rsqrt(spread + norm_eps) * gain_row + shift_row


def exact_gelu(values):
    return jax.nn.gelu(values, approximate=False)


def _gather_kernel(devices, x_ref, out_ref, send_sem, recv_sem):
    me = lax.axis_index("tensor")
    dp = lax.axis_index("dp")
    sib = me + 1 - 2 * lax.rem(me, 2)
    far = lax.rem(me + 2, devices)
    barrier = pltpu.get_barrier_semaphore()
    for peer in (sib, far):
        pl.semaphore_signal(barrier, inc=1, device_id=(dp, peer), device_id_type=MESH)
    pl.semaphore_wait(barrier, 2)
    near_copy = pltpu.make_async_remote_copy(
        src_ref=x_ref,
        dst_ref=out_ref.at[me],
        send_sem=send_sem.at[0],
        recv_sem=recv_sem.at[0],
        device_id=(dp, sib),
        device_id_type=MESH,
    )
    far_copy = pltpu.make_async_remote_copy(
        src_ref=x_ref,
        dst_ref=out_ref.at[me],
        send_sem=send_sem.at[1],
        recv_sem=recv_sem.at[1],
        device_id=(dp, far),
        device_id_type=MESH,
    )
    far_copy.start()
    near_copy.start()
    out_ref[me] = x_ref[...]
    far_copy.wait_recv()
    relay = pltpu.make_async_remote_copy(
        src_ref=out_ref.at[far],
        dst_ref=out_ref.at[far],
        send_sem=send_sem.at[2],
        recv_sem=recv_sem.at[2],
        device_id=(dp, sib),
        device_id_type=MESH,
    )
    relay.start()
    near_copy.wait_send()
    near_copy.wait_recv()
    far_copy.wait_send()
    relay.wait_send()
    relay.wait_recv()


def gather_rows(values):
    devices = lax.axis_size("tensor")
    if devices != 4:
        return collect(values, "tensor", 0)
    rows, width = values.shape
    parts = pl.pallas_call(
        functools.partial(_gather_kernel, devices),
        out_shape=jax.ShapeDtypeStruct((devices, rows, width), values.dtype),
        in_specs=[pl.BlockSpec(memory_space=pltpu.VMEM)],
        out_specs=pl.BlockSpec(memory_space=pltpu.VMEM),
        scratch_shapes=[
            pltpu.SemaphoreType.DMA((3,)),
            pltpu.SemaphoreType.DMA((3,)),
        ],
        compiler_params=pltpu.CompilerParams(collective_id=0, has_side_effects=True),
    )(values)
    return parts.reshape(devices * rows, width)


def _exchange_kernel(devices, x_ref, out_ref, send_sem, recv_sem):
    me = lax.axis_index("tensor")
    dp = lax.axis_index("dp")
    barrier = pltpu.get_barrier_semaphore()
    for step in range(1, devices):
        pl.semaphore_signal(
            barrier, inc=1, device_id=(dp, lax.rem(me + step, devices)), device_id_type=MESH
        )
    pl.semaphore_wait(barrier, devices - 1)
    copies = []
    for step in range(1, devices):
        peer = lax.rem(me + step, devices)
        copy = pltpu.make_async_remote_copy(
            src_ref=x_ref.at[peer],
            dst_ref=out_ref.at[me],
            send_sem=send_sem.at[step - 1],
            recv_sem=recv_sem.at[step - 1],
            device_id=(dp, peer),
            device_id_type=MESH,
        )
        copy.start()
        copies.append(copy)
    out_ref[me] = x_ref[me]
    for copy in copies:
        copy.wait()


def exchange_rows(parts):
    devices = parts.shape[0]
    return pl.pallas_call(
        functools.partial(_exchange_kernel, devices),
        out_shape=jax.ShapeDtypeStruct(parts.shape, parts.dtype),
        in_specs=[pl.BlockSpec(memory_space=pltpu.VMEM)],
        out_specs=pl.BlockSpec(memory_space=pltpu.VMEM),
        scratch_shapes=[
            pltpu.SemaphoreType.DMA((devices - 1,)),
            pltpu.SemaphoreType.DMA((devices - 1,)),
        ],
        compiler_params=pltpu.CompilerParams(collective_id=1, has_side_effects=True),
    )(parts)


def summed_over_tensor(value):
    devices = lax.axis_size("tensor")
    parts = exchange_rows(split_up(value, 0, devices))
    return jnp.sum(parts.astype(jnp.float32), axis=0)


def gather_forward(values):
    return gather_rows(values)


def gather_backward(values):
    return gather_rows(values)


def sum_forward(product, tok_rows):
    return summed_over_tensor(
        product(jnp.int32(0), tok_rows * lax.axis_size("tensor")).astype(jnp.bfloat16)
    )


def sum_backward(product, tok_rows):
    return summed_over_tensor(
        product(jnp.int32(0), tok_rows * lax.axis_size("tensor")).astype(jnp.bfloat16)
    )


def head_scores(query_head, key_head, allowed):
    raw = lax.dot_general(
        query_head, key_head, (((1,), (1,)), ((), ())), preferred_element_type=jnp.float32
    )
    return jnp.where(allowed, raw * HD ** (-0.5), masked_score)


def split_heads(queries, key_ext):
    heads_here = queries.shape[1] // HD
    query_heads = queries.reshape(queries.shape[0], heads_here, HD)
    key_heads = key_ext[0].reshape(key_ext.shape[1], heads_here, HD)
    value_heads = key_ext[1].reshape(key_ext.shape[1], heads_here, HD)
    return (heads_here, query_heads, key_heads, value_heads)


def merge_heads(per_head):
    return jnp.transpose(per_head, (1, 0, 2)).reshape(
        per_head.shape[1], per_head.shape[0] * per_head.shape[2]
    )


def attend_forward(queries, key_ext, allowed):
    heads_here, query_heads, key_heads, value_heads = split_heads(queries, key_ext)

    def one_head(head_index):
        query_head = lax.dynamic_index_in_dim(query_heads, head_index, 1, keepdims=False)
        key_head = lax.dynamic_index_in_dim(key_heads, head_index, 1, keepdims=False)
        value_head = lax.dynamic_index_in_dim(value_heads, head_index, 1, keepdims=False)
        scores = head_scores(query_head, key_head, allowed)
        row_top = jnp.max(scores, axis=1, keepdims=True)
        exponent = jnp.exp(scores - row_top)
        row_total = jnp.sum(exponent, axis=1, keepdims=True)
        prob_low = (exponent / row_total).astype(jnp.bfloat16)
        head_out = jnp.dot(prob_low, value_head, preferred_element_type=jnp.float32)
        return (head_out, (row_top + jnp.log(row_total))[:, 0])

    head_outs, log_norm = lax.map(one_head, jnp.arange(heads_here, dtype=jnp.int32))
    return (merge_heads(head_outs), log_norm)


def attend_backward(queries, key_ext, allowed, log_norm, grad_attended):
    heads_here, query_heads, key_heads, value_heads = split_heads(queries, key_ext)
    grad_heads = grad_attended.reshape(grad_attended.shape[0], heads_here, HD)

    def one_head(inputs):
        head_index, norm_row = inputs
        query_head = lax.dynamic_index_in_dim(query_heads, head_index, 1, keepdims=False)
        key_head = lax.dynamic_index_in_dim(key_heads, head_index, 1, keepdims=False)
        value_head = lax.dynamic_index_in_dim(value_heads, head_index, 1, keepdims=False)
        grad_head = lax.dynamic_index_in_dim(grad_heads, head_index, 1, keepdims=False)
        prob_full = jnp.exp(head_scores(query_head, key_head, allowed) - norm_row[:, None])
        prob_low = prob_full.astype(jnp.bfloat16)
        grad_value = lax.dot_general(
            prob_low, grad_head, (((0,), (0,)), ((), ())), preferred_element_type=jnp.float32
        )
        grad_prob = lax.dot_general(
            grad_head, value_head, (((1,), (1,)), ((), ())), preferred_element_type=jnp.float32
        )
        grad_score = (
            prob_full * (grad_prob - jnp.sum(prob_full * grad_prob, axis=1, keepdims=True))
        ).astype(jnp.bfloat16)
        grad_query = jnp.dot(grad_score, key_head, preferred_element_type=jnp.float32) * HD ** (
            -0.5
        )
        grad_key = lax.dot_general(
            grad_score, query_head, (((0,), (0,)), ((), ())), preferred_element_type=jnp.float32
        ) * HD ** (-0.5)
        return (grad_query, grad_key, grad_value)

    grad_queries, grad_keys, grad_values = lax.map(
        one_head, (jnp.arange(heads_here, dtype=jnp.int32), log_norm)
    )
    return (merge_heads(grad_queries), merge_heads(grad_keys), merge_heads(grad_values))


def local(
    tokens,
    segment,
    real_token,
    qkv_weight,
    out_weight,
    up_weight,
    down_weight,
    unit_bias,
    norm_gain,
    row_bias,
    cotangent,
):
    tok_rows = tokens.shape[0]
    tensor_size = lax.axis_size("tensor")
    group_rows = tok_rows * tensor_size
    margin = IMG - 1
    cols_here = qkv_weight.shape[3]
    dp_index = lax.axis_index("dp")
    tensor_index = lax.axis_index("tensor")
    group_first = dp_index * group_rows
    own_first = group_first + tensor_index * tok_rows
    segment_pad = jnp.pad(segment, (margin, margin), constant_values=-1)
    real_pad = jnp.pad(real_token, (margin, margin))
    segment_query = lax.dynamic_slice_in_dim(segment, group_first, group_rows, 0)
    segment_key = lax.dynamic_slice_in_dim(segment_pad, group_first, group_rows + 2 * margin, 0)
    real_key = lax.dynamic_slice_in_dim(real_pad, group_first, group_rows + 2 * margin, 0)
    place_query = jnp.arange(group_rows, dtype=jnp.int32)
    place_key = jnp.arange(group_rows + 2 * margin, dtype=jnp.int32) - margin
    allowed = (segment_query[:, None] == segment_key[None, :]) & (
        (real_key[None, :] == 1) | (place_query[:, None] == place_key[None, :])
    )
    own_real = lax.dynamic_slice_in_dim(real_token, own_first, tok_rows, 0).astype(jnp.float32)
    stream = tokens.astype(jnp.float32)
    layer_index = 0
    qkv_full = jnp.moveaxis(collect(jnp.moveaxis(qkv_weight[layer_index], 1, 0), "dp", 0), 0, 1)
    out_full = collect(out_weight[layer_index], "dp", 0)
    up_full = collect(up_weight[layer_index], "dp", 0)
    down_full = collect(down_weight[layer_index], "dp", 0)
    gathered = (qkv_full, out_full, up_full, down_full)
    gain_now = norm_gain[layer_index].astype(jnp.float32)
    shift_now = row_bias[layer_index].astype(jnp.float32)
    bias_now = unit_bias[layer_index].astype(jnp.float32)
    normed_full = gather_forward(layer_norm(stream, gain_now[0], shift_now[0]).astype(jnp.bfloat16))
    projected = jnp.einsum("gd,sde->sge", normed_full, qkv_full, preferred_element_type=jnp.float32)
    queries = (projected[0] + bias_now[0]).astype(jnp.bfloat16)
    key_value = jnp.stack([projected[1], projected[2] + bias_now[1]]).astype(jnp.bfloat16)
    key_ext = with_halo(key_value, (("dp", 1),), margin)
    attended, log_norm = attend_forward(queries, key_ext, allowed)
    attended = attended.astype(jnp.bfloat16)

    def attention_term(first_row, row_count):
        return lax.dot_general(
            attended, out_full, (((1,), (1,)), ((), ())), preferred_element_type=jnp.float32
        )

    middle = stream + sum_forward(attention_term, tok_rows) + shift_now[1]
    second_full = gather_forward(layer_norm(middle, gain_now[1], shift_now[2]).astype(jnp.bfloat16))
    hidden = (
        jnp.einsum("gd,dre->gre", second_full, up_full, preferred_element_type=jnp.float32)
        + bias_now[2:][None]
    )
    active = exact_gelu(hidden).astype(jnp.bfloat16)

    def feed_term(first_row, row_count):
        return jnp.einsum("gre,ore->go", active, down_full, preferred_element_type=jnp.float32)

    kept_weights = gathered
    records = [
        (
            stream,
            middle,
            normed_full,
            second_full,
            queries,
            key_ext,
            log_norm,
            attended,
            hidden,
            active,
            kept_weights,
        )
    ]
    stream = middle + sum_forward(feed_term, tok_rows) + shift_now[3]
    gradient = cotangent.astype(jnp.float32) * own_real[:, None]
    local_qkv = [None] * LAYERS
    local_out = [None] * LAYERS
    local_up = [None] * LAYERS
    local_down = [None] * LAYERS
    unit_grads = [None] * LAYERS
    gain_grads = [None] * LAYERS
    shift_grads = [None] * LAYERS
    for layer_index in reversed(range(LAYERS)):
        (
            stream_in,
            middle,
            normed_full,
            second_full,
            queries,
            key_ext,
            log_norm,
            attended,
            hidden,
            active,
            kept_weights,
        ) = records[layer_index]
        qkv_full, out_full, up_full, down_full = kept_weights
        gain_now = norm_gain[layer_index].astype(jnp.float32)
        shift_now = row_bias[layer_index].astype(jnp.float32)
        shift_three = jnp.sum(gradient, axis=0)
        grad_mlp = gather_backward(gradient.astype(jnp.bfloat16))
        down_grad = scatter_rows(
            jnp.einsum("go,gre->ore", grad_mlp, active, preferred_element_type=jnp.float32)
        )
        grad_active = jnp.einsum(
            "go,ore->gre", grad_mlp, down_full, preferred_element_type=jnp.float32
        )
        gelu_again, gelu_pull = jax.vjp(exact_gelu, hidden)
        grad_hidden = gelu_pull(grad_active)[0].astype(jnp.bfloat16)
        up_bias_grad = jnp.sum(grad_hidden.astype(jnp.float32), axis=0)
        up_grad = scatter_rows(
            jnp.einsum("gd,gre->dre", second_full, grad_hidden, preferred_element_type=jnp.float32)
        )

        def second_term(first_row, row_count):
            return jnp.einsum(
                "gre,dre->gd", grad_hidden, up_full, preferred_element_type=jnp.float32
            )

        grad_second = sum_backward(second_term, tok_rows)
        second_again, second_pull = jax.vjp(layer_norm, middle, gain_now[1], shift_now[2])
        grad_mid_norm, gain_one, shift_two = second_pull(grad_second)
        grad_middle = gradient + grad_mid_norm
        shift_one = jnp.sum(grad_middle, axis=0)
        grad_proj = gather_backward(grad_middle.astype(jnp.bfloat16))
        out_grad = scatter_rows(
            lax.dot_general(
                grad_proj, attended, (((0,), (0,)), ((), ())), preferred_element_type=jnp.float32
            )
        )
        grad_attended = jnp.dot(grad_proj, out_full, preferred_element_type=jnp.float32).astype(
            jnp.bfloat16
        )
        grad_query, grad_key_ext, grad_value_ext = attend_backward(
            queries, key_ext, allowed, log_norm, grad_attended
        )
        grad_pair_ext = jnp.stack([grad_key_ext, grad_value_ext])
        from_next = from_behind(grad_pair_ext[:, :margin].astype(jnp.bfloat16), "dp", -1).astype(
            jnp.float32
        )
        from_prev = from_behind(
            grad_pair_ext[:, margin + group_rows :].astype(jnp.bfloat16), "dp", 1
        ).astype(jnp.float32)
        grad_pair = grad_pair_ext[:, margin : margin + group_rows]
        grad_pair = (
            grad_pair.at[:, group_rows - margin :].add(from_next).at[:, :margin].add(from_prev)
        )
        grad_triple = jnp.concatenate(
            [grad_query.astype(jnp.bfloat16)[None], grad_pair.astype(jnp.bfloat16)], axis=0
        )
        qkv_grad = jnp.moveaxis(
            scatter_rows(
                jnp.einsum(
                    "gd,sge->dse", normed_full, grad_triple, preferred_element_type=jnp.float32
                )
            ),
            0,
            1,
        )
        triple_sums = jnp.sum(grad_triple.astype(jnp.float32), axis=1)

        def first_term(first_row, row_count):
            return jnp.einsum(
                "sge,sde->gd", grad_triple, qkv_full, preferred_element_type=jnp.float32
            )

        grad_first = sum_backward(first_term, tok_rows)
        first_again, first_pull = jax.vjp(layer_norm, stream_in, gain_now[0], shift_now[0])
        grad_in_norm, gain_zero, shift_zero = first_pull(grad_first)
        gradient = grad_middle + grad_in_norm
        unit_grads[layer_index] = jnp.concatenate(
            [triple_sums[0][None], triple_sums[2][None], up_bias_grad], axis=0
        )
        gain_grads[layer_index] = jnp.stack([gain_zero, gain_one])
        shift_grads[layer_index] = jnp.stack([shift_zero, shift_one, shift_two, shift_three])
        local_qkv[layer_index] = qkv_grad
        local_out[layer_index] = out_grad
        local_up[layer_index] = up_grad
        local_down[layer_index] = down_grad
    grad_qkv = jnp.stack(local_qkv).astype(jnp.float32)
    grad_out = jnp.stack(local_out).astype(jnp.float32)
    grad_up = jnp.stack(local_up).astype(jnp.float32)
    grad_down = jnp.stack(local_down).astype(jnp.float32)
    unit_local = jnp.stack(unit_grads)
    unit_wide = jnp.zeros((LAYERS, unit_local.shape[1], cols_here * tensor_size), jnp.float32)
    unit_wide = lax.dynamic_update_slice_in_dim(unit_wide, unit_local, tensor_index * cols_here, 2)
    small = jnp.concatenate(
        [jnp.stack(gain_grads), jnp.stack(shift_grads), unit_wide], axis=1
    )
    small_total = jnp.sum(from_everyone(small, "dp"), axis=0)
    small_total = jnp.sum(from_everyone(small_total, "tensor"), axis=0)
    gain_total = small_total[:, :2]
    shift_total = small_total[:, 2:6]
    unit_total = small_total[:, 6:]
    unit_mine = lax.dynamic_slice_in_dim(unit_total, tensor_index * cols_here, cols_here, 2)
    return (
        stream.astype(jnp.bfloat16),
        gradient.astype(jnp.bfloat16),
        grad_qkv,
        grad_out,
        grad_up,
        grad_down,
        unit_mine,
        gain_total,
        shift_total,
    )


def solution(mesh):
    placed = (
        P(("dp", "tensor"), None),
        P(),
        P(),
        P(None, None, "dp", "tensor"),
        P(None, "dp", "tensor"),
        P(None, "dp", None, "tensor"),
        P(None, "dp", None, "tensor"),
        P(None, None, "tensor"),
        P(),
        P(),
        P(("dp", "tensor"), None),
    )
    return jax.shard_map(
        local,
        mesh=mesh,
        in_specs=placed,
        out_specs=(
            P(("dp", "tensor"), None),
            P(("dp", "tensor"), None),
            P(None, None, "dp", "tensor"),
            P(None, "dp", "tensor"),
            P(None, "dp", None, "tensor"),
            P(None, "dp", None, "tensor"),
            P(None, None, "tensor"),
            P(),
            P(),
        ),
        check_vma=False,
    )
```

```python
import functools
import math

import jax
import jax.numpy as jnp
from jax import lax
from jax.experimental import pallas as pl
from jax.experimental.pallas import tpu as pltpu
from jax.sharding import PartitionSpec as P

MESH = pl.DeviceIdType.MESH

LAYERS = 1
IMG = 577
HD = 64


norm_eps = 1e-06
masked_score = -1e30


def from_everyone(value, axis):
    devices = lax.axis_size(axis)
    return lax.all_to_all(
        jnp.broadcast_to(value[None], (devices, *value.shape)), axis, 0, 0, tiled=True
    )


def joined_along(parts, dim):
    dims = list(parts.shape[1:])
    dims[dim] *= parts.shape[0]
    return jnp.moveaxis(parts, 0, dim).reshape(dims)


def collect(value, axis, dim):
    parts = from_everyone(value, axis)
    return joined_along(parts, dim)


def split_up(value, dim, devices):
    dims = value.shape
    parts = value.reshape(*dims[:dim], devices, dims[dim] // devices, *dims[dim + 1 :])
    return jnp.moveaxis(parts, dim, 0)


def summed_on_arrival(value, axis, dim):
    devices = lax.axis_size(axis)
    parts = lax.all_to_all(split_up(value, dim, devices), axis, 0, 0, tiled=True)
    return jnp.sum(parts.astype(jnp.float32), axis=0)


def rows_first(arrays, axis, dims):
    turned = [jnp.moveaxis(a, dim, 0) for a, dim in zip(arrays, dims)]
    both = jnp.concatenate([t.reshape(len(t), -1) for t in turned], axis=1)
    filled, at, outs = (lax.all_gather(both, axis, axis=0, tiled=True), 0, [])
    for t, dim in zip(turned, dims):
        slab = filled[:, at : at + t[0].size].reshape(-1, *t.shape[1:])
        outs.append(jnp.moveaxis(slab, 0, dim))
        at += t[0].size
    return tuple(outs)


def with_halo(value, sides, width):
    for axis, dim in sides:
        devices, length = (lax.axis_size(axis), value.shape[dim])
        up = [(i, (i + 1) % devices) for i in range(devices - 1)]
        down = [(j, i) for i, j in up]
        last = lax.slice_in_dim(value, length - width, length, axis=dim)
        initial = lax.slice_in_dim(value, 0, width, axis=dim)
        before = lax.ppermute(last, axis, up)
        after = lax.ppermute(initial, axis, down)
        value = jnp.concatenate([before, value, after], axis=dim)
    return value


def from_behind(block, axis, distance):
    devices = range(lax.axis_size(axis))
    route = [(i - distance, i) for i in devices if i - distance in devices]
    return lax.ppermute(block, axis, route)


def side_by_side(arrays, axis, dim, along):
    widths = [math.prod(a.shape[along:]) for a in arrays]
    both = jnp.concatenate(
        [a.reshape(*a.shape[:along], w) for a, w in zip(arrays, widths)], axis=along
    )
    filled = lax.psum_scatter(both, axis, scatter_dimension=dim, tiled=True)
    parts = jnp.split(filled, [sum(widths[:k]) for k in range(1, len(widths))], axis=along)
    return tuple(
        (b.reshape(*filled.shape[:along], *a.shape[along:]) for a, b in zip(arrays, parts))
    )


def scatter_rows(grad):
    return summed_on_arrival(grad.astype(jnp.bfloat16), "dp", 0)


def layer_norm(values, gain_row, shift_row):
    center = values - jnp.mean(values, axis=-1, keepdims=True)
    spread = jnp.mean(center * center, axis=-1, keepdims=True)
    return center * lax.rsqrt(spread + norm_eps) * gain_row + shift_row


def exact_gelu(values):
    return jax.nn.gelu(values, approximate=False)


def _gather_kernel(devices, x_ref, out_ref, send_sem, recv_sem):
    me = lax.axis_index("tensor")
    dp = lax.axis_index("dp")
    sib = me + 1 - 2 * lax.rem(me, 2)
    far = lax.rem(me + 2, devices)
    barrier = pltpu.get_barrier_semaphore()
    for peer in (sib, far):
        pl.semaphore_signal(barrier, inc=1, device_id=(dp, peer), device_id_type=MESH)
    pl.semaphore_wait(barrier, 2)
    near_copy = pltpu.make_async_remote_copy(
        src_ref=x_ref,
        dst_ref=out_ref.at[me],
        send_sem=send_sem.at[0],
        recv_sem=recv_sem.at[0],
        device_id=(dp, sib),
        device_id_type=MESH,
    )
    far_copy = pltpu.make_async_remote_copy(
        src_ref=x_ref,
        dst_ref=out_ref.at[me],
        send_sem=send_sem.at[1],
        recv_sem=recv_sem.at[1],
        device_id=(dp, far),
        device_id_type=MESH,
    )
    far_copy.start()
    near_copy.start()
    out_ref[me] = x_ref[...]
    far_copy.wait_recv()
    relay = pltpu.make_async_remote_copy(
        src_ref=out_ref.at[far],
        dst_ref=out_ref.at[far],
        send_sem=send_sem.at[2],
        recv_sem=recv_sem.at[2],
        device_id=(dp, sib),
        device_id_type=MESH,
    )
    relay.start()
    near_copy.wait_send()
    near_copy.wait_recv()
    far_copy.wait_send()
    relay.wait_send()
    relay.wait_recv()


def gather_rows(values):
    devices = lax.axis_size("tensor")
    if devices != 4:
        return collect(values, "tensor", 0)
    rows, width = values.shape
    parts = pl.pallas_call(
        functools.partial(_gather_kernel, devices),
        out_shape=jax.ShapeDtypeStruct((devices, rows, width), values.dtype),
        in_specs=[pl.BlockSpec(memory_space=pltpu.VMEM)],
        out_specs=pl.BlockSpec(memory_space=pltpu.VMEM),
        scratch_shapes=[
            pltpu.SemaphoreType.DMA((3,)),
            pltpu.SemaphoreType.DMA((3,)),
        ],
        compiler_params=pltpu.CompilerParams(collective_id=0, has_side_effects=True),
    )(values)
    return parts.reshape(devices * rows, width)


def _exchange_kernel(devices, x_ref, out_ref, send_sem, recv_sem):
    me = lax.axis_index("tensor")
    dp = lax.axis_index("dp")
    barrier = pltpu.get_barrier_semaphore()
    for step in range(1, devices):
        pl.semaphore_signal(
            barrier, inc=1, device_id=(dp, lax.rem(me + step, devices)), device_id_type=MESH
        )
    pl.semaphore_wait(barrier, devices - 1)
    copies = []
    for step in range(1, devices):
        peer = lax.rem(me + step, devices)
        copy = pltpu.make_async_remote_copy(
            src_ref=x_ref.at[peer],
            dst_ref=out_ref.at[me],
            send_sem=send_sem.at[step - 1],
            recv_sem=recv_sem.at[step - 1],
            device_id=(dp, peer),
            device_id_type=MESH,
        )
        copy.start()
        copies.append(copy)
    out_ref[me] = x_ref[me]
    for copy in copies:
        copy.wait()


def exchange_rows(parts):
    devices = parts.shape[0]
    return pl.pallas_call(
        functools.partial(_exchange_kernel, devices),
        out_shape=jax.ShapeDtypeStruct(parts.shape, parts.dtype),
        in_specs=[pl.BlockSpec(memory_space=pltpu.VMEM)],
        out_specs=pl.BlockSpec(memory_space=pltpu.VMEM),
        scratch_shapes=[
            pltpu.SemaphoreType.DMA((devices - 1,)),
            pltpu.SemaphoreType.DMA((devices - 1,)),
        ],
        compiler_params=pltpu.CompilerParams(collective_id=1, has_side_effects=True),
    )(parts)


def _reduce_kernel(devices, x_ref, out_ref, held, mate, pre, send_sem, recv_sem):
    me = lax.axis_index("tensor")
    dp = lax.axis_index("dp")
    sib = me + 1 - 2 * lax.rem(me, 2)
    far = lax.rem(me + 2, devices)
    other = lax.rem(sib + 2, devices)
    barrier = pltpu.get_barrier_semaphore()
    for peer in (sib, far):
        pl.semaphore_signal(barrier, inc=1, device_id=(dp, peer), device_id_type=MESH)
    pl.semaphore_wait(barrier, 2)
    own_copy = pltpu.make_async_remote_copy(
        src_ref=x_ref.at[sib],
        dst_ref=held.at[0],
        send_sem=send_sem.at[0],
        recv_sem=recv_sem.at[0],
        device_id=(dp, sib),
        device_id_type=MESH,
    )
    mate_copy = pltpu.make_async_remote_copy(
        src_ref=x_ref.at[other],
        dst_ref=mate,
        send_sem=send_sem.at[1],
        recv_sem=recv_sem.at[1],
        device_id=(dp, sib),
        device_id_type=MESH,
    )
    mate_copy.start()
    own_copy.start()
    mate_copy.wait_recv()
    pre[...] = (x_ref[far].astype(jnp.float32) + mate[...].astype(jnp.float32)).astype(pre.dtype)
    own_copy.wait_recv()
    out_ref[...] = x_ref[me].astype(jnp.float32) + held[0].astype(jnp.float32)
    far_copy = pltpu.make_async_remote_copy(
        src_ref=pre,
        dst_ref=held.at[1],
        send_sem=send_sem.at[2],
        recv_sem=recv_sem.at[2],
        device_id=(dp, far),
        device_id_type=MESH,
    )
    far_copy.start()
    far_copy.wait_recv()
    out_ref[...] += held[1].astype(jnp.float32)
    own_copy.wait_send()
    mate_copy.wait_send()
    far_copy.wait_send()


def summed_over_tensor(value):
    devices = lax.axis_size("tensor")
    parts = split_up(value, 0, devices)
    if devices != 4:
        return jnp.sum(exchange_rows(parts).astype(jnp.float32), axis=0)
    rows, width = parts.shape[1:]
    return pl.pallas_call(
        functools.partial(_reduce_kernel, devices),
        out_shape=jax.ShapeDtypeStruct((rows, width), jnp.float32),
        in_specs=[pl.BlockSpec(memory_space=pltpu.VMEM)],
        out_specs=pl.BlockSpec(memory_space=pltpu.VMEM),
        scratch_shapes=[
            pltpu.VMEM((2, rows, width), parts.dtype),
            pltpu.VMEM((rows, width), parts.dtype),
            pltpu.VMEM((rows, width), parts.dtype),
            pltpu.SemaphoreType.DMA((3,)),
            pltpu.SemaphoreType.DMA((3,)),
        ],
        compiler_params=pltpu.CompilerParams(collective_id=1, has_side_effects=True),
    )(parts)


def gather_forward(values):
    return gather_rows(values)


def gather_backward(values):
    return gather_rows(values)


def sum_forward(product, tok_rows):
    return summed_over_tensor(
        product(jnp.int32(0), tok_rows * lax.axis_size("tensor")).astype(jnp.bfloat16)
    )


def sum_backward(product, tok_rows):
    return summed_over_tensor(
        product(jnp.int32(0), tok_rows * lax.axis_size("tensor")).astype(jnp.bfloat16)
    )


def head_scores(query_head, key_head, allowed):
    raw = lax.dot_general(
        query_head, key_head, (((1,), (1,)), ((), ())), preferred_element_type=jnp.float32
    )
    return jnp.where(allowed, raw * HD ** (-0.5), masked_score)


def split_heads(queries, key_ext):
    heads_here = queries.shape[1] // HD
    query_heads = queries.reshape(queries.shape[0], heads_here, HD)
    key_heads = key_ext[0].reshape(key_ext.shape[1], heads_here, HD)
    value_heads = key_ext[1].reshape(key_ext.shape[1], heads_here, HD)
    return (heads_here, query_heads, key_heads, value_heads)


def merge_heads(per_head):
    return jnp.transpose(per_head, (1, 0, 2)).reshape(
        per_head.shape[1], per_head.shape[0] * per_head.shape[2]
    )


def attend_forward(queries, key_ext, allowed):
    heads_here, query_heads, key_heads, value_heads = split_heads(queries, key_ext)

    def one_head(head_index):
        query_head = lax.dynamic_index_in_dim(query_heads, head_index, 1, keepdims=False)
        key_head = lax.dynamic_index_in_dim(key_heads, head_index, 1, keepdims=False)
        value_head = lax.dynamic_index_in_dim(value_heads, head_index, 1, keepdims=False)
        scores = head_scores(query_head, key_head, allowed)
        row_top = jnp.max(scores, axis=1, keepdims=True)
        exponent = jnp.exp(scores - row_top)
        row_total = jnp.sum(exponent, axis=1, keepdims=True)
        prob_low = (exponent / row_total).astype(jnp.bfloat16)
        head_out = jnp.dot(prob_low, value_head, preferred_element_type=jnp.float32)
        return (head_out, (row_top + jnp.log(row_total))[:, 0])

    head_outs, log_norm = lax.map(one_head, jnp.arange(heads_here, dtype=jnp.int32))
    return (merge_heads(head_outs), log_norm)


def attend_backward(queries, key_ext, allowed, log_norm, grad_attended):
    heads_here, query_heads, key_heads, value_heads = split_heads(queries, key_ext)
    grad_heads = grad_attended.reshape(grad_attended.shape[0], heads_here, HD)

    def one_head(inputs):
        head_index, norm_row = inputs
        query_head = lax.dynamic_index_in_dim(query_heads, head_index, 1, keepdims=False)
        key_head = lax.dynamic_index_in_dim(key_heads, head_index, 1, keepdims=False)
        value_head = lax.dynamic_index_in_dim(value_heads, head_index, 1, keepdims=False)
        grad_head = lax.dynamic_index_in_dim(grad_heads, head_index, 1, keepdims=False)
        prob_full = jnp.exp(head_scores(query_head, key_head, allowed) - norm_row[:, None])
        prob_low = prob_full.astype(jnp.bfloat16)
        grad_value = lax.dot_general(
            prob_low, grad_head, (((0,), (0,)), ((), ())), preferred_element_type=jnp.float32
        )
        grad_prob = lax.dot_general(
            grad_head, value_head, (((1,), (1,)), ((), ())), preferred_element_type=jnp.float32
        )
        grad_score = (
            prob_full * (grad_prob - jnp.sum(prob_full * grad_prob, axis=1, keepdims=True))
        ).astype(jnp.bfloat16)
        grad_query = jnp.dot(grad_score, key_head, preferred_element_type=jnp.float32) * HD ** (
            -0.5
        )
        grad_key = lax.dot_general(
            grad_score, query_head, (((0,), (0,)), ((), ())), preferred_element_type=jnp.float32
        ) * HD ** (-0.5)
        return (grad_query, grad_key, grad_value)

    grad_queries, grad_keys, grad_values = lax.map(
        one_head, (jnp.arange(heads_here, dtype=jnp.int32), log_norm)
    )
    return (merge_heads(grad_queries), merge_heads(grad_keys), merge_heads(grad_values))


def local(
    tokens,
    segment,
    real_token,
    qkv_weight,
    out_weight,
    up_weight,
    down_weight,
    unit_bias,
    norm_gain,
    row_bias,
    cotangent,
):
    tok_rows = tokens.shape[0]
    tensor_size = lax.axis_size("tensor")
    group_rows = tok_rows * tensor_size
    margin = IMG - 1
    cols_here = qkv_weight.shape[3]
    dp_index = lax.axis_index("dp")
    tensor_index = lax.axis_index("tensor")
    group_first = dp_index * group_rows
    own_first = group_first + tensor_index * tok_rows
    segment_pad = jnp.pad(segment, (margin, margin), constant_values=-1)
    real_pad = jnp.pad(real_token, (margin, margin))
    segment_query = lax.dynamic_slice_in_dim(segment, group_first, group_rows, 0)
    segment_key = lax.dynamic_slice_in_dim(segment_pad, group_first, group_rows + 2 * margin, 0)
    real_key = lax.dynamic_slice_in_dim(real_pad, group_first, group_rows + 2 * margin, 0)
    place_query = jnp.arange(group_rows, dtype=jnp.int32)
    place_key = jnp.arange(group_rows + 2 * margin, dtype=jnp.int32) - margin
    allowed = (segment_query[:, None] == segment_key[None, :]) & (
        (real_key[None, :] == 1) | (place_query[:, None] == place_key[None, :])
    )
    own_real = lax.dynamic_slice_in_dim(real_token, own_first, tok_rows, 0).astype(jnp.float32)
    stream = tokens.astype(jnp.float32)
    layer_index = 0
    qkv_full = jnp.moveaxis(collect(jnp.moveaxis(qkv_weight[layer_index], 1, 0), "dp", 0), 0, 1)
    out_full = collect(out_weight[layer_index], "dp", 0)
    up_full = collect(up_weight[layer_index], "dp", 0)
    down_full = collect(down_weight[layer_index], "dp", 0)
    gathered = (qkv_full, out_full, up_full, down_full)
    gain_now = norm_gain[layer_index].astype(jnp.float32)
    shift_now = row_bias[layer_index].astype(jnp.float32)
    bias_now = unit_bias[layer_index].astype(jnp.float32)
    normed_full = gather_forward(layer_norm(stream, gain_now[0], shift_now[0]).astype(jnp.bfloat16))
    projected = jnp.einsum("gd,sde->sge", normed_full, qkv_full, preferred_element_type=jnp.float32)
    queries = (projected[0] + bias_now[0]).astype(jnp.bfloat16)
    key_value = jnp.stack([projected[1], projected[2] + bias_now[1]]).astype(jnp.bfloat16)
    key_ext = with_halo(key_value, (("dp", 1),), margin)
    attended, log_norm = attend_forward(queries, key_ext, allowed)
    attended = attended.astype(jnp.bfloat16)

    def attention_term(first_row, row_count):
        return lax.dot_general(
            attended, out_full, (((1,), (1,)), ((), ())), preferred_element_type=jnp.float32
        )

    middle = stream + sum_forward(attention_term, tok_rows) + shift_now[1]
    second_full = gather_forward(layer_norm(middle, gain_now[1], shift_now[2]).astype(jnp.bfloat16))
    hidden = (
        jnp.einsum("gd,dre->gre", second_full, up_full, preferred_element_type=jnp.float32)
        + bias_now[2:][None]
    )
    active = exact_gelu(hidden).astype(jnp.bfloat16)

    def feed_term(first_row, row_count):
        return jnp.einsum("gre,ore->go", active, down_full, preferred_element_type=jnp.float32)

    kept_weights = gathered
    records = [
        (
            stream,
            middle,
            normed_full,
            second_full,
            queries,
            key_ext,
            log_norm,
            attended,
            hidden,
            active,
            kept_weights,
        )
    ]
    stream = middle + sum_forward(feed_term, tok_rows) + shift_now[3]
    gradient = cotangent.astype(jnp.float32) * own_real[:, None]
    local_qkv = [None] * LAYERS
    local_out = [None] * LAYERS
    local_up = [None] * LAYERS
    local_down = [None] * LAYERS
    unit_grads = [None] * LAYERS
    gain_grads = [None] * LAYERS
    shift_grads = [None] * LAYERS
    for layer_index in reversed(range(LAYERS)):
        (
            stream_in,
            middle,
            normed_full,
            second_full,
            queries,
            key_ext,
            log_norm,
            attended,
            hidden,
            active,
            kept_weights,
        ) = records[layer_index]
        qkv_full, out_full, up_full, down_full = kept_weights
        gain_now = norm_gain[layer_index].astype(jnp.float32)
        shift_now = row_bias[layer_index].astype(jnp.float32)
        shift_three = jnp.sum(gradient, axis=0)
        grad_mlp = gather_backward(gradient.astype(jnp.bfloat16))
        down_grad = scatter_rows(
            jnp.einsum("go,gre->ore", grad_mlp, active, preferred_element_type=jnp.float32)
        )
        grad_active = jnp.einsum(
            "go,ore->gre", grad_mlp, down_full, preferred_element_type=jnp.float32
        )
        gelu_again, gelu_pull = jax.vjp(exact_gelu, hidden)
        grad_hidden = gelu_pull(grad_active)[0].astype(jnp.bfloat16)
        up_bias_grad = jnp.sum(grad_hidden.astype(jnp.float32), axis=0)
        up_grad = scatter_rows(
            jnp.einsum("gd,gre->dre", second_full, grad_hidden, preferred_element_type=jnp.float32)
        )

        def second_term(first_row, row_count):
            return jnp.einsum(
                "gre,dre->gd", grad_hidden, up_full, preferred_element_type=jnp.float32
            )

        grad_second = sum_backward(second_term, tok_rows)
        second_again, second_pull = jax.vjp(layer_norm, middle, gain_now[1], shift_now[2])
        grad_mid_norm, gain_one, shift_two = second_pull(grad_second)
        grad_middle = gradient + grad_mid_norm
        shift_one = jnp.sum(grad_middle, axis=0)
        grad_proj = gather_backward(grad_middle.astype(jnp.bfloat16))
        out_grad = scatter_rows(
            lax.dot_general(
                grad_proj, attended, (((0,), (0,)), ((), ())), preferred_element_type=jnp.float32
            )
        )
        grad_attended = jnp.dot(grad_proj, out_full, preferred_element_type=jnp.float32).astype(
            jnp.bfloat16
        )
        grad_query, grad_key_ext, grad_value_ext = attend_backward(
            queries, key_ext, allowed, log_norm, grad_attended
        )
        grad_pair_ext = jnp.stack([grad_key_ext, grad_value_ext])
        from_next = from_behind(grad_pair_ext[:, :margin].astype(jnp.bfloat16), "dp", -1).astype(
            jnp.float32
        )
        from_prev = from_behind(
            grad_pair_ext[:, margin + group_rows :].astype(jnp.bfloat16), "dp", 1
        ).astype(jnp.float32)
        grad_pair = grad_pair_ext[:, margin : margin + group_rows]
        grad_pair = (
            grad_pair.at[:, group_rows - margin :].add(from_next).at[:, :margin].add(from_prev)
        )
        grad_triple = jnp.concatenate(
            [grad_query.astype(jnp.bfloat16)[None], grad_pair.astype(jnp.bfloat16)], axis=0
        )
        qkv_grad = jnp.moveaxis(
            scatter_rows(
                jnp.einsum(
                    "gd,sge->dse", normed_full, grad_triple, preferred_element_type=jnp.float32
                )
            ),
            0,
            1,
        )
        triple_sums = jnp.sum(grad_triple.astype(jnp.float32), axis=1)

        def first_term(first_row, row_count):
            return jnp.einsum(
                "sge,sde->gd", grad_triple, qkv_full, preferred_element_type=jnp.float32
            )

        grad_first = sum_backward(first_term, tok_rows)
        first_again, first_pull = jax.vjp(layer_norm, stream_in, gain_now[0], shift_now[0])
        grad_in_norm, gain_zero, shift_zero = first_pull(grad_first)
        gradient = grad_middle + grad_in_norm
        unit_grads[layer_index] = jnp.concatenate(
            [triple_sums[0][None], triple_sums[2][None], up_bias_grad], axis=0
        )
        gain_grads[layer_index] = jnp.stack([gain_zero, gain_one])
        shift_grads[layer_index] = jnp.stack([shift_zero, shift_one, shift_two, shift_three])
        local_qkv[layer_index] = qkv_grad
        local_out[layer_index] = out_grad
        local_up[layer_index] = up_grad
        local_down[layer_index] = down_grad
    grad_qkv = jnp.stack(local_qkv).astype(jnp.float32)
    grad_out = jnp.stack(local_out).astype(jnp.float32)
    grad_up = jnp.stack(local_up).astype(jnp.float32)
    grad_down = jnp.stack(local_down).astype(jnp.float32)
    unit_local = jnp.stack(unit_grads)
    unit_wide = jnp.zeros((LAYERS, unit_local.shape[1], cols_here * tensor_size), jnp.float32)
    unit_wide = lax.dynamic_update_slice_in_dim(unit_wide, unit_local, tensor_index * cols_here, 2)
    small = jnp.concatenate(
        [jnp.stack(gain_grads), jnp.stack(shift_grads), unit_wide], axis=1
    )
    small_total = jnp.sum(from_everyone(small, "dp"), axis=0)
    small_total = jnp.sum(from_everyone(small_total, "tensor"), axis=0)
    gain_total = small_total[:, :2]
    shift_total = small_total[:, 2:6]
    unit_total = small_total[:, 6:]
    unit_mine = lax.dynamic_slice_in_dim(unit_total, tensor_index * cols_here, cols_here, 2)
    return (
        stream.astype(jnp.bfloat16),
        gradient.astype(jnp.bfloat16),
        grad_qkv,
        grad_out,
        grad_up,
        grad_down,
        unit_mine,
        gain_total,
        shift_total,
    )


def solution(mesh):
    placed = (
        P(("dp", "tensor"), None),
        P(),
        P(),
        P(None, None, "dp", "tensor"),
        P(None, "dp", "tensor"),
        P(None, "dp", None, "tensor"),
        P(None, "dp", None, "tensor"),
        P(None, None, "tensor"),
        P(),
        P(),
        P(("dp", "tensor"), None),
    )
    return jax.shard_map(
        local,
        mesh=mesh,
        in_specs=placed,
        out_specs=(
            P(("dp", "tensor"), None),
            P(("dp", "tensor"), None),
            P(None, None, "dp", "tensor"),
            P(None, "dp", "tensor"),
            P(None, "dp", None, "tensor"),
            P(None, "dp", None, "tensor"),
            P(None, None, "tensor"),
            P(),
            P(),
        ),
        check_vma=False,
    )
```

```python
import functools
import math

import jax
import jax.numpy as jnp
from jax import lax
from jax.experimental import pallas as pl
from jax.experimental.pallas import tpu as pltpu
from jax.sharding import PartitionSpec as P

MESH = pl.DeviceIdType.MESH

LAYERS = 1
IMG = 577
HD = 64


norm_eps = 1e-06
masked_score = -1e30


def from_everyone(value, axis):
    devices = lax.axis_size(axis)
    return lax.all_to_all(
        jnp.broadcast_to(value[None], (devices, *value.shape)), axis, 0, 0, tiled=True
    )


def joined_along(parts, dim):
    dims = list(parts.shape[1:])
    dims[dim] *= parts.shape[0]
    return jnp.moveaxis(parts, 0, dim).reshape(dims)


def collect(value, axis, dim):
    parts = from_everyone(value, axis)
    return joined_along(parts, dim)


def split_up(value, dim, devices):
    dims = value.shape
    parts = value.reshape(*dims[:dim], devices, dims[dim] // devices, *dims[dim + 1 :])
    return jnp.moveaxis(parts, dim, 0)


def summed_on_arrival(value, axis, dim):
    devices = lax.axis_size(axis)
    parts = lax.all_to_all(split_up(value, dim, devices), axis, 0, 0, tiled=True)
    return jnp.sum(parts.astype(jnp.float32), axis=0)


def rows_first(arrays, axis, dims):
    turned = [jnp.moveaxis(a, dim, 0) for a, dim in zip(arrays, dims)]
    both = jnp.concatenate([t.reshape(len(t), -1) for t in turned], axis=1)
    filled, at, outs = (lax.all_gather(both, axis, axis=0, tiled=True), 0, [])
    for t, dim in zip(turned, dims):
        slab = filled[:, at : at + t[0].size].reshape(-1, *t.shape[1:])
        outs.append(jnp.moveaxis(slab, 0, dim))
        at += t[0].size
    return tuple(outs)


def with_halo(value, sides, width):
    for axis, dim in sides:
        devices, length = (lax.axis_size(axis), value.shape[dim])
        up = [(i, (i + 1) % devices) for i in range(devices - 1)]
        down = [(j, i) for i, j in up]
        last = lax.slice_in_dim(value, length - width, length, axis=dim)
        initial = lax.slice_in_dim(value, 0, width, axis=dim)
        before = lax.ppermute(last, axis, up)
        after = lax.ppermute(initial, axis, down)
        value = jnp.concatenate([before, value, after], axis=dim)
    return value


def from_behind(block, axis, distance):
    devices = range(lax.axis_size(axis))
    route = [(i - distance, i) for i in devices if i - distance in devices]
    return lax.ppermute(block, axis, route)


def side_by_side(arrays, axis, dim, along):
    widths = [math.prod(a.shape[along:]) for a in arrays]
    both = jnp.concatenate(
        [a.reshape(*a.shape[:along], w) for a, w in zip(arrays, widths)], axis=along
    )
    filled = lax.psum_scatter(both, axis, scatter_dimension=dim, tiled=True)
    parts = jnp.split(filled, [sum(widths[:k]) for k in range(1, len(widths))], axis=along)
    return tuple(
        (b.reshape(*filled.shape[:along], *a.shape[along:]) for a, b in zip(arrays, parts))
    )


def scatter_rows(grad):
    return summed_on_arrival(grad.astype(jnp.bfloat16), "dp", 0)


def layer_norm(values, gain_row, shift_row):
    center = values - jnp.mean(values, axis=-1, keepdims=True)
    spread = jnp.mean(center * center, axis=-1, keepdims=True)
    return center * lax.rsqrt(spread + norm_eps) * gain_row + shift_row


def exact_gelu(values):
    return jax.nn.gelu(values, approximate=False)


def _gather_kernel(devices, x_ref, out_ref, send_sem, recv_sem):
    me = lax.axis_index("tensor")
    dp = lax.axis_index("dp")
    sib = me + 1 - 2 * lax.rem(me, 2)
    far = lax.rem(me + 2, devices)
    barrier = pltpu.get_barrier_semaphore()
    for peer in (sib, far):
        pl.semaphore_signal(barrier, inc=1, device_id=(dp, peer), device_id_type=MESH)
    pl.semaphore_wait(barrier, 2)
    near_copy = pltpu.make_async_remote_copy(
        src_ref=x_ref,
        dst_ref=out_ref.at[me],
        send_sem=send_sem.at[0],
        recv_sem=recv_sem.at[0],
        device_id=(dp, sib),
        device_id_type=MESH,
    )
    far_copy = pltpu.make_async_remote_copy(
        src_ref=x_ref,
        dst_ref=out_ref.at[me],
        send_sem=send_sem.at[1],
        recv_sem=recv_sem.at[1],
        device_id=(dp, far),
        device_id_type=MESH,
    )
    far_copy.start()
    near_copy.start()
    out_ref[me] = x_ref[...]
    far_copy.wait_recv()
    relay = pltpu.make_async_remote_copy(
        src_ref=out_ref.at[far],
        dst_ref=out_ref.at[far],
        send_sem=send_sem.at[2],
        recv_sem=recv_sem.at[2],
        device_id=(dp, sib),
        device_id_type=MESH,
    )
    relay.start()
    near_copy.wait_send()
    near_copy.wait_recv()
    far_copy.wait_send()
    relay.wait_send()
    relay.wait_recv()


def gather_rows(values):
    devices = lax.axis_size("tensor")
    if devices != 4:
        return collect(values, "tensor", 0)
    rows, width = values.shape
    parts = pl.pallas_call(
        functools.partial(_gather_kernel, devices),
        out_shape=jax.ShapeDtypeStruct((devices, rows, width), values.dtype),
        in_specs=[pl.BlockSpec(memory_space=pltpu.VMEM)],
        out_specs=pl.BlockSpec(memory_space=pltpu.VMEM),
        scratch_shapes=[
            pltpu.SemaphoreType.DMA((3,)),
            pltpu.SemaphoreType.DMA((3,)),
        ],
        compiler_params=pltpu.CompilerParams(collective_id=0, has_side_effects=True),
    )(values)
    return parts.reshape(devices * rows, width)


def _exchange_kernel(devices, x_ref, out_ref, send_sem, recv_sem):
    me = lax.axis_index("tensor")
    dp = lax.axis_index("dp")
    barrier = pltpu.get_barrier_semaphore()
    for step in range(1, devices):
        pl.semaphore_signal(
            barrier, inc=1, device_id=(dp, lax.rem(me + step, devices)), device_id_type=MESH
        )
    pl.semaphore_wait(barrier, devices - 1)
    copies = []
    for step in range(1, devices):
        peer = lax.rem(me + step, devices)
        copy = pltpu.make_async_remote_copy(
            src_ref=x_ref.at[peer],
            dst_ref=out_ref.at[me],
            send_sem=send_sem.at[step - 1],
            recv_sem=recv_sem.at[step - 1],
            device_id=(dp, peer),
            device_id_type=MESH,
        )
        copy.start()
        copies.append(copy)
    out_ref[me] = x_ref[me]
    for copy in copies:
        copy.wait()


def exchange_rows(parts):
    devices = parts.shape[0]
    return pl.pallas_call(
        functools.partial(_exchange_kernel, devices),
        out_shape=jax.ShapeDtypeStruct(parts.shape, parts.dtype),
        in_specs=[pl.BlockSpec(memory_space=pltpu.VMEM)],
        out_specs=pl.BlockSpec(memory_space=pltpu.VMEM),
        scratch_shapes=[
            pltpu.SemaphoreType.DMA((devices - 1,)),
            pltpu.SemaphoreType.DMA((devices - 1,)),
        ],
        compiler_params=pltpu.CompilerParams(collective_id=1, has_side_effects=True),
    )(parts)


def _reduce_kernel(devices, x_ref, out_ref, held, mate, pre, send_sem, recv_sem):
    me = lax.axis_index("tensor")
    dp = lax.axis_index("dp")
    sib = me + 1 - 2 * lax.rem(me, 2)
    far = lax.rem(me + 2, devices)
    other = lax.rem(sib + 2, devices)
    barrier = pltpu.get_barrier_semaphore()
    for peer in (sib, far):
        pl.semaphore_signal(barrier, inc=1, device_id=(dp, peer), device_id_type=MESH)
    pl.semaphore_wait(barrier, 2)
    own_copy = pltpu.make_async_remote_copy(
        src_ref=x_ref.at[sib],
        dst_ref=held.at[0],
        send_sem=send_sem.at[0],
        recv_sem=recv_sem.at[0],
        device_id=(dp, sib),
        device_id_type=MESH,
    )
    mate_copy = pltpu.make_async_remote_copy(
        src_ref=x_ref.at[other],
        dst_ref=mate,
        send_sem=send_sem.at[1],
        recv_sem=recv_sem.at[1],
        device_id=(dp, sib),
        device_id_type=MESH,
    )
    mate_copy.start()
    own_copy.start()
    mate_copy.wait_recv()
    pre[...] = (x_ref[far].astype(jnp.float32) + mate[...].astype(jnp.float32)).astype(pre.dtype)
    own_copy.wait_recv()
    out_ref[...] = x_ref[me].astype(jnp.float32) + held[0].astype(jnp.float32)
    far_copy = pltpu.make_async_remote_copy(
        src_ref=pre,
        dst_ref=held.at[1],
        send_sem=send_sem.at[2],
        recv_sem=recv_sem.at[2],
        device_id=(dp, far),
        device_id_type=MESH,
    )
    far_copy.start()
    far_copy.wait_recv()
    out_ref[...] += held[1].astype(jnp.float32)
    own_copy.wait_send()
    mate_copy.wait_send()
    far_copy.wait_send()


def summed_over_tensor(value):
    devices = lax.axis_size("tensor")
    parts = split_up(value, 0, devices)
    if devices != 4:
        return jnp.sum(exchange_rows(parts).astype(jnp.float32), axis=0)
    rows, width = parts.shape[1:]
    return pl.pallas_call(
        functools.partial(_reduce_kernel, devices),
        out_shape=jax.ShapeDtypeStruct((rows, width), jnp.float32),
        in_specs=[pl.BlockSpec(memory_space=pltpu.VMEM)],
        out_specs=pl.BlockSpec(memory_space=pltpu.VMEM),
        scratch_shapes=[
            pltpu.VMEM((2, rows, width), parts.dtype),
            pltpu.VMEM((rows, width), parts.dtype),
            pltpu.VMEM((rows, width), parts.dtype),
            pltpu.SemaphoreType.DMA((3,)),
            pltpu.SemaphoreType.DMA((3,)),
        ],
        compiler_params=pltpu.CompilerParams(collective_id=1, has_side_effects=True),
    )(parts)


def gather_forward(values):
    return gather_rows(values)


def gather_backward(values):
    return gather_rows(values)


def sum_forward(product, tok_rows):
    return summed_over_tensor(
        product(jnp.int32(0), tok_rows * lax.axis_size("tensor")).astype(jnp.bfloat16)
    )


def sum_backward(product, tok_rows):
    return summed_over_tensor(
        product(jnp.int32(0), tok_rows * lax.axis_size("tensor")).astype(jnp.bfloat16)
    )


def head_scores(query_head, key_head, allowed):
    raw = lax.dot_general(
        query_head, key_head, (((1,), (1,)), ((), ())), preferred_element_type=jnp.float32
    )
    return jnp.where(allowed, raw * HD ** (-0.5), masked_score)


def split_heads(queries, key_ext):
    heads_here = queries.shape[1] // HD
    query_heads = queries.reshape(queries.shape[0], heads_here, HD)
    key_heads = key_ext[0].reshape(key_ext.shape[1], heads_here, HD)
    value_heads = key_ext[1].reshape(key_ext.shape[1], heads_here, HD)
    return (heads_here, query_heads, key_heads, value_heads)


def merge_heads(per_head):
    return jnp.transpose(per_head, (1, 0, 2)).reshape(
        per_head.shape[1], per_head.shape[0] * per_head.shape[2]
    )


def attend_forward(queries, key_ext, allowed):
    heads_here, query_heads, key_heads, value_heads = split_heads(queries, key_ext)

    def one_head(head_index):
        query_head = lax.dynamic_index_in_dim(query_heads, head_index, 1, keepdims=False)
        key_head = lax.dynamic_index_in_dim(key_heads, head_index, 1, keepdims=False)
        value_head = lax.dynamic_index_in_dim(value_heads, head_index, 1, keepdims=False)
        scores = head_scores(query_head, key_head, allowed)
        row_top = jnp.max(scores, axis=1, keepdims=True)
        exponent = jnp.exp(scores - row_top)
        row_total = jnp.sum(exponent, axis=1, keepdims=True)
        prob_low = (exponent / row_total).astype(jnp.bfloat16)
        head_out = jnp.dot(prob_low, value_head, preferred_element_type=jnp.float32)
        return (head_out, (row_top + jnp.log(row_total))[:, 0])

    head_outs, log_norm = lax.map(one_head, jnp.arange(heads_here, dtype=jnp.int32))
    return (merge_heads(head_outs), log_norm)


def attend_backward(queries, key_ext, allowed, log_norm, grad_attended):
    heads_here, query_heads, key_heads, value_heads = split_heads(queries, key_ext)
    grad_heads = grad_attended.reshape(grad_attended.shape[0], heads_here, HD)

    def one_head(inputs):
        head_index, norm_row = inputs
        query_head = lax.dynamic_index_in_dim(query_heads, head_index, 1, keepdims=False)
        key_head = lax.dynamic_index_in_dim(key_heads, head_index, 1, keepdims=False)
        value_head = lax.dynamic_index_in_dim(value_heads, head_index, 1, keepdims=False)
        grad_head = lax.dynamic_index_in_dim(grad_heads, head_index, 1, keepdims=False)
        prob_full = jnp.exp(head_scores(query_head, key_head, allowed) - norm_row[:, None])
        prob_low = prob_full.astype(jnp.bfloat16)
        grad_value = lax.dot_general(
            prob_low, grad_head, (((0,), (0,)), ((), ())), preferred_element_type=jnp.float32
        )
        grad_prob = lax.dot_general(
            grad_head, value_head, (((1,), (1,)), ((), ())), preferred_element_type=jnp.float32
        )
        grad_score = (
            prob_full * (grad_prob - jnp.sum(prob_full * grad_prob, axis=1, keepdims=True))
        ).astype(jnp.bfloat16)
        grad_query = jnp.dot(grad_score, key_head, preferred_element_type=jnp.float32) * HD ** (
            -0.5
        )
        grad_key = lax.dot_general(
            grad_score, query_head, (((0,), (0,)), ((), ())), preferred_element_type=jnp.float32
        ) * HD ** (-0.5)
        return (grad_query, grad_key, grad_value)

    grad_queries, grad_keys, grad_values = lax.map(
        one_head, (jnp.arange(heads_here, dtype=jnp.int32), log_norm)
    )
    return (merge_heads(grad_queries), merge_heads(grad_keys), merge_heads(grad_values))


def local(
    tokens,
    segment,
    real_token,
    qkv_weight,
    out_weight,
    up_weight,
    down_weight,
    unit_bias,
    norm_gain,
    row_bias,
    cotangent,
):
    tok_rows = tokens.shape[0]
    tensor_size = lax.axis_size("tensor")
    group_rows = tok_rows * tensor_size
    margin = IMG - 1
    cols_here = qkv_weight.shape[3]
    dp_index = lax.axis_index("dp")
    tensor_index = lax.axis_index("tensor")
    group_first = dp_index * group_rows
    own_first = group_first + tensor_index * tok_rows
    segment_pad = jnp.pad(segment, (margin, margin), constant_values=-1)
    real_pad = jnp.pad(real_token, (margin, margin))
    segment_query = lax.dynamic_slice_in_dim(segment, group_first, group_rows, 0)
    segment_key = lax.dynamic_slice_in_dim(segment_pad, group_first, group_rows + 2 * margin, 0)
    real_key = lax.dynamic_slice_in_dim(real_pad, group_first, group_rows + 2 * margin, 0)
    place_query = jnp.arange(group_rows, dtype=jnp.int32)
    place_key = jnp.arange(group_rows + 2 * margin, dtype=jnp.int32) - margin
    allowed = (segment_query[:, None] == segment_key[None, :]) & (
        (real_key[None, :] == 1) | (place_query[:, None] == place_key[None, :])
    )
    own_real = lax.dynamic_slice_in_dim(real_token, own_first, tok_rows, 0).astype(jnp.float32)
    stream = tokens.astype(jnp.float32)
    layer_index = 0
    qkv_local = jnp.moveaxis(qkv_weight[layer_index], 1, 0)
    out_local, up_local, down_local = (
        out_weight[layer_index],
        up_weight[layer_index],
        down_weight[layer_index],
    )
    gain_now = norm_gain[layer_index].astype(jnp.float32)
    shift_now = row_bias[layer_index].astype(jnp.float32)
    bias_now = unit_bias[layer_index].astype(jnp.float32)
    normed_full = gather_forward(layer_norm(stream, gain_now[0], shift_now[0]).astype(jnp.bfloat16))
    normed_full, qkv_local = lax.optimization_barrier((normed_full, qkv_local))
    qkv_full = jnp.moveaxis(collect(qkv_local, "dp", 0), 0, 1)
    projected = jnp.einsum("gd,sde->sge", normed_full, qkv_full, preferred_element_type=jnp.float32)
    queries = (projected[0] + bias_now[0]).astype(jnp.bfloat16)
    queries, out_local, up_local, down_local = lax.optimization_barrier(
        (queries, out_local, up_local, down_local)
    )
    out_full = collect(out_local, "dp", 0)
    up_full = collect(up_local, "dp", 0)
    down_full = collect(down_local, "dp", 0)
    gathered = (qkv_full, out_full, up_full, down_full)
    key_value = jnp.stack([projected[1], projected[2] + bias_now[1]]).astype(jnp.bfloat16)
    key_ext = with_halo(key_value, (("dp", 1),), margin)
    attended, log_norm = attend_forward(queries, key_ext, allowed)
    attended = attended.astype(jnp.bfloat16)

    def attention_term(first_row, row_count):
        return lax.dot_general(
            attended, out_full, (((1,), (1,)), ((), ())), preferred_element_type=jnp.float32
        )

    middle = stream + sum_forward(attention_term, tok_rows) + shift_now[1]
    second_full = gather_forward(layer_norm(middle, gain_now[1], shift_now[2]).astype(jnp.bfloat16))
    hidden = (
        jnp.einsum("gd,dre->gre", second_full, up_full, preferred_element_type=jnp.float32)
        + bias_now[2:][None]
    )
    active = exact_gelu(hidden).astype(jnp.bfloat16)

    def feed_term(first_row, row_count):
        return jnp.einsum("gre,ore->go", active, down_full, preferred_element_type=jnp.float32)

    kept_weights = gathered
    records = [
        (
            stream,
            middle,
            normed_full,
            second_full,
            queries,
            key_ext,
            log_norm,
            attended,
            hidden,
            active,
            kept_weights,
        )
    ]
    stream = middle + sum_forward(feed_term, tok_rows) + shift_now[3]
    gradient = cotangent.astype(jnp.float32) * own_real[:, None]
    local_qkv = [None] * LAYERS
    local_out = [None] * LAYERS
    local_up = [None] * LAYERS
    local_down = [None] * LAYERS
    unit_grads = [None] * LAYERS
    gain_grads = [None] * LAYERS
    shift_grads = [None] * LAYERS
    for layer_index in reversed(range(LAYERS)):
        (
            stream_in,
            middle,
            normed_full,
            second_full,
            queries,
            key_ext,
            log_norm,
            attended,
            hidden,
            active,
            kept_weights,
        ) = records[layer_index]
        qkv_full, out_full, up_full, down_full = kept_weights
        gain_now = norm_gain[layer_index].astype(jnp.float32)
        shift_now = row_bias[layer_index].astype(jnp.float32)
        shift_three = jnp.sum(gradient, axis=0)
        grad_mlp = gather_backward(gradient.astype(jnp.bfloat16))
        down_grad = scatter_rows(
            jnp.einsum("go,gre->ore", grad_mlp, active, preferred_element_type=jnp.float32)
        )
        grad_active = jnp.einsum(
            "go,ore->gre", grad_mlp, down_full, preferred_element_type=jnp.float32
        )
        gelu_again, gelu_pull = jax.vjp(exact_gelu, hidden)
        grad_hidden = gelu_pull(grad_active)[0].astype(jnp.bfloat16)
        up_bias_grad = jnp.sum(grad_hidden.astype(jnp.float32), axis=0)
        up_grad = scatter_rows(
            jnp.einsum("gd,gre->dre", second_full, grad_hidden, preferred_element_type=jnp.float32)
        )

        def second_term(first_row, row_count):
            return jnp.einsum(
                "gre,dre->gd", grad_hidden, up_full, preferred_element_type=jnp.float32
            )

        grad_second = sum_backward(second_term, tok_rows)
        second_again, second_pull = jax.vjp(layer_norm, middle, gain_now[1], shift_now[2])
        grad_mid_norm, gain_one, shift_two = second_pull(grad_second)
        grad_middle = gradient + grad_mid_norm
        shift_one = jnp.sum(grad_middle, axis=0)
        grad_proj = gather_backward(grad_middle.astype(jnp.bfloat16))
        out_grad = scatter_rows(
            lax.dot_general(
                grad_proj, attended, (((0,), (0,)), ((), ())), preferred_element_type=jnp.float32
            )
        )
        grad_attended = jnp.dot(grad_proj, out_full, preferred_element_type=jnp.float32).astype(
            jnp.bfloat16
        )
        grad_query, grad_key_ext, grad_value_ext = attend_backward(
            queries, key_ext, allowed, log_norm, grad_attended
        )
        grad_pair_ext = jnp.stack([grad_key_ext, grad_value_ext])
        from_next = from_behind(grad_pair_ext[:, :margin].astype(jnp.bfloat16), "dp", -1).astype(
            jnp.float32
        )
        from_prev = from_behind(
            grad_pair_ext[:, margin + group_rows :].astype(jnp.bfloat16), "dp", 1
        ).astype(jnp.float32)
        grad_pair = grad_pair_ext[:, margin : margin + group_rows]
        grad_pair = (
            grad_pair.at[:, group_rows - margin :].add(from_next).at[:, :margin].add(from_prev)
        )
        grad_triple = jnp.concatenate(
            [grad_query.astype(jnp.bfloat16)[None], grad_pair.astype(jnp.bfloat16)], axis=0
        )
        qkv_grad = jnp.moveaxis(
            scatter_rows(
                jnp.einsum(
                    "gd,sge->dse", normed_full, grad_triple, preferred_element_type=jnp.float32
                )
            ),
            0,
            1,
        )
        triple_sums = jnp.sum(grad_triple.astype(jnp.float32), axis=1)

        def first_term(first_row, row_count):
            return jnp.einsum(
                "sge,sde->gd", grad_triple, qkv_full, preferred_element_type=jnp.float32
            )

        grad_first = sum_backward(first_term, tok_rows)
        first_again, first_pull = jax.vjp(layer_norm, stream_in, gain_now[0], shift_now[0])
        grad_in_norm, gain_zero, shift_zero = first_pull(grad_first)
        gradient = grad_middle + grad_in_norm
        unit_grads[layer_index] = jnp.concatenate(
            [triple_sums[0][None], triple_sums[2][None], up_bias_grad], axis=0
        )
        gain_grads[layer_index] = jnp.stack([gain_zero, gain_one])
        shift_grads[layer_index] = jnp.stack([shift_zero, shift_one, shift_two, shift_three])
        local_qkv[layer_index] = qkv_grad
        local_out[layer_index] = out_grad
        local_up[layer_index] = up_grad
        local_down[layer_index] = down_grad
    grad_qkv = jnp.stack(local_qkv).astype(jnp.float32)
    grad_out = jnp.stack(local_out).astype(jnp.float32)
    grad_up = jnp.stack(local_up).astype(jnp.float32)
    grad_down = jnp.stack(local_down).astype(jnp.float32)
    unit_local = jnp.stack(unit_grads)
    unit_wide = jnp.zeros((LAYERS, unit_local.shape[1], cols_here * tensor_size), jnp.float32)
    unit_wide = lax.dynamic_update_slice_in_dim(unit_wide, unit_local, tensor_index * cols_here, 2)
    small = jnp.concatenate(
        [jnp.stack(gain_grads), jnp.stack(shift_grads), unit_wide], axis=1
    )
    small_total = jnp.sum(from_everyone(small, "dp"), axis=0)
    small_total = jnp.sum(from_everyone(small_total, "tensor"), axis=0)
    gain_total = small_total[:, :2]
    shift_total = small_total[:, 2:6]
    unit_total = small_total[:, 6:]
    unit_mine = lax.dynamic_slice_in_dim(unit_total, tensor_index * cols_here, cols_here, 2)
    return (
        stream.astype(jnp.bfloat16),
        gradient.astype(jnp.bfloat16),
        grad_qkv,
        grad_out,
        grad_up,
        grad_down,
        unit_mine,
        gain_total,
        shift_total,
    )


def solution(mesh):
    placed = (
        P(("dp", "tensor"), None),
        P(),
        P(),
        P(None, None, "dp", "tensor"),
        P(None, "dp", "tensor"),
        P(None, "dp", None, "tensor"),
        P(None, "dp", None, "tensor"),
        P(None, None, "tensor"),
        P(),
        P(),
        P(("dp", "tensor"), None),
    )
    return jax.shard_map(
        local,
        mesh=mesh,
        in_specs=placed,
        out_specs=(
            P(("dp", "tensor"), None),
            P(("dp", "tensor"), None),
            P(None, None, "dp", "tensor"),
            P(None, "dp", "tensor"),
            P(None, "dp", None, "tensor"),
            P(None, "dp", None, "tensor"),
            P(None, None, "tensor"),
            P(),
            P(),
        ),
        check_vma=False,
    )
```

```python
import functools
import math

import jax
import jax.numpy as jnp
from jax import lax
from jax.experimental import pallas as pl
from jax.experimental.pallas import tpu as pltpu
from jax.sharding import PartitionSpec as P

MESH = pl.DeviceIdType.MESH

LAYERS = 1
IMG = 577
HD = 64


norm_eps = 1e-06
masked_score = -1e30


def from_everyone(value, axis):
    devices = lax.axis_size(axis)
    return lax.all_to_all(
        jnp.broadcast_to(value[None], (devices, *value.shape)), axis, 0, 0, tiled=True
    )


def joined_along(parts, dim):
    dims = list(parts.shape[1:])
    dims[dim] *= parts.shape[0]
    return jnp.moveaxis(parts, 0, dim).reshape(dims)


def collect(value, axis, dim):
    parts = from_everyone(value, axis)
    return joined_along(parts, dim)


def split_up(value, dim, devices):
    dims = value.shape
    parts = value.reshape(*dims[:dim], devices, dims[dim] // devices, *dims[dim + 1 :])
    return jnp.moveaxis(parts, dim, 0)


def summed_on_arrival(value, axis, dim):
    devices = lax.axis_size(axis)
    parts = lax.all_to_all(split_up(value, dim, devices), axis, 0, 0, tiled=True)
    return jnp.sum(parts.astype(jnp.float32), axis=0)


def rows_first(arrays, axis, dims):
    turned = [jnp.moveaxis(a, dim, 0) for a, dim in zip(arrays, dims)]
    both = jnp.concatenate([t.reshape(len(t), -1) for t in turned], axis=1)
    filled, at, outs = (lax.all_gather(both, axis, axis=0, tiled=True), 0, [])
    for t, dim in zip(turned, dims):
        slab = filled[:, at : at + t[0].size].reshape(-1, *t.shape[1:])
        outs.append(jnp.moveaxis(slab, 0, dim))
        at += t[0].size
    return tuple(outs)


def with_halo(value, sides, width):
    for axis, dim in sides:
        devices, length = (lax.axis_size(axis), value.shape[dim])
        up = [(i, (i + 1) % devices) for i in range(devices - 1)]
        down = [(j, i) for i, j in up]
        last = lax.slice_in_dim(value, length - width, length, axis=dim)
        initial = lax.slice_in_dim(value, 0, width, axis=dim)
        before = lax.ppermute(last, axis, up)
        after = lax.ppermute(initial, axis, down)
        value = jnp.concatenate([before, value, after], axis=dim)
    return value


def from_behind(block, axis, distance):
    devices = range(lax.axis_size(axis))
    route = [(i - distance, i) for i in devices if i - distance in devices]
    return lax.ppermute(block, axis, route)


def side_by_side(arrays, axis, dim, along):
    widths = [math.prod(a.shape[along:]) for a in arrays]
    both = jnp.concatenate(
        [a.reshape(*a.shape[:along], w) for a, w in zip(arrays, widths)], axis=along
    )
    filled = lax.psum_scatter(both, axis, scatter_dimension=dim, tiled=True)
    parts = jnp.split(filled, [sum(widths[:k]) for k in range(1, len(widths))], axis=along)
    return tuple(
        (b.reshape(*filled.shape[:along], *a.shape[along:]) for a, b in zip(arrays, parts))
    )


def scatter_rows(grad):
    return summed_on_arrival(grad.astype(jnp.bfloat16), "dp", 0)


def layer_norm(values, gain_row, shift_row):
    center = values - jnp.mean(values, axis=-1, keepdims=True)
    spread = jnp.mean(center * center, axis=-1, keepdims=True)
    return center * lax.rsqrt(spread + norm_eps) * gain_row + shift_row


def exact_gelu(values):
    return jax.nn.gelu(values, approximate=False)


def _gather_kernel(devices, x_ref, out_ref, send_sem, recv_sem):
    me = lax.axis_index("tensor")
    dp = lax.axis_index("dp")
    sib = me + 1 - 2 * lax.rem(me, 2)
    far = lax.rem(me + 2, devices)
    barrier = pltpu.get_barrier_semaphore()
    for peer in (sib, far):
        pl.semaphore_signal(barrier, inc=1, device_id=(dp, peer), device_id_type=MESH)
    pl.semaphore_wait(barrier, 2)
    near_copy = pltpu.make_async_remote_copy(
        src_ref=x_ref,
        dst_ref=out_ref.at[me],
        send_sem=send_sem.at[0],
        recv_sem=recv_sem.at[0],
        device_id=(dp, sib),
        device_id_type=MESH,
    )
    far_copy = pltpu.make_async_remote_copy(
        src_ref=x_ref,
        dst_ref=out_ref.at[me],
        send_sem=send_sem.at[1],
        recv_sem=recv_sem.at[1],
        device_id=(dp, far),
        device_id_type=MESH,
    )
    far_copy.start()
    near_copy.start()
    out_ref[me] = x_ref[...]
    far_copy.wait_recv()
    relay = pltpu.make_async_remote_copy(
        src_ref=out_ref.at[far],
        dst_ref=out_ref.at[far],
        send_sem=send_sem.at[2],
        recv_sem=recv_sem.at[2],
        device_id=(dp, sib),
        device_id_type=MESH,
    )
    relay.start()
    near_copy.wait_send()
    near_copy.wait_recv()
    far_copy.wait_send()
    relay.wait_send()
    relay.wait_recv()


def gather_rows(values):
    devices = lax.axis_size("tensor")
    if devices != 4:
        return collect(values, "tensor", 0)
    rows, width = values.shape
    parts = pl.pallas_call(
        functools.partial(_gather_kernel, devices),
        out_shape=jax.ShapeDtypeStruct((devices, rows, width), values.dtype),
        in_specs=[pl.BlockSpec(memory_space=pltpu.VMEM)],
        out_specs=pl.BlockSpec(memory_space=pltpu.VMEM),
        scratch_shapes=[
            pltpu.SemaphoreType.DMA((3,)),
            pltpu.SemaphoreType.DMA((3,)),
        ],
        compiler_params=pltpu.CompilerParams(collective_id=0, has_side_effects=True),
    )(values)
    return parts.reshape(devices * rows, width)


def _exchange_kernel(devices, x_ref, out_ref, send_sem, recv_sem):
    me = lax.axis_index("tensor")
    dp = lax.axis_index("dp")
    barrier = pltpu.get_barrier_semaphore()
    for step in range(1, devices):
        pl.semaphore_signal(
            barrier, inc=1, device_id=(dp, lax.rem(me + step, devices)), device_id_type=MESH
        )
    pl.semaphore_wait(barrier, devices - 1)
    copies = []
    for step in range(1, devices):
        peer = lax.rem(me + step, devices)
        copy = pltpu.make_async_remote_copy(
            src_ref=x_ref.at[peer],
            dst_ref=out_ref.at[me],
            send_sem=send_sem.at[step - 1],
            recv_sem=recv_sem.at[step - 1],
            device_id=(dp, peer),
            device_id_type=MESH,
        )
        copy.start()
        copies.append(copy)
    out_ref[me] = x_ref[me]
    for copy in copies:
        copy.wait()


def exchange_rows(parts):
    devices = parts.shape[0]
    return pl.pallas_call(
        functools.partial(_exchange_kernel, devices),
        out_shape=jax.ShapeDtypeStruct(parts.shape, parts.dtype),
        in_specs=[pl.BlockSpec(memory_space=pltpu.VMEM)],
        out_specs=pl.BlockSpec(memory_space=pltpu.VMEM),
        scratch_shapes=[
            pltpu.SemaphoreType.DMA((devices - 1,)),
            pltpu.SemaphoreType.DMA((devices - 1,)),
        ],
        compiler_params=pltpu.CompilerParams(collective_id=1, has_side_effects=True),
    )(parts)


def _reduce_kernel(devices, x_ref, out_ref, held, mate, pre, send_sem, recv_sem):
    me = lax.axis_index("tensor")
    dp = lax.axis_index("dp")
    sib = me + 1 - 2 * lax.rem(me, 2)
    far = lax.rem(me + 2, devices)
    other = lax.rem(sib + 2, devices)
    barrier = pltpu.get_barrier_semaphore()
    for peer in (sib, far):
        pl.semaphore_signal(barrier, inc=1, device_id=(dp, peer), device_id_type=MESH)
    pl.semaphore_wait(barrier, 2)
    own_copy = pltpu.make_async_remote_copy(
        src_ref=x_ref.at[sib],
        dst_ref=held.at[0],
        send_sem=send_sem.at[0],
        recv_sem=recv_sem.at[0],
        device_id=(dp, sib),
        device_id_type=MESH,
    )
    mate_copy = pltpu.make_async_remote_copy(
        src_ref=x_ref.at[other],
        dst_ref=mate,
        send_sem=send_sem.at[1],
        recv_sem=recv_sem.at[1],
        device_id=(dp, sib),
        device_id_type=MESH,
    )
    mate_copy.start()
    own_copy.start()
    mate_copy.wait_recv()
    pre[...] = (x_ref[far].astype(jnp.float32) + mate[...].astype(jnp.float32)).astype(pre.dtype)
    own_copy.wait_recv()
    out_ref[...] = x_ref[me].astype(jnp.float32) + held[0].astype(jnp.float32)
    far_copy = pltpu.make_async_remote_copy(
        src_ref=pre,
        dst_ref=held.at[1],
        send_sem=send_sem.at[2],
        recv_sem=recv_sem.at[2],
        device_id=(dp, far),
        device_id_type=MESH,
    )
    far_copy.start()
    far_copy.wait_recv()
    out_ref[...] += held[1].astype(jnp.float32)
    own_copy.wait_send()
    mate_copy.wait_send()
    far_copy.wait_send()


def summed_over_tensor(value):
    devices = lax.axis_size("tensor")
    parts = split_up(value, 0, devices)
    if devices != 4:
        return jnp.sum(exchange_rows(parts).astype(jnp.float32), axis=0)
    rows, width = parts.shape[1:]
    return pl.pallas_call(
        functools.partial(_reduce_kernel, devices),
        out_shape=jax.ShapeDtypeStruct((rows, width), jnp.float32),
        in_specs=[pl.BlockSpec(memory_space=pltpu.VMEM)],
        out_specs=pl.BlockSpec(memory_space=pltpu.VMEM),
        scratch_shapes=[
            pltpu.VMEM((2, rows, width), parts.dtype),
            pltpu.VMEM((rows, width), parts.dtype),
            pltpu.VMEM((rows, width), parts.dtype),
            pltpu.SemaphoreType.DMA((3,)),
            pltpu.SemaphoreType.DMA((3,)),
        ],
        compiler_params=pltpu.CompilerParams(collective_id=1, has_side_effects=True),
    )(parts)


def gather_forward(values):
    return gather_rows(values)


def gather_backward(values):
    return gather_rows(values)


def sum_forward(product, tok_rows):
    return summed_over_tensor(
        product(jnp.int32(0), tok_rows * lax.axis_size("tensor")).astype(jnp.bfloat16)
    )


def sum_backward(product, tok_rows):
    return summed_over_tensor(
        product(jnp.int32(0), tok_rows * lax.axis_size("tensor")).astype(jnp.bfloat16)
    )


def head_scores(query_head, key_head, allowed):
    raw = lax.dot_general(
        query_head, key_head, (((1,), (1,)), ((), ())), preferred_element_type=jnp.float32
    )
    return jnp.where(allowed, raw * HD ** (-0.5), masked_score)


def split_heads(queries, key_ext):
    heads_here = queries.shape[1] // HD
    query_heads = queries.reshape(queries.shape[0], heads_here, HD)
    key_heads = key_ext[0].reshape(key_ext.shape[1], heads_here, HD)
    value_heads = key_ext[1].reshape(key_ext.shape[1], heads_here, HD)
    return (heads_here, query_heads, key_heads, value_heads)


def merge_heads(per_head):
    return jnp.transpose(per_head, (1, 0, 2)).reshape(
        per_head.shape[1], per_head.shape[0] * per_head.shape[2]
    )


def attend_forward(queries, key_ext, allowed):
    heads_here, query_heads, key_heads, value_heads = split_heads(queries, key_ext)

    def one_head(head_index):
        query_head = lax.dynamic_index_in_dim(query_heads, head_index, 1, keepdims=False)
        key_head = lax.dynamic_index_in_dim(key_heads, head_index, 1, keepdims=False)
        value_head = lax.dynamic_index_in_dim(value_heads, head_index, 1, keepdims=False)
        scores = head_scores(query_head, key_head, allowed)
        row_top = jnp.max(scores, axis=1, keepdims=True)
        exponent = jnp.exp(scores - row_top)
        row_total = jnp.sum(exponent, axis=1, keepdims=True)
        prob_low = (exponent / row_total).astype(jnp.bfloat16)
        head_out = jnp.dot(prob_low, value_head, preferred_element_type=jnp.float32)
        return (head_out, (row_top + jnp.log(row_total))[:, 0])

    head_outs, log_norm = lax.map(one_head, jnp.arange(heads_here, dtype=jnp.int32))
    return (merge_heads(head_outs), log_norm)


def attend_backward(queries, key_ext, allowed, log_norm, grad_attended):
    heads_here, query_heads, key_heads, value_heads = split_heads(queries, key_ext)
    grad_heads = grad_attended.reshape(grad_attended.shape[0], heads_here, HD)

    def one_head(inputs):
        head_index, norm_row = inputs
        query_head = lax.dynamic_index_in_dim(query_heads, head_index, 1, keepdims=False)
        key_head = lax.dynamic_index_in_dim(key_heads, head_index, 1, keepdims=False)
        value_head = lax.dynamic_index_in_dim(value_heads, head_index, 1, keepdims=False)
        grad_head = lax.dynamic_index_in_dim(grad_heads, head_index, 1, keepdims=False)
        prob_full = jnp.exp(head_scores(query_head, key_head, allowed) - norm_row[:, None])
        prob_low = prob_full.astype(jnp.bfloat16)
        grad_value = lax.dot_general(
            prob_low, grad_head, (((0,), (0,)), ((), ())), preferred_element_type=jnp.float32
        )
        grad_prob = lax.dot_general(
            grad_head, value_head, (((1,), (1,)), ((), ())), preferred_element_type=jnp.float32
        )
        grad_score = (
            prob_full * (grad_prob - jnp.sum(prob_full * grad_prob, axis=1, keepdims=True))
        ).astype(jnp.bfloat16)
        grad_query = jnp.dot(grad_score, key_head, preferred_element_type=jnp.float32) * HD ** (
            -0.5
        )
        grad_key = lax.dot_general(
            grad_score, query_head, (((0,), (0,)), ((), ())), preferred_element_type=jnp.float32
        ) * HD ** (-0.5)
        return (grad_query, grad_key, grad_value)

    grad_queries, grad_keys, grad_values = lax.map(
        one_head, (jnp.arange(heads_here, dtype=jnp.int32), log_norm)
    )
    return (merge_heads(grad_queries), merge_heads(grad_keys), merge_heads(grad_values))


def local(
    tokens,
    segment,
    real_token,
    qkv_weight,
    out_weight,
    up_weight,
    down_weight,
    unit_bias,
    norm_gain,
    row_bias,
    cotangent,
):
    tok_rows = tokens.shape[0]
    tensor_size = lax.axis_size("tensor")
    group_rows = tok_rows * tensor_size
    margin = IMG - 1
    cols_here = qkv_weight.shape[3]
    dp_index = lax.axis_index("dp")
    tensor_index = lax.axis_index("tensor")
    group_first = dp_index * group_rows
    own_first = group_first + tensor_index * tok_rows
    segment_pad = jnp.pad(segment, (margin, margin), constant_values=-1)
    real_pad = jnp.pad(real_token, (margin, margin))
    segment_query = lax.dynamic_slice_in_dim(segment, group_first, group_rows, 0)
    segment_key = lax.dynamic_slice_in_dim(segment_pad, group_first, group_rows + 2 * margin, 0)
    real_key = lax.dynamic_slice_in_dim(real_pad, group_first, group_rows + 2 * margin, 0)
    place_query = jnp.arange(group_rows, dtype=jnp.int32)
    place_key = jnp.arange(group_rows + 2 * margin, dtype=jnp.int32) - margin
    allowed = (segment_query[:, None] == segment_key[None, :]) & (
        (real_key[None, :] == 1) | (place_query[:, None] == place_key[None, :])
    )
    own_real = lax.dynamic_slice_in_dim(real_token, own_first, tok_rows, 0).astype(jnp.float32)
    stream = tokens.astype(jnp.float32)
    layer_index = 0
    qkv_local = jnp.moveaxis(qkv_weight[layer_index], 1, 0)
    out_local, up_local, down_local = (
        out_weight[layer_index],
        up_weight[layer_index],
        down_weight[layer_index],
    )
    gain_now = norm_gain[layer_index].astype(jnp.float32)
    shift_now = row_bias[layer_index].astype(jnp.float32)
    bias_now = unit_bias[layer_index].astype(jnp.float32)
    normed_full = gather_forward(layer_norm(stream, gain_now[0], shift_now[0]).astype(jnp.bfloat16))
    normed_full, qkv_local = lax.optimization_barrier((normed_full, qkv_local))
    qkv_full = jnp.moveaxis(collect(qkv_local, "dp", 0), 0, 1)
    projected = jnp.einsum("gd,sde->sge", normed_full, qkv_full, preferred_element_type=jnp.float32)
    queries = (projected[0] + bias_now[0]).astype(jnp.bfloat16)
    queries, out_local, up_local, down_local = lax.optimization_barrier(
        (queries, out_local, up_local, down_local)
    )
    out_full = collect(out_local, "dp", 0)
    up_full = collect(up_local, "dp", 0)
    down_full = collect(down_local, "dp", 0)
    gathered = (qkv_full, out_full, up_full, down_full)
    key_value = jnp.stack([projected[1], projected[2] + bias_now[1]]).astype(jnp.bfloat16)
    key_ext = with_halo(key_value, (("dp", 1),), margin)
    attended, log_norm = attend_forward(queries, key_ext, allowed)
    attended = attended.astype(jnp.bfloat16)

    def attention_term(first_row, row_count):
        return lax.dot_general(
            attended, out_full, (((1,), (1,)), ((), ())), preferred_element_type=jnp.float32
        )

    middle = stream + sum_forward(attention_term, tok_rows) + shift_now[1]
    second_full = gather_forward(layer_norm(middle, gain_now[1], shift_now[2]).astype(jnp.bfloat16))
    hidden = (
        jnp.einsum("gd,dre->gre", second_full, up_full, preferred_element_type=jnp.float32)
        + bias_now[2:][None]
    )
    active = exact_gelu(hidden).astype(jnp.bfloat16)

    def feed_term(first_row, row_count):
        return jnp.einsum("gre,ore->go", active, down_full, preferred_element_type=jnp.float32)

    kept_weights = gathered
    records = [
        (
            stream,
            middle,
            normed_full,
            second_full,
            queries,
            key_ext,
            log_norm,
            attended,
            hidden,
            active,
            kept_weights,
        )
    ]
    stream = middle + sum_forward(feed_term, tok_rows) + shift_now[3]
    gradient = cotangent.astype(jnp.float32) * own_real[:, None]
    local_qkv = [None] * LAYERS
    local_out = [None] * LAYERS
    local_up = [None] * LAYERS
    local_down = [None] * LAYERS
    unit_grads = [None] * LAYERS
    gain_grads = [None] * LAYERS
    shift_grads = [None] * LAYERS
    for layer_index in reversed(range(LAYERS)):
        (
            stream_in,
            middle,
            normed_full,
            second_full,
            queries,
            key_ext,
            log_norm,
            attended,
            hidden,
            active,
            kept_weights,
        ) = records[layer_index]
        qkv_full, out_full, up_full, down_full = kept_weights
        gain_now = norm_gain[layer_index].astype(jnp.float32)
        shift_now = row_bias[layer_index].astype(jnp.float32)
        shift_three = jnp.sum(gradient, axis=0)
        grad_mlp = gather_backward(gradient.astype(jnp.bfloat16))
        down_grad = scatter_rows(
            jnp.einsum("go,gre->ore", grad_mlp, active, preferred_element_type=jnp.float32)
        )
        grad_active = jnp.einsum(
            "go,ore->gre", grad_mlp, down_full, preferred_element_type=jnp.float32
        )
        gelu_again, gelu_pull = jax.vjp(exact_gelu, hidden)
        grad_hidden = gelu_pull(grad_active)[0].astype(jnp.bfloat16)
        up_bias_grad = jnp.sum(grad_hidden.astype(jnp.float32), axis=0)
        up_grad = scatter_rows(
            jnp.einsum("gd,gre->dre", second_full, grad_hidden, preferred_element_type=jnp.float32)
        )

        def second_term(first_row, row_count):
            return jnp.einsum(
                "gre,dre->gd", grad_hidden, up_full, preferred_element_type=jnp.float32
            )

        grad_second = sum_backward(second_term, tok_rows)
        second_again, second_pull = jax.vjp(layer_norm, middle, gain_now[1], shift_now[2])
        grad_mid_norm, gain_one, shift_two = second_pull(grad_second)
        grad_middle = gradient + grad_mid_norm
        shift_one = jnp.sum(grad_middle, axis=0)
        grad_proj = gather_backward(grad_middle.astype(jnp.bfloat16))
        out_grad = scatter_rows(
            lax.dot_general(
                grad_proj, attended, (((0,), (0,)), ((), ())), preferred_element_type=jnp.float32
            )
        )
        grad_attended = jnp.dot(grad_proj, out_full, preferred_element_type=jnp.float32).astype(
            jnp.bfloat16
        )
        grad_query, grad_key_ext, grad_value_ext = attend_backward(
            queries, key_ext, allowed, log_norm, grad_attended
        )
        grad_pair_ext = jnp.stack([grad_key_ext, grad_value_ext])
        from_next = from_behind(grad_pair_ext[:, :margin].astype(jnp.bfloat16), "dp", -1).astype(
            jnp.float32
        )
        from_prev = from_behind(
            grad_pair_ext[:, margin + group_rows :].astype(jnp.bfloat16), "dp", 1
        ).astype(jnp.float32)
        grad_pair = grad_pair_ext[:, margin : margin + group_rows]
        grad_pair = (
            grad_pair.at[:, group_rows - margin :].add(from_next).at[:, :margin].add(from_prev)
        )
        grad_triple = jnp.concatenate(
            [grad_query.astype(jnp.bfloat16)[None], grad_pair.astype(jnp.bfloat16)], axis=0
        )
        qkv_grad = jnp.moveaxis(
            scatter_rows(
                jnp.einsum(
                    "gd,sge->dse", normed_full, grad_triple, preferred_element_type=jnp.float32
                )
            ),
            0,
            1,
        )
        triple_sums = jnp.sum(grad_triple.astype(jnp.float32), axis=1)

        def first_term(first_row, row_count):
            return jnp.einsum(
                "sge,sde->gd", grad_triple, qkv_full, preferred_element_type=jnp.float32
            )

        grad_first = sum_backward(first_term, tok_rows)
        first_again, first_pull = jax.vjp(layer_norm, stream_in, gain_now[0], shift_now[0])
        grad_in_norm, gain_zero, shift_zero = first_pull(grad_first)
        gradient = grad_middle + grad_in_norm
        unit_grads[layer_index] = jnp.concatenate(
            [triple_sums[0][None], triple_sums[2][None], up_bias_grad], axis=0
        )
        gain_grads[layer_index] = jnp.stack([gain_zero, gain_one])
        shift_grads[layer_index] = jnp.stack([shift_zero, shift_one, shift_two, shift_three])
        local_qkv[layer_index] = qkv_grad
        local_out[layer_index] = out_grad
        local_up[layer_index] = up_grad
        local_down[layer_index] = down_grad
    grad_qkv = jnp.stack(local_qkv).astype(jnp.float32)
    grad_out = jnp.stack(local_out).astype(jnp.float32)
    grad_up = jnp.stack(local_up).astype(jnp.float32)
    grad_down = jnp.stack(local_down).astype(jnp.float32)
    unit_local = jnp.stack(unit_grads)
    norm_local = jnp.concatenate([jnp.stack(gain_grads), jnp.stack(shift_grads)], axis=1)
    norm_group = jnp.sum(from_everyone(norm_local, "tensor"), axis=0)
    dp_size = lax.axis_size("dp")
    flat = jnp.concatenate([norm_group.reshape(-1), unit_local.reshape(-1)])
    piece = -(-flat.shape[0] // dp_size)
    flat = jnp.pad(flat, (0, piece * dp_size - flat.shape[0]))
    mine = jnp.sum(lax.all_to_all(flat.reshape(dp_size, piece), "dp", 0, 0, tiled=True), axis=0)
    total = collect(mine[None], "dp", 0).reshape(-1)
    norm_size = norm_group.size
    norm_total = total[:norm_size].reshape(norm_group.shape)
    gain_total = norm_total[:, :2]
    shift_total = norm_total[:, 2:6]
    unit_mine = total[norm_size : norm_size + unit_local.size].reshape(unit_local.shape)
    return (
        stream.astype(jnp.bfloat16),
        gradient.astype(jnp.bfloat16),
        grad_qkv,
        grad_out,
        grad_up,
        grad_down,
        unit_mine,
        gain_total,
        shift_total,
    )


def solution(mesh):
    placed = (
        P(("dp", "tensor"), None),
        P(),
        P(),
        P(None, None, "dp", "tensor"),
        P(None, "dp", "tensor"),
        P(None, "dp", None, "tensor"),
        P(None, "dp", None, "tensor"),
        P(None, None, "tensor"),
        P(),
        P(),
        P(("dp", "tensor"), None),
    )
    return jax.shard_map(
        local,
        mesh=mesh,
        in_specs=placed,
        out_specs=(
            P(("dp", "tensor"), None),
            P(("dp", "tensor"), None),
            P(None, None, "dp", "tensor"),
            P(None, "dp", "tensor"),
            P(None, "dp", None, "tensor"),
            P(None, "dp", None, "tensor"),
            P(None, None, "tensor"),
            P(),
            P(),
        ),
        check_vma=False,
    )
```

```python
import functools
import math

import jax
import jax.numpy as jnp
from jax import lax
from jax.experimental import pallas as pl
from jax.experimental.pallas import tpu as pltpu
from jax.sharding import PartitionSpec as P

MESH = pl.DeviceIdType.MESH

LAYERS = 1
IMG = 577
HD = 64


norm_eps = 1e-06
masked_score = -1e30


def from_everyone(value, axis):
    devices = lax.axis_size(axis)
    return lax.all_to_all(
        jnp.broadcast_to(value[None], (devices, *value.shape)), axis, 0, 0, tiled=True
    )


def joined_along(parts, dim):
    dims = list(parts.shape[1:])
    dims[dim] *= parts.shape[0]
    return jnp.moveaxis(parts, 0, dim).reshape(dims)


def collect(value, axis, dim):
    parts = from_everyone(value, axis)
    return joined_along(parts, dim)


def split_up(value, dim, devices):
    dims = value.shape
    parts = value.reshape(*dims[:dim], devices, dims[dim] // devices, *dims[dim + 1 :])
    return jnp.moveaxis(parts, dim, 0)


def summed_on_arrival(value, axis, dim):
    devices = lax.axis_size(axis)
    parts = lax.all_to_all(split_up(value, dim, devices), axis, 0, 0, tiled=True)
    return jnp.sum(parts.astype(jnp.float32), axis=0)


def rows_first(arrays, axis, dims):
    turned = [jnp.moveaxis(a, dim, 0) for a, dim in zip(arrays, dims)]
    both = jnp.concatenate([t.reshape(len(t), -1) for t in turned], axis=1)
    filled, at, outs = (lax.all_gather(both, axis, axis=0, tiled=True), 0, [])
    for t, dim in zip(turned, dims):
        slab = filled[:, at : at + t[0].size].reshape(-1, *t.shape[1:])
        outs.append(jnp.moveaxis(slab, 0, dim))
        at += t[0].size
    return tuple(outs)


def with_halo(value, sides, width):
    for axis, dim in sides:
        devices, length = (lax.axis_size(axis), value.shape[dim])
        up = [(i, (i + 1) % devices) for i in range(devices - 1)]
        down = [(j, i) for i, j in up]
        last = lax.slice_in_dim(value, length - width, length, axis=dim)
        initial = lax.slice_in_dim(value, 0, width, axis=dim)
        before = lax.ppermute(last, axis, up)
        after = lax.ppermute(initial, axis, down)
        value = jnp.concatenate([before, value, after], axis=dim)
    return value


def from_behind(block, axis, distance):
    devices = range(lax.axis_size(axis))
    route = [(i - distance, i) for i in devices if i - distance in devices]
    return lax.ppermute(block, axis, route)


def side_by_side(arrays, axis, dim, along):
    widths = [math.prod(a.shape[along:]) for a in arrays]
    both = jnp.concatenate(
        [a.reshape(*a.shape[:along], w) for a, w in zip(arrays, widths)], axis=along
    )
    filled = lax.psum_scatter(both, axis, scatter_dimension=dim, tiled=True)
    parts = jnp.split(filled, [sum(widths[:k]) for k in range(1, len(widths))], axis=along)
    return tuple(
        (b.reshape(*filled.shape[:along], *a.shape[along:]) for a, b in zip(arrays, parts))
    )


def scatter_rows(grad):
    return summed_on_arrival(grad.astype(jnp.bfloat16), "dp", 0)


def layer_norm(values, gain_row, shift_row):
    center = values - jnp.mean(values, axis=-1, keepdims=True)
    spread = jnp.mean(center * center, axis=-1, keepdims=True)
    return center * lax.rsqrt(spread + norm_eps) * gain_row + shift_row


def exact_gelu(values):
    return jax.nn.gelu(values, approximate=False)


def _gather_kernel(devices, x_ref, out_ref, send_sem, recv_sem):
    me = lax.axis_index("tensor")
    dp = lax.axis_index("dp")
    sib = me + 1 - 2 * lax.rem(me, 2)
    far = lax.rem(me + 2, devices)
    barrier = pltpu.get_barrier_semaphore()
    for peer in (sib, far):
        pl.semaphore_signal(barrier, inc=1, device_id=(dp, peer), device_id_type=MESH)
    pl.semaphore_wait(barrier, 2)
    near_copy = pltpu.make_async_remote_copy(
        src_ref=x_ref,
        dst_ref=out_ref.at[me],
        send_sem=send_sem.at[0],
        recv_sem=recv_sem.at[0],
        device_id=(dp, sib),
        device_id_type=MESH,
    )
    far_copy = pltpu.make_async_remote_copy(
        src_ref=x_ref,
        dst_ref=out_ref.at[me],
        send_sem=send_sem.at[1],
        recv_sem=recv_sem.at[1],
        device_id=(dp, far),
        device_id_type=MESH,
    )
    far_copy.start()
    near_copy.start()
    out_ref[me] = x_ref[...]
    far_copy.wait_recv()
    relay = pltpu.make_async_remote_copy(
        src_ref=out_ref.at[far],
        dst_ref=out_ref.at[far],
        send_sem=send_sem.at[2],
        recv_sem=recv_sem.at[2],
        device_id=(dp, sib),
        device_id_type=MESH,
    )
    relay.start()
    near_copy.wait_send()
    near_copy.wait_recv()
    far_copy.wait_send()
    relay.wait_send()
    relay.wait_recv()


def gather_rows(values):
    devices = lax.axis_size("tensor")
    if devices != 4:
        return collect(values, "tensor", 0)
    rows, width = values.shape
    parts = pl.pallas_call(
        functools.partial(_gather_kernel, devices),
        out_shape=jax.ShapeDtypeStruct((devices, rows, width), values.dtype),
        in_specs=[pl.BlockSpec(memory_space=pltpu.VMEM)],
        out_specs=pl.BlockSpec(memory_space=pltpu.VMEM),
        scratch_shapes=[
            pltpu.SemaphoreType.DMA((3,)),
            pltpu.SemaphoreType.DMA((3,)),
        ],
        compiler_params=pltpu.CompilerParams(collective_id=0, has_side_effects=True),
    )(values)
    return parts.reshape(devices * rows, width)


def _exchange_kernel(devices, x_ref, out_ref, send_sem, recv_sem):
    me = lax.axis_index("tensor")
    dp = lax.axis_index("dp")
    barrier = pltpu.get_barrier_semaphore()
    for step in range(1, devices):
        pl.semaphore_signal(
            barrier, inc=1, device_id=(dp, lax.rem(me + step, devices)), device_id_type=MESH
        )
    pl.semaphore_wait(barrier, devices - 1)
    copies = []
    for step in range(1, devices):
        peer = lax.rem(me + step, devices)
        copy = pltpu.make_async_remote_copy(
            src_ref=x_ref.at[peer],
            dst_ref=out_ref.at[me],
            send_sem=send_sem.at[step - 1],
            recv_sem=recv_sem.at[step - 1],
            device_id=(dp, peer),
            device_id_type=MESH,
        )
        copy.start()
        copies.append(copy)
    out_ref[me] = x_ref[me]
    for copy in copies:
        copy.wait()


def exchange_rows(parts):
    devices = parts.shape[0]
    return pl.pallas_call(
        functools.partial(_exchange_kernel, devices),
        out_shape=jax.ShapeDtypeStruct(parts.shape, parts.dtype),
        in_specs=[pl.BlockSpec(memory_space=pltpu.VMEM)],
        out_specs=pl.BlockSpec(memory_space=pltpu.VMEM),
        scratch_shapes=[
            pltpu.SemaphoreType.DMA((devices - 1,)),
            pltpu.SemaphoreType.DMA((devices - 1,)),
        ],
        compiler_params=pltpu.CompilerParams(collective_id=1, has_side_effects=True),
    )(parts)


def _reduce_kernel(devices, x_ref, out_ref, held, mate, pre, send_sem, recv_sem):
    me = lax.axis_index("tensor")
    dp = lax.axis_index("dp")
    sib = me + 1 - 2 * lax.rem(me, 2)
    far = lax.rem(me + 2, devices)
    other = lax.rem(sib + 2, devices)
    barrier = pltpu.get_barrier_semaphore()
    for peer in (sib, far):
        pl.semaphore_signal(barrier, inc=1, device_id=(dp, peer), device_id_type=MESH)
    pl.semaphore_wait(barrier, 2)
    own_copy = pltpu.make_async_remote_copy(
        src_ref=x_ref.at[sib],
        dst_ref=held.at[0],
        send_sem=send_sem.at[0],
        recv_sem=recv_sem.at[0],
        device_id=(dp, sib),
        device_id_type=MESH,
    )
    mate_copy = pltpu.make_async_remote_copy(
        src_ref=x_ref.at[other],
        dst_ref=mate,
        send_sem=send_sem.at[1],
        recv_sem=recv_sem.at[1],
        device_id=(dp, sib),
        device_id_type=MESH,
    )
    mate_copy.start()
    own_copy.start()
    mate_copy.wait_recv()
    pre[...] = (x_ref[far].astype(jnp.float32) + mate[...].astype(jnp.float32)).astype(pre.dtype)
    own_copy.wait_recv()
    out_ref[...] = x_ref[me].astype(jnp.float32) + held[0].astype(jnp.float32)
    far_copy = pltpu.make_async_remote_copy(
        src_ref=pre,
        dst_ref=held.at[1],
        send_sem=send_sem.at[2],
        recv_sem=recv_sem.at[2],
        device_id=(dp, far),
        device_id_type=MESH,
    )
    far_copy.start()
    far_copy.wait_recv()
    out_ref[...] += held[1].astype(jnp.float32)
    own_copy.wait_send()
    mate_copy.wait_send()
    far_copy.wait_send()


def summed_over_tensor(value):
    devices = lax.axis_size("tensor")
    parts = split_up(value, 0, devices)
    if devices != 4:
        return jnp.sum(exchange_rows(parts).astype(jnp.float32), axis=0)
    rows, width = parts.shape[1:]
    return pl.pallas_call(
        functools.partial(_reduce_kernel, devices),
        out_shape=jax.ShapeDtypeStruct((rows, width), jnp.float32),
        in_specs=[pl.BlockSpec(memory_space=pltpu.VMEM)],
        out_specs=pl.BlockSpec(memory_space=pltpu.VMEM),
        scratch_shapes=[
            pltpu.VMEM((2, rows, width), parts.dtype),
            pltpu.VMEM((rows, width), parts.dtype),
            pltpu.VMEM((rows, width), parts.dtype),
            pltpu.SemaphoreType.DMA((3,)),
            pltpu.SemaphoreType.DMA((3,)),
        ],
        compiler_params=pltpu.CompilerParams(collective_id=1, has_side_effects=True),
    )(parts)


def gather_forward(values):
    return gather_rows(values)


def gather_backward(values):
    return gather_rows(values)


def sum_forward(product, tok_rows):
    return summed_over_tensor(
        product(jnp.int32(0), tok_rows * lax.axis_size("tensor")).astype(jnp.bfloat16)
    )


def sum_backward(product, tok_rows):
    return summed_over_tensor(
        product(jnp.int32(0), tok_rows * lax.axis_size("tensor")).astype(jnp.bfloat16)
    )


def head_scores(query_head, key_head, allowed):
    raw = lax.dot_general(
        query_head, key_head, (((1,), (1,)), ((), ())), preferred_element_type=jnp.float32
    )
    return jnp.where(allowed, raw * HD ** (-0.5), masked_score)


def split_heads(queries, key_ext):
    heads_here = queries.shape[1] // HD
    query_heads = queries.reshape(queries.shape[0], heads_here, HD)
    key_heads = key_ext[0].reshape(key_ext.shape[1], heads_here, HD)
    value_heads = key_ext[1].reshape(key_ext.shape[1], heads_here, HD)
    return (heads_here, query_heads, key_heads, value_heads)


def merge_heads(per_head):
    return jnp.transpose(per_head, (1, 0, 2)).reshape(
        per_head.shape[1], per_head.shape[0] * per_head.shape[2]
    )


def attend_forward(queries, key_ext, allowed):
    heads_here, query_heads, key_heads, value_heads = split_heads(queries, key_ext)

    def one_head(head_index):
        query_head = lax.dynamic_index_in_dim(query_heads, head_index, 1, keepdims=False)
        key_head = lax.dynamic_index_in_dim(key_heads, head_index, 1, keepdims=False)
        value_head = lax.dynamic_index_in_dim(value_heads, head_index, 1, keepdims=False)
        scores = head_scores(query_head, key_head, allowed)
        row_top = jnp.max(scores, axis=1, keepdims=True)
        exponent = jnp.exp(scores - row_top)
        row_total = jnp.sum(exponent, axis=1, keepdims=True)
        prob_low = (exponent / row_total).astype(jnp.bfloat16)
        head_out = jnp.dot(prob_low, value_head, preferred_element_type=jnp.float32)
        return (head_out, (row_top + jnp.log(row_total))[:, 0])

    head_outs, log_norm = lax.map(one_head, jnp.arange(heads_here, dtype=jnp.int32))
    return (merge_heads(head_outs), log_norm)


def attend_backward(queries, key_ext, allowed, log_norm, grad_attended):
    heads_here, query_heads, key_heads, value_heads = split_heads(queries, key_ext)
    grad_heads = grad_attended.reshape(grad_attended.shape[0], heads_here, HD)

    def one_head(inputs):
        head_index, norm_row = inputs
        query_head = lax.dynamic_index_in_dim(query_heads, head_index, 1, keepdims=False)
        key_head = lax.dynamic_index_in_dim(key_heads, head_index, 1, keepdims=False)
        value_head = lax.dynamic_index_in_dim(value_heads, head_index, 1, keepdims=False)
        grad_head = lax.dynamic_index_in_dim(grad_heads, head_index, 1, keepdims=False)
        prob_full = jnp.exp(head_scores(query_head, key_head, allowed) - norm_row[:, None])
        prob_low = prob_full.astype(jnp.bfloat16)
        grad_value = lax.dot_general(
            prob_low, grad_head, (((0,), (0,)), ((), ())), preferred_element_type=jnp.float32
        )
        grad_prob = lax.dot_general(
            grad_head, value_head, (((1,), (1,)), ((), ())), preferred_element_type=jnp.float32
        )
        grad_score = (
            prob_full * (grad_prob - jnp.sum(prob_full * grad_prob, axis=1, keepdims=True))
        ).astype(jnp.bfloat16)
        grad_query = jnp.dot(grad_score, key_head, preferred_element_type=jnp.float32) * HD ** (
            -0.5
        )
        grad_key = lax.dot_general(
            grad_score, query_head, (((0,), (0,)), ((), ())), preferred_element_type=jnp.float32
        ) * HD ** (-0.5)
        return (grad_query, grad_key, grad_value)

    grad_queries, grad_keys, grad_values = lax.map(
        one_head, (jnp.arange(heads_here, dtype=jnp.int32), log_norm)
    )
    return (merge_heads(grad_queries), merge_heads(grad_keys), merge_heads(grad_values))


def local(
    tokens,
    segment,
    real_token,
    qkv_weight,
    out_weight,
    up_weight,
    down_weight,
    unit_bias,
    norm_gain,
    row_bias,
    cotangent,
):
    tok_rows = tokens.shape[0]
    tensor_size = lax.axis_size("tensor")
    group_rows = tok_rows * tensor_size
    margin = IMG - 1
    cols_here = qkv_weight.shape[3]
    dp_index = lax.axis_index("dp")
    tensor_index = lax.axis_index("tensor")
    group_first = dp_index * group_rows
    own_first = group_first + tensor_index * tok_rows
    segment_pad = jnp.pad(segment, (margin, margin), constant_values=-1)
    real_pad = jnp.pad(real_token, (margin, margin))
    segment_query = lax.dynamic_slice_in_dim(segment, group_first, group_rows, 0)
    segment_key = lax.dynamic_slice_in_dim(segment_pad, group_first, group_rows + 2 * margin, 0)
    real_key = lax.dynamic_slice_in_dim(real_pad, group_first, group_rows + 2 * margin, 0)
    place_query = jnp.arange(group_rows, dtype=jnp.int32)
    place_key = jnp.arange(group_rows + 2 * margin, dtype=jnp.int32) - margin
    allowed = (segment_query[:, None] == segment_key[None, :]) & (
        (real_key[None, :] == 1) | (place_query[:, None] == place_key[None, :])
    )
    own_real = lax.dynamic_slice_in_dim(real_token, own_first, tok_rows, 0).astype(jnp.float32)
    stream = tokens.astype(jnp.float32)
    layer_index = 0
    qkv_local = jnp.moveaxis(qkv_weight[layer_index], 1, 0)
    out_local, up_local, down_local = (
        out_weight[layer_index],
        up_weight[layer_index],
        down_weight[layer_index],
    )
    gain_now = norm_gain[layer_index].astype(jnp.float32)
    shift_now = row_bias[layer_index].astype(jnp.float32)
    bias_now = unit_bias[layer_index].astype(jnp.float32)
    normed_full = gather_forward(layer_norm(stream, gain_now[0], shift_now[0]).astype(jnp.bfloat16))
    normed_full, qkv_local = lax.optimization_barrier((normed_full, qkv_local))
    qkv_full = jnp.moveaxis(collect(qkv_local, "dp", 0), 0, 1)
    projected = jnp.einsum("gd,sde->sge", normed_full, qkv_full, preferred_element_type=jnp.float32)
    queries = (projected[0] + bias_now[0]).astype(jnp.bfloat16)
    queries, out_local, up_local, down_local = lax.optimization_barrier(
        (queries, out_local, up_local, down_local)
    )
    out_full = collect(out_local, "dp", 0)
    up_full = collect(up_local, "dp", 0)
    down_full = collect(down_local, "dp", 0)
    gathered = (qkv_full, out_full, up_full, down_full)
    key_value = jnp.stack([projected[1], projected[2] + bias_now[1]]).astype(jnp.bfloat16)
    key_ext = with_halo(key_value, (("dp", 1),), margin)
    attended, log_norm = attend_forward(queries, key_ext, allowed)
    attended = attended.astype(jnp.bfloat16)

    def attention_term(first_row, row_count):
        return lax.dot_general(
            attended, out_full, (((1,), (1,)), ((), ())), preferred_element_type=jnp.float32
        )

    middle = stream + sum_forward(attention_term, tok_rows) + shift_now[1]
    second_full = gather_forward(layer_norm(middle, gain_now[1], shift_now[2]).astype(jnp.bfloat16))
    hidden = (
        jnp.einsum("gd,dre->gre", second_full, up_full, preferred_element_type=jnp.float32)
        + bias_now[2:][None]
    )
    active = exact_gelu(hidden).astype(jnp.bfloat16)

    def feed_term(first_row, row_count):
        return jnp.einsum("gre,ore->go", active, down_full, preferred_element_type=jnp.float32)

    kept_weights = gathered
    records = [
        (
            stream,
            middle,
            normed_full,
            second_full,
            queries,
            key_ext,
            log_norm,
            attended,
            hidden,
            active,
            kept_weights,
        )
    ]
    stream = middle + sum_forward(feed_term, tok_rows) + shift_now[3]
    gradient = cotangent.astype(jnp.float32) * own_real[:, None]
    local_qkv = [None] * LAYERS
    local_out = [None] * LAYERS
    local_up = [None] * LAYERS
    local_down = [None] * LAYERS
    unit_grads = [None] * LAYERS
    gain_grads = [None] * LAYERS
    shift_grads = [None] * LAYERS
    for layer_index in reversed(range(LAYERS)):
        (
            stream_in,
            middle,
            normed_full,
            second_full,
            queries,
            key_ext,
            log_norm,
            attended,
            hidden,
            active,
            kept_weights,
        ) = records[layer_index]
        qkv_full, out_full, up_full, down_full = kept_weights
        gain_now = norm_gain[layer_index].astype(jnp.float32)
        shift_now = row_bias[layer_index].astype(jnp.float32)
        shift_three = jnp.sum(gradient, axis=0)
        grad_mlp = gather_backward(gradient.astype(jnp.bfloat16))
        down_grad = scatter_rows(
            jnp.einsum("go,gre->ore", grad_mlp, active, preferred_element_type=jnp.float32)
        )
        grad_active = jnp.einsum(
            "go,ore->gre", grad_mlp, down_full, preferred_element_type=jnp.float32
        )
        gelu_again, gelu_pull = jax.vjp(exact_gelu, hidden)
        grad_hidden = gelu_pull(grad_active)[0].astype(jnp.bfloat16)
        up_bias_grad = jnp.sum(grad_hidden.astype(jnp.float32), axis=0)
        up_local = jnp.einsum(
            "gd,gre->dre", second_full, grad_hidden, preferred_element_type=jnp.float32
        )

        def second_term(first_row, row_count):
            return jnp.einsum(
                "gre,dre->gd", grad_hidden, up_full, preferred_element_type=jnp.float32
            )

        grad_second = sum_backward(second_term, tok_rows)
        second_again, second_pull = jax.vjp(layer_norm, middle, gain_now[1], shift_now[2])
        grad_mid_norm, gain_one, shift_two = second_pull(grad_second)
        grad_middle = gradient + grad_mid_norm
        shift_one = jnp.sum(grad_middle, axis=0)
        grad_proj = gather_backward(grad_middle.astype(jnp.bfloat16))
        out_local = lax.dot_general(
            grad_proj, attended, (((0,), (0,)), ((), ())), preferred_element_type=jnp.float32
        )
        grad_attended = jnp.dot(grad_proj, out_full, preferred_element_type=jnp.float32).astype(
            jnp.bfloat16
        )
        grad_attended, down_grad, up_local = lax.optimization_barrier(
            (grad_attended, down_grad, up_local)
        )
        up_grad = scatter_rows(up_local)
        grad_query, grad_key_ext, grad_value_ext = attend_backward(
            queries, key_ext, allowed, log_norm, grad_attended
        )
        grad_query, up_grad, out_local = lax.optimization_barrier((grad_query, up_grad, out_local))
        out_grad = scatter_rows(out_local)
        grad_pair_ext = jnp.stack([grad_key_ext, grad_value_ext])
        from_next = from_behind(grad_pair_ext[:, :margin].astype(jnp.bfloat16), "dp", -1).astype(
            jnp.float32
        )
        from_prev = from_behind(
            grad_pair_ext[:, margin + group_rows :].astype(jnp.bfloat16), "dp", 1
        ).astype(jnp.float32)
        grad_pair = grad_pair_ext[:, margin : margin + group_rows]
        grad_pair = (
            grad_pair.at[:, group_rows - margin :].add(from_next).at[:, :margin].add(from_prev)
        )
        grad_triple = jnp.concatenate(
            [grad_query.astype(jnp.bfloat16)[None], grad_pair.astype(jnp.bfloat16)], axis=0
        )
        qkv_grad = jnp.moveaxis(
            scatter_rows(
                jnp.einsum(
                    "gd,sge->dse", normed_full, grad_triple, preferred_element_type=jnp.float32
                )
            ),
            0,
            1,
        )
        triple_sums = jnp.sum(grad_triple.astype(jnp.float32), axis=1)

        def first_term(first_row, row_count):
            return jnp.einsum(
                "sge,sde->gd", grad_triple, qkv_full, preferred_element_type=jnp.float32
            )

        grad_first = sum_backward(first_term, tok_rows)
        first_again, first_pull = jax.vjp(layer_norm, stream_in, gain_now[0], shift_now[0])
        grad_in_norm, gain_zero, shift_zero = first_pull(grad_first)
        gradient = grad_middle + grad_in_norm
        unit_grads[layer_index] = jnp.concatenate(
            [triple_sums[0][None], triple_sums[2][None], up_bias_grad], axis=0
        )
        gain_grads[layer_index] = jnp.stack([gain_zero, gain_one])
        shift_grads[layer_index] = jnp.stack([shift_zero, shift_one, shift_two, shift_three])
        local_qkv[layer_index] = qkv_grad
        local_out[layer_index] = out_grad
        local_up[layer_index] = up_grad
        local_down[layer_index] = down_grad
    grad_qkv = jnp.stack(local_qkv).astype(jnp.float32)
    grad_out = jnp.stack(local_out).astype(jnp.float32)
    grad_up = jnp.stack(local_up).astype(jnp.float32)
    grad_down = jnp.stack(local_down).astype(jnp.float32)
    unit_local = jnp.stack(unit_grads)
    norm_local = jnp.concatenate([jnp.stack(gain_grads), jnp.stack(shift_grads)], axis=1)
    norm_group = jnp.sum(from_everyone(norm_local, "tensor"), axis=0)
    dp_size = lax.axis_size("dp")
    flat = jnp.concatenate([norm_group.reshape(-1), unit_local.reshape(-1)])
    piece = -(-flat.shape[0] // dp_size)
    flat = jnp.pad(flat, (0, piece * dp_size - flat.shape[0]))
    mine = jnp.sum(lax.all_to_all(flat.reshape(dp_size, piece), "dp", 0, 0, tiled=True), axis=0)
    total = collect(mine[None], "dp", 0).reshape(-1)
    norm_size = norm_group.size
    norm_total = total[:norm_size].reshape(norm_group.shape)
    gain_total = norm_total[:, :2]
    shift_total = norm_total[:, 2:6]
    unit_mine = total[norm_size : norm_size + unit_local.size].reshape(unit_local.shape)
    return (
        stream.astype(jnp.bfloat16),
        gradient.astype(jnp.bfloat16),
        grad_qkv,
        grad_out,
        grad_up,
        grad_down,
        unit_mine,
        gain_total,
        shift_total,
    )


def solution(mesh):
    placed = (
        P(("dp", "tensor"), None),
        P(),
        P(),
        P(None, None, "dp", "tensor"),
        P(None, "dp", "tensor"),
        P(None, "dp", None, "tensor"),
        P(None, "dp", None, "tensor"),
        P(None, None, "tensor"),
        P(),
        P(),
        P(("dp", "tensor"), None),
    )
    return jax.shard_map(
        local,
        mesh=mesh,
        in_specs=placed,
        out_specs=(
            P(("dp", "tensor"), None),
            P(("dp", "tensor"), None),
            P(None, None, "dp", "tensor"),
            P(None, "dp", "tensor"),
            P(None, "dp", None, "tensor"),
            P(None, "dp", None, "tensor"),
            P(None, None, "tensor"),
            P(),
            P(),
        ),
        check_vma=False,
    )
```

```python
import functools
import math

import jax
import jax.numpy as jnp
from jax import lax
from jax.experimental import pallas as pl
from jax.experimental.pallas import tpu as pltpu
from jax.sharding import PartitionSpec as P

MESH = pl.DeviceIdType.MESH

LAYERS = 1
IMG = 577
HD = 64


norm_eps = 1e-06
masked_score = -1e30


def from_everyone(value, axis):
    devices = lax.axis_size(axis)
    return lax.all_to_all(
        jnp.broadcast_to(value[None], (devices, *value.shape)), axis, 0, 0, tiled=True
    )


def joined_along(parts, dim):
    dims = list(parts.shape[1:])
    dims[dim] *= parts.shape[0]
    return jnp.moveaxis(parts, 0, dim).reshape(dims)


def collect(value, axis, dim):
    parts = from_everyone(value, axis)
    return joined_along(parts, dim)


def split_up(value, dim, devices):
    dims = value.shape
    parts = value.reshape(*dims[:dim], devices, dims[dim] // devices, *dims[dim + 1 :])
    return jnp.moveaxis(parts, dim, 0)


def summed_on_arrival(value, axis, dim):
    devices = lax.axis_size(axis)
    parts = lax.all_to_all(split_up(value, dim, devices), axis, 0, 0, tiled=True)
    return jnp.sum(parts.astype(jnp.float32), axis=0)


def rows_first(arrays, axis, dims):
    turned = [jnp.moveaxis(a, dim, 0) for a, dim in zip(arrays, dims)]
    both = jnp.concatenate([t.reshape(len(t), -1) for t in turned], axis=1)
    filled, at, outs = (lax.all_gather(both, axis, axis=0, tiled=True), 0, [])
    for t, dim in zip(turned, dims):
        slab = filled[:, at : at + t[0].size].reshape(-1, *t.shape[1:])
        outs.append(jnp.moveaxis(slab, 0, dim))
        at += t[0].size
    return tuple(outs)


def with_halo(value, sides, width):
    for axis, dim in sides:
        devices, length = (lax.axis_size(axis), value.shape[dim])
        up = [(i, (i + 1) % devices) for i in range(devices - 1)]
        down = [(j, i) for i, j in up]
        last = lax.slice_in_dim(value, length - width, length, axis=dim)
        initial = lax.slice_in_dim(value, 0, width, axis=dim)
        before = lax.ppermute(last, axis, up)
        after = lax.ppermute(initial, axis, down)
        value = jnp.concatenate([before, value, after], axis=dim)
    return value


def from_behind(block, axis, distance):
    devices = range(lax.axis_size(axis))
    route = [(i - distance, i) for i in devices if i - distance in devices]
    return lax.ppermute(block, axis, route)


def side_by_side(arrays, axis, dim, along):
    widths = [math.prod(a.shape[along:]) for a in arrays]
    both = jnp.concatenate(
        [a.reshape(*a.shape[:along], w) for a, w in zip(arrays, widths)], axis=along
    )
    filled = lax.psum_scatter(both, axis, scatter_dimension=dim, tiled=True)
    parts = jnp.split(filled, [sum(widths[:k]) for k in range(1, len(widths))], axis=along)
    return tuple(
        (b.reshape(*filled.shape[:along], *a.shape[along:]) for a, b in zip(arrays, parts))
    )


def scatter_rows(grad):
    return summed_on_arrival(grad.astype(jnp.bfloat16), "dp", 0)


def layer_norm(values, gain_row, shift_row):
    center = values - jnp.mean(values, axis=-1, keepdims=True)
    spread = jnp.mean(center * center, axis=-1, keepdims=True)
    return center * lax.rsqrt(spread + norm_eps) * gain_row + shift_row


def exact_gelu(values):
    return jax.nn.gelu(values, approximate=False)


def _gather_kernel(devices, x_ref, out_ref, send_sem, recv_sem):
    me = lax.axis_index("tensor")
    dp = lax.axis_index("dp")
    sib = me + 1 - 2 * lax.rem(me, 2)
    far = lax.rem(me + 2, devices)
    barrier = pltpu.get_barrier_semaphore()
    for peer in (sib, far):
        pl.semaphore_signal(barrier, inc=1, device_id=(dp, peer), device_id_type=MESH)
    pl.semaphore_wait(barrier, 2)
    near_copy = pltpu.make_async_remote_copy(
        src_ref=x_ref,
        dst_ref=out_ref.at[me],
        send_sem=send_sem.at[0],
        recv_sem=recv_sem.at[0],
        device_id=(dp, sib),
        device_id_type=MESH,
    )
    far_copy = pltpu.make_async_remote_copy(
        src_ref=x_ref,
        dst_ref=out_ref.at[me],
        send_sem=send_sem.at[1],
        recv_sem=recv_sem.at[1],
        device_id=(dp, far),
        device_id_type=MESH,
    )
    far_copy.start()
    near_copy.start()
    out_ref[me] = x_ref[...]
    far_copy.wait_recv()
    relay = pltpu.make_async_remote_copy(
        src_ref=out_ref.at[far],
        dst_ref=out_ref.at[far],
        send_sem=send_sem.at[2],
        recv_sem=recv_sem.at[2],
        device_id=(dp, sib),
        device_id_type=MESH,
    )
    relay.start()
    near_copy.wait_send()
    near_copy.wait_recv()
    far_copy.wait_send()
    relay.wait_send()
    relay.wait_recv()


def gather_rows(values):
    devices = lax.axis_size("tensor")
    if devices != 4:
        return collect(values, "tensor", 0)
    rows, width = values.shape
    parts = pl.pallas_call(
        functools.partial(_gather_kernel, devices),
        out_shape=jax.ShapeDtypeStruct((devices, rows, width), values.dtype),
        in_specs=[pl.BlockSpec(memory_space=pltpu.VMEM)],
        out_specs=pl.BlockSpec(memory_space=pltpu.VMEM),
        scratch_shapes=[
            pltpu.SemaphoreType.DMA((3,)),
            pltpu.SemaphoreType.DMA((3,)),
        ],
        compiler_params=pltpu.CompilerParams(collective_id=0, has_side_effects=True),
    )(values)
    return parts.reshape(devices * rows, width)


def _exchange_kernel(devices, x_ref, out_ref, send_sem, recv_sem):
    me = lax.axis_index("tensor")
    dp = lax.axis_index("dp")
    barrier = pltpu.get_barrier_semaphore()
    for step in range(1, devices):
        pl.semaphore_signal(
            barrier, inc=1, device_id=(dp, lax.rem(me + step, devices)), device_id_type=MESH
        )
    pl.semaphore_wait(barrier, devices - 1)
    copies = []
    for step in range(1, devices):
        peer = lax.rem(me + step, devices)
        copy = pltpu.make_async_remote_copy(
            src_ref=x_ref.at[peer],
            dst_ref=out_ref.at[me],
            send_sem=send_sem.at[step - 1],
            recv_sem=recv_sem.at[step - 1],
            device_id=(dp, peer),
            device_id_type=MESH,
        )
        copy.start()
        copies.append(copy)
    out_ref[me] = x_ref[me]
    for copy in copies:
        copy.wait()


def exchange_rows(parts):
    devices = parts.shape[0]
    return pl.pallas_call(
        functools.partial(_exchange_kernel, devices),
        out_shape=jax.ShapeDtypeStruct(parts.shape, parts.dtype),
        in_specs=[pl.BlockSpec(memory_space=pltpu.VMEM)],
        out_specs=pl.BlockSpec(memory_space=pltpu.VMEM),
        scratch_shapes=[
            pltpu.SemaphoreType.DMA((devices - 1,)),
            pltpu.SemaphoreType.DMA((devices - 1,)),
        ],
        compiler_params=pltpu.CompilerParams(collective_id=1, has_side_effects=True),
    )(parts)


def _reduce_kernel(devices, x_ref, out_ref, held, mate, pre, send_sem, recv_sem):
    me = lax.axis_index("tensor")
    dp = lax.axis_index("dp")
    sib = me + 1 - 2 * lax.rem(me, 2)
    far = lax.rem(me + 2, devices)
    other = lax.rem(sib + 2, devices)
    barrier = pltpu.get_barrier_semaphore()
    for peer in (sib, far):
        pl.semaphore_signal(barrier, inc=1, device_id=(dp, peer), device_id_type=MESH)
    pl.semaphore_wait(barrier, 2)
    own_copy = pltpu.make_async_remote_copy(
        src_ref=x_ref.at[sib],
        dst_ref=held.at[0],
        send_sem=send_sem.at[0],
        recv_sem=recv_sem.at[0],
        device_id=(dp, sib),
        device_id_type=MESH,
    )
    mate_copy = pltpu.make_async_remote_copy(
        src_ref=x_ref.at[other],
        dst_ref=mate,
        send_sem=send_sem.at[1],
        recv_sem=recv_sem.at[1],
        device_id=(dp, sib),
        device_id_type=MESH,
    )
    mate_copy.start()
    own_copy.start()
    mate_copy.wait_recv()
    pre[...] = (x_ref[far].astype(jnp.float32) + mate[...].astype(jnp.float32)).astype(pre.dtype)
    own_copy.wait_recv()
    out_ref[...] = x_ref[me].astype(jnp.float32) + held[0].astype(jnp.float32)
    far_copy = pltpu.make_async_remote_copy(
        src_ref=pre,
        dst_ref=held.at[1],
        send_sem=send_sem.at[2],
        recv_sem=recv_sem.at[2],
        device_id=(dp, far),
        device_id_type=MESH,
    )
    far_copy.start()
    far_copy.wait_recv()
    out_ref[...] += held[1].astype(jnp.float32)
    own_copy.wait_send()
    mate_copy.wait_send()
    far_copy.wait_send()


def summed_over_tensor(value):
    devices = lax.axis_size("tensor")
    parts = split_up(value, 0, devices)
    if devices != 4:
        return jnp.sum(exchange_rows(parts).astype(jnp.float32), axis=0)
    rows, width = parts.shape[1:]
    return pl.pallas_call(
        functools.partial(_reduce_kernel, devices),
        out_shape=jax.ShapeDtypeStruct((rows, width), jnp.float32),
        in_specs=[pl.BlockSpec(memory_space=pltpu.VMEM)],
        out_specs=pl.BlockSpec(memory_space=pltpu.VMEM),
        scratch_shapes=[
            pltpu.VMEM((2, rows, width), parts.dtype),
            pltpu.VMEM((rows, width), parts.dtype),
            pltpu.VMEM((rows, width), parts.dtype),
            pltpu.SemaphoreType.DMA((3,)),
            pltpu.SemaphoreType.DMA((3,)),
        ],
        compiler_params=pltpu.CompilerParams(collective_id=1, has_side_effects=True),
    )(parts)


def gather_forward(values):
    return gather_rows(values)


def gather_backward(values):
    return gather_rows(values)


def sum_forward(product, tok_rows):
    return summed_over_tensor(
        product(jnp.int32(0), tok_rows * lax.axis_size("tensor")).astype(jnp.bfloat16)
    )


def sum_backward(product, tok_rows):
    return summed_over_tensor(
        product(jnp.int32(0), tok_rows * lax.axis_size("tensor")).astype(jnp.bfloat16)
    )


def head_scores(query_head, key_head, allowed):
    raw = lax.dot_general(
        query_head, key_head, (((1,), (1,)), ((), ())), preferred_element_type=jnp.float32
    )
    return jnp.where(allowed, raw * HD ** (-0.5), masked_score)


def split_heads(queries, key_ext):
    heads_here = queries.shape[1] // HD
    query_heads = queries.reshape(queries.shape[0], heads_here, HD)
    key_heads = key_ext[0].reshape(key_ext.shape[1], heads_here, HD)
    value_heads = key_ext[1].reshape(key_ext.shape[1], heads_here, HD)
    return (heads_here, query_heads, key_heads, value_heads)


def merge_heads(per_head):
    return jnp.transpose(per_head, (1, 0, 2)).reshape(
        per_head.shape[1], per_head.shape[0] * per_head.shape[2]
    )


def _attend_kernel(q_ref, k_ref, v_ref, mask_ref, o_ref, lse_ref):
    scores = lax.dot_general(
        q_ref[...], k_ref[...], (((1,), (1,)), ((), ())), preferred_element_type=jnp.float32
    )
    scores = jnp.where(mask_ref[...] != 0, scores * HD ** (-0.5), masked_score)
    row_top = jnp.max(scores, axis=1, keepdims=True)
    exponent = jnp.exp(scores - row_top)
    row_total = jnp.sum(exponent, axis=1, keepdims=True)
    prob_low = (exponent / row_total).astype(jnp.bfloat16)
    o_ref[...] = jnp.dot(prob_low, v_ref[...], preferred_element_type=jnp.float32)
    lse_ref[...] = row_top + jnp.log(row_total)


def attend_forward(queries, key_ext, allowed):
    heads_here = queries.shape[1] // HD
    rows, keys = allowed.shape
    query_heads = jnp.transpose(queries.reshape(rows, heads_here, HD), (1, 0, 2))
    key_heads = jnp.transpose(key_ext[0].reshape(keys, heads_here, HD), (1, 0, 2))
    value_heads = jnp.transpose(key_ext[1].reshape(keys, heads_here, HD), (1, 0, 2))
    head_outs, log_norm = pl.pallas_call(
        _attend_kernel,
        grid=(heads_here,),
        out_shape=(
            jax.ShapeDtypeStruct((heads_here, rows, HD), jnp.float32),
            jax.ShapeDtypeStruct((heads_here, rows, 1), jnp.float32),
        ),
        in_specs=[
            pl.BlockSpec((None, rows, HD), lambda h: (h, 0, 0)),
            pl.BlockSpec((None, keys, HD), lambda h: (h, 0, 0)),
            pl.BlockSpec((None, keys, HD), lambda h: (h, 0, 0)),
            pl.BlockSpec((rows, keys), lambda h: (0, 0)),
        ],
        out_specs=(
            pl.BlockSpec((None, rows, HD), lambda h: (h, 0, 0)),
            pl.BlockSpec((None, rows, 1), lambda h: (h, 0, 0)),
        ),
        compiler_params=pltpu.CompilerParams(vmem_limit_bytes=60 * 1024 * 1024),
    )(query_heads, key_heads, value_heads, allowed.astype(jnp.int32))
    return (merge_heads(head_outs), log_norm[:, :, 0])


def attend_forward_xla(queries, key_ext, allowed):
    heads_here, query_heads, key_heads, value_heads = split_heads(queries, key_ext)

    def one_head(head_index):
        query_head = lax.dynamic_index_in_dim(query_heads, head_index, 1, keepdims=False)
        key_head = lax.dynamic_index_in_dim(key_heads, head_index, 1, keepdims=False)
        value_head = lax.dynamic_index_in_dim(value_heads, head_index, 1, keepdims=False)
        scores = head_scores(query_head, key_head, allowed)
        row_top = jnp.max(scores, axis=1, keepdims=True)
        exponent = jnp.exp(scores - row_top)
        row_total = jnp.sum(exponent, axis=1, keepdims=True)
        prob_low = (exponent / row_total).astype(jnp.bfloat16)
        head_out = jnp.dot(prob_low, value_head, preferred_element_type=jnp.float32)
        return (head_out, (row_top + jnp.log(row_total))[:, 0])

    head_outs, log_norm = lax.map(one_head, jnp.arange(heads_here, dtype=jnp.int32))
    return (merge_heads(head_outs), log_norm)


def attend_backward(queries, key_ext, allowed, log_norm, grad_attended):
    heads_here, query_heads, key_heads, value_heads = split_heads(queries, key_ext)
    grad_heads = grad_attended.reshape(grad_attended.shape[0], heads_here, HD)

    def one_head(inputs):
        head_index, norm_row = inputs
        query_head = lax.dynamic_index_in_dim(query_heads, head_index, 1, keepdims=False)
        key_head = lax.dynamic_index_in_dim(key_heads, head_index, 1, keepdims=False)
        value_head = lax.dynamic_index_in_dim(value_heads, head_index, 1, keepdims=False)
        grad_head = lax.dynamic_index_in_dim(grad_heads, head_index, 1, keepdims=False)
        prob_full = jnp.exp(head_scores(query_head, key_head, allowed) - norm_row[:, None])
        prob_low = prob_full.astype(jnp.bfloat16)
        grad_value = lax.dot_general(
            prob_low, grad_head, (((0,), (0,)), ((), ())), preferred_element_type=jnp.float32
        )
        grad_prob = lax.dot_general(
            grad_head, value_head, (((1,), (1,)), ((), ())), preferred_element_type=jnp.float32
        )
        grad_score = (
            prob_full * (grad_prob - jnp.sum(prob_full * grad_prob, axis=1, keepdims=True))
        ).astype(jnp.bfloat16)
        grad_query = jnp.dot(grad_score, key_head, preferred_element_type=jnp.float32) * HD ** (
            -0.5
        )
        grad_key = lax.dot_general(
            grad_score, query_head, (((0,), (0,)), ((), ())), preferred_element_type=jnp.float32
        ) * HD ** (-0.5)
        return (grad_query, grad_key, grad_value)

    grad_queries, grad_keys, grad_values = lax.map(
        one_head, (jnp.arange(heads_here, dtype=jnp.int32), log_norm)
    )
    return (merge_heads(grad_queries), merge_heads(grad_keys), merge_heads(grad_values))


def local(
    tokens,
    segment,
    real_token,
    qkv_weight,
    out_weight,
    up_weight,
    down_weight,
    unit_bias,
    norm_gain,
    row_bias,
    cotangent,
):
    tok_rows = tokens.shape[0]
    tensor_size = lax.axis_size("tensor")
    group_rows = tok_rows * tensor_size
    margin = IMG - 1
    cols_here = qkv_weight.shape[3]
    dp_index = lax.axis_index("dp")
    tensor_index = lax.axis_index("tensor")
    group_first = dp_index * group_rows
    own_first = group_first + tensor_index * tok_rows
    segment_pad = jnp.pad(segment, (margin, margin), constant_values=-1)
    real_pad = jnp.pad(real_token, (margin, margin))
    segment_query = lax.dynamic_slice_in_dim(segment, group_first, group_rows, 0)
    segment_key = lax.dynamic_slice_in_dim(segment_pad, group_first, group_rows + 2 * margin, 0)
    real_key = lax.dynamic_slice_in_dim(real_pad, group_first, group_rows + 2 * margin, 0)
    place_query = jnp.arange(group_rows, dtype=jnp.int32)
    place_key = jnp.arange(group_rows + 2 * margin, dtype=jnp.int32) - margin
    allowed = (segment_query[:, None] == segment_key[None, :]) & (
        (real_key[None, :] == 1) | (place_query[:, None] == place_key[None, :])
    )
    own_real = lax.dynamic_slice_in_dim(real_token, own_first, tok_rows, 0).astype(jnp.float32)
    stream = tokens.astype(jnp.float32)
    layer_index = 0
    qkv_local = jnp.moveaxis(qkv_weight[layer_index], 1, 0)
    out_local, up_local, down_local = (
        out_weight[layer_index],
        up_weight[layer_index],
        down_weight[layer_index],
    )
    gain_now = norm_gain[layer_index].astype(jnp.float32)
    shift_now = row_bias[layer_index].astype(jnp.float32)
    bias_now = unit_bias[layer_index].astype(jnp.float32)
    normed_full = gather_forward(layer_norm(stream, gain_now[0], shift_now[0]).astype(jnp.bfloat16))
    normed_full, qkv_local = lax.optimization_barrier((normed_full, qkv_local))
    qkv_full = jnp.moveaxis(collect(qkv_local, "dp", 0), 0, 1)
    projected = jnp.einsum("gd,sde->sge", normed_full, qkv_full, preferred_element_type=jnp.float32)
    queries = (projected[0] + bias_now[0]).astype(jnp.bfloat16)
    queries, out_local, up_local, down_local = lax.optimization_barrier(
        (queries, out_local, up_local, down_local)
    )
    out_full = collect(out_local, "dp", 0)
    up_full = collect(up_local, "dp", 0)
    down_full = collect(down_local, "dp", 0)
    gathered = (qkv_full, out_full, up_full, down_full)
    key_value = jnp.stack([projected[1], projected[2] + bias_now[1]]).astype(jnp.bfloat16)
    key_ext = with_halo(key_value, (("dp", 1),), margin)
    attended, log_norm = attend_forward(queries, key_ext, allowed)
    attended = attended.astype(jnp.bfloat16)

    def attention_term(first_row, row_count):
        return lax.dot_general(
            attended, out_full, (((1,), (1,)), ((), ())), preferred_element_type=jnp.float32
        )

    middle = stream + sum_forward(attention_term, tok_rows) + shift_now[1]
    second_full = gather_forward(layer_norm(middle, gain_now[1], shift_now[2]).astype(jnp.bfloat16))
    hidden = (
        jnp.einsum("gd,dre->gre", second_full, up_full, preferred_element_type=jnp.float32)
        + bias_now[2:][None]
    )
    active = exact_gelu(hidden).astype(jnp.bfloat16)

    def feed_term(first_row, row_count):
        return jnp.einsum("gre,ore->go", active, down_full, preferred_element_type=jnp.float32)

    kept_weights = gathered
    records = [
        (
            stream,
            middle,
            normed_full,
            second_full,
            queries,
            key_ext,
            log_norm,
            attended,
            hidden,
            active,
            kept_weights,
        )
    ]
    stream = middle + sum_forward(feed_term, tok_rows) + shift_now[3]
    gradient = cotangent.astype(jnp.float32) * own_real[:, None]
    local_qkv = [None] * LAYERS
    local_out = [None] * LAYERS
    local_up = [None] * LAYERS
    local_down = [None] * LAYERS
    unit_grads = [None] * LAYERS
    gain_grads = [None] * LAYERS
    shift_grads = [None] * LAYERS
    for layer_index in reversed(range(LAYERS)):
        (
            stream_in,
            middle,
            normed_full,
            second_full,
            queries,
            key_ext,
            log_norm,
            attended,
            hidden,
            active,
            kept_weights,
        ) = records[layer_index]
        qkv_full, out_full, up_full, down_full = kept_weights
        gain_now = norm_gain[layer_index].astype(jnp.float32)
        shift_now = row_bias[layer_index].astype(jnp.float32)
        shift_three = jnp.sum(gradient, axis=0)
        grad_mlp = gather_backward(gradient.astype(jnp.bfloat16))
        down_grad = scatter_rows(
            jnp.einsum("go,gre->ore", grad_mlp, active, preferred_element_type=jnp.float32)
        )
        grad_active = jnp.einsum(
            "go,ore->gre", grad_mlp, down_full, preferred_element_type=jnp.float32
        )
        gelu_again, gelu_pull = jax.vjp(exact_gelu, hidden)
        grad_hidden = gelu_pull(grad_active)[0].astype(jnp.bfloat16)
        up_bias_grad = jnp.sum(grad_hidden.astype(jnp.float32), axis=0)
        up_grad = scatter_rows(
            jnp.einsum("gd,gre->dre", second_full, grad_hidden, preferred_element_type=jnp.float32)
        )

        def second_term(first_row, row_count):
            return jnp.einsum(
                "gre,dre->gd", grad_hidden, up_full, preferred_element_type=jnp.float32
            )

        grad_second = sum_backward(second_term, tok_rows)
        second_again, second_pull = jax.vjp(layer_norm, middle, gain_now[1], shift_now[2])
        grad_mid_norm, gain_one, shift_two = second_pull(grad_second)
        grad_middle = gradient + grad_mid_norm
        shift_one = jnp.sum(grad_middle, axis=0)
        grad_proj = gather_backward(grad_middle.astype(jnp.bfloat16))
        out_grad = scatter_rows(
            lax.dot_general(
                grad_proj, attended, (((0,), (0,)), ((), ())), preferred_element_type=jnp.float32
            )
        )
        grad_attended = jnp.dot(grad_proj, out_full, preferred_element_type=jnp.float32).astype(
            jnp.bfloat16
        )
        grad_query, grad_key_ext, grad_value_ext = attend_backward(
            queries, key_ext, allowed, log_norm, grad_attended
        )
        grad_pair_ext = jnp.stack([grad_key_ext, grad_value_ext])
        from_next = from_behind(grad_pair_ext[:, :margin].astype(jnp.bfloat16), "dp", -1).astype(
            jnp.float32
        )
        from_prev = from_behind(
            grad_pair_ext[:, margin + group_rows :].astype(jnp.bfloat16), "dp", 1
        ).astype(jnp.float32)
        grad_pair = grad_pair_ext[:, margin : margin + group_rows]
        grad_pair = (
            grad_pair.at[:, group_rows - margin :].add(from_next).at[:, :margin].add(from_prev)
        )
        grad_triple = jnp.concatenate(
            [grad_query.astype(jnp.bfloat16)[None], grad_pair.astype(jnp.bfloat16)], axis=0
        )
        qkv_grad = jnp.moveaxis(
            scatter_rows(
                jnp.einsum(
                    "gd,sge->dse", normed_full, grad_triple, preferred_element_type=jnp.float32
                )
            ),
            0,
            1,
        )
        triple_sums = jnp.sum(grad_triple.astype(jnp.float32), axis=1)

        def first_term(first_row, row_count):
            return jnp.einsum(
                "sge,sde->gd", grad_triple, qkv_full, preferred_element_type=jnp.float32
            )

        grad_first = sum_backward(first_term, tok_rows)
        first_again, first_pull = jax.vjp(layer_norm, stream_in, gain_now[0], shift_now[0])
        grad_in_norm, gain_zero, shift_zero = first_pull(grad_first)
        gradient = grad_middle + grad_in_norm
        unit_grads[layer_index] = jnp.concatenate(
            [triple_sums[0][None], triple_sums[2][None], up_bias_grad], axis=0
        )
        gain_grads[layer_index] = jnp.stack([gain_zero, gain_one])
        shift_grads[layer_index] = jnp.stack([shift_zero, shift_one, shift_two, shift_three])
        local_qkv[layer_index] = qkv_grad
        local_out[layer_index] = out_grad
        local_up[layer_index] = up_grad
        local_down[layer_index] = down_grad
    grad_qkv = jnp.stack(local_qkv).astype(jnp.float32)
    grad_out = jnp.stack(local_out).astype(jnp.float32)
    grad_up = jnp.stack(local_up).astype(jnp.float32)
    grad_down = jnp.stack(local_down).astype(jnp.float32)
    unit_local = jnp.stack(unit_grads)
    unit_wide = jnp.zeros((LAYERS, unit_local.shape[1], cols_here * tensor_size), jnp.float32)
    unit_wide = lax.dynamic_update_slice_in_dim(unit_wide, unit_local, tensor_index * cols_here, 2)
    small = jnp.concatenate(
        [jnp.stack(gain_grads), jnp.stack(shift_grads), unit_wide], axis=1
    )
    small_total = jnp.sum(from_everyone(small, "dp"), axis=0)
    small_total = jnp.sum(from_everyone(small_total, "tensor"), axis=0)
    gain_total = small_total[:, :2]
    shift_total = small_total[:, 2:6]
    unit_total = small_total[:, 6:]
    unit_mine = lax.dynamic_slice_in_dim(unit_total, tensor_index * cols_here, cols_here, 2)
    return (
        stream.astype(jnp.bfloat16),
        gradient.astype(jnp.bfloat16),
        grad_qkv,
        grad_out,
        grad_up,
        grad_down,
        unit_mine,
        gain_total,
        shift_total,
    )


def solution(mesh):
    placed = (
        P(("dp", "tensor"), None),
        P(),
        P(),
        P(None, None, "dp", "tensor"),
        P(None, "dp", "tensor"),
        P(None, "dp", None, "tensor"),
        P(None, "dp", None, "tensor"),
        P(None, None, "tensor"),
        P(),
        P(),
        P(("dp", "tensor"), None),
    )
    return jax.shard_map(
        local,
        mesh=mesh,
        in_specs=placed,
        out_specs=(
            P(("dp", "tensor"), None),
            P(("dp", "tensor"), None),
            P(None, None, "dp", "tensor"),
            P(None, "dp", "tensor"),
            P(None, "dp", None, "tensor"),
            P(None, "dp", None, "tensor"),
            P(None, None, "tensor"),
            P(),
            P(),
        ),
        check_vma=False,
    )
```

```python
import functools
import math

import jax
import jax.numpy as jnp
from jax import lax
from jax.experimental import pallas as pl
from jax.experimental.pallas import tpu as pltpu
from jax.sharding import PartitionSpec as P

MESH = pl.DeviceIdType.MESH

LAYERS = 1
IMG = 577
HD = 64


norm_eps = 1e-06
masked_score = -1e30


def from_everyone(value, axis):
    devices = lax.axis_size(axis)
    return lax.all_to_all(
        jnp.broadcast_to(value[None], (devices, *value.shape)), axis, 0, 0, tiled=True
    )


def joined_along(parts, dim):
    dims = list(parts.shape[1:])
    dims[dim] *= parts.shape[0]
    return jnp.moveaxis(parts, 0, dim).reshape(dims)


def collect(value, axis, dim):
    parts = from_everyone(value, axis)
    return joined_along(parts, dim)


def split_up(value, dim, devices):
    dims = value.shape
    parts = value.reshape(*dims[:dim], devices, dims[dim] // devices, *dims[dim + 1 :])
    return jnp.moveaxis(parts, dim, 0)


def summed_on_arrival(value, axis, dim):
    devices = lax.axis_size(axis)
    parts = lax.all_to_all(split_up(value, dim, devices), axis, 0, 0, tiled=True)
    return jnp.sum(parts.astype(jnp.float32), axis=0)


def rows_first(arrays, axis, dims):
    turned = [jnp.moveaxis(a, dim, 0) for a, dim in zip(arrays, dims)]
    both = jnp.concatenate([t.reshape(len(t), -1) for t in turned], axis=1)
    filled, at, outs = (lax.all_gather(both, axis, axis=0, tiled=True), 0, [])
    for t, dim in zip(turned, dims):
        slab = filled[:, at : at + t[0].size].reshape(-1, *t.shape[1:])
        outs.append(jnp.moveaxis(slab, 0, dim))
        at += t[0].size
    return tuple(outs)


def with_halo(value, sides, width):
    for axis, dim in sides:
        devices, length = (lax.axis_size(axis), value.shape[dim])
        up = [(i, (i + 1) % devices) for i in range(devices - 1)]
        down = [(j, i) for i, j in up]
        last = lax.slice_in_dim(value, length - width, length, axis=dim)
        initial = lax.slice_in_dim(value, 0, width, axis=dim)
        before = lax.ppermute(last, axis, up)
        after = lax.ppermute(initial, axis, down)
        value = jnp.concatenate([before, value, after], axis=dim)
    return value


def from_behind(block, axis, distance):
    devices = range(lax.axis_size(axis))
    route = [(i - distance, i) for i in devices if i - distance in devices]
    return lax.ppermute(block, axis, route)


def side_by_side(arrays, axis, dim, along):
    widths = [math.prod(a.shape[along:]) for a in arrays]
    both = jnp.concatenate(
        [a.reshape(*a.shape[:along], w) for a, w in zip(arrays, widths)], axis=along
    )
    filled = lax.psum_scatter(both, axis, scatter_dimension=dim, tiled=True)
    parts = jnp.split(filled, [sum(widths[:k]) for k in range(1, len(widths))], axis=along)
    return tuple(
        (b.reshape(*filled.shape[:along], *a.shape[along:]) for a, b in zip(arrays, parts))
    )


def scatter_rows(grad):
    return summed_on_arrival(grad.astype(jnp.bfloat16), "dp", 0)


def layer_norm(values, gain_row, shift_row):
    center = values - jnp.mean(values, axis=-1, keepdims=True)
    spread = jnp.mean(center * center, axis=-1, keepdims=True)
    return center * lax.rsqrt(spread + norm_eps) * gain_row + shift_row


def exact_gelu(values):
    return jax.nn.gelu(values, approximate=False)


def _gather_kernel(devices, x_ref, out_ref, send_sem, recv_sem):
    me = lax.axis_index("tensor")
    dp = lax.axis_index("dp")
    sib = me + 1 - 2 * lax.rem(me, 2)
    far = lax.rem(me + 2, devices)
    barrier = pltpu.get_barrier_semaphore()
    for peer in (sib, far):
        pl.semaphore_signal(barrier, inc=1, device_id=(dp, peer), device_id_type=MESH)
    pl.semaphore_wait(barrier, 2)
    near_copy = pltpu.make_async_remote_copy(
        src_ref=x_ref,
        dst_ref=out_ref.at[me],
        send_sem=send_sem.at[0],
        recv_sem=recv_sem.at[0],
        device_id=(dp, sib),
        device_id_type=MESH,
    )
    far_copy = pltpu.make_async_remote_copy(
        src_ref=x_ref,
        dst_ref=out_ref.at[me],
        send_sem=send_sem.at[1],
        recv_sem=recv_sem.at[1],
        device_id=(dp, far),
        device_id_type=MESH,
    )
    far_copy.start()
    near_copy.start()
    out_ref[me] = x_ref[...]
    far_copy.wait_recv()
    relay = pltpu.make_async_remote_copy(
        src_ref=out_ref.at[far],
        dst_ref=out_ref.at[far],
        send_sem=send_sem.at[2],
        recv_sem=recv_sem.at[2],
        device_id=(dp, sib),
        device_id_type=MESH,
    )
    relay.start()
    near_copy.wait_send()
    near_copy.wait_recv()
    far_copy.wait_send()
    relay.wait_send()
    relay.wait_recv()


def gather_rows(values):
    devices = lax.axis_size("tensor")
    if devices != 4:
        return collect(values, "tensor", 0)
    rows, width = values.shape
    parts = pl.pallas_call(
        functools.partial(_gather_kernel, devices),
        out_shape=jax.ShapeDtypeStruct((devices, rows, width), values.dtype),
        in_specs=[pl.BlockSpec(memory_space=pltpu.VMEM)],
        out_specs=pl.BlockSpec(memory_space=pltpu.VMEM),
        scratch_shapes=[
            pltpu.SemaphoreType.DMA((3,)),
            pltpu.SemaphoreType.DMA((3,)),
        ],
        compiler_params=pltpu.CompilerParams(collective_id=0, has_side_effects=True),
    )(values)
    return parts.reshape(devices * rows, width)


def _exchange_kernel(devices, x_ref, out_ref, send_sem, recv_sem):
    me = lax.axis_index("tensor")
    dp = lax.axis_index("dp")
    barrier = pltpu.get_barrier_semaphore()
    for step in range(1, devices):
        pl.semaphore_signal(
            barrier, inc=1, device_id=(dp, lax.rem(me + step, devices)), device_id_type=MESH
        )
    pl.semaphore_wait(barrier, devices - 1)
    copies = []
    for step in range(1, devices):
        peer = lax.rem(me + step, devices)
        copy = pltpu.make_async_remote_copy(
            src_ref=x_ref.at[peer],
            dst_ref=out_ref.at[me],
            send_sem=send_sem.at[step - 1],
            recv_sem=recv_sem.at[step - 1],
            device_id=(dp, peer),
            device_id_type=MESH,
        )
        copy.start()
        copies.append(copy)
    out_ref[me] = x_ref[me]
    for copy in copies:
        copy.wait()


def exchange_rows(parts):
    devices = parts.shape[0]
    return pl.pallas_call(
        functools.partial(_exchange_kernel, devices),
        out_shape=jax.ShapeDtypeStruct(parts.shape, parts.dtype),
        in_specs=[pl.BlockSpec(memory_space=pltpu.VMEM)],
        out_specs=pl.BlockSpec(memory_space=pltpu.VMEM),
        scratch_shapes=[
            pltpu.SemaphoreType.DMA((devices - 1,)),
            pltpu.SemaphoreType.DMA((devices - 1,)),
        ],
        compiler_params=pltpu.CompilerParams(collective_id=1, has_side_effects=True),
    )(parts)


def _reduce_kernel(devices, x_ref, out_ref, held, mate, pre, send_sem, recv_sem):
    me = lax.axis_index("tensor")
    dp = lax.axis_index("dp")
    sib = me + 1 - 2 * lax.rem(me, 2)
    far = lax.rem(me + 2, devices)
    other = lax.rem(sib + 2, devices)
    barrier = pltpu.get_barrier_semaphore()
    for peer in (sib, far):
        pl.semaphore_signal(barrier, inc=1, device_id=(dp, peer), device_id_type=MESH)
    pl.semaphore_wait(barrier, 2)
    own_copy = pltpu.make_async_remote_copy(
        src_ref=x_ref.at[sib],
        dst_ref=held.at[0],
        send_sem=send_sem.at[0],
        recv_sem=recv_sem.at[0],
        device_id=(dp, sib),
        device_id_type=MESH,
    )
    mate_copy = pltpu.make_async_remote_copy(
        src_ref=x_ref.at[other],
        dst_ref=mate,
        send_sem=send_sem.at[1],
        recv_sem=recv_sem.at[1],
        device_id=(dp, sib),
        device_id_type=MESH,
    )
    mate_copy.start()
    own_copy.start()
    mate_copy.wait_recv()
    pre[...] = (x_ref[far].astype(jnp.float32) + mate[...].astype(jnp.float32)).astype(pre.dtype)
    own_copy.wait_recv()
    out_ref[...] = x_ref[me].astype(jnp.float32) + held[0].astype(jnp.float32)
    far_copy = pltpu.make_async_remote_copy(
        src_ref=pre,
        dst_ref=held.at[1],
        send_sem=send_sem.at[2],
        recv_sem=recv_sem.at[2],
        device_id=(dp, far),
        device_id_type=MESH,
    )
    far_copy.start()
    far_copy.wait_recv()
    out_ref[...] += held[1].astype(jnp.float32)
    own_copy.wait_send()
    mate_copy.wait_send()
    far_copy.wait_send()


def summed_over_tensor(value):
    devices = lax.axis_size("tensor")
    parts = split_up(value, 0, devices)
    if devices != 4:
        return jnp.sum(exchange_rows(parts).astype(jnp.float32), axis=0)
    rows, width = parts.shape[1:]
    return pl.pallas_call(
        functools.partial(_reduce_kernel, devices),
        out_shape=jax.ShapeDtypeStruct((rows, width), jnp.float32),
        in_specs=[pl.BlockSpec(memory_space=pltpu.VMEM)],
        out_specs=pl.BlockSpec(memory_space=pltpu.VMEM),
        scratch_shapes=[
            pltpu.VMEM((2, rows, width), parts.dtype),
            pltpu.VMEM((rows, width), parts.dtype),
            pltpu.VMEM((rows, width), parts.dtype),
            pltpu.SemaphoreType.DMA((3,)),
            pltpu.SemaphoreType.DMA((3,)),
        ],
        compiler_params=pltpu.CompilerParams(collective_id=1, has_side_effects=True),
    )(parts)


def gather_forward(values):
    return gather_rows(values)


def gather_backward(values):
    return gather_rows(values)


def sum_forward(product, tok_rows):
    return summed_over_tensor(
        product(jnp.int32(0), tok_rows * lax.axis_size("tensor")).astype(jnp.bfloat16)
    )


def sum_backward(product, tok_rows):
    return summed_over_tensor(
        product(jnp.int32(0), tok_rows * lax.axis_size("tensor")).astype(jnp.bfloat16)
    )


def head_scores(query_head, key_head, allowed):
    raw = lax.dot_general(
        query_head, key_head, (((1,), (1,)), ((), ())), preferred_element_type=jnp.float32
    )
    return jnp.where(allowed, raw * HD ** (-0.5), masked_score)


def split_heads(queries, key_ext):
    heads_here = queries.shape[1] // HD
    query_heads = queries.reshape(queries.shape[0], heads_here, HD)
    key_heads = key_ext[0].reshape(key_ext.shape[1], heads_here, HD)
    value_heads = key_ext[1].reshape(key_ext.shape[1], heads_here, HD)
    return (heads_here, query_heads, key_heads, value_heads)


def merge_heads(per_head):
    return jnp.transpose(per_head, (1, 0, 2)).reshape(
        per_head.shape[1], per_head.shape[0] * per_head.shape[2]
    )


def _attend_kernel(q_ref, k_ref, v_ref, mask_ref, o_ref, lse_ref):
    scores = lax.dot_general(
        q_ref[...], k_ref[...], (((1,), (1,)), ((), ())), preferred_element_type=jnp.float32
    )
    scores = jnp.where(mask_ref[...] != 0, scores * HD ** (-0.5), masked_score)
    row_top = jnp.max(scores, axis=1, keepdims=True)
    exponent = jnp.exp(scores - row_top)
    row_total = jnp.sum(exponent, axis=1, keepdims=True)
    prob_low = (exponent / row_total).astype(jnp.bfloat16)
    o_ref[...] = jnp.dot(prob_low, v_ref[...], preferred_element_type=jnp.float32)
    lse_ref[...] = row_top + jnp.log(row_total)


def attend_forward(queries, key_ext, allowed):
    heads_here = queries.shape[1] // HD
    rows, keys = allowed.shape
    query_heads = jnp.transpose(queries.reshape(rows, heads_here, HD), (1, 0, 2))
    key_heads = jnp.transpose(key_ext[0].reshape(keys, heads_here, HD), (1, 0, 2))
    value_heads = jnp.transpose(key_ext[1].reshape(keys, heads_here, HD), (1, 0, 2))
    head_outs, log_norm = pl.pallas_call(
        _attend_kernel,
        grid=(heads_here,),
        out_shape=(
            jax.ShapeDtypeStruct((heads_here, rows, HD), jnp.float32),
            jax.ShapeDtypeStruct((heads_here, rows, 1), jnp.float32),
        ),
        in_specs=[
            pl.BlockSpec((None, rows, HD), lambda h: (h, 0, 0)),
            pl.BlockSpec((None, keys, HD), lambda h: (h, 0, 0)),
            pl.BlockSpec((None, keys, HD), lambda h: (h, 0, 0)),
            pl.BlockSpec((rows, keys), lambda h: (0, 0)),
        ],
        out_specs=(
            pl.BlockSpec((None, rows, HD), lambda h: (h, 0, 0)),
            pl.BlockSpec((None, rows, 1), lambda h: (h, 0, 0)),
        ),
        compiler_params=pltpu.CompilerParams(vmem_limit_bytes=60 * 1024 * 1024),
    )(query_heads, key_heads, value_heads, allowed.astype(jnp.int32))
    return (merge_heads(head_outs), log_norm[:, :, 0])


def attend_forward_xla(queries, key_ext, allowed):
    heads_here, query_heads, key_heads, value_heads = split_heads(queries, key_ext)

    def one_head(head_index):
        query_head = lax.dynamic_index_in_dim(query_heads, head_index, 1, keepdims=False)
        key_head = lax.dynamic_index_in_dim(key_heads, head_index, 1, keepdims=False)
        value_head = lax.dynamic_index_in_dim(value_heads, head_index, 1, keepdims=False)
        scores = head_scores(query_head, key_head, allowed)
        row_top = jnp.max(scores, axis=1, keepdims=True)
        exponent = jnp.exp(scores - row_top)
        row_total = jnp.sum(exponent, axis=1, keepdims=True)
        prob_low = (exponent / row_total).astype(jnp.bfloat16)
        head_out = jnp.dot(prob_low, value_head, preferred_element_type=jnp.float32)
        return (head_out, (row_top + jnp.log(row_total))[:, 0])

    head_outs, log_norm = lax.map(one_head, jnp.arange(heads_here, dtype=jnp.int32))
    return (merge_heads(head_outs), log_norm)


def _attend_back_kernel(q_ref, k_ref, v_ref, g_ref, lse_ref, mask_ref, dq_ref, dk_ref, dv_ref):
    query_head, key_head, grad_head = q_ref[...], k_ref[...], g_ref[...]
    scores = lax.dot_general(
        query_head, key_head, (((1,), (1,)), ((), ())), preferred_element_type=jnp.float32
    )
    scores = jnp.where(mask_ref[...] != 0, scores * HD ** (-0.5), masked_score)
    prob_full = jnp.exp(scores - lse_ref[...])
    prob_low = prob_full.astype(jnp.bfloat16)
    dv_ref[...] = lax.dot_general(
        prob_low, grad_head, (((0,), (0,)), ((), ())), preferred_element_type=jnp.float32
    )
    grad_prob = lax.dot_general(
        grad_head, v_ref[...], (((1,), (1,)), ((), ())), preferred_element_type=jnp.float32
    )
    grad_score = (
        prob_full * (grad_prob - jnp.sum(prob_full * grad_prob, axis=1, keepdims=True))
    ).astype(jnp.bfloat16)
    dq_ref[...] = jnp.dot(grad_score, key_head, preferred_element_type=jnp.float32) * HD ** (-0.5)
    dk_ref[...] = lax.dot_general(
        grad_score, query_head, (((0,), (0,)), ((), ())), preferred_element_type=jnp.float32
    ) * HD ** (-0.5)


def attend_backward(queries, key_ext, allowed, log_norm, grad_attended):
    heads_here = queries.shape[1] // HD
    rows, keys = allowed.shape

    def by_head(values, count):
        return jnp.transpose(values.reshape(count, heads_here, HD), (1, 0, 2))

    row_spec = pl.BlockSpec((None, rows, HD), lambda h: (h, 0, 0))
    key_spec = pl.BlockSpec((None, keys, HD), lambda h: (h, 0, 0))
    grad_queries, grad_keys, grad_values = pl.pallas_call(
        _attend_back_kernel,
        grid=(heads_here,),
        out_shape=(
            jax.ShapeDtypeStruct((heads_here, rows, HD), jnp.float32),
            jax.ShapeDtypeStruct((heads_here, keys, HD), jnp.float32),
            jax.ShapeDtypeStruct((heads_here, keys, HD), jnp.float32),
        ),
        in_specs=[
            row_spec,
            key_spec,
            key_spec,
            row_spec,
            pl.BlockSpec((None, rows, 1), lambda h: (h, 0, 0)),
            pl.BlockSpec((rows, keys), lambda h: (0, 0)),
        ],
        out_specs=(row_spec, key_spec, key_spec),
        compiler_params=pltpu.CompilerParams(vmem_limit_bytes=60 * 1024 * 1024),
    )(
        by_head(queries, rows),
        by_head(key_ext[0], keys),
        by_head(key_ext[1], keys),
        by_head(grad_attended, rows),
        log_norm[:, :, None],
        allowed.astype(jnp.int32),
    )
    return (merge_heads(grad_queries), merge_heads(grad_keys), merge_heads(grad_values))


def attend_backward_xla(queries, key_ext, allowed, log_norm, grad_attended):
    heads_here, query_heads, key_heads, value_heads = split_heads(queries, key_ext)
    grad_heads = grad_attended.reshape(grad_attended.shape[0], heads_here, HD)

    def one_head(inputs):
        head_index, norm_row = inputs
        query_head = lax.dynamic_index_in_dim(query_heads, head_index, 1, keepdims=False)
        key_head = lax.dynamic_index_in_dim(key_heads, head_index, 1, keepdims=False)
        value_head = lax.dynamic_index_in_dim(value_heads, head_index, 1, keepdims=False)
        grad_head = lax.dynamic_index_in_dim(grad_heads, head_index, 1, keepdims=False)
        prob_full = jnp.exp(head_scores(query_head, key_head, allowed) - norm_row[:, None])
        prob_low = prob_full.astype(jnp.bfloat16)
        grad_value = lax.dot_general(
            prob_low, grad_head, (((0,), (0,)), ((), ())), preferred_element_type=jnp.float32
        )
        grad_prob = lax.dot_general(
            grad_head, value_head, (((1,), (1,)), ((), ())), preferred_element_type=jnp.float32
        )
        grad_score = (
            prob_full * (grad_prob - jnp.sum(prob_full * grad_prob, axis=1, keepdims=True))
        ).astype(jnp.bfloat16)
        grad_query = jnp.dot(grad_score, key_head, preferred_element_type=jnp.float32) * HD ** (
            -0.5
        )
        grad_key = lax.dot_general(
            grad_score, query_head, (((0,), (0,)), ((), ())), preferred_element_type=jnp.float32
        ) * HD ** (-0.5)
        return (grad_query, grad_key, grad_value)

    grad_queries, grad_keys, grad_values = lax.map(
        one_head, (jnp.arange(heads_here, dtype=jnp.int32), log_norm)
    )
    return (merge_heads(grad_queries), merge_heads(grad_keys), merge_heads(grad_values))


def local(
    tokens,
    segment,
    real_token,
    qkv_weight,
    out_weight,
    up_weight,
    down_weight,
    unit_bias,
    norm_gain,
    row_bias,
    cotangent,
):
    tok_rows = tokens.shape[0]
    tensor_size = lax.axis_size("tensor")
    group_rows = tok_rows * tensor_size
    margin = IMG - 1
    cols_here = qkv_weight.shape[3]
    dp_index = lax.axis_index("dp")
    tensor_index = lax.axis_index("tensor")
    group_first = dp_index * group_rows
    own_first = group_first + tensor_index * tok_rows
    segment_pad = jnp.pad(segment, (margin, margin), constant_values=-1)
    real_pad = jnp.pad(real_token, (margin, margin))
    segment_query = lax.dynamic_slice_in_dim(segment, group_first, group_rows, 0)
    segment_key = lax.dynamic_slice_in_dim(segment_pad, group_first, group_rows + 2 * margin, 0)
    real_key = lax.dynamic_slice_in_dim(real_pad, group_first, group_rows + 2 * margin, 0)
    place_query = jnp.arange(group_rows, dtype=jnp.int32)
    place_key = jnp.arange(group_rows + 2 * margin, dtype=jnp.int32) - margin
    allowed = (segment_query[:, None] == segment_key[None, :]) & (
        (real_key[None, :] == 1) | (place_query[:, None] == place_key[None, :])
    )
    own_real = lax.dynamic_slice_in_dim(real_token, own_first, tok_rows, 0).astype(jnp.float32)
    stream = tokens.astype(jnp.float32)
    layer_index = 0
    qkv_local = jnp.moveaxis(qkv_weight[layer_index], 1, 0)
    out_local, up_local, down_local = (
        out_weight[layer_index],
        up_weight[layer_index],
        down_weight[layer_index],
    )
    gain_now = norm_gain[layer_index].astype(jnp.float32)
    shift_now = row_bias[layer_index].astype(jnp.float32)
    bias_now = unit_bias[layer_index].astype(jnp.float32)
    normed_full = gather_forward(layer_norm(stream, gain_now[0], shift_now[0]).astype(jnp.bfloat16))
    normed_full, qkv_local = lax.optimization_barrier((normed_full, qkv_local))
    qkv_full = jnp.moveaxis(collect(qkv_local, "dp", 0), 0, 1)
    projected = jnp.einsum("gd,sde->sge", normed_full, qkv_full, preferred_element_type=jnp.float32)
    queries = (projected[0] + bias_now[0]).astype(jnp.bfloat16)
    queries, out_local, up_local, down_local = lax.optimization_barrier(
        (queries, out_local, up_local, down_local)
    )
    out_full = collect(out_local, "dp", 0)
    up_full = collect(up_local, "dp", 0)
    down_full = collect(down_local, "dp", 0)
    gathered = (qkv_full, out_full, up_full, down_full)
    key_value = jnp.stack([projected[1], projected[2] + bias_now[1]]).astype(jnp.bfloat16)
    key_ext = with_halo(key_value, (("dp", 1),), margin)
    attended, log_norm = attend_forward(queries, key_ext, allowed)
    attended = attended.astype(jnp.bfloat16)

    def attention_term(first_row, row_count):
        return lax.dot_general(
            attended, out_full, (((1,), (1,)), ((), ())), preferred_element_type=jnp.float32
        )

    middle = stream + sum_forward(attention_term, tok_rows) + shift_now[1]
    second_full = gather_forward(layer_norm(middle, gain_now[1], shift_now[2]).astype(jnp.bfloat16))
    hidden = (
        jnp.einsum("gd,dre->gre", second_full, up_full, preferred_element_type=jnp.float32)
        + bias_now[2:][None]
    )
    active = exact_gelu(hidden).astype(jnp.bfloat16)

    def feed_term(first_row, row_count):
        return jnp.einsum("gre,ore->go", active, down_full, preferred_element_type=jnp.float32)

    kept_weights = gathered
    records = [
        (
            stream,
            middle,
            normed_full,
            second_full,
            queries,
            key_ext,
            log_norm,
            attended,
            hidden,
            active,
            kept_weights,
        )
    ]
    stream = middle + sum_forward(feed_term, tok_rows) + shift_now[3]
    gradient = cotangent.astype(jnp.float32) * own_real[:, None]
    local_qkv = [None] * LAYERS
    local_out = [None] * LAYERS
    local_up = [None] * LAYERS
    local_down = [None] * LAYERS
    unit_grads = [None] * LAYERS
    gain_grads = [None] * LAYERS
    shift_grads = [None] * LAYERS
    for layer_index in reversed(range(LAYERS)):
        (
            stream_in,
            middle,
            normed_full,
            second_full,
            queries,
            key_ext,
            log_norm,
            attended,
            hidden,
            active,
            kept_weights,
        ) = records[layer_index]
        qkv_full, out_full, up_full, down_full = kept_weights
        gain_now = norm_gain[layer_index].astype(jnp.float32)
        shift_now = row_bias[layer_index].astype(jnp.float32)
        shift_three = jnp.sum(gradient, axis=0)
        grad_mlp = gather_backward(gradient.astype(jnp.bfloat16))
        down_grad = scatter_rows(
            jnp.einsum("go,gre->ore", grad_mlp, active, preferred_element_type=jnp.float32)
        )
        grad_active = jnp.einsum(
            "go,ore->gre", grad_mlp, down_full, preferred_element_type=jnp.float32
        )
        gelu_again, gelu_pull = jax.vjp(exact_gelu, hidden)
        grad_hidden = gelu_pull(grad_active)[0].astype(jnp.bfloat16)
        up_bias_grad = jnp.sum(grad_hidden.astype(jnp.float32), axis=0)
        up_grad = scatter_rows(
            jnp.einsum("gd,gre->dre", second_full, grad_hidden, preferred_element_type=jnp.float32)
        )

        def second_term(first_row, row_count):
            return jnp.einsum(
                "gre,dre->gd", grad_hidden, up_full, preferred_element_type=jnp.float32
            )

        grad_second = sum_backward(second_term, tok_rows)
        second_again, second_pull = jax.vjp(layer_norm, middle, gain_now[1], shift_now[2])
        grad_mid_norm, gain_one, shift_two = second_pull(grad_second)
        grad_middle = gradient + grad_mid_norm
        shift_one = jnp.sum(grad_middle, axis=0)
        grad_proj = gather_backward(grad_middle.astype(jnp.bfloat16))
        out_grad = scatter_rows(
            lax.dot_general(
                grad_proj, attended, (((0,), (0,)), ((), ())), preferred_element_type=jnp.float32
            )
        )
        grad_attended = jnp.dot(grad_proj, out_full, preferred_element_type=jnp.float32).astype(
            jnp.bfloat16
        )
        grad_query, grad_key_ext, grad_value_ext = attend_backward(
            queries, key_ext, allowed, log_norm, grad_attended
        )
        grad_pair_ext = jnp.stack([grad_key_ext, grad_value_ext])
        from_next = from_behind(grad_pair_ext[:, :margin].astype(jnp.bfloat16), "dp", -1).astype(
            jnp.float32
        )
        from_prev = from_behind(
            grad_pair_ext[:, margin + group_rows :].astype(jnp.bfloat16), "dp", 1
        ).astype(jnp.float32)
        grad_pair = grad_pair_ext[:, margin : margin + group_rows]
        grad_pair = (
            grad_pair.at[:, group_rows - margin :].add(from_next).at[:, :margin].add(from_prev)
        )
        grad_triple = jnp.concatenate(
            [grad_query.astype(jnp.bfloat16)[None], grad_pair.astype(jnp.bfloat16)], axis=0
        )
        qkv_grad = jnp.moveaxis(
            scatter_rows(
                jnp.einsum(
                    "gd,sge->dse", normed_full, grad_triple, preferred_element_type=jnp.float32
                )
            ),
            0,
            1,
        )
        triple_sums = jnp.sum(grad_triple.astype(jnp.float32), axis=1)

        def first_term(first_row, row_count):
            return jnp.einsum(
                "sge,sde->gd", grad_triple, qkv_full, preferred_element_type=jnp.float32
            )

        grad_first = sum_backward(first_term, tok_rows)
        first_again, first_pull = jax.vjp(layer_norm, stream_in, gain_now[0], shift_now[0])
        grad_in_norm, gain_zero, shift_zero = first_pull(grad_first)
        gradient = grad_middle + grad_in_norm
        unit_grads[layer_index] = jnp.concatenate(
            [triple_sums[0][None], triple_sums[2][None], up_bias_grad], axis=0
        )
        gain_grads[layer_index] = jnp.stack([gain_zero, gain_one])
        shift_grads[layer_index] = jnp.stack([shift_zero, shift_one, shift_two, shift_three])
        local_qkv[layer_index] = qkv_grad
        local_out[layer_index] = out_grad
        local_up[layer_index] = up_grad
        local_down[layer_index] = down_grad
    grad_qkv = jnp.stack(local_qkv).astype(jnp.float32)
    grad_out = jnp.stack(local_out).astype(jnp.float32)
    grad_up = jnp.stack(local_up).astype(jnp.float32)
    grad_down = jnp.stack(local_down).astype(jnp.float32)
    unit_local = jnp.stack(unit_grads)
    unit_wide = jnp.zeros((LAYERS, unit_local.shape[1], cols_here * tensor_size), jnp.float32)
    unit_wide = lax.dynamic_update_slice_in_dim(unit_wide, unit_local, tensor_index * cols_here, 2)
    small = jnp.concatenate(
        [jnp.stack(gain_grads), jnp.stack(shift_grads), unit_wide], axis=1
    )
    small_total = jnp.sum(from_everyone(small, "dp"), axis=0)
    small_total = jnp.sum(from_everyone(small_total, "tensor"), axis=0)
    gain_total = small_total[:, :2]
    shift_total = small_total[:, 2:6]
    unit_total = small_total[:, 6:]
    unit_mine = lax.dynamic_slice_in_dim(unit_total, tensor_index * cols_here, cols_here, 2)
    return (
        stream.astype(jnp.bfloat16),
        gradient.astype(jnp.bfloat16),
        grad_qkv,
        grad_out,
        grad_up,
        grad_down,
        unit_mine,
        gain_total,
        shift_total,
    )


def solution(mesh):
    placed = (
        P(("dp", "tensor"), None),
        P(),
        P(),
        P(None, None, "dp", "tensor"),
        P(None, "dp", "tensor"),
        P(None, "dp", None, "tensor"),
        P(None, "dp", None, "tensor"),
        P(None, None, "tensor"),
        P(),
        P(),
        P(("dp", "tensor"), None),
    )
    return jax.shard_map(
        local,
        mesh=mesh,
        in_specs=placed,
        out_specs=(
            P(("dp", "tensor"), None),
            P(("dp", "tensor"), None),
            P(None, None, "dp", "tensor"),
            P(None, "dp", "tensor"),
            P(None, "dp", None, "tensor"),
            P(None, "dp", None, "tensor"),
            P(None, None, "tensor"),
            P(),
            P(),
        ),
        check_vma=False,
    )
```

```python
import functools
import math

import jax
import jax.numpy as jnp
from jax import lax
from jax.experimental import pallas as pl
from jax.experimental.pallas import tpu as pltpu
from jax.sharding import PartitionSpec as P

MESH = pl.DeviceIdType.MESH

LAYERS = 1
IMG = 577
HD = 64


norm_eps = 1e-06
masked_score = -1e30


def from_everyone(value, axis):
    devices = lax.axis_size(axis)
    return lax.all_to_all(
        jnp.broadcast_to(value[None], (devices, *value.shape)), axis, 0, 0, tiled=True
    )


def joined_along(parts, dim):
    dims = list(parts.shape[1:])
    dims[dim] *= parts.shape[0]
    return jnp.moveaxis(parts, 0, dim).reshape(dims)


def collect(value, axis, dim):
    parts = from_everyone(value, axis)
    return joined_along(parts, dim)


def split_up(value, dim, devices):
    dims = value.shape
    parts = value.reshape(*dims[:dim], devices, dims[dim] // devices, *dims[dim + 1 :])
    return jnp.moveaxis(parts, dim, 0)


def summed_on_arrival(value, axis, dim):
    devices = lax.axis_size(axis)
    parts = lax.all_to_all(split_up(value, dim, devices), axis, 0, 0, tiled=True)
    return jnp.sum(parts.astype(jnp.float32), axis=0)


def rows_first(arrays, axis, dims):
    turned = [jnp.moveaxis(a, dim, 0) for a, dim in zip(arrays, dims)]
    both = jnp.concatenate([t.reshape(len(t), -1) for t in turned], axis=1)
    filled, at, outs = (lax.all_gather(both, axis, axis=0, tiled=True), 0, [])
    for t, dim in zip(turned, dims):
        slab = filled[:, at : at + t[0].size].reshape(-1, *t.shape[1:])
        outs.append(jnp.moveaxis(slab, 0, dim))
        at += t[0].size
    return tuple(outs)


def with_halo(value, sides, width):
    for axis, dim in sides:
        devices, length = (lax.axis_size(axis), value.shape[dim])
        up = [(i, (i + 1) % devices) for i in range(devices - 1)]
        down = [(j, i) for i, j in up]
        last = lax.slice_in_dim(value, length - width, length, axis=dim)
        initial = lax.slice_in_dim(value, 0, width, axis=dim)
        before = lax.ppermute(last, axis, up)
        after = lax.ppermute(initial, axis, down)
        value = jnp.concatenate([before, value, after], axis=dim)
    return value


def from_behind(block, axis, distance):
    devices = range(lax.axis_size(axis))
    route = [(i - distance, i) for i in devices if i - distance in devices]
    return lax.ppermute(block, axis, route)


def side_by_side(arrays, axis, dim, along):
    widths = [math.prod(a.shape[along:]) for a in arrays]
    both = jnp.concatenate(
        [a.reshape(*a.shape[:along], w) for a, w in zip(arrays, widths)], axis=along
    )
    filled = lax.psum_scatter(both, axis, scatter_dimension=dim, tiled=True)
    parts = jnp.split(filled, [sum(widths[:k]) for k in range(1, len(widths))], axis=along)
    return tuple(
        (b.reshape(*filled.shape[:along], *a.shape[along:]) for a, b in zip(arrays, parts))
    )


def scatter_rows(grad):
    return summed_on_arrival(grad.astype(jnp.bfloat16), "dp", 0)


def layer_norm(values, gain_row, shift_row):
    center = values - jnp.mean(values, axis=-1, keepdims=True)
    spread = jnp.mean(center * center, axis=-1, keepdims=True)
    return center * lax.rsqrt(spread + norm_eps) * gain_row + shift_row


def exact_gelu(values):
    return jax.nn.gelu(values, approximate=False)


def _gather_kernel(devices, x_ref, out_ref, send_sem, recv_sem):
    me = lax.axis_index("tensor")
    dp = lax.axis_index("dp")
    sib = me + 1 - 2 * lax.rem(me, 2)
    far = lax.rem(me + 2, devices)
    barrier = pltpu.get_barrier_semaphore()
    for peer in (sib, far):
        pl.semaphore_signal(barrier, inc=1, device_id=(dp, peer), device_id_type=MESH)
    pl.semaphore_wait(barrier, 2)
    near_copy = pltpu.make_async_remote_copy(
        src_ref=x_ref,
        dst_ref=out_ref.at[me],
        send_sem=send_sem.at[0],
        recv_sem=recv_sem.at[0],
        device_id=(dp, sib),
        device_id_type=MESH,
    )
    far_copy = pltpu.make_async_remote_copy(
        src_ref=x_ref,
        dst_ref=out_ref.at[me],
        send_sem=send_sem.at[1],
        recv_sem=recv_sem.at[1],
        device_id=(dp, far),
        device_id_type=MESH,
    )
    far_copy.start()
    near_copy.start()
    out_ref[me] = x_ref[...]
    far_copy.wait_recv()
    relay = pltpu.make_async_remote_copy(
        src_ref=out_ref.at[far],
        dst_ref=out_ref.at[far],
        send_sem=send_sem.at[2],
        recv_sem=recv_sem.at[2],
        device_id=(dp, sib),
        device_id_type=MESH,
    )
    relay.start()
    near_copy.wait_send()
    near_copy.wait_recv()
    far_copy.wait_send()
    relay.wait_send()
    relay.wait_recv()


def gather_rows(values):
    devices = lax.axis_size("tensor")
    if devices != 4:
        return collect(values, "tensor", 0)
    rows, width = values.shape
    parts = pl.pallas_call(
        functools.partial(_gather_kernel, devices),
        out_shape=jax.ShapeDtypeStruct((devices, rows, width), values.dtype),
        in_specs=[pl.BlockSpec(memory_space=pltpu.VMEM)],
        out_specs=pl.BlockSpec(memory_space=pltpu.VMEM),
        scratch_shapes=[
            pltpu.SemaphoreType.DMA((3,)),
            pltpu.SemaphoreType.DMA((3,)),
        ],
        compiler_params=pltpu.CompilerParams(collective_id=0, has_side_effects=True),
    )(values)
    return parts.reshape(devices * rows, width)


def _exchange_kernel(devices, x_ref, out_ref, send_sem, recv_sem):
    me = lax.axis_index("tensor")
    dp = lax.axis_index("dp")
    barrier = pltpu.get_barrier_semaphore()
    for step in range(1, devices):
        pl.semaphore_signal(
            barrier, inc=1, device_id=(dp, lax.rem(me + step, devices)), device_id_type=MESH
        )
    pl.semaphore_wait(barrier, devices - 1)
    copies = []
    for step in range(1, devices):
        peer = lax.rem(me + step, devices)
        copy = pltpu.make_async_remote_copy(
            src_ref=x_ref.at[peer],
            dst_ref=out_ref.at[me],
            send_sem=send_sem.at[step - 1],
            recv_sem=recv_sem.at[step - 1],
            device_id=(dp, peer),
            device_id_type=MESH,
        )
        copy.start()
        copies.append(copy)
    out_ref[me] = x_ref[me]
    for copy in copies:
        copy.wait()


def exchange_rows(parts):
    devices = parts.shape[0]
    return pl.pallas_call(
        functools.partial(_exchange_kernel, devices),
        out_shape=jax.ShapeDtypeStruct(parts.shape, parts.dtype),
        in_specs=[pl.BlockSpec(memory_space=pltpu.VMEM)],
        out_specs=pl.BlockSpec(memory_space=pltpu.VMEM),
        scratch_shapes=[
            pltpu.SemaphoreType.DMA((devices - 1,)),
            pltpu.SemaphoreType.DMA((devices - 1,)),
        ],
        compiler_params=pltpu.CompilerParams(collective_id=1, has_side_effects=True),
    )(parts)


def _reduce_kernel(devices, x_ref, out_ref, held, mate, pre, send_sem, recv_sem):
    me = lax.axis_index("tensor")
    dp = lax.axis_index("dp")
    sib = me + 1 - 2 * lax.rem(me, 2)
    far = lax.rem(me + 2, devices)
    other = lax.rem(sib + 2, devices)
    barrier = pltpu.get_barrier_semaphore()
    for peer in (sib, far):
        pl.semaphore_signal(barrier, inc=1, device_id=(dp, peer), device_id_type=MESH)
    pl.semaphore_wait(barrier, 2)
    own_copy = pltpu.make_async_remote_copy(
        src_ref=x_ref.at[sib],
        dst_ref=held.at[0],
        send_sem=send_sem.at[0],
        recv_sem=recv_sem.at[0],
        device_id=(dp, sib),
        device_id_type=MESH,
    )
    mate_copy = pltpu.make_async_remote_copy(
        src_ref=x_ref.at[other],
        dst_ref=mate,
        send_sem=send_sem.at[1],
        recv_sem=recv_sem.at[1],
        device_id=(dp, sib),
        device_id_type=MESH,
    )
    mate_copy.start()
    own_copy.start()
    mate_copy.wait_recv()
    pre[...] = (x_ref[far].astype(jnp.float32) + mate[...].astype(jnp.float32)).astype(pre.dtype)
    own_copy.wait_recv()
    out_ref[...] = x_ref[me].astype(jnp.float32) + held[0].astype(jnp.float32)
    far_copy = pltpu.make_async_remote_copy(
        src_ref=pre,
        dst_ref=held.at[1],
        send_sem=send_sem.at[2],
        recv_sem=recv_sem.at[2],
        device_id=(dp, far),
        device_id_type=MESH,
    )
    far_copy.start()
    far_copy.wait_recv()
    out_ref[...] += held[1].astype(jnp.float32)
    own_copy.wait_send()
    mate_copy.wait_send()
    far_copy.wait_send()


def summed_over_tensor(value):
    devices = lax.axis_size("tensor")
    parts = split_up(value, 0, devices)
    if devices != 4:
        return jnp.sum(exchange_rows(parts).astype(jnp.float32), axis=0)
    rows, width = parts.shape[1:]
    return pl.pallas_call(
        functools.partial(_reduce_kernel, devices),
        out_shape=jax.ShapeDtypeStruct((rows, width), jnp.float32),
        in_specs=[pl.BlockSpec(memory_space=pltpu.VMEM)],
        out_specs=pl.BlockSpec(memory_space=pltpu.VMEM),
        scratch_shapes=[
            pltpu.VMEM((2, rows, width), parts.dtype),
            pltpu.VMEM((rows, width), parts.dtype),
            pltpu.VMEM((rows, width), parts.dtype),
            pltpu.SemaphoreType.DMA((3,)),
            pltpu.SemaphoreType.DMA((3,)),
        ],
        compiler_params=pltpu.CompilerParams(collective_id=1, has_side_effects=True),
    )(parts)


def gather_forward(values):
    return gather_rows(values)


def gather_backward(values):
    return gather_rows(values)


def sum_forward(product, tok_rows):
    return summed_over_tensor(
        product(jnp.int32(0), tok_rows * lax.axis_size("tensor")).astype(jnp.bfloat16)
    )


def sum_backward(product, tok_rows):
    return summed_over_tensor(
        product(jnp.int32(0), tok_rows * lax.axis_size("tensor")).astype(jnp.bfloat16)
    )


def head_scores(query_head, key_head, allowed):
    raw = lax.dot_general(
        query_head, key_head, (((1,), (1,)), ((), ())), preferred_element_type=jnp.float32
    )
    return jnp.where(allowed, raw * HD ** (-0.5), masked_score)


def split_heads(queries, key_ext):
    heads_here = queries.shape[1] // HD
    query_heads = queries.reshape(queries.shape[0], heads_here, HD)
    key_heads = key_ext[0].reshape(key_ext.shape[1], heads_here, HD)
    value_heads = key_ext[1].reshape(key_ext.shape[1], heads_here, HD)
    return (heads_here, query_heads, key_heads, value_heads)


def merge_heads(per_head):
    return jnp.transpose(per_head, (1, 0, 2)).reshape(
        per_head.shape[1], per_head.shape[0] * per_head.shape[2]
    )


def _attend_kernel(q_ref, k_ref, v_ref, mask_ref, o_ref, lse_ref):
    scores = lax.dot_general(
        q_ref[...], k_ref[...], (((1,), (1,)), ((), ())), preferred_element_type=jnp.float32
    )
    scores = jnp.where(mask_ref[...] != 0, scores * HD ** (-0.5), masked_score)
    row_top = jnp.max(scores, axis=1, keepdims=True)
    exponent = jnp.exp(scores - row_top)
    row_total = jnp.sum(exponent, axis=1, keepdims=True)
    prob_low = (exponent / row_total).astype(jnp.bfloat16)
    o_ref[...] = jnp.dot(prob_low, v_ref[...], preferred_element_type=jnp.float32)
    lse_ref[...] = row_top + jnp.log(row_total)


def attend_forward(queries, key_ext, allowed):
    heads_here = queries.shape[1] // HD
    rows, keys = allowed.shape
    query_heads = jnp.transpose(queries.reshape(rows, heads_here, HD), (1, 0, 2))
    key_heads = jnp.transpose(key_ext[0].reshape(keys, heads_here, HD), (1, 0, 2))
    value_heads = jnp.transpose(key_ext[1].reshape(keys, heads_here, HD), (1, 0, 2))
    head_outs, log_norm = pl.pallas_call(
        _attend_kernel,
        grid=(heads_here,),
        out_shape=(
            jax.ShapeDtypeStruct((heads_here, rows, HD), jnp.float32),
            jax.ShapeDtypeStruct((heads_here, rows, 1), jnp.float32),
        ),
        in_specs=[
            pl.BlockSpec((None, rows, HD), lambda h: (h, 0, 0)),
            pl.BlockSpec((None, keys, HD), lambda h: (h, 0, 0)),
            pl.BlockSpec((None, keys, HD), lambda h: (h, 0, 0)),
            pl.BlockSpec((rows, keys), lambda h: (0, 0)),
        ],
        out_specs=(
            pl.BlockSpec((None, rows, HD), lambda h: (h, 0, 0)),
            pl.BlockSpec((None, rows, 1), lambda h: (h, 0, 0)),
        ),
        compiler_params=pltpu.CompilerParams(vmem_limit_bytes=60 * 1024 * 1024),
    )(query_heads, key_heads, value_heads, allowed.astype(jnp.int32))
    return (merge_heads(head_outs), log_norm[:, :, 0])


def attend_forward_xla(queries, key_ext, allowed):
    heads_here, query_heads, key_heads, value_heads = split_heads(queries, key_ext)

    def one_head(head_index):
        query_head = lax.dynamic_index_in_dim(query_heads, head_index, 1, keepdims=False)
        key_head = lax.dynamic_index_in_dim(key_heads, head_index, 1, keepdims=False)
        value_head = lax.dynamic_index_in_dim(value_heads, head_index, 1, keepdims=False)
        scores = head_scores(query_head, key_head, allowed)
        row_top = jnp.max(scores, axis=1, keepdims=True)
        exponent = jnp.exp(scores - row_top)
        row_total = jnp.sum(exponent, axis=1, keepdims=True)
        prob_low = (exponent / row_total).astype(jnp.bfloat16)
        head_out = jnp.dot(prob_low, value_head, preferred_element_type=jnp.float32)
        return (head_out, (row_top + jnp.log(row_total))[:, 0])

    head_outs, log_norm = lax.map(one_head, jnp.arange(heads_here, dtype=jnp.int32))
    return (merge_heads(head_outs), log_norm)


def _attend_back_kernel(q_ref, k_ref, v_ref, g_ref, lse_ref, mask_ref, dq_ref, dk_ref, dv_ref):
    query_head, key_head, grad_head = q_ref[...], k_ref[...], g_ref[...]
    scores = lax.dot_general(
        query_head, key_head, (((1,), (1,)), ((), ())), preferred_element_type=jnp.float32
    )
    scores = jnp.where(mask_ref[...] != 0, scores * HD ** (-0.5), masked_score)
    prob_full = jnp.exp(scores - lse_ref[...])
    prob_low = prob_full.astype(jnp.bfloat16)
    dv_ref[...] = lax.dot_general(
        prob_low, grad_head, (((0,), (0,)), ((), ())), preferred_element_type=jnp.float32
    )
    grad_prob = lax.dot_general(
        grad_head, v_ref[...], (((1,), (1,)), ((), ())), preferred_element_type=jnp.float32
    )
    grad_score = (
        prob_full * (grad_prob - jnp.sum(prob_full * grad_prob, axis=1, keepdims=True))
    ).astype(jnp.bfloat16)
    dq_ref[...] = jnp.dot(grad_score, key_head, preferred_element_type=jnp.float32) * HD ** (-0.5)
    dk_ref[...] = lax.dot_general(
        grad_score, query_head, (((0,), (0,)), ((), ())), preferred_element_type=jnp.float32
    ) * HD ** (-0.5)


def attend_backward(queries, key_ext, allowed, log_norm, grad_attended):
    heads_here = queries.shape[1] // HD
    rows, keys = allowed.shape

    def by_head(values, count):
        return jnp.transpose(values.reshape(count, heads_here, HD), (1, 0, 2))

    row_spec = pl.BlockSpec((None, rows, HD), lambda h: (h, 0, 0))
    key_spec = pl.BlockSpec((None, keys, HD), lambda h: (h, 0, 0))
    grad_queries, grad_keys, grad_values = pl.pallas_call(
        _attend_back_kernel,
        grid=(heads_here,),
        out_shape=(
            jax.ShapeDtypeStruct((heads_here, rows, HD), jnp.float32),
            jax.ShapeDtypeStruct((heads_here, keys, HD), jnp.float32),
            jax.ShapeDtypeStruct((heads_here, keys, HD), jnp.float32),
        ),
        in_specs=[
            row_spec,
            key_spec,
            key_spec,
            row_spec,
            pl.BlockSpec((None, rows, 1), lambda h: (h, 0, 0)),
            pl.BlockSpec((rows, keys), lambda h: (0, 0)),
        ],
        out_specs=(row_spec, key_spec, key_spec),
        compiler_params=pltpu.CompilerParams(vmem_limit_bytes=60 * 1024 * 1024),
    )(
        by_head(queries, rows),
        by_head(key_ext[0], keys),
        by_head(key_ext[1], keys),
        by_head(grad_attended, rows),
        log_norm[:, :, None],
        allowed.astype(jnp.int32),
    )
    return (merge_heads(grad_queries), merge_heads(grad_keys), merge_heads(grad_values))


def attend_backward_xla(queries, key_ext, allowed, log_norm, grad_attended):
    heads_here, query_heads, key_heads, value_heads = split_heads(queries, key_ext)
    grad_heads = grad_attended.reshape(grad_attended.shape[0], heads_here, HD)

    def one_head(inputs):
        head_index, norm_row = inputs
        query_head = lax.dynamic_index_in_dim(query_heads, head_index, 1, keepdims=False)
        key_head = lax.dynamic_index_in_dim(key_heads, head_index, 1, keepdims=False)
        value_head = lax.dynamic_index_in_dim(value_heads, head_index, 1, keepdims=False)
        grad_head = lax.dynamic_index_in_dim(grad_heads, head_index, 1, keepdims=False)
        prob_full = jnp.exp(head_scores(query_head, key_head, allowed) - norm_row[:, None])
        prob_low = prob_full.astype(jnp.bfloat16)
        grad_value = lax.dot_general(
            prob_low, grad_head, (((0,), (0,)), ((), ())), preferred_element_type=jnp.float32
        )
        grad_prob = lax.dot_general(
            grad_head, value_head, (((1,), (1,)), ((), ())), preferred_element_type=jnp.float32
        )
        grad_score = (
            prob_full * (grad_prob - jnp.sum(prob_full * grad_prob, axis=1, keepdims=True))
        ).astype(jnp.bfloat16)
        grad_query = jnp.dot(grad_score, key_head, preferred_element_type=jnp.float32) * HD ** (
            -0.5
        )
        grad_key = lax.dot_general(
            grad_score, query_head, (((0,), (0,)), ((), ())), preferred_element_type=jnp.float32
        ) * HD ** (-0.5)
        return (grad_query, grad_key, grad_value)

    grad_queries, grad_keys, grad_values = lax.map(
        one_head, (jnp.arange(heads_here, dtype=jnp.int32), log_norm)
    )
    return (merge_heads(grad_queries), merge_heads(grad_keys), merge_heads(grad_values))


def local(
    tokens,
    segment,
    real_token,
    qkv_weight,
    out_weight,
    up_weight,
    down_weight,
    unit_bias,
    norm_gain,
    row_bias,
    cotangent,
):
    tok_rows = tokens.shape[0]
    tensor_size = lax.axis_size("tensor")
    group_rows = tok_rows * tensor_size
    margin = IMG - 1
    cols_here = qkv_weight.shape[3]
    dp_index = lax.axis_index("dp")
    tensor_index = lax.axis_index("tensor")
    group_first = dp_index * group_rows
    own_first = group_first + tensor_index * tok_rows
    segment_pad = jnp.pad(segment, (margin, margin), constant_values=-1)
    real_pad = jnp.pad(real_token, (margin, margin))
    segment_query = lax.dynamic_slice_in_dim(segment, group_first, group_rows, 0)
    segment_key = lax.dynamic_slice_in_dim(segment_pad, group_first, group_rows + 2 * margin, 0)
    real_key = lax.dynamic_slice_in_dim(real_pad, group_first, group_rows + 2 * margin, 0)
    place_query = jnp.arange(group_rows, dtype=jnp.int32)
    place_key = jnp.arange(group_rows + 2 * margin, dtype=jnp.int32) - margin
    allowed = (segment_query[:, None] == segment_key[None, :]) & (
        (real_key[None, :] == 1) | (place_query[:, None] == place_key[None, :])
    )
    own_real = lax.dynamic_slice_in_dim(real_token, own_first, tok_rows, 0).astype(jnp.float32)
    stream = tokens.astype(jnp.float32)
    layer_index = 0
    qkv_local = jnp.moveaxis(qkv_weight[layer_index], 1, 0)
    out_local, up_local, down_local = (
        out_weight[layer_index],
        up_weight[layer_index],
        down_weight[layer_index],
    )
    gain_now = norm_gain[layer_index].astype(jnp.float32)
    shift_now = row_bias[layer_index].astype(jnp.float32)
    bias_now = unit_bias[layer_index].astype(jnp.float32)
    normed_full = gather_forward(layer_norm(stream, gain_now[0], shift_now[0]).astype(jnp.bfloat16))
    normed_full, qkv_local = lax.optimization_barrier((normed_full, qkv_local))
    qkv_full = jnp.moveaxis(collect(qkv_local, "dp", 0), 0, 1)
    projected = jnp.einsum("gd,sde->sge", normed_full, qkv_full, preferred_element_type=jnp.float32)
    queries = (projected[0] + bias_now[0]).astype(jnp.bfloat16)
    queries, out_local, up_local, down_local = lax.optimization_barrier(
        (queries, out_local, up_local, down_local)
    )
    out_full = collect(out_local, "dp", 0)
    up_full = collect(up_local, "dp", 0)
    down_full = collect(down_local, "dp", 0)
    gathered = (qkv_full, out_full, up_full, down_full)
    key_value = jnp.stack([projected[1], projected[2] + bias_now[1]]).astype(jnp.bfloat16)
    key_ext = with_halo(key_value, (("dp", 1),), margin)
    attended, log_norm = attend_forward(queries, key_ext, allowed)
    attended = attended.astype(jnp.bfloat16)

    def attention_term(first_row, row_count):
        return lax.dot_general(
            attended, out_full, (((1,), (1,)), ((), ())), preferred_element_type=jnp.float32
        )

    middle = stream + sum_forward(attention_term, tok_rows) + shift_now[1]
    second_full = gather_forward(layer_norm(middle, gain_now[1], shift_now[2]).astype(jnp.bfloat16))
    hidden = (
        jnp.einsum("gd,dre->gre", second_full, up_full, preferred_element_type=jnp.float32)
        + bias_now[2:][None]
    )
    active = exact_gelu(hidden).astype(jnp.bfloat16)

    def feed_term(first_row, row_count):
        return jnp.einsum("gre,ore->go", active, down_full, preferred_element_type=jnp.float32)

    kept_weights = gathered
    records = [
        (
            stream,
            middle,
            normed_full,
            second_full,
            queries,
            key_ext,
            log_norm,
            attended,
            hidden,
            active,
            kept_weights,
        )
    ]
    stream = middle + sum_forward(feed_term, tok_rows) + shift_now[3]
    gradient = cotangent.astype(jnp.float32) * own_real[:, None]
    local_qkv = [None] * LAYERS
    local_out = [None] * LAYERS
    local_up = [None] * LAYERS
    local_down = [None] * LAYERS
    unit_grads = [None] * LAYERS
    gain_grads = [None] * LAYERS
    shift_grads = [None] * LAYERS
    for layer_index in reversed(range(LAYERS)):
        (
            stream_in,
            middle,
            normed_full,
            second_full,
            queries,
            key_ext,
            log_norm,
            attended,
            hidden,
            active,
            kept_weights,
        ) = records[layer_index]
        qkv_full, out_full, up_full, down_full = kept_weights
        gain_now = norm_gain[layer_index].astype(jnp.float32)
        shift_now = row_bias[layer_index].astype(jnp.float32)
        shift_three = jnp.sum(gradient, axis=0)
        grad_mlp = gather_backward(gradient.astype(jnp.bfloat16))
        down_grad = scatter_rows(
            jnp.einsum("go,gre->ore", grad_mlp, active, preferred_element_type=jnp.float32)
        )
        grad_active = jnp.einsum(
            "go,ore->gre", grad_mlp, down_full, preferred_element_type=jnp.float32
        )
        gelu_again, gelu_pull = jax.vjp(exact_gelu, hidden)
        grad_hidden = gelu_pull(grad_active)[0].astype(jnp.bfloat16)
        up_bias_grad = jnp.sum(grad_hidden.astype(jnp.float32), axis=0)
        up_grad = scatter_rows(
            jnp.einsum("gd,gre->dre", second_full, grad_hidden, preferred_element_type=jnp.float32)
        )

        def second_term(first_row, row_count):
            return jnp.einsum(
                "gre,dre->gd", grad_hidden, up_full, preferred_element_type=jnp.float32
            )

        grad_second = sum_backward(second_term, tok_rows)
        second_again, second_pull = jax.vjp(layer_norm, middle, gain_now[1], shift_now[2])
        grad_mid_norm, gain_one, shift_two = second_pull(grad_second)
        grad_middle = gradient + grad_mid_norm
        shift_one = jnp.sum(grad_middle, axis=0)
        grad_proj = gather_backward(grad_middle.astype(jnp.bfloat16))
        out_grad = scatter_rows(
            lax.dot_general(
                grad_proj, attended, (((0,), (0,)), ((), ())), preferred_element_type=jnp.float32
            )
        )
        grad_attended = jnp.dot(grad_proj, out_full, preferred_element_type=jnp.float32).astype(
            jnp.bfloat16
        )
        grad_query, grad_key_ext, grad_value_ext = attend_backward(
            queries, key_ext, allowed, log_norm, grad_attended
        )
        grad_pair_ext = jnp.stack([grad_key_ext, grad_value_ext])
        from_next = from_behind(grad_pair_ext[:, :margin].astype(jnp.bfloat16), "dp", -1).astype(
            jnp.float32
        )
        from_prev = from_behind(
            grad_pair_ext[:, margin + group_rows :].astype(jnp.bfloat16), "dp", 1
        ).astype(jnp.float32)
        grad_pair = grad_pair_ext[:, margin : margin + group_rows]
        grad_pair = (
            grad_pair.at[:, group_rows - margin :].add(from_next).at[:, :margin].add(from_prev)
        )
        grad_triple = jnp.concatenate(
            [grad_query.astype(jnp.bfloat16)[None], grad_pair.astype(jnp.bfloat16)], axis=0
        )
        qkv_grad = jnp.moveaxis(
            scatter_rows(
                jnp.einsum(
                    "gd,sge->dse", normed_full, grad_triple, preferred_element_type=jnp.float32
                )
            ),
            0,
            1,
        )
        triple_sums = jnp.sum(grad_triple.astype(jnp.float32), axis=1)

        def first_term(first_row, row_count):
            return jnp.einsum(
                "sge,sde->gd", grad_triple, qkv_full, preferred_element_type=jnp.float32
            )

        grad_first = sum_backward(first_term, tok_rows)
        grad_first, qkv_grad = lax.optimization_barrier((grad_first, qkv_grad))
        first_again, first_pull = jax.vjp(layer_norm, stream_in, gain_now[0], shift_now[0])
        grad_in_norm, gain_zero, shift_zero = first_pull(grad_first)
        gradient = grad_middle + grad_in_norm
        unit_grads[layer_index] = jnp.concatenate(
            [triple_sums[0][None], triple_sums[2][None], up_bias_grad], axis=0
        )
        gain_grads[layer_index] = jnp.stack([gain_zero, gain_one])
        shift_grads[layer_index] = jnp.stack([shift_zero, shift_one, shift_two, shift_three])
        local_qkv[layer_index] = qkv_grad
        local_out[layer_index] = out_grad
        local_up[layer_index] = up_grad
        local_down[layer_index] = down_grad
    grad_qkv = jnp.stack(local_qkv).astype(jnp.float32)
    grad_out = jnp.stack(local_out).astype(jnp.float32)
    grad_up = jnp.stack(local_up).astype(jnp.float32)
    grad_down = jnp.stack(local_down).astype(jnp.float32)
    unit_local = jnp.stack(unit_grads)
    norm_local = jnp.concatenate([jnp.stack(gain_grads), jnp.stack(shift_grads)], axis=1)
    norm_group = jnp.sum(from_everyone(norm_local, "tensor"), axis=0)
    flat = jnp.concatenate([norm_group.reshape(-1), unit_local.reshape(-1)])
    total = jnp.sum(from_everyone(flat, "dp"), axis=0)
    norm_size = norm_group.size
    norm_total = total[:norm_size].reshape(norm_group.shape)
    gain_total = norm_total[:, :2]
    shift_total = norm_total[:, 2:6]
    unit_mine = total[norm_size:].reshape(unit_local.shape)
    return (
        stream.astype(jnp.bfloat16),
        gradient.astype(jnp.bfloat16),
        grad_qkv,
        grad_out,
        grad_up,
        grad_down,
        unit_mine,
        gain_total,
        shift_total,
    )


def solution(mesh):
    placed = (
        P(("dp", "tensor"), None),
        P(),
        P(),
        P(None, None, "dp", "tensor"),
        P(None, "dp", "tensor"),
        P(None, "dp", None, "tensor"),
        P(None, "dp", None, "tensor"),
        P(None, None, "tensor"),
        P(),
        P(),
        P(("dp", "tensor"), None),
    )
    return jax.shard_map(
        local,
        mesh=mesh,
        in_specs=placed,
        out_specs=(
            P(("dp", "tensor"), None),
            P(("dp", "tensor"), None),
            P(None, None, "dp", "tensor"),
            P(None, "dp", "tensor"),
            P(None, "dp", None, "tensor"),
            P(None, "dp", None, "tensor"),
            P(None, None, "tensor"),
            P(),
            P(),
        ),
        check_vma=False,
    )
```

```python
import functools
import math

import jax
import jax.numpy as jnp
from jax import lax
from jax.experimental import pallas as pl
from jax.experimental.pallas import tpu as pltpu
from jax.sharding import PartitionSpec as P

MESH = pl.DeviceIdType.MESH

LAYERS = 1
IMG = 577
HD = 64


norm_eps = 1e-06
masked_score = -1e30


def from_everyone(value, axis):
    devices = lax.axis_size(axis)
    return lax.all_to_all(
        jnp.broadcast_to(value[None], (devices, *value.shape)), axis, 0, 0, tiled=True
    )


def joined_along(parts, dim):
    dims = list(parts.shape[1:])
    dims[dim] *= parts.shape[0]
    return jnp.moveaxis(parts, 0, dim).reshape(dims)


def collect(value, axis, dim):
    parts = from_everyone(value, axis)
    return joined_along(parts, dim)


def split_up(value, dim, devices):
    dims = value.shape
    parts = value.reshape(*dims[:dim], devices, dims[dim] // devices, *dims[dim + 1 :])
    return jnp.moveaxis(parts, dim, 0)


def summed_on_arrival(value, axis, dim):
    devices = lax.axis_size(axis)
    parts = lax.all_to_all(split_up(value, dim, devices), axis, 0, 0, tiled=True)
    return jnp.sum(parts.astype(jnp.float32), axis=0)


def rows_first(arrays, axis, dims):
    turned = [jnp.moveaxis(a, dim, 0) for a, dim in zip(arrays, dims)]
    both = jnp.concatenate([t.reshape(len(t), -1) for t in turned], axis=1)
    filled, at, outs = (lax.all_gather(both, axis, axis=0, tiled=True), 0, [])
    for t, dim in zip(turned, dims):
        slab = filled[:, at : at + t[0].size].reshape(-1, *t.shape[1:])
        outs.append(jnp.moveaxis(slab, 0, dim))
        at += t[0].size
    return tuple(outs)


def with_halo(value, sides, width):
    for axis, dim in sides:
        devices, length = (lax.axis_size(axis), value.shape[dim])
        up = [(i, (i + 1) % devices) for i in range(devices - 1)]
        down = [(j, i) for i, j in up]
        last = lax.slice_in_dim(value, length - width, length, axis=dim)
        initial = lax.slice_in_dim(value, 0, width, axis=dim)
        before = lax.ppermute(last, axis, up)
        after = lax.ppermute(initial, axis, down)
        value = jnp.concatenate([before, value, after], axis=dim)
    return value


def from_behind(block, axis, distance):
    devices = range(lax.axis_size(axis))
    route = [(i - distance, i) for i in devices if i - distance in devices]
    return lax.ppermute(block, axis, route)


def side_by_side(arrays, axis, dim, along):
    widths = [math.prod(a.shape[along:]) for a in arrays]
    both = jnp.concatenate(
        [a.reshape(*a.shape[:along], w) for a, w in zip(arrays, widths)], axis=along
    )
    filled = lax.psum_scatter(both, axis, scatter_dimension=dim, tiled=True)
    parts = jnp.split(filled, [sum(widths[:k]) for k in range(1, len(widths))], axis=along)
    return tuple(
        (b.reshape(*filled.shape[:along], *a.shape[along:]) for a, b in zip(arrays, parts))
    )


def scatter_rows(grad):
    return summed_on_arrival(grad.astype(jnp.bfloat16), "dp", 0)


def layer_norm(values, gain_row, shift_row):
    center = values - jnp.mean(values, axis=-1, keepdims=True)
    spread = jnp.mean(center * center, axis=-1, keepdims=True)
    return center * lax.rsqrt(spread + norm_eps) * gain_row + shift_row


def exact_gelu(values):
    return jax.nn.gelu(values, approximate=False)


def _gather_kernel(devices, x_ref, out_ref, send_sem, recv_sem):
    me = lax.axis_index("tensor")
    dp = lax.axis_index("dp")
    sib = me + 1 - 2 * lax.rem(me, 2)
    far = lax.rem(me + 2, devices)
    barrier = pltpu.get_barrier_semaphore()
    for peer in (sib, far):
        pl.semaphore_signal(barrier, inc=1, device_id=(dp, peer), device_id_type=MESH)
    pl.semaphore_wait(barrier, 2)
    near_copy = pltpu.make_async_remote_copy(
        src_ref=x_ref,
        dst_ref=out_ref.at[me],
        send_sem=send_sem.at[0],
        recv_sem=recv_sem.at[0],
        device_id=(dp, sib),
        device_id_type=MESH,
    )
    far_copy = pltpu.make_async_remote_copy(
        src_ref=x_ref,
        dst_ref=out_ref.at[me],
        send_sem=send_sem.at[1],
        recv_sem=recv_sem.at[1],
        device_id=(dp, far),
        device_id_type=MESH,
    )
    far_copy.start()
    near_copy.start()
    out_ref[me] = x_ref[...]
    far_copy.wait_recv()
    relay = pltpu.make_async_remote_copy(
        src_ref=out_ref.at[far],
        dst_ref=out_ref.at[far],
        send_sem=send_sem.at[2],
        recv_sem=recv_sem.at[2],
        device_id=(dp, sib),
        device_id_type=MESH,
    )
    relay.start()
    near_copy.wait_send()
    near_copy.wait_recv()
    far_copy.wait_send()
    relay.wait_send()
    relay.wait_recv()


def gather_rows(values):
    devices = lax.axis_size("tensor")
    if devices != 4:
        return collect(values, "tensor", 0)
    rows, width = values.shape
    parts = pl.pallas_call(
        functools.partial(_gather_kernel, devices),
        out_shape=jax.ShapeDtypeStruct((devices, rows, width), values.dtype),
        in_specs=[pl.BlockSpec(memory_space=pltpu.VMEM)],
        out_specs=pl.BlockSpec(memory_space=pltpu.VMEM),
        scratch_shapes=[
            pltpu.SemaphoreType.DMA((3,)),
            pltpu.SemaphoreType.DMA((3,)),
        ],
        compiler_params=pltpu.CompilerParams(collective_id=0, has_side_effects=True),
    )(values)
    return parts.reshape(devices * rows, width)


def _exchange_kernel(devices, x_ref, out_ref, send_sem, recv_sem):
    me = lax.axis_index("tensor")
    dp = lax.axis_index("dp")
    barrier = pltpu.get_barrier_semaphore()
    for step in range(1, devices):
        pl.semaphore_signal(
            barrier, inc=1, device_id=(dp, lax.rem(me + step, devices)), device_id_type=MESH
        )
    pl.semaphore_wait(barrier, devices - 1)
    copies = []
    for step in range(1, devices):
        peer = lax.rem(me + step, devices)
        copy = pltpu.make_async_remote_copy(
            src_ref=x_ref.at[peer],
            dst_ref=out_ref.at[me],
            send_sem=send_sem.at[step - 1],
            recv_sem=recv_sem.at[step - 1],
            device_id=(dp, peer),
            device_id_type=MESH,
        )
        copy.start()
        copies.append(copy)
    out_ref[me] = x_ref[me]
    for copy in copies:
        copy.wait()


def exchange_rows(parts):
    devices = parts.shape[0]
    return pl.pallas_call(
        functools.partial(_exchange_kernel, devices),
        out_shape=jax.ShapeDtypeStruct(parts.shape, parts.dtype),
        in_specs=[pl.BlockSpec(memory_space=pltpu.VMEM)],
        out_specs=pl.BlockSpec(memory_space=pltpu.VMEM),
        scratch_shapes=[
            pltpu.SemaphoreType.DMA((devices - 1,)),
            pltpu.SemaphoreType.DMA((devices - 1,)),
        ],
        compiler_params=pltpu.CompilerParams(collective_id=1, has_side_effects=True),
    )(parts)


def _reduce_kernel(devices, x_ref, out_ref, held, mate, pre, send_sem, recv_sem):
    me = lax.axis_index("tensor")
    dp = lax.axis_index("dp")
    sib = me + 1 - 2 * lax.rem(me, 2)
    far = lax.rem(me + 2, devices)
    other = lax.rem(sib + 2, devices)
    barrier = pltpu.get_barrier_semaphore()
    for peer in (sib, far):
        pl.semaphore_signal(barrier, inc=1, device_id=(dp, peer), device_id_type=MESH)
    pl.semaphore_wait(barrier, 2)
    own_copy = pltpu.make_async_remote_copy(
        src_ref=x_ref.at[sib],
        dst_ref=held.at[0],
        send_sem=send_sem.at[0],
        recv_sem=recv_sem.at[0],
        device_id=(dp, sib),
        device_id_type=MESH,
    )
    mate_copy = pltpu.make_async_remote_copy(
        src_ref=x_ref.at[other],
        dst_ref=mate,
        send_sem=send_sem.at[1],
        recv_sem=recv_sem.at[1],
        device_id=(dp, sib),
        device_id_type=MESH,
    )
    mate_copy.start()
    own_copy.start()
    mate_copy.wait_recv()
    pre[...] = (x_ref[far].astype(jnp.float32) + mate[...].astype(jnp.float32)).astype(pre.dtype)
    own_copy.wait_recv()
    out_ref[...] = x_ref[me].astype(jnp.float32) + held[0].astype(jnp.float32)
    far_copy = pltpu.make_async_remote_copy(
        src_ref=pre,
        dst_ref=held.at[1],
        send_sem=send_sem.at[2],
        recv_sem=recv_sem.at[2],
        device_id=(dp, far),
        device_id_type=MESH,
    )
    far_copy.start()
    far_copy.wait_recv()
    out_ref[...] += held[1].astype(jnp.float32)
    own_copy.wait_send()
    mate_copy.wait_send()
    far_copy.wait_send()


def summed_over_tensor(value):
    devices = lax.axis_size("tensor")
    parts = split_up(value, 0, devices)
    if devices != 4:
        return jnp.sum(exchange_rows(parts).astype(jnp.float32), axis=0)
    rows, width = parts.shape[1:]
    return pl.pallas_call(
        functools.partial(_reduce_kernel, devices),
        out_shape=jax.ShapeDtypeStruct((rows, width), jnp.float32),
        in_specs=[pl.BlockSpec(memory_space=pltpu.VMEM)],
        out_specs=pl.BlockSpec(memory_space=pltpu.VMEM),
        scratch_shapes=[
            pltpu.VMEM((2, rows, width), parts.dtype),
            pltpu.VMEM((rows, width), parts.dtype),
            pltpu.VMEM((rows, width), parts.dtype),
            pltpu.SemaphoreType.DMA((3,)),
            pltpu.SemaphoreType.DMA((3,)),
        ],
        compiler_params=pltpu.CompilerParams(collective_id=1, has_side_effects=True),
    )(parts)


def gather_forward(values):
    return gather_rows(values)


def gather_backward(values):
    return gather_rows(values)


def sum_forward(product, tok_rows):
    return summed_over_tensor(
        product(jnp.int32(0), tok_rows * lax.axis_size("tensor")).astype(jnp.bfloat16)
    )


def sum_backward(product, tok_rows):
    return summed_over_tensor(
        product(jnp.int32(0), tok_rows * lax.axis_size("tensor")).astype(jnp.bfloat16)
    )


def head_scores(query_head, key_head, allowed):
    raw = lax.dot_general(
        query_head, key_head, (((1,), (1,)), ((), ())), preferred_element_type=jnp.float32
    )
    return jnp.where(allowed, raw * HD ** (-0.5), masked_score)


def split_heads(queries, key_ext):
    heads_here = queries.shape[1] // HD
    query_heads = queries.reshape(queries.shape[0], heads_here, HD)
    key_heads = key_ext[0].reshape(key_ext.shape[1], heads_here, HD)
    value_heads = key_ext[1].reshape(key_ext.shape[1], heads_here, HD)
    return (heads_here, query_heads, key_heads, value_heads)


def merge_heads(per_head):
    return jnp.transpose(per_head, (1, 0, 2)).reshape(
        per_head.shape[1], per_head.shape[0] * per_head.shape[2]
    )


def _attend_kernel(q_ref, k_ref, v_ref, mask_ref, o_ref, lse_ref):
    scores = lax.dot_general(
        q_ref[...], k_ref[...], (((1,), (1,)), ((), ())), preferred_element_type=jnp.float32
    )
    scores = jnp.where(mask_ref[...] != 0, scores * HD ** (-0.5), masked_score)
    row_top = jnp.max(scores, axis=1, keepdims=True)
    exponent = jnp.exp(scores - row_top)
    row_total = jnp.sum(exponent, axis=1, keepdims=True)
    prob_low = (exponent / row_total).astype(jnp.bfloat16)
    o_ref[...] = jnp.dot(prob_low, v_ref[...], preferred_element_type=jnp.float32)
    lse_ref[...] = row_top + jnp.log(row_total)


def attend_forward(queries, key_ext, allowed):
    heads_here = queries.shape[1] // HD
    rows, keys = allowed.shape
    query_heads = jnp.transpose(queries.reshape(rows, heads_here, HD), (1, 0, 2))
    key_heads = jnp.transpose(key_ext[0].reshape(keys, heads_here, HD), (1, 0, 2))
    value_heads = jnp.transpose(key_ext[1].reshape(keys, heads_here, HD), (1, 0, 2))
    head_outs, log_norm = pl.pallas_call(
        _attend_kernel,
        grid=(heads_here,),
        out_shape=(
            jax.ShapeDtypeStruct((heads_here, rows, HD), jnp.float32),
            jax.ShapeDtypeStruct((heads_here, rows, 1), jnp.float32),
        ),
        in_specs=[
            pl.BlockSpec((None, rows, HD), lambda h: (h, 0, 0)),
            pl.BlockSpec((None, keys, HD), lambda h: (h, 0, 0)),
            pl.BlockSpec((None, keys, HD), lambda h: (h, 0, 0)),
            pl.BlockSpec((rows, keys), lambda h: (0, 0)),
        ],
        out_specs=(
            pl.BlockSpec((None, rows, HD), lambda h: (h, 0, 0)),
            pl.BlockSpec((None, rows, 1), lambda h: (h, 0, 0)),
        ),
        compiler_params=pltpu.CompilerParams(vmem_limit_bytes=60 * 1024 * 1024),
    )(query_heads, key_heads, value_heads, allowed.astype(jnp.int32))
    return (merge_heads(head_outs), log_norm[:, :, 0])


def attend_forward_xla(queries, key_ext, allowed):
    heads_here, query_heads, key_heads, value_heads = split_heads(queries, key_ext)

    def one_head(head_index):
        query_head = lax.dynamic_index_in_dim(query_heads, head_index, 1, keepdims=False)
        key_head = lax.dynamic_index_in_dim(key_heads, head_index, 1, keepdims=False)
        value_head = lax.dynamic_index_in_dim(value_heads, head_index, 1, keepdims=False)
        scores = head_scores(query_head, key_head, allowed)
        row_top = jnp.max(scores, axis=1, keepdims=True)
        exponent = jnp.exp(scores - row_top)
        row_total = jnp.sum(exponent, axis=1, keepdims=True)
        prob_low = (exponent / row_total).astype(jnp.bfloat16)
        head_out = jnp.dot(prob_low, value_head, preferred_element_type=jnp.float32)
        return (head_out, (row_top + jnp.log(row_total))[:, 0])

    head_outs, log_norm = lax.map(one_head, jnp.arange(heads_here, dtype=jnp.int32))
    return (merge_heads(head_outs), log_norm)


def _attend_back_kernel(q_ref, k_ref, v_ref, g_ref, lse_ref, mask_ref, dq_ref, dk_ref, dv_ref):
    query_head, key_head, grad_head = q_ref[...], k_ref[...], g_ref[...]
    scores = lax.dot_general(
        query_head, key_head, (((1,), (1,)), ((), ())), preferred_element_type=jnp.float32
    )
    scores = jnp.where(mask_ref[...] != 0, scores * HD ** (-0.5), masked_score)
    prob_full = jnp.exp(scores - lse_ref[...])
    prob_low = prob_full.astype(jnp.bfloat16)
    dv_ref[...] = lax.dot_general(
        prob_low, grad_head, (((0,), (0,)), ((), ())), preferred_element_type=jnp.float32
    )
    grad_prob = lax.dot_general(
        grad_head, v_ref[...], (((1,), (1,)), ((), ())), preferred_element_type=jnp.float32
    )
    grad_score = (
        prob_full * (grad_prob - jnp.sum(prob_full * grad_prob, axis=1, keepdims=True))
    ).astype(jnp.bfloat16)
    dq_ref[...] = jnp.dot(grad_score, key_head, preferred_element_type=jnp.float32) * HD ** (-0.5)
    dk_ref[...] = lax.dot_general(
        grad_score, query_head, (((0,), (0,)), ((), ())), preferred_element_type=jnp.float32
    ) * HD ** (-0.5)


def attend_backward(queries, key_ext, allowed, log_norm, grad_attended):
    heads_here = queries.shape[1] // HD
    rows, keys = allowed.shape

    def by_head(values, count):
        return jnp.transpose(values.reshape(count, heads_here, HD), (1, 0, 2))

    row_spec = pl.BlockSpec((None, rows, HD), lambda h: (h, 0, 0))
    key_spec = pl.BlockSpec((None, keys, HD), lambda h: (h, 0, 0))
    grad_queries, grad_keys, grad_values = pl.pallas_call(
        _attend_back_kernel,
        grid=(heads_here,),
        out_shape=(
            jax.ShapeDtypeStruct((heads_here, rows, HD), jnp.float32),
            jax.ShapeDtypeStruct((heads_here, keys, HD), jnp.float32),
            jax.ShapeDtypeStruct((heads_here, keys, HD), jnp.float32),
        ),
        in_specs=[
            row_spec,
            key_spec,
            key_spec,
            row_spec,
            pl.BlockSpec((None, rows, 1), lambda h: (h, 0, 0)),
            pl.BlockSpec((rows, keys), lambda h: (0, 0)),
        ],
        out_specs=(row_spec, key_spec, key_spec),
        compiler_params=pltpu.CompilerParams(vmem_limit_bytes=60 * 1024 * 1024),
    )(
        by_head(queries, rows),
        by_head(key_ext[0], keys),
        by_head(key_ext[1], keys),
        by_head(grad_attended, rows),
        log_norm[:, :, None],
        allowed.astype(jnp.int32),
    )
    return (merge_heads(grad_queries), merge_heads(grad_keys), merge_heads(grad_values))


def attend_backward_xla(queries, key_ext, allowed, log_norm, grad_attended):
    heads_here, query_heads, key_heads, value_heads = split_heads(queries, key_ext)
    grad_heads = grad_attended.reshape(grad_attended.shape[0], heads_here, HD)

    def one_head(inputs):
        head_index, norm_row = inputs
        query_head = lax.dynamic_index_in_dim(query_heads, head_index, 1, keepdims=False)
        key_head = lax.dynamic_index_in_dim(key_heads, head_index, 1, keepdims=False)
        value_head = lax.dynamic_index_in_dim(value_heads, head_index, 1, keepdims=False)
        grad_head = lax.dynamic_index_in_dim(grad_heads, head_index, 1, keepdims=False)
        prob_full = jnp.exp(head_scores(query_head, key_head, allowed) - norm_row[:, None])
        prob_low = prob_full.astype(jnp.bfloat16)
        grad_value = lax.dot_general(
            prob_low, grad_head, (((0,), (0,)), ((), ())), preferred_element_type=jnp.float32
        )
        grad_prob = lax.dot_general(
            grad_head, value_head, (((1,), (1,)), ((), ())), preferred_element_type=jnp.float32
        )
        grad_score = (
            prob_full * (grad_prob - jnp.sum(prob_full * grad_prob, axis=1, keepdims=True))
        ).astype(jnp.bfloat16)
        grad_query = jnp.dot(grad_score, key_head, preferred_element_type=jnp.float32) * HD ** (
            -0.5
        )
        grad_key = lax.dot_general(
            grad_score, query_head, (((0,), (0,)), ((), ())), preferred_element_type=jnp.float32
        ) * HD ** (-0.5)
        return (grad_query, grad_key, grad_value)

    grad_queries, grad_keys, grad_values = lax.map(
        one_head, (jnp.arange(heads_here, dtype=jnp.int32), log_norm)
    )
    return (merge_heads(grad_queries), merge_heads(grad_keys), merge_heads(grad_values))


def local(
    tokens,
    segment,
    real_token,
    qkv_weight,
    out_weight,
    up_weight,
    down_weight,
    unit_bias,
    norm_gain,
    row_bias,
    cotangent,
):
    tok_rows = tokens.shape[0]
    tensor_size = lax.axis_size("tensor")
    group_rows = tok_rows * tensor_size
    margin = IMG - 1
    cols_here = qkv_weight.shape[3]
    dp_index = lax.axis_index("dp")
    tensor_index = lax.axis_index("tensor")
    group_first = dp_index * group_rows
    own_first = group_first + tensor_index * tok_rows
    segment_pad = jnp.pad(segment, (margin, margin), constant_values=-1)
    real_pad = jnp.pad(real_token, (margin, margin))
    segment_query = lax.dynamic_slice_in_dim(segment, group_first, group_rows, 0)
    segment_key = lax.dynamic_slice_in_dim(segment_pad, group_first, group_rows + 2 * margin, 0)
    real_key = lax.dynamic_slice_in_dim(real_pad, group_first, group_rows + 2 * margin, 0)
    place_query = jnp.arange(group_rows, dtype=jnp.int32)
    place_key = jnp.arange(group_rows + 2 * margin, dtype=jnp.int32) - margin
    allowed = (segment_query[:, None] == segment_key[None, :]) & (
        (real_key[None, :] == 1) | (place_query[:, None] == place_key[None, :])
    )
    own_real = lax.dynamic_slice_in_dim(real_token, own_first, tok_rows, 0).astype(jnp.float32)
    stream = tokens.astype(jnp.float32)
    layer_index = 0
    qkv_local = jnp.moveaxis(qkv_weight[layer_index], 1, 0)
    out_local, up_local, down_local = (
        out_weight[layer_index],
        up_weight[layer_index],
        down_weight[layer_index],
    )
    gain_now = norm_gain[layer_index].astype(jnp.float32)
    shift_now = row_bias[layer_index].astype(jnp.float32)
    bias_now = unit_bias[layer_index].astype(jnp.float32)
    normed_full = gather_forward(layer_norm(stream, gain_now[0], shift_now[0]).astype(jnp.bfloat16))
    normed_full, qkv_local = lax.optimization_barrier((normed_full, qkv_local))
    qkv_full = jnp.moveaxis(collect(qkv_local, "dp", 0), 0, 1)
    projected = jnp.einsum("gd,sde->sge", normed_full, qkv_full, preferred_element_type=jnp.float32)
    queries = (projected[0] + bias_now[0]).astype(jnp.bfloat16)
    queries, out_local, up_local, down_local = lax.optimization_barrier(
        (queries, out_local, up_local, down_local)
    )
    out_full = collect(out_local, "dp", 0)
    ff_width = up_local.shape[1] * up_local.shape[2]
    ff_rows = collect(
        jnp.concatenate(
            [up_local.reshape(-1, ff_width), down_local.reshape(-1, ff_width)], axis=1
        ),
        "dp",
        0,
    )
    up_full = ff_rows[:, :ff_width].reshape(-1, *up_local.shape[1:])
    down_full = ff_rows[:, ff_width:].reshape(-1, *down_local.shape[1:])
    gathered = (qkv_full, out_full, up_full, down_full)
    key_value = jnp.stack([projected[1], projected[2] + bias_now[1]]).astype(jnp.bfloat16)
    key_ext = with_halo(key_value, (("dp", 1),), margin)
    attended, log_norm = attend_forward(queries, key_ext, allowed)
    attended = attended.astype(jnp.bfloat16)

    def attention_term(first_row, row_count):
        return lax.dot_general(
            attended, out_full, (((1,), (1,)), ((), ())), preferred_element_type=jnp.float32
        )

    middle = stream + sum_forward(attention_term, tok_rows) + shift_now[1]
    second_full = gather_forward(layer_norm(middle, gain_now[1], shift_now[2]).astype(jnp.bfloat16))
    hidden = (
        jnp.einsum("gd,dre->gre", second_full, up_full, preferred_element_type=jnp.float32)
        + bias_now[2:][None]
    )
    active = exact_gelu(hidden).astype(jnp.bfloat16)

    def feed_term(first_row, row_count):
        return jnp.einsum("gre,ore->go", active, down_full, preferred_element_type=jnp.float32)

    kept_weights = gathered
    records = [
        (
            stream,
            middle,
            normed_full,
            second_full,
            queries,
            key_ext,
            log_norm,
            attended,
            hidden,
            active,
            kept_weights,
        )
    ]
    stream = middle + sum_forward(feed_term, tok_rows) + shift_now[3]
    gradient = cotangent.astype(jnp.float32) * own_real[:, None]
    local_qkv = [None] * LAYERS
    local_out = [None] * LAYERS
    local_up = [None] * LAYERS
    local_down = [None] * LAYERS
    unit_grads = [None] * LAYERS
    gain_grads = [None] * LAYERS
    shift_grads = [None] * LAYERS
    for layer_index in reversed(range(LAYERS)):
        (
            stream_in,
            middle,
            normed_full,
            second_full,
            queries,
            key_ext,
            log_norm,
            attended,
            hidden,
            active,
            kept_weights,
        ) = records[layer_index]
        qkv_full, out_full, up_full, down_full = kept_weights
        gain_now = norm_gain[layer_index].astype(jnp.float32)
        shift_now = row_bias[layer_index].astype(jnp.float32)
        shift_three = jnp.sum(gradient, axis=0)
        grad_mlp = gather_backward(gradient.astype(jnp.bfloat16))
        down_grad = scatter_rows(
            jnp.einsum("go,gre->ore", grad_mlp, active, preferred_element_type=jnp.float32)
        )
        grad_active = jnp.einsum(
            "go,ore->gre", grad_mlp, down_full, preferred_element_type=jnp.float32
        )
        gelu_again, gelu_pull = jax.vjp(exact_gelu, hidden)
        grad_hidden = gelu_pull(grad_active)[0].astype(jnp.bfloat16)
        up_bias_grad = jnp.sum(grad_hidden.astype(jnp.float32), axis=0)
        up_grad = scatter_rows(
            jnp.einsum("gd,gre->dre", second_full, grad_hidden, preferred_element_type=jnp.float32)
        )

        def second_term(first_row, row_count):
            return jnp.einsum(
                "gre,dre->gd", grad_hidden, up_full, preferred_element_type=jnp.float32
            )

        grad_second = sum_backward(second_term, tok_rows)
        second_again, second_pull = jax.vjp(layer_norm, middle, gain_now[1], shift_now[2])
        grad_mid_norm, gain_one, shift_two = second_pull(grad_second)
        grad_middle = gradient + grad_mid_norm
        shift_one = jnp.sum(grad_middle, axis=0)
        grad_proj = gather_backward(grad_middle.astype(jnp.bfloat16))
        out_grad = scatter_rows(
            lax.dot_general(
                grad_proj, attended, (((0,), (0,)), ((), ())), preferred_element_type=jnp.float32
            )
        )
        grad_attended = jnp.dot(grad_proj, out_full, preferred_element_type=jnp.float32).astype(
            jnp.bfloat16
        )
        grad_query, grad_key_ext, grad_value_ext = attend_backward(
            queries, key_ext, allowed, log_norm, grad_attended
        )
        grad_pair_ext = jnp.stack([grad_key_ext, grad_value_ext])
        from_next = from_behind(grad_pair_ext[:, :margin].astype(jnp.bfloat16), "dp", -1).astype(
            jnp.float32
        )
        from_prev = from_behind(
            grad_pair_ext[:, margin + group_rows :].astype(jnp.bfloat16), "dp", 1
        ).astype(jnp.float32)
        grad_pair = grad_pair_ext[:, margin : margin + group_rows]
        grad_pair = (
            grad_pair.at[:, group_rows - margin :].add(from_next).at[:, :margin].add(from_prev)
        )
        grad_triple = jnp.concatenate(
            [grad_query.astype(jnp.bfloat16)[None], grad_pair.astype(jnp.bfloat16)], axis=0
        )
        qkv_grad = jnp.moveaxis(
            scatter_rows(
                jnp.einsum(
                    "gd,sge->dse", normed_full, grad_triple, preferred_element_type=jnp.float32
                )
            ),
            0,
            1,
        )
        triple_sums = jnp.sum(grad_triple.astype(jnp.float32), axis=1)

        def first_term(first_row, row_count):
            return jnp.einsum(
                "sge,sde->gd", grad_triple, qkv_full, preferred_element_type=jnp.float32
            )

        grad_first = sum_backward(first_term, tok_rows)
        first_again, first_pull = jax.vjp(layer_norm, stream_in, gain_now[0], shift_now[0])
        grad_in_norm, gain_zero, shift_zero = first_pull(grad_first)
        gradient = grad_middle + grad_in_norm
        unit_grads[layer_index] = jnp.concatenate(
            [triple_sums[0][None], triple_sums[2][None], up_bias_grad], axis=0
        )
        gain_grads[layer_index] = jnp.stack([gain_zero, gain_one])
        shift_grads[layer_index] = jnp.stack([shift_zero, shift_one, shift_two, shift_three])
        local_qkv[layer_index] = qkv_grad
        local_out[layer_index] = out_grad
        local_up[layer_index] = up_grad
        local_down[layer_index] = down_grad
    grad_qkv = jnp.stack(local_qkv).astype(jnp.float32)
    grad_out = jnp.stack(local_out).astype(jnp.float32)
    grad_up = jnp.stack(local_up).astype(jnp.float32)
    grad_down = jnp.stack(local_down).astype(jnp.float32)
    unit_local = jnp.stack(unit_grads)
    unit_wide = jnp.zeros((LAYERS, unit_local.shape[1], cols_here * tensor_size), jnp.float32)
    unit_wide = lax.dynamic_update_slice_in_dim(unit_wide, unit_local, tensor_index * cols_here, 2)
    small = jnp.concatenate(
        [jnp.stack(gain_grads), jnp.stack(shift_grads), unit_wide], axis=1
    )
    small_total = jnp.sum(from_everyone(small, "dp"), axis=0)
    small_total = jnp.sum(from_everyone(small_total, "tensor"), axis=0)
    gain_total = small_total[:, :2]
    shift_total = small_total[:, 2:6]
    unit_total = small_total[:, 6:]
    unit_mine = lax.dynamic_slice_in_dim(unit_total, tensor_index * cols_here, cols_here, 2)
    return (
        stream.astype(jnp.bfloat16),
        gradient.astype(jnp.bfloat16),
        grad_qkv,
        grad_out,
        grad_up,
        grad_down,
        unit_mine,
        gain_total,
        shift_total,
    )


def solution(mesh):
    placed = (
        P(("dp", "tensor"), None),
        P(),
        P(),
        P(None, None, "dp", "tensor"),
        P(None, "dp", "tensor"),
        P(None, "dp", None, "tensor"),
        P(None, "dp", None, "tensor"),
        P(None, None, "tensor"),
        P(),
        P(),
        P(("dp", "tensor"), None),
    )
    return jax.shard_map(
        local,
        mesh=mesh,
        in_specs=placed,
        out_specs=(
            P(("dp", "tensor"), None),
            P(("dp", "tensor"), None),
            P(None, None, "dp", "tensor"),
            P(None, "dp", "tensor"),
            P(None, "dp", None, "tensor"),
            P(None, "dp", None, "tensor"),
            P(None, None, "tensor"),
            P(),
            P(),
        ),
        check_vma=False,
    )
```

```python
import functools
import math

import jax
import jax.numpy as jnp
from jax import lax
from jax.experimental import pallas as pl
from jax.experimental.pallas import tpu as pltpu
from jax.sharding import PartitionSpec as P

MESH = pl.DeviceIdType.MESH

LAYERS = 1
IMG = 577
HD = 64


norm_eps = 1e-06
masked_score = -1e30


def from_everyone(value, axis):
    devices = lax.axis_size(axis)
    return lax.all_to_all(
        jnp.broadcast_to(value[None], (devices, *value.shape)), axis, 0, 0, tiled=True
    )


def joined_along(parts, dim):
    dims = list(parts.shape[1:])
    dims[dim] *= parts.shape[0]
    return jnp.moveaxis(parts, 0, dim).reshape(dims)


def collect(value, axis, dim):
    parts = from_everyone(value, axis)
    return joined_along(parts, dim)


def split_up(value, dim, devices):
    dims = value.shape
    parts = value.reshape(*dims[:dim], devices, dims[dim] // devices, *dims[dim + 1 :])
    return jnp.moveaxis(parts, dim, 0)


def summed_on_arrival(value, axis, dim):
    devices = lax.axis_size(axis)
    parts = lax.all_to_all(split_up(value, dim, devices), axis, 0, 0, tiled=True)
    return jnp.sum(parts.astype(jnp.float32), axis=0)


def rows_first(arrays, axis, dims):
    turned = [jnp.moveaxis(a, dim, 0) for a, dim in zip(arrays, dims)]
    both = jnp.concatenate([t.reshape(len(t), -1) for t in turned], axis=1)
    filled, at, outs = (lax.all_gather(both, axis, axis=0, tiled=True), 0, [])
    for t, dim in zip(turned, dims):
        slab = filled[:, at : at + t[0].size].reshape(-1, *t.shape[1:])
        outs.append(jnp.moveaxis(slab, 0, dim))
        at += t[0].size
    return tuple(outs)


def with_halo(value, sides, width):
    for axis, dim in sides:
        devices, length = (lax.axis_size(axis), value.shape[dim])
        up = [(i, (i + 1) % devices) for i in range(devices - 1)]
        down = [(j, i) for i, j in up]
        last = lax.slice_in_dim(value, length - width, length, axis=dim)
        initial = lax.slice_in_dim(value, 0, width, axis=dim)
        before = lax.ppermute(last, axis, up)
        after = lax.ppermute(initial, axis, down)
        value = jnp.concatenate([before, value, after], axis=dim)
    return value


def from_behind(block, axis, distance):
    devices = range(lax.axis_size(axis))
    route = [(i - distance, i) for i in devices if i - distance in devices]
    return lax.ppermute(block, axis, route)


def side_by_side(arrays, axis, dim, along):
    widths = [math.prod(a.shape[along:]) for a in arrays]
    both = jnp.concatenate(
        [a.reshape(*a.shape[:along], w) for a, w in zip(arrays, widths)], axis=along
    )
    filled = lax.psum_scatter(both, axis, scatter_dimension=dim, tiled=True)
    parts = jnp.split(filled, [sum(widths[:k]) for k in range(1, len(widths))], axis=along)
    return tuple(
        (b.reshape(*filled.shape[:along], *a.shape[along:]) for a, b in zip(arrays, parts))
    )


def scatter_rows(grad):
    return summed_on_arrival(grad.astype(jnp.bfloat16), "dp", 0)


def layer_norm(values, gain_row, shift_row):
    center = values - jnp.mean(values, axis=-1, keepdims=True)
    spread = jnp.mean(center * center, axis=-1, keepdims=True)
    return center * lax.rsqrt(spread + norm_eps) * gain_row + shift_row


def exact_gelu(values):
    return jax.nn.gelu(values, approximate=False)


def _gather_kernel(devices, x_ref, out_ref, send_sem, recv_sem):
    me = lax.axis_index("tensor")
    dp = lax.axis_index("dp")
    sib = me + 1 - 2 * lax.rem(me, 2)
    far = lax.rem(me + 2, devices)
    barrier = pltpu.get_barrier_semaphore()
    for peer in (sib, far):
        pl.semaphore_signal(barrier, inc=1, device_id=(dp, peer), device_id_type=MESH)
    pl.semaphore_wait(barrier, 2)
    near_copy = pltpu.make_async_remote_copy(
        src_ref=x_ref,
        dst_ref=out_ref.at[me],
        send_sem=send_sem.at[0],
        recv_sem=recv_sem.at[0],
        device_id=(dp, sib),
        device_id_type=MESH,
    )
    far_copy = pltpu.make_async_remote_copy(
        src_ref=x_ref,
        dst_ref=out_ref.at[me],
        send_sem=send_sem.at[1],
        recv_sem=recv_sem.at[1],
        device_id=(dp, far),
        device_id_type=MESH,
    )
    far_copy.start()
    near_copy.start()
    out_ref[me] = x_ref[...]
    far_copy.wait_recv()
    relay = pltpu.make_async_remote_copy(
        src_ref=out_ref.at[far],
        dst_ref=out_ref.at[far],
        send_sem=send_sem.at[2],
        recv_sem=recv_sem.at[2],
        device_id=(dp, sib),
        device_id_type=MESH,
    )
    relay.start()
    near_copy.wait_send()
    near_copy.wait_recv()
    far_copy.wait_send()
    relay.wait_send()
    relay.wait_recv()


def gather_rows(values):
    devices = lax.axis_size("tensor")
    if devices != 4:
        return collect(values, "tensor", 0)
    rows, width = values.shape
    parts = pl.pallas_call(
        functools.partial(_gather_kernel, devices),
        out_shape=jax.ShapeDtypeStruct((devices, rows, width), values.dtype),
        in_specs=[pl.BlockSpec(memory_space=pltpu.VMEM)],
        out_specs=pl.BlockSpec(memory_space=pltpu.VMEM),
        scratch_shapes=[
            pltpu.SemaphoreType.DMA((3,)),
            pltpu.SemaphoreType.DMA((3,)),
        ],
        compiler_params=pltpu.CompilerParams(collective_id=0, has_side_effects=True),
    )(values)
    return parts.reshape(devices * rows, width)


def _exchange_kernel(devices, x_ref, out_ref, send_sem, recv_sem):
    me = lax.axis_index("tensor")
    dp = lax.axis_index("dp")
    barrier = pltpu.get_barrier_semaphore()
    for step in range(1, devices):
        pl.semaphore_signal(
            barrier, inc=1, device_id=(dp, lax.rem(me + step, devices)), device_id_type=MESH
        )
    pl.semaphore_wait(barrier, devices - 1)
    copies = []
    for step in range(1, devices):
        peer = lax.rem(me + step, devices)
        copy = pltpu.make_async_remote_copy(
            src_ref=x_ref.at[peer],
            dst_ref=out_ref.at[me],
            send_sem=send_sem.at[step - 1],
            recv_sem=recv_sem.at[step - 1],
            device_id=(dp, peer),
            device_id_type=MESH,
        )
        copy.start()
        copies.append(copy)
    out_ref[me] = x_ref[me]
    for copy in copies:
        copy.wait()


def exchange_rows(parts):
    devices = parts.shape[0]
    return pl.pallas_call(
        functools.partial(_exchange_kernel, devices),
        out_shape=jax.ShapeDtypeStruct(parts.shape, parts.dtype),
        in_specs=[pl.BlockSpec(memory_space=pltpu.VMEM)],
        out_specs=pl.BlockSpec(memory_space=pltpu.VMEM),
        scratch_shapes=[
            pltpu.SemaphoreType.DMA((devices - 1,)),
            pltpu.SemaphoreType.DMA((devices - 1,)),
        ],
        compiler_params=pltpu.CompilerParams(collective_id=1, has_side_effects=True),
    )(parts)


def _reduce_kernel(devices, x_ref, out_ref, held, mate, pre, send_sem, recv_sem):
    me = lax.axis_index("tensor")
    dp = lax.axis_index("dp")
    sib = me + 1 - 2 * lax.rem(me, 2)
    far = lax.rem(me + 2, devices)
    other = lax.rem(sib + 2, devices)
    barrier = pltpu.get_barrier_semaphore()
    for peer in (sib, far):
        pl.semaphore_signal(barrier, inc=1, device_id=(dp, peer), device_id_type=MESH)
    pl.semaphore_wait(barrier, 2)
    own_copy = pltpu.make_async_remote_copy(
        src_ref=x_ref.at[sib],
        dst_ref=held.at[0],
        send_sem=send_sem.at[0],
        recv_sem=recv_sem.at[0],
        device_id=(dp, sib),
        device_id_type=MESH,
    )
    mate_copy = pltpu.make_async_remote_copy(
        src_ref=x_ref.at[other],
        dst_ref=mate,
        send_sem=send_sem.at[1],
        recv_sem=recv_sem.at[1],
        device_id=(dp, sib),
        device_id_type=MESH,
    )
    mate_copy.start()
    own_copy.start()
    mate_copy.wait_recv()
    pre[...] = (x_ref[far].astype(jnp.float32) + mate[...].astype(jnp.float32)).astype(pre.dtype)
    own_copy.wait_recv()
    out_ref[...] = x_ref[me].astype(jnp.float32) + held[0].astype(jnp.float32)
    far_copy = pltpu.make_async_remote_copy(
        src_ref=pre,
        dst_ref=held.at[1],
        send_sem=send_sem.at[2],
        recv_sem=recv_sem.at[2],
        device_id=(dp, far),
        device_id_type=MESH,
    )
    far_copy.start()
    far_copy.wait_recv()
    out_ref[...] += held[1].astype(jnp.float32)
    own_copy.wait_send()
    mate_copy.wait_send()
    far_copy.wait_send()


def summed_over_tensor(value):
    devices = lax.axis_size("tensor")
    parts = split_up(value, 0, devices)
    if devices != 4:
        return jnp.sum(exchange_rows(parts).astype(jnp.float32), axis=0)
    rows, width = parts.shape[1:]
    return pl.pallas_call(
        functools.partial(_reduce_kernel, devices),
        out_shape=jax.ShapeDtypeStruct((rows, width), jnp.float32),
        in_specs=[pl.BlockSpec(memory_space=pltpu.VMEM)],
        out_specs=pl.BlockSpec(memory_space=pltpu.VMEM),
        scratch_shapes=[
            pltpu.VMEM((2, rows, width), parts.dtype),
            pltpu.VMEM((rows, width), parts.dtype),
            pltpu.VMEM((rows, width), parts.dtype),
            pltpu.SemaphoreType.DMA((3,)),
            pltpu.SemaphoreType.DMA((3,)),
        ],
        compiler_params=pltpu.CompilerParams(collective_id=1, has_side_effects=True),
    )(parts)


def gather_forward(values):
    return gather_rows(values)


def gather_backward(values):
    return gather_rows(values)


def sum_forward(product, tok_rows):
    return summed_over_tensor(
        product(jnp.int32(0), tok_rows * lax.axis_size("tensor")).astype(jnp.bfloat16)
    )


def sum_backward(product, tok_rows):
    return summed_over_tensor(
        product(jnp.int32(0), tok_rows * lax.axis_size("tensor")).astype(jnp.bfloat16)
    )


def head_scores(query_head, key_head, allowed):
    raw = lax.dot_general(
        query_head, key_head, (((1,), (1,)), ((), ())), preferred_element_type=jnp.float32
    )
    return jnp.where(allowed, raw * HD ** (-0.5), masked_score)


def split_heads(queries, key_ext):
    heads_here = queries.shape[1] // HD
    query_heads = queries.reshape(queries.shape[0], heads_here, HD)
    key_heads = key_ext[0].reshape(key_ext.shape[1], heads_here, HD)
    value_heads = key_ext[1].reshape(key_ext.shape[1], heads_here, HD)
    return (heads_here, query_heads, key_heads, value_heads)


def merge_heads(per_head):
    return jnp.transpose(per_head, (1, 0, 2)).reshape(
        per_head.shape[1], per_head.shape[0] * per_head.shape[2]
    )


def _mask_from(sq_ref, pq_ref, sk_ref, rk_ref, pk_ref):
    return (sq_ref[...] == sk_ref[...]) & ((rk_ref[...] == 1) | (pq_ref[...] == pk_ref[...]))


def _mask_specs(rows, keys):
    column = pl.BlockSpec((rows, 1), lambda h: (0, 0))
    row = pl.BlockSpec((1, keys), lambda h: (0, 0))
    return [column, column, row, row, row]


def _attend_kernel(q_ref, k_ref, v_ref, sq_ref, pq_ref, sk_ref, rk_ref, pk_ref, o_ref, lse_ref):
    scores = lax.dot_general(
        q_ref[...], k_ref[...], (((1,), (1,)), ((), ())), preferred_element_type=jnp.float32
    )
    allowed = _mask_from(sq_ref, pq_ref, sk_ref, rk_ref, pk_ref)
    scores = jnp.where(allowed, scores * HD ** (-0.5), masked_score)
    row_top = jnp.max(scores, axis=1, keepdims=True)
    exponent = jnp.exp(scores - row_top)
    row_total = jnp.sum(exponent, axis=1, keepdims=True)
    prob_low = (exponent / row_total).astype(jnp.bfloat16)
    o_ref[...] = jnp.dot(prob_low, v_ref[...], preferred_element_type=jnp.float32)
    lse_ref[...] = row_top + jnp.log(row_total)


def attend_forward(queries, key_ext, mask_parts):
    heads_here = queries.shape[1] // HD
    rows, keys = mask_parts[0].shape[0], mask_parts[2].shape[1]
    query_heads = jnp.transpose(queries.reshape(rows, heads_here, HD), (1, 0, 2))
    key_heads = jnp.transpose(key_ext[0].reshape(keys, heads_here, HD), (1, 0, 2))
    value_heads = jnp.transpose(key_ext[1].reshape(keys, heads_here, HD), (1, 0, 2))
    head_outs, log_norm = pl.pallas_call(
        _attend_kernel,
        grid=(heads_here,),
        out_shape=(
            jax.ShapeDtypeStruct((heads_here, rows, HD), jnp.float32),
            jax.ShapeDtypeStruct((heads_here, rows, 1), jnp.float32),
        ),
        in_specs=[
            pl.BlockSpec((None, rows, HD), lambda h: (h, 0, 0)),
            pl.BlockSpec((None, keys, HD), lambda h: (h, 0, 0)),
            pl.BlockSpec((None, keys, HD), lambda h: (h, 0, 0)),
            *_mask_specs(rows, keys),
        ],
        out_specs=(
            pl.BlockSpec((None, rows, HD), lambda h: (h, 0, 0)),
            pl.BlockSpec((None, rows, 1), lambda h: (h, 0, 0)),
        ),
        compiler_params=pltpu.CompilerParams(vmem_limit_bytes=60 * 1024 * 1024),
    )(query_heads, key_heads, value_heads, *mask_parts)
    return (merge_heads(head_outs), log_norm[:, :, 0])


def attend_forward_xla(queries, key_ext, allowed):
    heads_here, query_heads, key_heads, value_heads = split_heads(queries, key_ext)

    def one_head(head_index):
        query_head = lax.dynamic_index_in_dim(query_heads, head_index, 1, keepdims=False)
        key_head = lax.dynamic_index_in_dim(key_heads, head_index, 1, keepdims=False)
        value_head = lax.dynamic_index_in_dim(value_heads, head_index, 1, keepdims=False)
        scores = head_scores(query_head, key_head, allowed)
        row_top = jnp.max(scores, axis=1, keepdims=True)
        exponent = jnp.exp(scores - row_top)
        row_total = jnp.sum(exponent, axis=1, keepdims=True)
        prob_low = (exponent / row_total).astype(jnp.bfloat16)
        head_out = jnp.dot(prob_low, value_head, preferred_element_type=jnp.float32)
        return (head_out, (row_top + jnp.log(row_total))[:, 0])

    head_outs, log_norm = lax.map(one_head, jnp.arange(heads_here, dtype=jnp.int32))
    return (merge_heads(head_outs), log_norm)


def _attend_back_kernel(
    q_ref, k_ref, v_ref, g_ref, lse_ref, sq_ref, pq_ref, sk_ref, rk_ref, pk_ref, dq_ref, dk_ref, dv_ref
):
    query_head, key_head, grad_head = q_ref[...], k_ref[...], g_ref[...]
    scores = lax.dot_general(
        query_head, key_head, (((1,), (1,)), ((), ())), preferred_element_type=jnp.float32
    )
    allowed = _mask_from(sq_ref, pq_ref, sk_ref, rk_ref, pk_ref)
    scores = jnp.where(allowed, scores * HD ** (-0.5), masked_score)
    prob_full = jnp.exp(scores - lse_ref[...])
    prob_low = prob_full.astype(jnp.bfloat16)
    dv_ref[...] = lax.dot_general(
        prob_low, grad_head, (((0,), (0,)), ((), ())), preferred_element_type=jnp.float32
    )
    grad_prob = lax.dot_general(
        grad_head, v_ref[...], (((1,), (1,)), ((), ())), preferred_element_type=jnp.float32
    )
    grad_score = (
        prob_full * (grad_prob - jnp.sum(prob_full * grad_prob, axis=1, keepdims=True))
    ).astype(jnp.bfloat16)
    dq_ref[...] = jnp.dot(grad_score, key_head, preferred_element_type=jnp.float32) * HD ** (-0.5)
    dk_ref[...] = lax.dot_general(
        grad_score, query_head, (((0,), (0,)), ((), ())), preferred_element_type=jnp.float32
    ) * HD ** (-0.5)


def attend_backward(queries, key_ext, mask_parts, log_norm, grad_attended):
    heads_here = queries.shape[1] // HD
    rows, keys = mask_parts[0].shape[0], mask_parts[2].shape[1]

    def by_head(values, count):
        return jnp.transpose(values.reshape(count, heads_here, HD), (1, 0, 2))

    row_spec = pl.BlockSpec((None, rows, HD), lambda h: (h, 0, 0))
    key_spec = pl.BlockSpec((None, keys, HD), lambda h: (h, 0, 0))
    grad_queries, grad_keys, grad_values = pl.pallas_call(
        _attend_back_kernel,
        grid=(heads_here,),
        out_shape=(
            jax.ShapeDtypeStruct((heads_here, rows, HD), jnp.float32),
            jax.ShapeDtypeStruct((heads_here, keys, HD), jnp.float32),
            jax.ShapeDtypeStruct((heads_here, keys, HD), jnp.float32),
        ),
        in_specs=[
            row_spec,
            key_spec,
            key_spec,
            row_spec,
            pl.BlockSpec((None, rows, 1), lambda h: (h, 0, 0)),
            *_mask_specs(rows, keys),
        ],
        out_specs=(row_spec, key_spec, key_spec),
        compiler_params=pltpu.CompilerParams(vmem_limit_bytes=60 * 1024 * 1024),
    )(
        by_head(queries, rows),
        by_head(key_ext[0], keys),
        by_head(key_ext[1], keys),
        by_head(grad_attended, rows),
        log_norm[:, :, None],
        *mask_parts,
    )
    return (merge_heads(grad_queries), merge_heads(grad_keys), merge_heads(grad_values))


def attend_backward_xla(queries, key_ext, allowed, log_norm, grad_attended):
    heads_here, query_heads, key_heads, value_heads = split_heads(queries, key_ext)
    grad_heads = grad_attended.reshape(grad_attended.shape[0], heads_here, HD)

    def one_head(inputs):
        head_index, norm_row = inputs
        query_head = lax.dynamic_index_in_dim(query_heads, head_index, 1, keepdims=False)
        key_head = lax.dynamic_index_in_dim(key_heads, head_index, 1, keepdims=False)
        value_head = lax.dynamic_index_in_dim(value_heads, head_index, 1, keepdims=False)
        grad_head = lax.dynamic_index_in_dim(grad_heads, head_index, 1, keepdims=False)
        prob_full = jnp.exp(head_scores(query_head, key_head, allowed) - norm_row[:, None])
        prob_low = prob_full.astype(jnp.bfloat16)
        grad_value = lax.dot_general(
            prob_low, grad_head, (((0,), (0,)), ((), ())), preferred_element_type=jnp.float32
        )
        grad_prob = lax.dot_general(
            grad_head, value_head, (((1,), (1,)), ((), ())), preferred_element_type=jnp.float32
        )
        grad_score = (
            prob_full * (grad_prob - jnp.sum(prob_full * grad_prob, axis=1, keepdims=True))
        ).astype(jnp.bfloat16)
        grad_query = jnp.dot(grad_score, key_head, preferred_element_type=jnp.float32) * HD ** (
            -0.5
        )
        grad_key = lax.dot_general(
            grad_score, query_head, (((0,), (0,)), ((), ())), preferred_element_type=jnp.float32
        ) * HD ** (-0.5)
        return (grad_query, grad_key, grad_value)

    grad_queries, grad_keys, grad_values = lax.map(
        one_head, (jnp.arange(heads_here, dtype=jnp.int32), log_norm)
    )
    return (merge_heads(grad_queries), merge_heads(grad_keys), merge_heads(grad_values))


def local(
    tokens,
    segment,
    real_token,
    qkv_weight,
    out_weight,
    up_weight,
    down_weight,
    unit_bias,
    norm_gain,
    row_bias,
    cotangent,
):
    tok_rows = tokens.shape[0]
    tensor_size = lax.axis_size("tensor")
    group_rows = tok_rows * tensor_size
    margin = IMG - 1
    cols_here = qkv_weight.shape[3]
    dp_index = lax.axis_index("dp")
    tensor_index = lax.axis_index("tensor")
    group_first = dp_index * group_rows
    own_first = group_first + tensor_index * tok_rows
    segment_pad = jnp.pad(segment, (margin, margin), constant_values=-1)
    real_pad = jnp.pad(real_token, (margin, margin))
    segment_query = lax.dynamic_slice_in_dim(segment, group_first, group_rows, 0)
    segment_key = lax.dynamic_slice_in_dim(segment_pad, group_first, group_rows + 2 * margin, 0)
    real_key = lax.dynamic_slice_in_dim(real_pad, group_first, group_rows + 2 * margin, 0)
    place_query = jnp.arange(group_rows, dtype=jnp.int32)
    place_key = jnp.arange(group_rows + 2 * margin, dtype=jnp.int32) - margin
    allowed = (
        segment_query[:, None],
        place_query[:, None],
        segment_key[None, :],
        real_key[None, :],
        place_key[None, :],
    )
    own_real = lax.dynamic_slice_in_dim(real_token, own_first, tok_rows, 0).astype(jnp.float32)
    stream = tokens.astype(jnp.float32)
    layer_index = 0
    qkv_local = jnp.moveaxis(qkv_weight[layer_index], 1, 0)
    out_local, up_local, down_local = (
        out_weight[layer_index],
        up_weight[layer_index],
        down_weight[layer_index],
    )
    gain_now = norm_gain[layer_index].astype(jnp.float32)
    shift_now = row_bias[layer_index].astype(jnp.float32)
    bias_now = unit_bias[layer_index].astype(jnp.float32)
    normed_full = gather_forward(layer_norm(stream, gain_now[0], shift_now[0]).astype(jnp.bfloat16))
    normed_full, qkv_local = lax.optimization_barrier((normed_full, qkv_local))
    qkv_full = jnp.moveaxis(collect(qkv_local, "dp", 0), 0, 1)
    projected = jnp.einsum("gd,sde->sge", normed_full, qkv_full, preferred_element_type=jnp.float32)
    queries = (projected[0] + bias_now[0]).astype(jnp.bfloat16)
    queries, out_local, up_local, down_local = lax.optimization_barrier(
        (queries, out_local, up_local, down_local)
    )
    out_full = collect(out_local, "dp", 0)
    up_full = collect(up_local, "dp", 0)
    down_full = collect(down_local, "dp", 0)
    gathered = (qkv_full, out_full, up_full, down_full)
    key_value = jnp.stack([projected[1], projected[2] + bias_now[1]]).astype(jnp.bfloat16)
    key_ext = with_halo(key_value, (("dp", 1),), margin)
    attended, log_norm = attend_forward(queries, key_ext, allowed)
    attended = attended.astype(jnp.bfloat16)

    def attention_term(first_row, row_count):
        return lax.dot_general(
            attended, out_full, (((1,), (1,)), ((), ())), preferred_element_type=jnp.float32
        )

    middle = stream + sum_forward(attention_term, tok_rows) + shift_now[1]
    second_full = gather_forward(layer_norm(middle, gain_now[1], shift_now[2]).astype(jnp.bfloat16))
    hidden = (
        jnp.einsum("gd,dre->gre", second_full, up_full, preferred_element_type=jnp.float32)
        + bias_now[2:][None]
    )
    active = exact_gelu(hidden).astype(jnp.bfloat16)

    def feed_term(first_row, row_count):
        return jnp.einsum("gre,ore->go", active, down_full, preferred_element_type=jnp.float32)

    kept_weights = gathered
    records = [
        (
            stream,
            middle,
            normed_full,
            second_full,
            queries,
            key_ext,
            log_norm,
            attended,
            hidden,
            active,
            kept_weights,
        )
    ]
    stream = middle + sum_forward(feed_term, tok_rows) + shift_now[3]
    gradient = cotangent.astype(jnp.float32) * own_real[:, None]
    local_qkv = [None] * LAYERS
    local_out = [None] * LAYERS
    local_up = [None] * LAYERS
    local_down = [None] * LAYERS
    unit_grads = [None] * LAYERS
    gain_grads = [None] * LAYERS
    shift_grads = [None] * LAYERS
    for layer_index in reversed(range(LAYERS)):
        (
            stream_in,
            middle,
            normed_full,
            second_full,
            queries,
            key_ext,
            log_norm,
            attended,
            hidden,
            active,
            kept_weights,
        ) = records[layer_index]
        qkv_full, out_full, up_full, down_full = kept_weights
        gain_now = norm_gain[layer_index].astype(jnp.float32)
        shift_now = row_bias[layer_index].astype(jnp.float32)
        shift_three = jnp.sum(gradient, axis=0)
        grad_mlp = gather_backward(gradient.astype(jnp.bfloat16))
        down_grad = scatter_rows(
            jnp.einsum("go,gre->ore", grad_mlp, active, preferred_element_type=jnp.float32)
        )
        grad_active = jnp.einsum(
            "go,ore->gre", grad_mlp, down_full, preferred_element_type=jnp.float32
        )
        gelu_again, gelu_pull = jax.vjp(exact_gelu, hidden)
        grad_hidden = gelu_pull(grad_active)[0].astype(jnp.bfloat16)
        up_bias_grad = jnp.sum(grad_hidden.astype(jnp.float32), axis=0)
        up_grad = scatter_rows(
            jnp.einsum("gd,gre->dre", second_full, grad_hidden, preferred_element_type=jnp.float32)
        )

        def second_term(first_row, row_count):
            return jnp.einsum(
                "gre,dre->gd", grad_hidden, up_full, preferred_element_type=jnp.float32
            )

        grad_second = sum_backward(second_term, tok_rows)
        second_again, second_pull = jax.vjp(layer_norm, middle, gain_now[1], shift_now[2])
        grad_mid_norm, gain_one, shift_two = second_pull(grad_second)
        grad_middle = gradient + grad_mid_norm
        shift_one = jnp.sum(grad_middle, axis=0)
        grad_proj = gather_backward(grad_middle.astype(jnp.bfloat16))
        out_grad = scatter_rows(
            lax.dot_general(
                grad_proj, attended, (((0,), (0,)), ((), ())), preferred_element_type=jnp.float32
            )
        )
        grad_attended = jnp.dot(grad_proj, out_full, preferred_element_type=jnp.float32).astype(
            jnp.bfloat16
        )
        grad_query, grad_key_ext, grad_value_ext = attend_backward(
            queries, key_ext, allowed, log_norm, grad_attended
        )
        grad_pair_ext = jnp.stack([grad_key_ext, grad_value_ext])
        from_next = from_behind(grad_pair_ext[:, :margin].astype(jnp.bfloat16), "dp", -1).astype(
            jnp.float32
        )
        from_prev = from_behind(
            grad_pair_ext[:, margin + group_rows :].astype(jnp.bfloat16), "dp", 1
        ).astype(jnp.float32)
        grad_pair = grad_pair_ext[:, margin : margin + group_rows]
        grad_pair = (
            grad_pair.at[:, group_rows - margin :].add(from_next).at[:, :margin].add(from_prev)
        )
        grad_triple = jnp.concatenate(
            [grad_query.astype(jnp.bfloat16)[None], grad_pair.astype(jnp.bfloat16)], axis=0
        )
        qkv_grad = jnp.moveaxis(
            scatter_rows(
                jnp.einsum(
                    "gd,sge->dse", normed_full, grad_triple, preferred_element_type=jnp.float32
                )
            ),
            0,
            1,
        )
        triple_sums = jnp.sum(grad_triple.astype(jnp.float32), axis=1)

        def first_term(first_row, row_count):
            return jnp.einsum(
                "sge,sde->gd", grad_triple, qkv_full, preferred_element_type=jnp.float32
            )

        grad_first = sum_backward(first_term, tok_rows)
        first_again, first_pull = jax.vjp(layer_norm, stream_in, gain_now[0], shift_now[0])
        grad_in_norm, gain_zero, shift_zero = first_pull(grad_first)
        gradient = grad_middle + grad_in_norm
        unit_grads[layer_index] = jnp.concatenate(
            [triple_sums[0][None], triple_sums[2][None], up_bias_grad], axis=0
        )
        gain_grads[layer_index] = jnp.stack([gain_zero, gain_one])
        shift_grads[layer_index] = jnp.stack([shift_zero, shift_one, shift_two, shift_three])
        local_qkv[layer_index] = qkv_grad
        local_out[layer_index] = out_grad
        local_up[layer_index] = up_grad
        local_down[layer_index] = down_grad
    grad_qkv = jnp.stack(local_qkv).astype(jnp.float32)
    grad_out = jnp.stack(local_out).astype(jnp.float32)
    grad_up = jnp.stack(local_up).astype(jnp.float32)
    grad_down = jnp.stack(local_down).astype(jnp.float32)
    unit_local = jnp.stack(unit_grads)
    unit_wide = jnp.zeros((LAYERS, unit_local.shape[1], cols_here * tensor_size), jnp.float32)
    unit_wide = lax.dynamic_update_slice_in_dim(unit_wide, unit_local, tensor_index * cols_here, 2)
    small = jnp.concatenate(
        [jnp.stack(gain_grads), jnp.stack(shift_grads), unit_wide], axis=1
    )
    small_total = jnp.sum(from_everyone(small, "dp"), axis=0)
    small_total = jnp.sum(from_everyone(small_total, "tensor"), axis=0)
    gain_total = small_total[:, :2]
    shift_total = small_total[:, 2:6]
    unit_total = small_total[:, 6:]
    unit_mine = lax.dynamic_slice_in_dim(unit_total, tensor_index * cols_here, cols_here, 2)
    return (
        stream.astype(jnp.bfloat16),
        gradient.astype(jnp.bfloat16),
        grad_qkv,
        grad_out,
        grad_up,
        grad_down,
        unit_mine,
        gain_total,
        shift_total,
    )


def solution(mesh):
    placed = (
        P(("dp", "tensor"), None),
        P(),
        P(),
        P(None, None, "dp", "tensor"),
        P(None, "dp", "tensor"),
        P(None, "dp", None, "tensor"),
        P(None, "dp", None, "tensor"),
        P(None, None, "tensor"),
        P(),
        P(),
        P(("dp", "tensor"), None),
    )
    return jax.shard_map(
        local,
        mesh=mesh,
        in_specs=placed,
        out_specs=(
            P(("dp", "tensor"), None),
            P(("dp", "tensor"), None),
            P(None, None, "dp", "tensor"),
            P(None, "dp", "tensor"),
            P(None, "dp", None, "tensor"),
            P(None, "dp", None, "tensor"),
            P(None, None, "tensor"),
            P(),
            P(),
        ),
        check_vma=False,
    )
```

```python
import functools
import math

import jax
import jax.numpy as jnp
from jax import lax
from jax.experimental import pallas as pl
from jax.experimental.pallas import tpu as pltpu
from jax.sharding import PartitionSpec as P

MESH = pl.DeviceIdType.MESH

LAYERS = 1
IMG = 577
HD = 64


norm_eps = 1e-06
masked_score = -1e30


def from_everyone(value, axis):
    devices = lax.axis_size(axis)
    return lax.all_to_all(
        jnp.broadcast_to(value[None], (devices, *value.shape)), axis, 0, 0, tiled=True
    )


def joined_along(parts, dim):
    dims = list(parts.shape[1:])
    dims[dim] *= parts.shape[0]
    return jnp.moveaxis(parts, 0, dim).reshape(dims)


def collect(value, axis, dim):
    parts = from_everyone(value, axis)
    return joined_along(parts, dim)


def split_up(value, dim, devices):
    dims = value.shape
    parts = value.reshape(*dims[:dim], devices, dims[dim] // devices, *dims[dim + 1 :])
    return jnp.moveaxis(parts, dim, 0)


def summed_on_arrival(value, axis, dim):
    devices = lax.axis_size(axis)
    parts = lax.all_to_all(split_up(value, dim, devices), axis, 0, 0, tiled=True)
    return jnp.sum(parts.astype(jnp.float32), axis=0)


def rows_first(arrays, axis, dims):
    turned = [jnp.moveaxis(a, dim, 0) for a, dim in zip(arrays, dims)]
    both = jnp.concatenate([t.reshape(len(t), -1) for t in turned], axis=1)
    filled, at, outs = (lax.all_gather(both, axis, axis=0, tiled=True), 0, [])
    for t, dim in zip(turned, dims):
        slab = filled[:, at : at + t[0].size].reshape(-1, *t.shape[1:])
        outs.append(jnp.moveaxis(slab, 0, dim))
        at += t[0].size
    return tuple(outs)


def with_halo(value, sides, width):
    for axis, dim in sides:
        devices, length = (lax.axis_size(axis), value.shape[dim])
        up = [(i, (i + 1) % devices) for i in range(devices - 1)]
        down = [(j, i) for i, j in up]
        last = lax.slice_in_dim(value, length - width, length, axis=dim)
        initial = lax.slice_in_dim(value, 0, width, axis=dim)
        before = lax.ppermute(last, axis, up)
        after = lax.ppermute(initial, axis, down)
        value = jnp.concatenate([before, value, after], axis=dim)
    return value


def from_behind(block, axis, distance):
    devices = range(lax.axis_size(axis))
    route = [(i - distance, i) for i in devices if i - distance in devices]
    return lax.ppermute(block, axis, route)


def side_by_side(arrays, axis, dim, along):
    widths = [math.prod(a.shape[along:]) for a in arrays]
    both = jnp.concatenate(
        [a.reshape(*a.shape[:along], w) for a, w in zip(arrays, widths)], axis=along
    )
    filled = lax.psum_scatter(both, axis, scatter_dimension=dim, tiled=True)
    parts = jnp.split(filled, [sum(widths[:k]) for k in range(1, len(widths))], axis=along)
    return tuple(
        (b.reshape(*filled.shape[:along], *a.shape[along:]) for a, b in zip(arrays, parts))
    )


def scatter_rows(grad):
    return summed_on_arrival(grad.astype(jnp.bfloat16), "dp", 0)


def layer_norm(values, gain_row, shift_row):
    center = values - jnp.mean(values, axis=-1, keepdims=True)
    spread = jnp.mean(center * center, axis=-1, keepdims=True)
    return center * lax.rsqrt(spread + norm_eps) * gain_row + shift_row


def exact_gelu(values):
    return jax.nn.gelu(values, approximate=False)


def _gather_kernel(devices, x_ref, out_ref, send_sem, recv_sem):
    me = lax.axis_index("tensor")
    dp = lax.axis_index("dp")
    sib = me + 1 - 2 * lax.rem(me, 2)
    far = lax.rem(me + 2, devices)
    barrier = pltpu.get_barrier_semaphore()
    for peer in (sib, far):
        pl.semaphore_signal(barrier, inc=1, device_id=(dp, peer), device_id_type=MESH)
    pl.semaphore_wait(barrier, 2)
    near_copy = pltpu.make_async_remote_copy(
        src_ref=x_ref,
        dst_ref=out_ref.at[me],
        send_sem=send_sem.at[0],
        recv_sem=recv_sem.at[0],
        device_id=(dp, sib),
        device_id_type=MESH,
    )
    far_copy = pltpu.make_async_remote_copy(
        src_ref=x_ref,
        dst_ref=out_ref.at[me],
        send_sem=send_sem.at[1],
        recv_sem=recv_sem.at[1],
        device_id=(dp, far),
        device_id_type=MESH,
    )
    far_copy.start()
    near_copy.start()
    out_ref[me] = x_ref[...]
    far_copy.wait_recv()
    relay = pltpu.make_async_remote_copy(
        src_ref=out_ref.at[far],
        dst_ref=out_ref.at[far],
        send_sem=send_sem.at[2],
        recv_sem=recv_sem.at[2],
        device_id=(dp, sib),
        device_id_type=MESH,
    )
    relay.start()
    near_copy.wait_send()
    near_copy.wait_recv()
    far_copy.wait_send()
    relay.wait_send()
    relay.wait_recv()


def gather_rows(values):
    devices = lax.axis_size("tensor")
    if devices != 4:
        return collect(values, "tensor", 0)
    rows, width = values.shape
    parts = pl.pallas_call(
        functools.partial(_gather_kernel, devices),
        out_shape=jax.ShapeDtypeStruct((devices, rows, width), values.dtype),
        in_specs=[pl.BlockSpec(memory_space=pltpu.VMEM)],
        out_specs=pl.BlockSpec(memory_space=pltpu.VMEM),
        scratch_shapes=[
            pltpu.SemaphoreType.DMA((3,)),
            pltpu.SemaphoreType.DMA((3,)),
        ],
        compiler_params=pltpu.CompilerParams(collective_id=0, has_side_effects=True),
    )(values)
    return parts.reshape(devices * rows, width)


def _exchange_kernel(devices, x_ref, out_ref, send_sem, recv_sem):
    me = lax.axis_index("tensor")
    dp = lax.axis_index("dp")
    barrier = pltpu.get_barrier_semaphore()
    for step in range(1, devices):
        pl.semaphore_signal(
            barrier, inc=1, device_id=(dp, lax.rem(me + step, devices)), device_id_type=MESH
        )
    pl.semaphore_wait(barrier, devices - 1)
    copies = []
    for step in range(1, devices):
        peer = lax.rem(me + step, devices)
        copy = pltpu.make_async_remote_copy(
            src_ref=x_ref.at[peer],
            dst_ref=out_ref.at[me],
            send_sem=send_sem.at[step - 1],
            recv_sem=recv_sem.at[step - 1],
            device_id=(dp, peer),
            device_id_type=MESH,
        )
        copy.start()
        copies.append(copy)
    out_ref[me] = x_ref[me]
    for copy in copies:
        copy.wait()


def exchange_rows(parts):
    devices = parts.shape[0]
    return pl.pallas_call(
        functools.partial(_exchange_kernel, devices),
        out_shape=jax.ShapeDtypeStruct(parts.shape, parts.dtype),
        in_specs=[pl.BlockSpec(memory_space=pltpu.VMEM)],
        out_specs=pl.BlockSpec(memory_space=pltpu.VMEM),
        scratch_shapes=[
            pltpu.SemaphoreType.DMA((devices - 1,)),
            pltpu.SemaphoreType.DMA((devices - 1,)),
        ],
        compiler_params=pltpu.CompilerParams(collective_id=1, has_side_effects=True),
    )(parts)


def _reduce_kernel(devices, x_ref, out_ref, held, mate, pre, send_sem, recv_sem):
    me = lax.axis_index("tensor")
    dp = lax.axis_index("dp")
    sib = me + 1 - 2 * lax.rem(me, 2)
    far = lax.rem(me + 2, devices)
    other = lax.rem(sib + 2, devices)
    barrier = pltpu.get_barrier_semaphore()
    for peer in (sib, far):
        pl.semaphore_signal(barrier, inc=1, device_id=(dp, peer), device_id_type=MESH)
    pl.semaphore_wait(barrier, 2)
    own_copy = pltpu.make_async_remote_copy(
        src_ref=x_ref.at[sib],
        dst_ref=held.at[0],
        send_sem=send_sem.at[0],
        recv_sem=recv_sem.at[0],
        device_id=(dp, sib),
        device_id_type=MESH,
    )
    mate_copy = pltpu.make_async_remote_copy(
        src_ref=x_ref.at[other],
        dst_ref=mate,
        send_sem=send_sem.at[1],
        recv_sem=recv_sem.at[1],
        device_id=(dp, sib),
        device_id_type=MESH,
    )
    mate_copy.start()
    own_copy.start()
    mate_copy.wait_recv()
    pre[...] = (x_ref[far].astype(jnp.float32) + mate[...].astype(jnp.float32)).astype(pre.dtype)
    own_copy.wait_recv()
    out_ref[...] = x_ref[me].astype(jnp.float32) + held[0].astype(jnp.float32)
    far_copy = pltpu.make_async_remote_copy(
        src_ref=pre,
        dst_ref=held.at[1],
        send_sem=send_sem.at[2],
        recv_sem=recv_sem.at[2],
        device_id=(dp, far),
        device_id_type=MESH,
    )
    far_copy.start()
    far_copy.wait_recv()
    out_ref[...] += held[1].astype(jnp.float32)
    own_copy.wait_send()
    mate_copy.wait_send()
    far_copy.wait_send()


def summed_over_tensor(value):
    devices = lax.axis_size("tensor")
    parts = split_up(value, 0, devices)
    if devices != 4:
        return jnp.sum(exchange_rows(parts).astype(jnp.float32), axis=0)
    rows, width = parts.shape[1:]
    return pl.pallas_call(
        functools.partial(_reduce_kernel, devices),
        out_shape=jax.ShapeDtypeStruct((rows, width), jnp.float32),
        in_specs=[pl.BlockSpec(memory_space=pltpu.VMEM)],
        out_specs=pl.BlockSpec(memory_space=pltpu.VMEM),
        scratch_shapes=[
            pltpu.VMEM((2, rows, width), parts.dtype),
            pltpu.VMEM((rows, width), parts.dtype),
            pltpu.VMEM((rows, width), parts.dtype),
            pltpu.SemaphoreType.DMA((3,)),
            pltpu.SemaphoreType.DMA((3,)),
        ],
        compiler_params=pltpu.CompilerParams(collective_id=1, has_side_effects=True),
    )(parts)


def gather_forward(values):
    return gather_rows(values)


def gather_backward(values):
    return gather_rows(values)


def sum_forward(product, tok_rows):
    return summed_over_tensor(
        product(jnp.int32(0), tok_rows * lax.axis_size("tensor")).astype(jnp.bfloat16)
    )


def sum_backward(product, tok_rows):
    return summed_over_tensor(
        product(jnp.int32(0), tok_rows * lax.axis_size("tensor")).astype(jnp.bfloat16)
    )


def head_scores(query_head, key_head, allowed):
    raw = lax.dot_general(
        query_head, key_head, (((1,), (1,)), ((), ())), preferred_element_type=jnp.float32
    )
    return jnp.where(allowed, raw * HD ** (-0.5), masked_score)


def split_heads(queries, key_ext):
    heads_here = queries.shape[1] // HD
    query_heads = queries.reshape(queries.shape[0], heads_here, HD)
    key_heads = key_ext[0].reshape(key_ext.shape[1], heads_here, HD)
    value_heads = key_ext[1].reshape(key_ext.shape[1], heads_here, HD)
    return (heads_here, query_heads, key_heads, value_heads)


def merge_heads(per_head):
    return jnp.transpose(per_head, (1, 0, 2)).reshape(
        per_head.shape[1], per_head.shape[0] * per_head.shape[2]
    )


def _mask_from(sq_ref, pq_ref, sk_ref, rk_ref, pk_ref):
    return (sq_ref[...] == sk_ref[...]) & ((rk_ref[...] == 1) | (pq_ref[...] == pk_ref[...]))


def _mask_specs(rows, keys):
    column = pl.BlockSpec((rows, 1), lambda h: (0, 0))
    row = pl.BlockSpec((1, keys), lambda h: (0, 0))
    return [column, column, row, row, row]


def _attend_kernel(q_ref, k_ref, v_ref, sq_ref, pq_ref, sk_ref, rk_ref, pk_ref, o_ref, lse_ref):
    scores = lax.dot_general(
        q_ref[...], k_ref[...], (((1,), (1,)), ((), ())), preferred_element_type=jnp.float32
    )
    allowed = _mask_from(sq_ref, pq_ref, sk_ref, rk_ref, pk_ref)
    scores = jnp.where(allowed, scores * HD ** (-0.5), masked_score)
    row_top = jnp.max(scores, axis=1, keepdims=True)
    exponent = jnp.exp(scores - row_top)
    row_total = jnp.sum(exponent, axis=1, keepdims=True)
    prob_low = (exponent / row_total).astype(jnp.bfloat16)
    o_ref[...] = jnp.dot(prob_low, v_ref[...], preferred_element_type=jnp.float32)
    lse_ref[...] = row_top + jnp.log(row_total)


def attend_forward(queries, key_ext, mask_parts):
    heads_here = queries.shape[1] // HD
    rows, keys = mask_parts[0].shape[0], mask_parts[2].shape[1]
    query_heads = jnp.transpose(queries.reshape(rows, heads_here, HD), (1, 0, 2))
    key_heads = jnp.transpose(key_ext[0].reshape(keys, heads_here, HD), (1, 0, 2))
    value_heads = jnp.transpose(key_ext[1].reshape(keys, heads_here, HD), (1, 0, 2))
    head_outs, log_norm = pl.pallas_call(
        _attend_kernel,
        grid=(heads_here,),
        out_shape=(
            jax.ShapeDtypeStruct((heads_here, rows, HD), jnp.float32),
            jax.ShapeDtypeStruct((heads_here, rows, 1), jnp.float32),
        ),
        in_specs=[
            pl.BlockSpec((None, rows, HD), lambda h: (h, 0, 0)),
            pl.BlockSpec((None, keys, HD), lambda h: (h, 0, 0)),
            pl.BlockSpec((None, keys, HD), lambda h: (h, 0, 0)),
            *_mask_specs(rows, keys),
        ],
        out_specs=(
            pl.BlockSpec((None, rows, HD), lambda h: (h, 0, 0)),
            pl.BlockSpec((None, rows, 1), lambda h: (h, 0, 0)),
        ),
        compiler_params=pltpu.CompilerParams(vmem_limit_bytes=60 * 1024 * 1024),
    )(query_heads, key_heads, value_heads, *mask_parts)
    return (merge_heads(head_outs), log_norm[:, :, 0])


def attend_forward_xla(queries, key_ext, allowed):
    heads_here, query_heads, key_heads, value_heads = split_heads(queries, key_ext)

    def one_head(head_index):
        query_head = lax.dynamic_index_in_dim(query_heads, head_index, 1, keepdims=False)
        key_head = lax.dynamic_index_in_dim(key_heads, head_index, 1, keepdims=False)
        value_head = lax.dynamic_index_in_dim(value_heads, head_index, 1, keepdims=False)
        scores = head_scores(query_head, key_head, allowed)
        row_top = jnp.max(scores, axis=1, keepdims=True)
        exponent = jnp.exp(scores - row_top)
        row_total = jnp.sum(exponent, axis=1, keepdims=True)
        prob_low = (exponent / row_total).astype(jnp.bfloat16)
        head_out = jnp.dot(prob_low, value_head, preferred_element_type=jnp.float32)
        return (head_out, (row_top + jnp.log(row_total))[:, 0])

    head_outs, log_norm = lax.map(one_head, jnp.arange(heads_here, dtype=jnp.int32))
    return (merge_heads(head_outs), log_norm)


def _attend_back_kernel(
    q_ref, k_ref, v_ref, g_ref, lse_ref, sq_ref, pq_ref, sk_ref, rk_ref, pk_ref, dq_ref, dk_ref, dv_ref
):
    query_head, key_head, grad_head = q_ref[...], k_ref[...], g_ref[...]
    scores = lax.dot_general(
        query_head, key_head, (((1,), (1,)), ((), ())), preferred_element_type=jnp.float32
    )
    allowed = _mask_from(sq_ref, pq_ref, sk_ref, rk_ref, pk_ref)
    scores = jnp.where(allowed, scores * HD ** (-0.5), masked_score)
    prob_full = jnp.exp(scores - lse_ref[...])
    prob_low = prob_full.astype(jnp.bfloat16)
    dv_ref[...] = lax.dot_general(
        prob_low, grad_head, (((0,), (0,)), ((), ())), preferred_element_type=jnp.float32
    )
    grad_prob = lax.dot_general(
        grad_head, v_ref[...], (((1,), (1,)), ((), ())), preferred_element_type=jnp.float32
    )
    grad_score = (
        prob_full * (grad_prob - jnp.sum(prob_full * grad_prob, axis=1, keepdims=True))
    ).astype(jnp.bfloat16)
    dq_ref[...] = jnp.dot(grad_score, key_head, preferred_element_type=jnp.float32) * HD ** (-0.5)
    dk_ref[...] = lax.dot_general(
        grad_score, query_head, (((0,), (0,)), ((), ())), preferred_element_type=jnp.float32
    ) * HD ** (-0.5)


def attend_backward(queries, key_ext, mask_parts, log_norm, grad_attended):
    heads_here = queries.shape[1] // HD
    rows, keys = mask_parts[0].shape[0], mask_parts[2].shape[1]

    def by_head(values, count):
        return jnp.transpose(values.reshape(count, heads_here, HD), (1, 0, 2))

    row_spec = pl.BlockSpec((None, rows, HD), lambda h: (h, 0, 0))
    key_spec = pl.BlockSpec((None, keys, HD), lambda h: (h, 0, 0))
    grad_queries, grad_keys, grad_values = pl.pallas_call(
        _attend_back_kernel,
        grid=(heads_here,),
        out_shape=(
            jax.ShapeDtypeStruct((heads_here, rows, HD), jnp.float32),
            jax.ShapeDtypeStruct((heads_here, keys, HD), jnp.float32),
            jax.ShapeDtypeStruct((heads_here, keys, HD), jnp.float32),
        ),
        in_specs=[
            row_spec,
            key_spec,
            key_spec,
            row_spec,
            pl.BlockSpec((None, rows, 1), lambda h: (h, 0, 0)),
            *_mask_specs(rows, keys),
        ],
        out_specs=(row_spec, key_spec, key_spec),
        compiler_params=pltpu.CompilerParams(vmem_limit_bytes=60 * 1024 * 1024),
    )(
        by_head(queries, rows),
        by_head(key_ext[0], keys),
        by_head(key_ext[1], keys),
        by_head(grad_attended, rows),
        log_norm[:, :, None],
        *mask_parts,
    )
    return (merge_heads(grad_queries), merge_heads(grad_keys), merge_heads(grad_values))


def attend_backward_xla(queries, key_ext, allowed, log_norm, grad_attended):
    heads_here, query_heads, key_heads, value_heads = split_heads(queries, key_ext)
    grad_heads = grad_attended.reshape(grad_attended.shape[0], heads_here, HD)

    def one_head(inputs):
        head_index, norm_row = inputs
        query_head = lax.dynamic_index_in_dim(query_heads, head_index, 1, keepdims=False)
        key_head = lax.dynamic_index_in_dim(key_heads, head_index, 1, keepdims=False)
        value_head = lax.dynamic_index_in_dim(value_heads, head_index, 1, keepdims=False)
        grad_head = lax.dynamic_index_in_dim(grad_heads, head_index, 1, keepdims=False)
        prob_full = jnp.exp(head_scores(query_head, key_head, allowed) - norm_row[:, None])
        prob_low = prob_full.astype(jnp.bfloat16)
        grad_value = lax.dot_general(
            prob_low, grad_head, (((0,), (0,)), ((), ())), preferred_element_type=jnp.float32
        )
        grad_prob = lax.dot_general(
            grad_head, value_head, (((1,), (1,)), ((), ())), preferred_element_type=jnp.float32
        )
        grad_score = (
            prob_full * (grad_prob - jnp.sum(prob_full * grad_prob, axis=1, keepdims=True))
        ).astype(jnp.bfloat16)
        grad_query = jnp.dot(grad_score, key_head, preferred_element_type=jnp.float32) * HD ** (
            -0.5
        )
        grad_key = lax.dot_general(
            grad_score, query_head, (((0,), (0,)), ((), ())), preferred_element_type=jnp.float32
        ) * HD ** (-0.5)
        return (grad_query, grad_key, grad_value)

    grad_queries, grad_keys, grad_values = lax.map(
        one_head, (jnp.arange(heads_here, dtype=jnp.int32), log_norm)
    )
    return (merge_heads(grad_queries), merge_heads(grad_keys), merge_heads(grad_values))


def local(
    tokens,
    segment,
    real_token,
    qkv_weight,
    out_weight,
    up_weight,
    down_weight,
    unit_bias,
    norm_gain,
    row_bias,
    cotangent,
):
    tok_rows = tokens.shape[0]
    tensor_size = lax.axis_size("tensor")
    group_rows = tok_rows * tensor_size
    margin = IMG - 1
    cols_here = qkv_weight.shape[3]
    dp_index = lax.axis_index("dp")
    tensor_index = lax.axis_index("tensor")
    group_first = dp_index * group_rows
    own_first = group_first + tensor_index * tok_rows
    segment_pad = jnp.pad(segment, (margin, margin), constant_values=-1)
    real_pad = jnp.pad(real_token, (margin, margin))
    segment_query = lax.dynamic_slice_in_dim(segment, group_first, group_rows, 0)
    segment_key = lax.dynamic_slice_in_dim(segment_pad, group_first, group_rows + 2 * margin, 0)
    real_key = lax.dynamic_slice_in_dim(real_pad, group_first, group_rows + 2 * margin, 0)
    place_query = jnp.arange(group_rows, dtype=jnp.int32)
    place_key = jnp.arange(group_rows + 2 * margin, dtype=jnp.int32) - margin
    allowed = (
        segment_query[:, None],
        place_query[:, None],
        segment_key[None, :],
        real_key[None, :],
        place_key[None, :],
    )
    own_real = lax.dynamic_slice_in_dim(real_token, own_first, tok_rows, 0).astype(jnp.float32)
    stream = tokens.astype(jnp.float32)
    layer_index = 0
    qkv_local = jnp.moveaxis(qkv_weight[layer_index], 1, 0)
    out_local, up_local, down_local = (
        out_weight[layer_index],
        up_weight[layer_index],
        down_weight[layer_index],
    )
    gain_now = norm_gain[layer_index].astype(jnp.float32)
    shift_now = row_bias[layer_index].astype(jnp.float32)
    bias_now = unit_bias[layer_index].astype(jnp.float32)
    normed_full = gather_forward(layer_norm(stream, gain_now[0], shift_now[0]).astype(jnp.bfloat16))
    qkv_full = jnp.moveaxis(collect(qkv_local, "dp", 0), 0, 1)
    projected = jnp.einsum("gd,sde->sge", normed_full, qkv_full, preferred_element_type=jnp.float32)
    queries = (projected[0] + bias_now[0]).astype(jnp.bfloat16)
    queries, out_local, up_local, down_local = lax.optimization_barrier(
        (queries, out_local, up_local, down_local)
    )
    out_full = collect(out_local, "dp", 0)
    up_full = collect(up_local, "dp", 0)
    down_full = collect(down_local, "dp", 0)
    gathered = (qkv_full, out_full, up_full, down_full)
    key_value = jnp.stack([projected[1], projected[2] + bias_now[1]]).astype(jnp.bfloat16)
    key_ext = with_halo(key_value, (("dp", 1),), margin)
    attended, log_norm = attend_forward(queries, key_ext, allowed)
    attended = attended.astype(jnp.bfloat16)

    def attention_term(first_row, row_count):
        return lax.dot_general(
            attended, out_full, (((1,), (1,)), ((), ())), preferred_element_type=jnp.float32
        )

    middle = stream + sum_forward(attention_term, tok_rows) + shift_now[1]
    second_full = gather_forward(layer_norm(middle, gain_now[1], shift_now[2]).astype(jnp.bfloat16))
    hidden = (
        jnp.einsum("gd,dre->gre", second_full, up_full, preferred_element_type=jnp.float32)
        + bias_now[2:][None]
    )
    active = exact_gelu(hidden).astype(jnp.bfloat16)

    def feed_term(first_row, row_count):
        return jnp.einsum("gre,ore->go", active, down_full, preferred_element_type=jnp.float32)

    kept_weights = gathered
    records = [
        (
            stream,
            middle,
            normed_full,
            second_full,
            queries,
            key_ext,
            log_norm,
            attended,
            hidden,
            active,
            kept_weights,
        )
    ]
    stream = middle + sum_forward(feed_term, tok_rows) + shift_now[3]
    gradient = cotangent.astype(jnp.float32) * own_real[:, None]
    local_qkv = [None] * LAYERS
    local_out = [None] * LAYERS
    local_up = [None] * LAYERS
    local_down = [None] * LAYERS
    unit_grads = [None] * LAYERS
    gain_grads = [None] * LAYERS
    shift_grads = [None] * LAYERS
    for layer_index in reversed(range(LAYERS)):
        (
            stream_in,
            middle,
            normed_full,
            second_full,
            queries,
            key_ext,
            log_norm,
            attended,
            hidden,
            active,
            kept_weights,
        ) = records[layer_index]
        qkv_full, out_full, up_full, down_full = kept_weights
        gain_now = norm_gain[layer_index].astype(jnp.float32)
        shift_now = row_bias[layer_index].astype(jnp.float32)
        shift_three = jnp.sum(gradient, axis=0)
        grad_mlp = gather_backward(gradient.astype(jnp.bfloat16))
        down_grad = scatter_rows(
            jnp.einsum("go,gre->ore", grad_mlp, active, preferred_element_type=jnp.float32)
        )
        grad_active = jnp.einsum(
            "go,ore->gre", grad_mlp, down_full, preferred_element_type=jnp.float32
        )
        gelu_again, gelu_pull = jax.vjp(exact_gelu, hidden)
        grad_hidden = gelu_pull(grad_active)[0].astype(jnp.bfloat16)
        up_bias_grad = jnp.sum(grad_hidden.astype(jnp.float32), axis=0)
        up_grad = scatter_rows(
            jnp.einsum("gd,gre->dre", second_full, grad_hidden, preferred_element_type=jnp.float32)
        )

        def second_term(first_row, row_count):
            return jnp.einsum(
                "gre,dre->gd", grad_hidden, up_full, preferred_element_type=jnp.float32
            )

        grad_second = sum_backward(second_term, tok_rows)
        second_again, second_pull = jax.vjp(layer_norm, middle, gain_now[1], shift_now[2])
        grad_mid_norm, gain_one, shift_two = second_pull(grad_second)
        grad_middle = gradient + grad_mid_norm
        shift_one = jnp.sum(grad_middle, axis=0)
        grad_proj = gather_backward(grad_middle.astype(jnp.bfloat16))
        out_grad = scatter_rows(
            lax.dot_general(
                grad_proj, attended, (((0,), (0,)), ((), ())), preferred_element_type=jnp.float32
            )
        )
        grad_attended = jnp.dot(grad_proj, out_full, preferred_element_type=jnp.float32).astype(
            jnp.bfloat16
        )
        grad_query, grad_key_ext, grad_value_ext = attend_backward(
            queries, key_ext, allowed, log_norm, grad_attended
        )
        grad_pair_ext = jnp.stack([grad_key_ext, grad_value_ext])
        from_next = from_behind(grad_pair_ext[:, :margin].astype(jnp.bfloat16), "dp", -1).astype(
            jnp.float32
        )
        from_prev = from_behind(
            grad_pair_ext[:, margin + group_rows :].astype(jnp.bfloat16), "dp", 1
        ).astype(jnp.float32)
        grad_pair = grad_pair_ext[:, margin : margin + group_rows]
        grad_pair = (
            grad_pair.at[:, group_rows - margin :].add(from_next).at[:, :margin].add(from_prev)
        )
        grad_triple = jnp.concatenate(
            [grad_query.astype(jnp.bfloat16)[None], grad_pair.astype(jnp.bfloat16)], axis=0
        )
        qkv_grad = jnp.moveaxis(
            scatter_rows(
                jnp.einsum(
                    "gd,sge->dse", normed_full, grad_triple, preferred_element_type=jnp.float32
                )
            ),
            0,
            1,
        )
        triple_sums = jnp.sum(grad_triple.astype(jnp.float32), axis=1)

        def first_term(first_row, row_count):
            return jnp.einsum(
                "sge,sde->gd", grad_triple, qkv_full, preferred_element_type=jnp.float32
            )

        grad_first = sum_backward(first_term, tok_rows)
        first_again, first_pull = jax.vjp(layer_norm, stream_in, gain_now[0], shift_now[0])
        grad_in_norm, gain_zero, shift_zero = first_pull(grad_first)
        gradient = grad_middle + grad_in_norm
        unit_grads[layer_index] = jnp.concatenate(
            [triple_sums[0][None], triple_sums[2][None], up_bias_grad], axis=0
        )
        gain_grads[layer_index] = jnp.stack([gain_zero, gain_one])
        shift_grads[layer_index] = jnp.stack([shift_zero, shift_one, shift_two, shift_three])
        local_qkv[layer_index] = qkv_grad
        local_out[layer_index] = out_grad
        local_up[layer_index] = up_grad
        local_down[layer_index] = down_grad
    grad_qkv = jnp.stack(local_qkv).astype(jnp.float32)
    grad_out = jnp.stack(local_out).astype(jnp.float32)
    grad_up = jnp.stack(local_up).astype(jnp.float32)
    grad_down = jnp.stack(local_down).astype(jnp.float32)
    unit_local = jnp.stack(unit_grads)
    unit_wide = jnp.zeros((LAYERS, unit_local.shape[1], cols_here * tensor_size), jnp.float32)
    unit_wide = lax.dynamic_update_slice_in_dim(unit_wide, unit_local, tensor_index * cols_here, 2)
    small = jnp.concatenate(
        [jnp.stack(gain_grads), jnp.stack(shift_grads), unit_wide], axis=1
    )
    small_total = jnp.sum(from_everyone(small, "dp"), axis=0)
    small_total = jnp.sum(from_everyone(small_total, "tensor"), axis=0)
    gain_total = small_total[:, :2]
    shift_total = small_total[:, 2:6]
    unit_total = small_total[:, 6:]
    unit_mine = lax.dynamic_slice_in_dim(unit_total, tensor_index * cols_here, cols_here, 2)
    return (
        stream.astype(jnp.bfloat16),
        gradient.astype(jnp.bfloat16),
        grad_qkv,
        grad_out,
        grad_up,
        grad_down,
        unit_mine,
        gain_total,
        shift_total,
    )


def solution(mesh):
    placed = (
        P(("dp", "tensor"), None),
        P(),
        P(),
        P(None, None, "dp", "tensor"),
        P(None, "dp", "tensor"),
        P(None, "dp", None, "tensor"),
        P(None, "dp", None, "tensor"),
        P(None, None, "tensor"),
        P(),
        P(),
        P(("dp", "tensor"), None),
    )
    return jax.shard_map(
        local,
        mesh=mesh,
        in_specs=placed,
        out_specs=(
            P(("dp", "tensor"), None),
            P(("dp", "tensor"), None),
            P(None, None, "dp", "tensor"),
            P(None, "dp", "tensor"),
            P(None, "dp", None, "tensor"),
            P(None, "dp", None, "tensor"),
            P(None, None, "tensor"),
            P(),
            P(),
        ),
        check_vma=False,
    )
```

```python
import functools
import math

import jax
import jax.numpy as jnp
from jax import lax
from jax.experimental import pallas as pl
from jax.experimental.pallas import tpu as pltpu
from jax.sharding import PartitionSpec as P

MESH = pl.DeviceIdType.MESH

LAYERS = 1
IMG = 577
HD = 64


norm_eps = 1e-06
masked_score = -1e30


def from_everyone(value, axis):
    devices = lax.axis_size(axis)
    return lax.all_to_all(
        jnp.broadcast_to(value[None], (devices, *value.shape)), axis, 0, 0, tiled=True
    )


def joined_along(parts, dim):
    dims = list(parts.shape[1:])
    dims[dim] *= parts.shape[0]
    return jnp.moveaxis(parts, 0, dim).reshape(dims)


def collect(value, axis, dim):
    parts = from_everyone(value, axis)
    return joined_along(parts, dim)


def split_up(value, dim, devices):
    dims = value.shape
    parts = value.reshape(*dims[:dim], devices, dims[dim] // devices, *dims[dim + 1 :])
    return jnp.moveaxis(parts, dim, 0)


def summed_on_arrival(value, axis, dim):
    devices = lax.axis_size(axis)
    parts = lax.all_to_all(split_up(value, dim, devices), axis, 0, 0, tiled=True)
    return jnp.sum(parts.astype(jnp.float32), axis=0)


def rows_first(arrays, axis, dims):
    turned = [jnp.moveaxis(a, dim, 0) for a, dim in zip(arrays, dims)]
    both = jnp.concatenate([t.reshape(len(t), -1) for t in turned], axis=1)
    filled, at, outs = (lax.all_gather(both, axis, axis=0, tiled=True), 0, [])
    for t, dim in zip(turned, dims):
        slab = filled[:, at : at + t[0].size].reshape(-1, *t.shape[1:])
        outs.append(jnp.moveaxis(slab, 0, dim))
        at += t[0].size
    return tuple(outs)


def with_halo(value, sides, width):
    for axis, dim in sides:
        devices, length = (lax.axis_size(axis), value.shape[dim])
        up = [(i, (i + 1) % devices) for i in range(devices - 1)]
        down = [(j, i) for i, j in up]
        last = lax.slice_in_dim(value, length - width, length, axis=dim)
        initial = lax.slice_in_dim(value, 0, width, axis=dim)
        before = lax.ppermute(last, axis, up)
        after = lax.ppermute(initial, axis, down)
        value = jnp.concatenate([before, value, after], axis=dim)
    return value


def from_behind(block, axis, distance):
    devices = range(lax.axis_size(axis))
    route = [(i - distance, i) for i in devices if i - distance in devices]
    return lax.ppermute(block, axis, route)


def side_by_side(arrays, axis, dim, along):
    widths = [math.prod(a.shape[along:]) for a in arrays]
    both = jnp.concatenate(
        [a.reshape(*a.shape[:along], w) for a, w in zip(arrays, widths)], axis=along
    )
    filled = lax.psum_scatter(both, axis, scatter_dimension=dim, tiled=True)
    parts = jnp.split(filled, [sum(widths[:k]) for k in range(1, len(widths))], axis=along)
    return tuple(
        (b.reshape(*filled.shape[:along], *a.shape[along:]) for a, b in zip(arrays, parts))
    )


def scatter_rows(grad):
    return summed_on_arrival(grad.astype(jnp.bfloat16), "dp", 0)


def layer_norm(values, gain_row, shift_row):
    center = values - jnp.mean(values, axis=-1, keepdims=True)
    spread = jnp.mean(center * center, axis=-1, keepdims=True)
    return center * lax.rsqrt(spread + norm_eps) * gain_row + shift_row


def exact_gelu(values):
    return jax.nn.gelu(values, approximate=False)


def _gather_kernel(devices, x_ref, out_ref, send_sem, recv_sem):
    me = lax.axis_index("tensor")
    dp = lax.axis_index("dp")
    sib = me + 1 - 2 * lax.rem(me, 2)
    far = lax.rem(me + 2, devices)
    barrier = pltpu.get_barrier_semaphore()
    for peer in (sib, far):
        pl.semaphore_signal(barrier, inc=1, device_id=(dp, peer), device_id_type=MESH)
    pl.semaphore_wait(barrier, 2)
    near_copy = pltpu.make_async_remote_copy(
        src_ref=x_ref,
        dst_ref=out_ref.at[me],
        send_sem=send_sem.at[0],
        recv_sem=recv_sem.at[0],
        device_id=(dp, sib),
        device_id_type=MESH,
    )
    far_copy = pltpu.make_async_remote_copy(
        src_ref=x_ref,
        dst_ref=out_ref.at[me],
        send_sem=send_sem.at[1],
        recv_sem=recv_sem.at[1],
        device_id=(dp, far),
        device_id_type=MESH,
    )
    far_copy.start()
    near_copy.start()
    out_ref[me] = x_ref[...]
    far_copy.wait_recv()
    relay = pltpu.make_async_remote_copy(
        src_ref=out_ref.at[far],
        dst_ref=out_ref.at[far],
        send_sem=send_sem.at[2],
        recv_sem=recv_sem.at[2],
        device_id=(dp, sib),
        device_id_type=MESH,
    )
    relay.start()
    near_copy.wait_send()
    near_copy.wait_recv()
    far_copy.wait_send()
    relay.wait_send()
    relay.wait_recv()


def gather_rows(values):
    devices = lax.axis_size("tensor")
    if devices != 4:
        return collect(values, "tensor", 0)
    rows, width = values.shape
    parts = pl.pallas_call(
        functools.partial(_gather_kernel, devices),
        out_shape=jax.ShapeDtypeStruct((devices, rows, width), values.dtype),
        in_specs=[pl.BlockSpec(memory_space=pltpu.VMEM)],
        out_specs=pl.BlockSpec(memory_space=pltpu.VMEM),
        scratch_shapes=[
            pltpu.SemaphoreType.DMA((3,)),
            pltpu.SemaphoreType.DMA((3,)),
        ],
        compiler_params=pltpu.CompilerParams(collective_id=0, has_side_effects=True),
    )(values)
    return parts.reshape(devices * rows, width)


def _exchange_kernel(devices, x_ref, out_ref, send_sem, recv_sem):
    me = lax.axis_index("tensor")
    dp = lax.axis_index("dp")
    barrier = pltpu.get_barrier_semaphore()
    for step in range(1, devices):
        pl.semaphore_signal(
            barrier, inc=1, device_id=(dp, lax.rem(me + step, devices)), device_id_type=MESH
        )
    pl.semaphore_wait(barrier, devices - 1)
    copies = []
    for step in range(1, devices):
        peer = lax.rem(me + step, devices)
        copy = pltpu.make_async_remote_copy(
            src_ref=x_ref.at[peer],
            dst_ref=out_ref.at[me],
            send_sem=send_sem.at[step - 1],
            recv_sem=recv_sem.at[step - 1],
            device_id=(dp, peer),
            device_id_type=MESH,
        )
        copy.start()
        copies.append(copy)
    out_ref[me] = x_ref[me]
    for copy in copies:
        copy.wait()


def exchange_rows(parts):
    devices = parts.shape[0]
    return pl.pallas_call(
        functools.partial(_exchange_kernel, devices),
        out_shape=jax.ShapeDtypeStruct(parts.shape, parts.dtype),
        in_specs=[pl.BlockSpec(memory_space=pltpu.VMEM)],
        out_specs=pl.BlockSpec(memory_space=pltpu.VMEM),
        scratch_shapes=[
            pltpu.SemaphoreType.DMA((devices - 1,)),
            pltpu.SemaphoreType.DMA((devices - 1,)),
        ],
        compiler_params=pltpu.CompilerParams(collective_id=1, has_side_effects=True),
    )(parts)


def _reduce_kernel(devices, x_ref, out_ref, held, mate, pre, send_sem, recv_sem):
    me = lax.axis_index("tensor")
    dp = lax.axis_index("dp")
    sib = me + 1 - 2 * lax.rem(me, 2)
    far = lax.rem(me + 2, devices)
    other = lax.rem(sib + 2, devices)
    barrier = pltpu.get_barrier_semaphore()
    for peer in (sib, far):
        pl.semaphore_signal(barrier, inc=1, device_id=(dp, peer), device_id_type=MESH)
    pl.semaphore_wait(barrier, 2)
    own_copy = pltpu.make_async_remote_copy(
        src_ref=x_ref.at[sib],
        dst_ref=held.at[0],
        send_sem=send_sem.at[0],
        recv_sem=recv_sem.at[0],
        device_id=(dp, sib),
        device_id_type=MESH,
    )
    mate_copy = pltpu.make_async_remote_copy(
        src_ref=x_ref.at[other],
        dst_ref=mate,
        send_sem=send_sem.at[1],
        recv_sem=recv_sem.at[1],
        device_id=(dp, sib),
        device_id_type=MESH,
    )
    mate_copy.start()
    own_copy.start()
    mate_copy.wait_recv()
    pre[...] = (x_ref[far].astype(jnp.float32) + mate[...].astype(jnp.float32)).astype(pre.dtype)
    own_copy.wait_recv()
    out_ref[...] = x_ref[me].astype(jnp.float32) + held[0].astype(jnp.float32)
    far_copy = pltpu.make_async_remote_copy(
        src_ref=pre,
        dst_ref=held.at[1],
        send_sem=send_sem.at[2],
        recv_sem=recv_sem.at[2],
        device_id=(dp, far),
        device_id_type=MESH,
    )
    far_copy.start()
    far_copy.wait_recv()
    out_ref[...] += held[1].astype(jnp.float32)
    own_copy.wait_send()
    mate_copy.wait_send()
    far_copy.wait_send()


def summed_over_tensor(value):
    devices = lax.axis_size("tensor")
    parts = split_up(value, 0, devices)
    if devices != 4:
        return jnp.sum(exchange_rows(parts).astype(jnp.float32), axis=0)
    rows, width = parts.shape[1:]
    return pl.pallas_call(
        functools.partial(_reduce_kernel, devices),
        out_shape=jax.ShapeDtypeStruct((rows, width), jnp.float32),
        in_specs=[pl.BlockSpec(memory_space=pltpu.VMEM)],
        out_specs=pl.BlockSpec(memory_space=pltpu.VMEM),
        scratch_shapes=[
            pltpu.VMEM((2, rows, width), parts.dtype),
            pltpu.VMEM((rows, width), parts.dtype),
            pltpu.VMEM((rows, width), parts.dtype),
            pltpu.SemaphoreType.DMA((3,)),
            pltpu.SemaphoreType.DMA((3,)),
        ],
        compiler_params=pltpu.CompilerParams(collective_id=1, has_side_effects=True),
    )(parts)


def gather_forward(values):
    return gather_rows(values)


def gather_backward(values):
    return gather_rows(values)


def sum_forward(product, tok_rows):
    return summed_over_tensor(
        product(jnp.int32(0), tok_rows * lax.axis_size("tensor")).astype(jnp.bfloat16)
    )


def sum_backward(product, tok_rows):
    return summed_over_tensor(
        product(jnp.int32(0), tok_rows * lax.axis_size("tensor")).astype(jnp.bfloat16)
    )


def head_scores(query_head, key_head, allowed):
    raw = lax.dot_general(
        query_head, key_head, (((1,), (1,)), ((), ())), preferred_element_type=jnp.float32
    )
    return jnp.where(allowed, raw * HD ** (-0.5), masked_score)


def split_heads(queries, key_ext):
    heads_here = queries.shape[1] // HD
    query_heads = queries.reshape(queries.shape[0], heads_here, HD)
    key_heads = key_ext[0].reshape(key_ext.shape[1], heads_here, HD)
    value_heads = key_ext[1].reshape(key_ext.shape[1], heads_here, HD)
    return (heads_here, query_heads, key_heads, value_heads)


def merge_heads(per_head):
    return jnp.transpose(per_head, (1, 0, 2)).reshape(
        per_head.shape[1], per_head.shape[0] * per_head.shape[2]
    )


def _mask_from(sq_ref, pq_ref, sk_ref, rk_ref, pk_ref):
    return (sq_ref[...] == sk_ref[...]) & ((rk_ref[...] == 1) | (pq_ref[...] == pk_ref[...]))


def _mask_specs(rows, keys):
    column = pl.BlockSpec((rows, 1), lambda h: (0, 0))
    row = pl.BlockSpec((1, keys), lambda h: (0, 0))
    return [column, column, row, row, row]


def _attend_kernel(q_ref, k_ref, v_ref, sq_ref, pq_ref, sk_ref, rk_ref, pk_ref, o_ref, lse_ref):
    scores = lax.dot_general(
        q_ref[...], k_ref[...], (((1,), (1,)), ((), ())), preferred_element_type=jnp.float32
    )
    allowed = _mask_from(sq_ref, pq_ref, sk_ref, rk_ref, pk_ref)
    scores = jnp.where(allowed, scores * HD ** (-0.5), masked_score)
    row_top = jnp.max(scores, axis=1, keepdims=True)
    exponent = jnp.exp(scores - row_top)
    row_total = jnp.sum(exponent, axis=1, keepdims=True)
    prob_low = (exponent / row_total).astype(jnp.bfloat16)
    o_ref[...] = jnp.dot(prob_low, v_ref[...], preferred_element_type=jnp.float32)
    lse_ref[...] = row_top + jnp.log(row_total)


def attend_forward(queries, key_ext, mask_parts):
    heads_here = queries.shape[1] // HD
    rows, keys = mask_parts[0].shape[0], mask_parts[2].shape[1]
    query_heads = jnp.transpose(queries.reshape(rows, heads_here, HD), (1, 0, 2))
    key_heads = jnp.transpose(key_ext[0].reshape(keys, heads_here, HD), (1, 0, 2))
    value_heads = jnp.transpose(key_ext[1].reshape(keys, heads_here, HD), (1, 0, 2))
    head_outs, log_norm = pl.pallas_call(
        _attend_kernel,
        grid=(heads_here,),
        out_shape=(
            jax.ShapeDtypeStruct((heads_here, rows, HD), jnp.float32),
            jax.ShapeDtypeStruct((heads_here, rows, 1), jnp.float32),
        ),
        in_specs=[
            pl.BlockSpec((None, rows, HD), lambda h: (h, 0, 0)),
            pl.BlockSpec((None, keys, HD), lambda h: (h, 0, 0)),
            pl.BlockSpec((None, keys, HD), lambda h: (h, 0, 0)),
            *_mask_specs(rows, keys),
        ],
        out_specs=(
            pl.BlockSpec((None, rows, HD), lambda h: (h, 0, 0)),
            pl.BlockSpec((None, rows, 1), lambda h: (h, 0, 0)),
        ),
        compiler_params=pltpu.CompilerParams(vmem_limit_bytes=60 * 1024 * 1024),
    )(query_heads, key_heads, value_heads, *mask_parts)
    return (merge_heads(head_outs), log_norm[:, :, 0])


def attend_forward_xla(queries, key_ext, allowed):
    heads_here, query_heads, key_heads, value_heads = split_heads(queries, key_ext)

    def one_head(head_index):
        query_head = lax.dynamic_index_in_dim(query_heads, head_index, 1, keepdims=False)
        key_head = lax.dynamic_index_in_dim(key_heads, head_index, 1, keepdims=False)
        value_head = lax.dynamic_index_in_dim(value_heads, head_index, 1, keepdims=False)
        scores = head_scores(query_head, key_head, allowed)
        row_top = jnp.max(scores, axis=1, keepdims=True)
        exponent = jnp.exp(scores - row_top)
        row_total = jnp.sum(exponent, axis=1, keepdims=True)
        prob_low = (exponent / row_total).astype(jnp.bfloat16)
        head_out = jnp.dot(prob_low, value_head, preferred_element_type=jnp.float32)
        return (head_out, (row_top + jnp.log(row_total))[:, 0])

    head_outs, log_norm = lax.map(one_head, jnp.arange(heads_here, dtype=jnp.int32))
    return (merge_heads(head_outs), log_norm)


def _attend_back_kernel(
    q_ref, k_ref, v_ref, g_ref, lse_ref, sq_ref, pq_ref, sk_ref, rk_ref, pk_ref, dq_ref, dk_ref, dv_ref
):
    query_head, key_head, grad_head = q_ref[...], k_ref[...], g_ref[...]
    scores = lax.dot_general(
        query_head, key_head, (((1,), (1,)), ((), ())), preferred_element_type=jnp.float32
    )
    allowed = _mask_from(sq_ref, pq_ref, sk_ref, rk_ref, pk_ref)
    scores = jnp.where(allowed, scores * HD ** (-0.5), masked_score)
    prob_full = jnp.exp(scores - lse_ref[...])
    prob_low = prob_full.astype(jnp.bfloat16)
    dv_ref[...] = lax.dot_general(
        prob_low, grad_head, (((0,), (0,)), ((), ())), preferred_element_type=jnp.float32
    )
    grad_prob = lax.dot_general(
        grad_head, v_ref[...], (((1,), (1,)), ((), ())), preferred_element_type=jnp.float32
    )
    grad_score = (
        prob_full * (grad_prob - jnp.sum(prob_full * grad_prob, axis=1, keepdims=True))
    ).astype(jnp.bfloat16)
    dq_ref[...] = jnp.dot(grad_score, key_head, preferred_element_type=jnp.float32) * HD ** (-0.5)
    dk_ref[...] = lax.dot_general(
        grad_score, query_head, (((0,), (0,)), ((), ())), preferred_element_type=jnp.float32
    ) * HD ** (-0.5)


def attend_backward(queries, key_ext, mask_parts, log_norm, grad_attended):
    heads_here = queries.shape[1] // HD
    rows, keys = mask_parts[0].shape[0], mask_parts[2].shape[1]

    def by_head(values, count):
        return jnp.transpose(values.reshape(count, heads_here, HD), (1, 0, 2))

    row_spec = pl.BlockSpec((None, rows, HD), lambda h: (h, 0, 0))
    key_spec = pl.BlockSpec((None, keys, HD), lambda h: (h, 0, 0))
    grad_queries, grad_keys, grad_values = pl.pallas_call(
        _attend_back_kernel,
        grid=(heads_here,),
        out_shape=(
            jax.ShapeDtypeStruct((heads_here, rows, HD), jnp.float32),
            jax.ShapeDtypeStruct((heads_here, keys, HD), jnp.float32),
            jax.ShapeDtypeStruct((heads_here, keys, HD), jnp.float32),
        ),
        in_specs=[
            row_spec,
            key_spec,
            key_spec,
            row_spec,
            pl.BlockSpec((None, rows, 1), lambda h: (h, 0, 0)),
            *_mask_specs(rows, keys),
        ],
        out_specs=(row_spec, key_spec, key_spec),
        compiler_params=pltpu.CompilerParams(vmem_limit_bytes=60 * 1024 * 1024),
    )(
        by_head(queries, rows),
        by_head(key_ext[0], keys),
        by_head(key_ext[1], keys),
        by_head(grad_attended, rows),
        log_norm[:, :, None],
        *mask_parts,
    )
    return (merge_heads(grad_queries), merge_heads(grad_keys), merge_heads(grad_values))


def attend_backward_xla(queries, key_ext, allowed, log_norm, grad_attended):
    heads_here, query_heads, key_heads, value_heads = split_heads(queries, key_ext)
    grad_heads = grad_attended.reshape(grad_attended.shape[0], heads_here, HD)

    def one_head(inputs):
        head_index, norm_row = inputs
        query_head = lax.dynamic_index_in_dim(query_heads, head_index, 1, keepdims=False)
        key_head = lax.dynamic_index_in_dim(key_heads, head_index, 1, keepdims=False)
        value_head = lax.dynamic_index_in_dim(value_heads, head_index, 1, keepdims=False)
        grad_head = lax.dynamic_index_in_dim(grad_heads, head_index, 1, keepdims=False)
        prob_full = jnp.exp(head_scores(query_head, key_head, allowed) - norm_row[:, None])
        prob_low = prob_full.astype(jnp.bfloat16)
        grad_value = lax.dot_general(
            prob_low, grad_head, (((0,), (0,)), ((), ())), preferred_element_type=jnp.float32
        )
        grad_prob = lax.dot_general(
            grad_head, value_head, (((1,), (1,)), ((), ())), preferred_element_type=jnp.float32
        )
        grad_score = (
            prob_full * (grad_prob - jnp.sum(prob_full * grad_prob, axis=1, keepdims=True))
        ).astype(jnp.bfloat16)
        grad_query = jnp.dot(grad_score, key_head, preferred_element_type=jnp.float32) * HD ** (
            -0.5
        )
        grad_key = lax.dot_general(
            grad_score, query_head, (((0,), (0,)), ((), ())), preferred_element_type=jnp.float32
        ) * HD ** (-0.5)
        return (grad_query, grad_key, grad_value)

    grad_queries, grad_keys, grad_values = lax.map(
        one_head, (jnp.arange(heads_here, dtype=jnp.int32), log_norm)
    )
    return (merge_heads(grad_queries), merge_heads(grad_keys), merge_heads(grad_values))


def local(
    tokens,
    segment,
    real_token,
    qkv_weight,
    out_weight,
    up_weight,
    down_weight,
    unit_bias,
    norm_gain,
    row_bias,
    cotangent,
):
    tok_rows = tokens.shape[0]
    tensor_size = lax.axis_size("tensor")
    group_rows = tok_rows * tensor_size
    margin = IMG - 1
    cols_here = qkv_weight.shape[3]
    dp_index = lax.axis_index("dp")
    tensor_index = lax.axis_index("tensor")
    group_first = dp_index * group_rows
    own_first = group_first + tensor_index * tok_rows
    segment_pad = jnp.pad(segment, (margin, margin), constant_values=-1)
    real_pad = jnp.pad(real_token, (margin, margin))
    segment_query = lax.dynamic_slice_in_dim(segment, group_first, group_rows, 0)
    segment_key = lax.dynamic_slice_in_dim(segment_pad, group_first, group_rows + 2 * margin, 0)
    real_key = lax.dynamic_slice_in_dim(real_pad, group_first, group_rows + 2 * margin, 0)
    place_query = jnp.arange(group_rows, dtype=jnp.int32)
    place_key = jnp.arange(group_rows + 2 * margin, dtype=jnp.int32) - margin
    allowed = (
        segment_query[:, None],
        place_query[:, None],
        segment_key[None, :],
        real_key[None, :],
        place_key[None, :],
    )
    own_real = lax.dynamic_slice_in_dim(real_token, own_first, tok_rows, 0).astype(jnp.float32)
    stream = tokens.astype(jnp.float32)
    layer_index = 0
    qkv_local = jnp.moveaxis(qkv_weight[layer_index], 1, 0)
    out_local, up_local, down_local = (
        out_weight[layer_index],
        up_weight[layer_index],
        down_weight[layer_index],
    )
    gain_now = norm_gain[layer_index].astype(jnp.float32)
    shift_now = row_bias[layer_index].astype(jnp.float32)
    bias_now = unit_bias[layer_index].astype(jnp.float32)
    normed_full = gather_forward(layer_norm(stream, gain_now[0], shift_now[0]).astype(jnp.bfloat16))
    qkv_full = jnp.moveaxis(collect(qkv_local, "dp", 0), 0, 1)
    projected = jnp.einsum("gd,sde->sge", normed_full, qkv_full, preferred_element_type=jnp.float32)
    queries = (projected[0] + bias_now[0]).astype(jnp.bfloat16)
    queries, up_local, down_local = lax.optimization_barrier((queries, up_local, down_local))
    out_full = collect(out_local, "dp", 0)
    up_full = collect(up_local, "dp", 0)
    down_full = collect(down_local, "dp", 0)
    gathered = (qkv_full, out_full, up_full, down_full)
    key_value = jnp.stack([projected[1], projected[2] + bias_now[1]]).astype(jnp.bfloat16)
    key_ext = with_halo(key_value, (("dp", 1),), margin)
    attended, log_norm = attend_forward(queries, key_ext, allowed)
    attended = attended.astype(jnp.bfloat16)

    def attention_term(first_row, row_count):
        return lax.dot_general(
            attended, out_full, (((1,), (1,)), ((), ())), preferred_element_type=jnp.float32
        )

    middle = stream + sum_forward(attention_term, tok_rows) + shift_now[1]
    second_full = gather_forward(layer_norm(middle, gain_now[1], shift_now[2]).astype(jnp.bfloat16))
    hidden = (
        jnp.einsum("gd,dre->gre", second_full, up_full, preferred_element_type=jnp.float32)
        + bias_now[2:][None]
    )
    active = exact_gelu(hidden).astype(jnp.bfloat16)

    def feed_term(first_row, row_count):
        return jnp.einsum("gre,ore->go", active, down_full, preferred_element_type=jnp.float32)

    kept_weights = gathered
    records = [
        (
            stream,
            middle,
            normed_full,
            second_full,
            queries,
            key_ext,
            log_norm,
            attended,
            hidden,
            active,
            kept_weights,
        )
    ]
    stream = middle + sum_forward(feed_term, tok_rows) + shift_now[3]
    gradient = cotangent.astype(jnp.float32) * own_real[:, None]
    local_qkv = [None] * LAYERS
    local_out = [None] * LAYERS
    local_up = [None] * LAYERS
    local_down = [None] * LAYERS
    unit_grads = [None] * LAYERS
    gain_grads = [None] * LAYERS
    shift_grads = [None] * LAYERS
    for layer_index in reversed(range(LAYERS)):
        (
            stream_in,
            middle,
            normed_full,
            second_full,
            queries,
            key_ext,
            log_norm,
            attended,
            hidden,
            active,
            kept_weights,
        ) = records[layer_index]
        qkv_full, out_full, up_full, down_full = kept_weights
        gain_now = norm_gain[layer_index].astype(jnp.float32)
        shift_now = row_bias[layer_index].astype(jnp.float32)
        shift_three = jnp.sum(gradient, axis=0)
        grad_mlp = gather_backward(gradient.astype(jnp.bfloat16))
        down_grad = scatter_rows(
            jnp.einsum("go,gre->ore", grad_mlp, active, preferred_element_type=jnp.float32)
        )
        grad_active = jnp.einsum(
            "go,ore->gre", grad_mlp, down_full, preferred_element_type=jnp.float32
        )
        gelu_again, gelu_pull = jax.vjp(exact_gelu, hidden)
        grad_hidden = gelu_pull(grad_active)[0].astype(jnp.bfloat16)
        up_bias_grad = jnp.sum(grad_hidden.astype(jnp.float32), axis=0)
        up_grad = scatter_rows(
            jnp.einsum("gd,gre->dre", second_full, grad_hidden, preferred_element_type=jnp.float32)
        )

        def second_term(first_row, row_count):
            return jnp.einsum(
                "gre,dre->gd", grad_hidden, up_full, preferred_element_type=jnp.float32
            )

        grad_second = sum_backward(second_term, tok_rows)
        second_again, second_pull = jax.vjp(layer_norm, middle, gain_now[1], shift_now[2])
        grad_mid_norm, gain_one, shift_two = second_pull(grad_second)
        grad_middle = gradient + grad_mid_norm
        shift_one = jnp.sum(grad_middle, axis=0)
        grad_proj = gather_backward(grad_middle.astype(jnp.bfloat16))
        out_grad = scatter_rows(
            lax.dot_general(
                grad_proj, attended, (((0,), (0,)), ((), ())), preferred_element_type=jnp.float32
            )
        )
        grad_attended = jnp.dot(grad_proj, out_full, preferred_element_type=jnp.float32).astype(
            jnp.bfloat16
        )
        grad_query, grad_key_ext, grad_value_ext = attend_backward(
            queries, key_ext, allowed, log_norm, grad_attended
        )
        grad_pair_ext = jnp.stack([grad_key_ext, grad_value_ext])
        from_next = from_behind(grad_pair_ext[:, :margin].astype(jnp.bfloat16), "dp", -1).astype(
            jnp.float32
        )
        from_prev = from_behind(
            grad_pair_ext[:, margin + group_rows :].astype(jnp.bfloat16), "dp", 1
        ).astype(jnp.float32)
        grad_pair = grad_pair_ext[:, margin : margin + group_rows]
        grad_pair = (
            grad_pair.at[:, group_rows - margin :].add(from_next).at[:, :margin].add(from_prev)
        )
        grad_triple = jnp.concatenate(
            [grad_query.astype(jnp.bfloat16)[None], grad_pair.astype(jnp.bfloat16)], axis=0
        )
        qkv_grad = jnp.moveaxis(
            scatter_rows(
                jnp.einsum(
                    "gd,sge->dse", normed_full, grad_triple, preferred_element_type=jnp.float32
                )
            ),
            0,
            1,
        )
        triple_sums = jnp.sum(grad_triple.astype(jnp.float32), axis=1)

        def first_term(first_row, row_count):
            return jnp.einsum(
                "sge,sde->gd", grad_triple, qkv_full, preferred_element_type=jnp.float32
            )

        grad_first = sum_backward(first_term, tok_rows)
        first_again, first_pull = jax.vjp(layer_norm, stream_in, gain_now[0], shift_now[0])
        grad_in_norm, gain_zero, shift_zero = first_pull(grad_first)
        gradient = grad_middle + grad_in_norm
        unit_grads[layer_index] = jnp.concatenate(
            [triple_sums[0][None], triple_sums[2][None], up_bias_grad], axis=0
        )
        gain_grads[layer_index] = jnp.stack([gain_zero, gain_one])
        shift_grads[layer_index] = jnp.stack([shift_zero, shift_one, shift_two, shift_three])
        local_qkv[layer_index] = qkv_grad
        local_out[layer_index] = out_grad
        local_up[layer_index] = up_grad
        local_down[layer_index] = down_grad
    grad_qkv = jnp.stack(local_qkv).astype(jnp.float32)
    grad_out = jnp.stack(local_out).astype(jnp.float32)
    grad_up = jnp.stack(local_up).astype(jnp.float32)
    grad_down = jnp.stack(local_down).astype(jnp.float32)
    unit_local = jnp.stack(unit_grads)
    unit_wide = jnp.zeros((LAYERS, unit_local.shape[1], cols_here * tensor_size), jnp.float32)
    unit_wide = lax.dynamic_update_slice_in_dim(unit_wide, unit_local, tensor_index * cols_here, 2)
    small = jnp.concatenate(
        [jnp.stack(gain_grads), jnp.stack(shift_grads), unit_wide], axis=1
    )
    small_total = jnp.sum(from_everyone(small, "dp"), axis=0)
    small_total = jnp.sum(from_everyone(small_total, "tensor"), axis=0)
    gain_total = small_total[:, :2]
    shift_total = small_total[:, 2:6]
    unit_total = small_total[:, 6:]
    unit_mine = lax.dynamic_slice_in_dim(unit_total, tensor_index * cols_here, cols_here, 2)
    return (
        stream.astype(jnp.bfloat16),
        gradient.astype(jnp.bfloat16),
        grad_qkv,
        grad_out,
        grad_up,
        grad_down,
        unit_mine,
        gain_total,
        shift_total,
    )


def solution(mesh):
    placed = (
        P(("dp", "tensor"), None),
        P(),
        P(),
        P(None, None, "dp", "tensor"),
        P(None, "dp", "tensor"),
        P(None, "dp", None, "tensor"),
        P(None, "dp", None, "tensor"),
        P(None, None, "tensor"),
        P(),
        P(),
        P(("dp", "tensor"), None),
    )
    return jax.shard_map(
        local,
        mesh=mesh,
        in_specs=placed,
        out_specs=(
            P(("dp", "tensor"), None),
            P(("dp", "tensor"), None),
            P(None, None, "dp", "tensor"),
            P(None, "dp", "tensor"),
            P(None, "dp", None, "tensor"),
            P(None, "dp", None, "tensor"),
            P(None, None, "tensor"),
            P(),
            P(),
        ),
        check_vma=False,
    )
```

```python
import functools
import math

import jax
import jax.numpy as jnp
from jax import lax
from jax.experimental import pallas as pl
from jax.experimental.pallas import tpu as pltpu
from jax.sharding import PartitionSpec as P

MESH = pl.DeviceIdType.MESH

LAYERS = 1
IMG = 577
HD = 64


norm_eps = 1e-06
masked_score = -1e30


def from_everyone(value, axis):
    devices = lax.axis_size(axis)
    return lax.all_to_all(
        jnp.broadcast_to(value[None], (devices, *value.shape)), axis, 0, 0, tiled=True
    )


def joined_along(parts, dim):
    dims = list(parts.shape[1:])
    dims[dim] *= parts.shape[0]
    return jnp.moveaxis(parts, 0, dim).reshape(dims)


def collect(value, axis, dim):
    parts = from_everyone(value, axis)
    return joined_along(parts, dim)


def split_up(value, dim, devices):
    dims = value.shape
    parts = value.reshape(*dims[:dim], devices, dims[dim] // devices, *dims[dim + 1 :])
    return jnp.moveaxis(parts, dim, 0)


def summed_on_arrival(value, axis, dim):
    devices = lax.axis_size(axis)
    parts = lax.all_to_all(split_up(value, dim, devices), axis, 0, 0, tiled=True)
    return jnp.sum(parts.astype(jnp.float32), axis=0)


def rows_first(arrays, axis, dims):
    turned = [jnp.moveaxis(a, dim, 0) for a, dim in zip(arrays, dims)]
    both = jnp.concatenate([t.reshape(len(t), -1) for t in turned], axis=1)
    filled, at, outs = (lax.all_gather(both, axis, axis=0, tiled=True), 0, [])
    for t, dim in zip(turned, dims):
        slab = filled[:, at : at + t[0].size].reshape(-1, *t.shape[1:])
        outs.append(jnp.moveaxis(slab, 0, dim))
        at += t[0].size
    return tuple(outs)


def with_halo(value, sides, width):
    for axis, dim in sides:
        devices, length = (lax.axis_size(axis), value.shape[dim])
        up = [(i, (i + 1) % devices) for i in range(devices - 1)]
        down = [(j, i) for i, j in up]
        last = lax.slice_in_dim(value, length - width, length, axis=dim)
        initial = lax.slice_in_dim(value, 0, width, axis=dim)
        before = lax.ppermute(last, axis, up)
        after = lax.ppermute(initial, axis, down)
        value = jnp.concatenate([before, value, after], axis=dim)
    return value


def from_behind(block, axis, distance):
    devices = range(lax.axis_size(axis))
    route = [(i - distance, i) for i in devices if i - distance in devices]
    return lax.ppermute(block, axis, route)


def side_by_side(arrays, axis, dim, along):
    widths = [math.prod(a.shape[along:]) for a in arrays]
    both = jnp.concatenate(
        [a.reshape(*a.shape[:along], w) for a, w in zip(arrays, widths)], axis=along
    )
    filled = lax.psum_scatter(both, axis, scatter_dimension=dim, tiled=True)
    parts = jnp.split(filled, [sum(widths[:k]) for k in range(1, len(widths))], axis=along)
    return tuple(
        (b.reshape(*filled.shape[:along], *a.shape[along:]) for a, b in zip(arrays, parts))
    )


def scatter_rows(grad):
    return summed_on_arrival(grad.astype(jnp.bfloat16), "dp", 0)


def layer_norm(values, gain_row, shift_row):
    center = values - jnp.mean(values, axis=-1, keepdims=True)
    spread = jnp.mean(center * center, axis=-1, keepdims=True)
    return center * lax.rsqrt(spread + norm_eps) * gain_row + shift_row


def exact_gelu(values):
    return jax.nn.gelu(values, approximate=False)


def _gather_kernel(devices, x_ref, out_ref, send_sem, recv_sem):
    me = lax.axis_index("tensor")
    dp = lax.axis_index("dp")
    sib = me + 1 - 2 * lax.rem(me, 2)
    far = lax.rem(me + 2, devices)
    barrier = pltpu.get_barrier_semaphore()
    for peer in (sib, far):
        pl.semaphore_signal(barrier, inc=1, device_id=(dp, peer), device_id_type=MESH)
    pl.semaphore_wait(barrier, 2)
    near_copy = pltpu.make_async_remote_copy(
        src_ref=x_ref,
        dst_ref=out_ref.at[me],
        send_sem=send_sem.at[0],
        recv_sem=recv_sem.at[0],
        device_id=(dp, sib),
        device_id_type=MESH,
    )
    far_copy = pltpu.make_async_remote_copy(
        src_ref=x_ref,
        dst_ref=out_ref.at[me],
        send_sem=send_sem.at[1],
        recv_sem=recv_sem.at[1],
        device_id=(dp, far),
        device_id_type=MESH,
    )
    far_copy.start()
    near_copy.start()
    out_ref[me] = x_ref[...]
    far_copy.wait_recv()
    relay = pltpu.make_async_remote_copy(
        src_ref=out_ref.at[far],
        dst_ref=out_ref.at[far],
        send_sem=send_sem.at[2],
        recv_sem=recv_sem.at[2],
        device_id=(dp, sib),
        device_id_type=MESH,
    )
    relay.start()
    near_copy.wait_send()
    near_copy.wait_recv()
    far_copy.wait_send()
    relay.wait_send()
    relay.wait_recv()


def gather_rows(values):
    devices = lax.axis_size("tensor")
    if devices != 4:
        return collect(values, "tensor", 0)
    rows, width = values.shape
    parts = pl.pallas_call(
        functools.partial(_gather_kernel, devices),
        out_shape=jax.ShapeDtypeStruct((devices, rows, width), values.dtype),
        in_specs=[pl.BlockSpec(memory_space=pltpu.VMEM)],
        out_specs=pl.BlockSpec(memory_space=pltpu.VMEM),
        scratch_shapes=[
            pltpu.SemaphoreType.DMA((3,)),
            pltpu.SemaphoreType.DMA((3,)),
        ],
        compiler_params=pltpu.CompilerParams(collective_id=0, has_side_effects=True),
    )(values)
    return parts.reshape(devices * rows, width)


def _exchange_kernel(devices, x_ref, out_ref, send_sem, recv_sem):
    me = lax.axis_index("tensor")
    dp = lax.axis_index("dp")
    barrier = pltpu.get_barrier_semaphore()
    for step in range(1, devices):
        pl.semaphore_signal(
            barrier, inc=1, device_id=(dp, lax.rem(me + step, devices)), device_id_type=MESH
        )
    pl.semaphore_wait(barrier, devices - 1)
    copies = []
    for step in range(1, devices):
        peer = lax.rem(me + step, devices)
        copy = pltpu.make_async_remote_copy(
            src_ref=x_ref.at[peer],
            dst_ref=out_ref.at[me],
            send_sem=send_sem.at[step - 1],
            recv_sem=recv_sem.at[step - 1],
            device_id=(dp, peer),
            device_id_type=MESH,
        )
        copy.start()
        copies.append(copy)
    out_ref[me] = x_ref[me]
    for copy in copies:
        copy.wait()


def exchange_rows(parts):
    devices = parts.shape[0]
    return pl.pallas_call(
        functools.partial(_exchange_kernel, devices),
        out_shape=jax.ShapeDtypeStruct(parts.shape, parts.dtype),
        in_specs=[pl.BlockSpec(memory_space=pltpu.VMEM)],
        out_specs=pl.BlockSpec(memory_space=pltpu.VMEM),
        scratch_shapes=[
            pltpu.SemaphoreType.DMA((devices - 1,)),
            pltpu.SemaphoreType.DMA((devices - 1,)),
        ],
        compiler_params=pltpu.CompilerParams(collective_id=1, has_side_effects=True),
    )(parts)


def _reduce_kernel(devices, x_ref, out_ref, held, mate, pre, send_sem, recv_sem):
    me = lax.axis_index("tensor")
    dp = lax.axis_index("dp")
    sib = me + 1 - 2 * lax.rem(me, 2)
    far = lax.rem(me + 2, devices)
    other = lax.rem(sib + 2, devices)
    barrier = pltpu.get_barrier_semaphore()
    for peer in (sib, far):
        pl.semaphore_signal(barrier, inc=1, device_id=(dp, peer), device_id_type=MESH)
    pl.semaphore_wait(barrier, 2)
    own_copy = pltpu.make_async_remote_copy(
        src_ref=x_ref.at[sib],
        dst_ref=held.at[0],
        send_sem=send_sem.at[0],
        recv_sem=recv_sem.at[0],
        device_id=(dp, sib),
        device_id_type=MESH,
    )
    mate_copy = pltpu.make_async_remote_copy(
        src_ref=x_ref.at[other],
        dst_ref=mate,
        send_sem=send_sem.at[1],
        recv_sem=recv_sem.at[1],
        device_id=(dp, sib),
        device_id_type=MESH,
    )
    mate_copy.start()
    own_copy.start()
    mate_copy.wait_recv()
    pre[...] = (x_ref[far].astype(jnp.float32) + mate[...].astype(jnp.float32)).astype(pre.dtype)
    out_ref[...] = x_ref[me].astype(jnp.float32)
    far_copy = pltpu.make_async_remote_copy(
        src_ref=pre,
        dst_ref=held.at[1],
        send_sem=send_sem.at[2],
        recv_sem=recv_sem.at[2],
        device_id=(dp, far),
        device_id_type=MESH,
    )
    far_copy.start()
    own_copy.wait_recv()
    out_ref[...] += held[0].astype(jnp.float32)
    far_copy.wait_recv()
    out_ref[...] += held[1].astype(jnp.float32)
    own_copy.wait_send()
    mate_copy.wait_send()
    far_copy.wait_send()


def summed_over_tensor(value):
    devices = lax.axis_size("tensor")
    parts = split_up(value, 0, devices)
    if devices != 4:
        return jnp.sum(exchange_rows(parts).astype(jnp.float32), axis=0)
    rows, width = parts.shape[1:]
    return pl.pallas_call(
        functools.partial(_reduce_kernel, devices),
        out_shape=jax.ShapeDtypeStruct((rows, width), jnp.float32),
        in_specs=[pl.BlockSpec(memory_space=pltpu.VMEM)],
        out_specs=pl.BlockSpec(memory_space=pltpu.VMEM),
        scratch_shapes=[
            pltpu.VMEM((2, rows, width), parts.dtype),
            pltpu.VMEM((rows, width), parts.dtype),
            pltpu.VMEM((rows, width), parts.dtype),
            pltpu.SemaphoreType.DMA((3,)),
            pltpu.SemaphoreType.DMA((3,)),
        ],
        compiler_params=pltpu.CompilerParams(collective_id=1, has_side_effects=True),
    )(parts)


def gather_forward(values):
    return gather_rows(values)


def gather_backward(values):
    return gather_rows(values)


def sum_forward(product, tok_rows):
    return summed_over_tensor(
        product(jnp.int32(0), tok_rows * lax.axis_size("tensor")).astype(jnp.bfloat16)
    )


def sum_backward(product, tok_rows):
    return summed_over_tensor(
        product(jnp.int32(0), tok_rows * lax.axis_size("tensor")).astype(jnp.bfloat16)
    )


def head_scores(query_head, key_head, allowed):
    raw = lax.dot_general(
        query_head, key_head, (((1,), (1,)), ((), ())), preferred_element_type=jnp.float32
    )
    return jnp.where(allowed, raw * HD ** (-0.5), masked_score)


def split_heads(queries, key_ext):
    heads_here = queries.shape[1] // HD
    query_heads = queries.reshape(queries.shape[0], heads_here, HD)
    key_heads = key_ext[0].reshape(key_ext.shape[1], heads_here, HD)
    value_heads = key_ext[1].reshape(key_ext.shape[1], heads_here, HD)
    return (heads_here, query_heads, key_heads, value_heads)


def merge_heads(per_head):
    return jnp.transpose(per_head, (1, 0, 2)).reshape(
        per_head.shape[1], per_head.shape[0] * per_head.shape[2]
    )


def _mask_from(sq_ref, pq_ref, sk_ref, rk_ref, pk_ref):
    return (sq_ref[...] == sk_ref[...]) & ((rk_ref[...] == 1) | (pq_ref[...] == pk_ref[...]))


def _mask_specs(rows, keys):
    column = pl.BlockSpec((rows, 1), lambda h: (0, 0))
    row = pl.BlockSpec((1, keys), lambda h: (0, 0))
    return [column, column, row, row, row]


def _attend_kernel(q_ref, k_ref, v_ref, sq_ref, pq_ref, sk_ref, rk_ref, pk_ref, o_ref, lse_ref):
    scores = lax.dot_general(
        q_ref[...], k_ref[...], (((1,), (1,)), ((), ())), preferred_element_type=jnp.float32
    )
    allowed = _mask_from(sq_ref, pq_ref, sk_ref, rk_ref, pk_ref)
    scores = jnp.where(allowed, scores * HD ** (-0.5), masked_score)
    row_top = jnp.max(scores, axis=1, keepdims=True)
    exponent = jnp.exp(scores - row_top)
    row_total = jnp.sum(exponent, axis=1, keepdims=True)
    prob_low = (exponent / row_total).astype(jnp.bfloat16)
    o_ref[...] = jnp.dot(prob_low, v_ref[...], preferred_element_type=jnp.float32)
    lse_ref[...] = row_top + jnp.log(row_total)


def attend_forward(queries, key_ext, mask_parts):
    heads_here = queries.shape[1] // HD
    rows, keys = mask_parts[0].shape[0], mask_parts[2].shape[1]
    query_heads = jnp.transpose(queries.reshape(rows, heads_here, HD), (1, 0, 2))
    key_heads = jnp.transpose(key_ext[0].reshape(keys, heads_here, HD), (1, 0, 2))
    value_heads = jnp.transpose(key_ext[1].reshape(keys, heads_here, HD), (1, 0, 2))
    head_outs, log_norm = pl.pallas_call(
        _attend_kernel,
        grid=(heads_here,),
        out_shape=(
            jax.ShapeDtypeStruct((heads_here, rows, HD), jnp.float32),
            jax.ShapeDtypeStruct((heads_here, rows, 1), jnp.float32),
        ),
        in_specs=[
            pl.BlockSpec((None, rows, HD), lambda h: (h, 0, 0)),
            pl.BlockSpec((None, keys, HD), lambda h: (h, 0, 0)),
            pl.BlockSpec((None, keys, HD), lambda h: (h, 0, 0)),
            *_mask_specs(rows, keys),
        ],
        out_specs=(
            pl.BlockSpec((None, rows, HD), lambda h: (h, 0, 0)),
            pl.BlockSpec((None, rows, 1), lambda h: (h, 0, 0)),
        ),
        compiler_params=pltpu.CompilerParams(vmem_limit_bytes=60 * 1024 * 1024),
    )(query_heads, key_heads, value_heads, *mask_parts)
    return (merge_heads(head_outs), log_norm[:, :, 0])


def attend_forward_xla(queries, key_ext, allowed):
    heads_here, query_heads, key_heads, value_heads = split_heads(queries, key_ext)

    def one_head(head_index):
        query_head = lax.dynamic_index_in_dim(query_heads, head_index, 1, keepdims=False)
        key_head = lax.dynamic_index_in_dim(key_heads, head_index, 1, keepdims=False)
        value_head = lax.dynamic_index_in_dim(value_heads, head_index, 1, keepdims=False)
        scores = head_scores(query_head, key_head, allowed)
        row_top = jnp.max(scores, axis=1, keepdims=True)
        exponent = jnp.exp(scores - row_top)
        row_total = jnp.sum(exponent, axis=1, keepdims=True)
        prob_low = (exponent / row_total).astype(jnp.bfloat16)
        head_out = jnp.dot(prob_low, value_head, preferred_element_type=jnp.float32)
        return (head_out, (row_top + jnp.log(row_total))[:, 0])

    head_outs, log_norm = lax.map(one_head, jnp.arange(heads_here, dtype=jnp.int32))
    return (merge_heads(head_outs), log_norm)


def _attend_back_kernel(
    q_ref, k_ref, v_ref, g_ref, lse_ref, sq_ref, pq_ref, sk_ref, rk_ref, pk_ref, dq_ref, dk_ref, dv_ref
):
    query_head, key_head, grad_head = q_ref[...], k_ref[...], g_ref[...]
    scores = lax.dot_general(
        query_head, key_head, (((1,), (1,)), ((), ())), preferred_element_type=jnp.float32
    )
    allowed = _mask_from(sq_ref, pq_ref, sk_ref, rk_ref, pk_ref)
    scores = jnp.where(allowed, scores * HD ** (-0.5), masked_score)
    prob_full = jnp.exp(scores - lse_ref[...])
    prob_low = prob_full.astype(jnp.bfloat16)
    dv_ref[...] = lax.dot_general(
        prob_low, grad_head, (((0,), (0,)), ((), ())), preferred_element_type=jnp.float32
    )
    grad_prob = lax.dot_general(
        grad_head, v_ref[...], (((1,), (1,)), ((), ())), preferred_element_type=jnp.float32
    )
    grad_score = (
        prob_full * (grad_prob - jnp.sum(prob_full * grad_prob, axis=1, keepdims=True))
    ).astype(jnp.bfloat16)
    dq_ref[...] = jnp.dot(grad_score, key_head, preferred_element_type=jnp.float32) * HD ** (-0.5)
    dk_ref[...] = lax.dot_general(
        grad_score, query_head, (((0,), (0,)), ((), ())), preferred_element_type=jnp.float32
    ) * HD ** (-0.5)


def attend_backward(queries, key_ext, mask_parts, log_norm, grad_attended):
    heads_here = queries.shape[1] // HD
    rows, keys = mask_parts[0].shape[0], mask_parts[2].shape[1]

    def by_head(values, count):
        return jnp.transpose(values.reshape(count, heads_here, HD), (1, 0, 2))

    row_spec = pl.BlockSpec((None, rows, HD), lambda h: (h, 0, 0))
    key_spec = pl.BlockSpec((None, keys, HD), lambda h: (h, 0, 0))
    grad_queries, grad_keys, grad_values = pl.pallas_call(
        _attend_back_kernel,
        grid=(heads_here,),
        out_shape=(
            jax.ShapeDtypeStruct((heads_here, rows, HD), jnp.float32),
            jax.ShapeDtypeStruct((heads_here, keys, HD), jnp.float32),
            jax.ShapeDtypeStruct((heads_here, keys, HD), jnp.float32),
        ),
        in_specs=[
            row_spec,
            key_spec,
            key_spec,
            row_spec,
            pl.BlockSpec((None, rows, 1), lambda h: (h, 0, 0)),
            *_mask_specs(rows, keys),
        ],
        out_specs=(row_spec, key_spec, key_spec),
        compiler_params=pltpu.CompilerParams(vmem_limit_bytes=60 * 1024 * 1024),
    )(
        by_head(queries, rows),
        by_head(key_ext[0], keys),
        by_head(key_ext[1], keys),
        by_head(grad_attended, rows),
        log_norm[:, :, None],
        *mask_parts,
    )
    return (merge_heads(grad_queries), merge_heads(grad_keys), merge_heads(grad_values))


def attend_backward_xla(queries, key_ext, allowed, log_norm, grad_attended):
    heads_here, query_heads, key_heads, value_heads = split_heads(queries, key_ext)
    grad_heads = grad_attended.reshape(grad_attended.shape[0], heads_here, HD)

    def one_head(inputs):
        head_index, norm_row = inputs
        query_head = lax.dynamic_index_in_dim(query_heads, head_index, 1, keepdims=False)
        key_head = lax.dynamic_index_in_dim(key_heads, head_index, 1, keepdims=False)
        value_head = lax.dynamic_index_in_dim(value_heads, head_index, 1, keepdims=False)
        grad_head = lax.dynamic_index_in_dim(grad_heads, head_index, 1, keepdims=False)
        prob_full = jnp.exp(head_scores(query_head, key_head, allowed) - norm_row[:, None])
        prob_low = prob_full.astype(jnp.bfloat16)
        grad_value = lax.dot_general(
            prob_low, grad_head, (((0,), (0,)), ((), ())), preferred_element_type=jnp.float32
        )
        grad_prob = lax.dot_general(
            grad_head, value_head, (((1,), (1,)), ((), ())), preferred_element_type=jnp.float32
        )
        grad_score = (
            prob_full * (grad_prob - jnp.sum(prob_full * grad_prob, axis=1, keepdims=True))
        ).astype(jnp.bfloat16)
        grad_query = jnp.dot(grad_score, key_head, preferred_element_type=jnp.float32) * HD ** (
            -0.5
        )
        grad_key = lax.dot_general(
            grad_score, query_head, (((0,), (0,)), ((), ())), preferred_element_type=jnp.float32
        ) * HD ** (-0.5)
        return (grad_query, grad_key, grad_value)

    grad_queries, grad_keys, grad_values = lax.map(
        one_head, (jnp.arange(heads_here, dtype=jnp.int32), log_norm)
    )
    return (merge_heads(grad_queries), merge_heads(grad_keys), merge_heads(grad_values))


def local(
    tokens,
    segment,
    real_token,
    qkv_weight,
    out_weight,
    up_weight,
    down_weight,
    unit_bias,
    norm_gain,
    row_bias,
    cotangent,
):
    tok_rows = tokens.shape[0]
    tensor_size = lax.axis_size("tensor")
    group_rows = tok_rows * tensor_size
    margin = IMG - 1
    cols_here = qkv_weight.shape[3]
    dp_index = lax.axis_index("dp")
    tensor_index = lax.axis_index("tensor")
    group_first = dp_index * group_rows
    own_first = group_first + tensor_index * tok_rows
    segment_pad = jnp.pad(segment, (margin, margin), constant_values=-1)
    real_pad = jnp.pad(real_token, (margin, margin))
    segment_query = lax.dynamic_slice_in_dim(segment, group_first, group_rows, 0)
    segment_key = lax.dynamic_slice_in_dim(segment_pad, group_first, group_rows + 2 * margin, 0)
    real_key = lax.dynamic_slice_in_dim(real_pad, group_first, group_rows + 2 * margin, 0)
    place_query = jnp.arange(group_rows, dtype=jnp.int32)
    place_key = jnp.arange(group_rows + 2 * margin, dtype=jnp.int32) - margin
    allowed = (
        segment_query[:, None],
        place_query[:, None],
        segment_key[None, :],
        real_key[None, :],
        place_key[None, :],
    )
    own_real = lax.dynamic_slice_in_dim(real_token, own_first, tok_rows, 0).astype(jnp.float32)
    stream = tokens.astype(jnp.float32)
    layer_index = 0
    qkv_local = jnp.moveaxis(qkv_weight[layer_index], 1, 0)
    out_local, up_local, down_local = (
        out_weight[layer_index],
        up_weight[layer_index],
        down_weight[layer_index],
    )
    gain_now = norm_gain[layer_index].astype(jnp.float32)
    shift_now = row_bias[layer_index].astype(jnp.float32)
    bias_now = unit_bias[layer_index].astype(jnp.float32)
    normed_full = gather_forward(layer_norm(stream, gain_now[0], shift_now[0]).astype(jnp.bfloat16))
    qkv_full = jnp.moveaxis(collect(qkv_local, "dp", 0), 0, 1)
    projected = jnp.einsum("gd,sde->sge", normed_full, qkv_full, preferred_element_type=jnp.float32)
    queries = (projected[0] + bias_now[0]).astype(jnp.bfloat16)
    queries, out_local, up_local, down_local = lax.optimization_barrier(
        (queries, out_local, up_local, down_local)
    )
    out_full = collect(out_local, "dp", 0)
    up_full = collect(up_local, "dp", 0)
    down_full = collect(down_local, "dp", 0)
    gathered = (qkv_full, out_full, up_full, down_full)
    key_value = jnp.stack([projected[1], projected[2] + bias_now[1]]).astype(jnp.bfloat16)
    key_ext = with_halo(key_value, (("dp", 1),), margin)
    attended, log_norm = attend_forward(queries, key_ext, allowed)
    attended = attended.astype(jnp.bfloat16)

    def attention_term(first_row, row_count):
        return lax.dot_general(
            attended, out_full, (((1,), (1,)), ((), ())), preferred_element_type=jnp.float32
        )

    middle = stream + sum_forward(attention_term, tok_rows) + shift_now[1]
    second_full = gather_forward(layer_norm(middle, gain_now[1], shift_now[2]).astype(jnp.bfloat16))
    hidden = (
        jnp.einsum("gd,dre->gre", second_full, up_full, preferred_element_type=jnp.float32)
        + bias_now[2:][None]
    )
    active = exact_gelu(hidden).astype(jnp.bfloat16)

    def feed_term(first_row, row_count):
        return jnp.einsum("gre,ore->go", active, down_full, preferred_element_type=jnp.float32)

    kept_weights = gathered
    records = [
        (
            stream,
            middle,
            normed_full,
            second_full,
            queries,
            key_ext,
            log_norm,
            attended,
            hidden,
            active,
            kept_weights,
        )
    ]
    stream = middle + sum_forward(feed_term, tok_rows) + shift_now[3]
    gradient = cotangent.astype(jnp.float32) * own_real[:, None]
    local_qkv = [None] * LAYERS
    local_out = [None] * LAYERS
    local_up = [None] * LAYERS
    local_down = [None] * LAYERS
    unit_grads = [None] * LAYERS
    gain_grads = [None] * LAYERS
    shift_grads = [None] * LAYERS
    for layer_index in reversed(range(LAYERS)):
        (
            stream_in,
            middle,
            normed_full,
            second_full,
            queries,
            key_ext,
            log_norm,
            attended,
            hidden,
            active,
            kept_weights,
        ) = records[layer_index]
        qkv_full, out_full, up_full, down_full = kept_weights
        gain_now = norm_gain[layer_index].astype(jnp.float32)
        shift_now = row_bias[layer_index].astype(jnp.float32)
        shift_three = jnp.sum(gradient, axis=0)
        grad_mlp = gather_backward(gradient.astype(jnp.bfloat16))
        down_grad = scatter_rows(
            jnp.einsum("go,gre->ore", grad_mlp, active, preferred_element_type=jnp.float32)
        )
        grad_active = jnp.einsum(
            "go,ore->gre", grad_mlp, down_full, preferred_element_type=jnp.float32
        )
        gelu_again, gelu_pull = jax.vjp(exact_gelu, hidden)
        grad_hidden = gelu_pull(grad_active)[0].astype(jnp.bfloat16)
        up_bias_grad = jnp.sum(grad_hidden.astype(jnp.float32), axis=0)
        up_grad = scatter_rows(
            jnp.einsum("gd,gre->dre", second_full, grad_hidden, preferred_element_type=jnp.float32)
        )

        def second_term(first_row, row_count):
            return jnp.einsum(
                "gre,dre->gd", grad_hidden, up_full, preferred_element_type=jnp.float32
            )

        grad_second = sum_backward(second_term, tok_rows)
        second_again, second_pull = jax.vjp(layer_norm, middle, gain_now[1], shift_now[2])
        grad_mid_norm, gain_one, shift_two = second_pull(grad_second)
        grad_middle = gradient + grad_mid_norm
        shift_one = jnp.sum(grad_middle, axis=0)
        grad_proj = gather_backward(grad_middle.astype(jnp.bfloat16))
        out_grad = scatter_rows(
            lax.dot_general(
                grad_proj, attended, (((0,), (0,)), ((), ())), preferred_element_type=jnp.float32
            )
        )
        grad_attended = jnp.dot(grad_proj, out_full, preferred_element_type=jnp.float32).astype(
            jnp.bfloat16
        )
        grad_query, grad_key_ext, grad_value_ext = attend_backward(
            queries, key_ext, allowed, log_norm, grad_attended
        )
        grad_pair_ext = jnp.stack([grad_key_ext, grad_value_ext])
        from_next = from_behind(grad_pair_ext[:, :margin].astype(jnp.bfloat16), "dp", -1).astype(
            jnp.float32
        )
        from_prev = from_behind(
            grad_pair_ext[:, margin + group_rows :].astype(jnp.bfloat16), "dp", 1
        ).astype(jnp.float32)
        grad_pair = grad_pair_ext[:, margin : margin + group_rows]
        grad_pair = (
            grad_pair.at[:, group_rows - margin :].add(from_next).at[:, :margin].add(from_prev)
        )
        grad_triple = jnp.concatenate(
            [grad_query.astype(jnp.bfloat16)[None], grad_pair.astype(jnp.bfloat16)], axis=0
        )
        qkv_grad = jnp.moveaxis(
            scatter_rows(
                jnp.einsum(
                    "gd,sge->dse", normed_full, grad_triple, preferred_element_type=jnp.float32
                )
            ),
            0,
            1,
        )
        triple_sums = jnp.sum(grad_triple.astype(jnp.float32), axis=1)

        def first_term(first_row, row_count):
            return jnp.einsum(
                "sge,sde->gd", grad_triple, qkv_full, preferred_element_type=jnp.float32
            )

        grad_first = sum_backward(first_term, tok_rows)
        first_again, first_pull = jax.vjp(layer_norm, stream_in, gain_now[0], shift_now[0])
        grad_in_norm, gain_zero, shift_zero = first_pull(grad_first)
        gradient = grad_middle + grad_in_norm
        unit_grads[layer_index] = jnp.concatenate(
            [triple_sums[0][None], triple_sums[2][None], up_bias_grad], axis=0
        )
        gain_grads[layer_index] = jnp.stack([gain_zero, gain_one])
        shift_grads[layer_index] = jnp.stack([shift_zero, shift_one, shift_two, shift_three])
        local_qkv[layer_index] = qkv_grad
        local_out[layer_index] = out_grad
        local_up[layer_index] = up_grad
        local_down[layer_index] = down_grad
    grad_qkv = jnp.stack(local_qkv).astype(jnp.float32)
    grad_out = jnp.stack(local_out).astype(jnp.float32)
    grad_up = jnp.stack(local_up).astype(jnp.float32)
    grad_down = jnp.stack(local_down).astype(jnp.float32)
    unit_local = jnp.stack(unit_grads)
    unit_wide = jnp.zeros((LAYERS, unit_local.shape[1], cols_here * tensor_size), jnp.float32)
    unit_wide = lax.dynamic_update_slice_in_dim(unit_wide, unit_local, tensor_index * cols_here, 2)
    small = jnp.concatenate(
        [jnp.stack(gain_grads), jnp.stack(shift_grads), unit_wide], axis=1
    )
    small_total = jnp.sum(from_everyone(small, "dp"), axis=0)
    small_total = jnp.sum(from_everyone(small_total, "tensor"), axis=0)
    gain_total = small_total[:, :2]
    shift_total = small_total[:, 2:6]
    unit_total = small_total[:, 6:]
    unit_mine = lax.dynamic_slice_in_dim(unit_total, tensor_index * cols_here, cols_here, 2)
    return (
        stream.astype(jnp.bfloat16),
        gradient.astype(jnp.bfloat16),
        grad_qkv,
        grad_out,
        grad_up,
        grad_down,
        unit_mine,
        gain_total,
        shift_total,
    )


def solution(mesh):
    placed = (
        P(("dp", "tensor"), None),
        P(),
        P(),
        P(None, None, "dp", "tensor"),
        P(None, "dp", "tensor"),
        P(None, "dp", None, "tensor"),
        P(None, "dp", None, "tensor"),
        P(None, None, "tensor"),
        P(),
        P(),
        P(("dp", "tensor"), None),
    )
    return jax.shard_map(
        local,
        mesh=mesh,
        in_specs=placed,
        out_specs=(
            P(("dp", "tensor"), None),
            P(("dp", "tensor"), None),
            P(None, None, "dp", "tensor"),
            P(None, "dp", "tensor"),
            P(None, "dp", None, "tensor"),
            P(None, "dp", None, "tensor"),
            P(None, None, "tensor"),
            P(),
            P(),
        ),
        check_vma=False,
    )
```

```python
import functools
import math

import jax
import jax.numpy as jnp
from jax import lax
from jax.experimental import pallas as pl
from jax.experimental.pallas import tpu as pltpu
from jax.sharding import PartitionSpec as P

MESH = pl.DeviceIdType.MESH

LAYERS = 1
IMG = 577
HD = 64


norm_eps = 1e-06
masked_score = -1e30


def from_everyone(value, axis):
    devices = lax.axis_size(axis)
    return lax.all_to_all(
        jnp.broadcast_to(value[None], (devices, *value.shape)), axis, 0, 0, tiled=True
    )


def joined_along(parts, dim):
    dims = list(parts.shape[1:])
    dims[dim] *= parts.shape[0]
    return jnp.moveaxis(parts, 0, dim).reshape(dims)


def collect(value, axis, dim):
    parts = from_everyone(value, axis)
    return joined_along(parts, dim)


def split_up(value, dim, devices):
    dims = value.shape
    parts = value.reshape(*dims[:dim], devices, dims[dim] // devices, *dims[dim + 1 :])
    return jnp.moveaxis(parts, dim, 0)


def summed_on_arrival(value, axis, dim):
    devices = lax.axis_size(axis)
    parts = lax.all_to_all(split_up(value, dim, devices), axis, 0, 0, tiled=True)
    return jnp.sum(parts.astype(jnp.float32), axis=0)


def rows_first(arrays, axis, dims):
    turned = [jnp.moveaxis(a, dim, 0) for a, dim in zip(arrays, dims)]
    both = jnp.concatenate([t.reshape(len(t), -1) for t in turned], axis=1)
    filled, at, outs = (lax.all_gather(both, axis, axis=0, tiled=True), 0, [])
    for t, dim in zip(turned, dims):
        slab = filled[:, at : at + t[0].size].reshape(-1, *t.shape[1:])
        outs.append(jnp.moveaxis(slab, 0, dim))
        at += t[0].size
    return tuple(outs)


def with_halo(value, sides, width):
    for axis, dim in sides:
        devices, length = (lax.axis_size(axis), value.shape[dim])
        up = [(i, (i + 1) % devices) for i in range(devices - 1)]
        down = [(j, i) for i, j in up]
        last = lax.slice_in_dim(value, length - width, length, axis=dim)
        initial = lax.slice_in_dim(value, 0, width, axis=dim)
        before = lax.ppermute(last, axis, up)
        after = lax.ppermute(initial, axis, down)
        value = jnp.concatenate([before, value, after], axis=dim)
    return value


def from_behind(block, axis, distance):
    devices = range(lax.axis_size(axis))
    route = [(i - distance, i) for i in devices if i - distance in devices]
    return lax.ppermute(block, axis, route)


def side_by_side(arrays, axis, dim, along):
    widths = [math.prod(a.shape[along:]) for a in arrays]
    both = jnp.concatenate(
        [a.reshape(*a.shape[:along], w) for a, w in zip(arrays, widths)], axis=along
    )
    filled = lax.psum_scatter(both, axis, scatter_dimension=dim, tiled=True)
    parts = jnp.split(filled, [sum(widths[:k]) for k in range(1, len(widths))], axis=along)
    return tuple(
        (b.reshape(*filled.shape[:along], *a.shape[along:]) for a, b in zip(arrays, parts))
    )


def scatter_rows(grad):
    return summed_on_arrival(grad.astype(jnp.bfloat16), "dp", 0)


def layer_norm(values, gain_row, shift_row):
    center = values - jnp.mean(values, axis=-1, keepdims=True)
    spread = jnp.mean(center * center, axis=-1, keepdims=True)
    return center * lax.rsqrt(spread + norm_eps) * gain_row + shift_row


def exact_gelu(values):
    return jax.nn.gelu(values, approximate=False)


def _gather_kernel(devices, x_ref, out_ref, send_sem, recv_sem):
    me = lax.axis_index("tensor")
    dp = lax.axis_index("dp")
    sib = me + 1 - 2 * lax.rem(me, 2)
    far = lax.rem(me + 2, devices)
    barrier = pltpu.get_barrier_semaphore()
    for peer in (sib, far):
        pl.semaphore_signal(barrier, inc=1, device_id=(dp, peer), device_id_type=MESH)
    pl.semaphore_wait(barrier, 2)
    near_copy = pltpu.make_async_remote_copy(
        src_ref=x_ref,
        dst_ref=out_ref.at[me],
        send_sem=send_sem.at[0],
        recv_sem=recv_sem.at[0],
        device_id=(dp, sib),
        device_id_type=MESH,
    )
    half = x_ref.shape[0] // 2
    pieces = (pl.ds(0, half), pl.ds(half, x_ref.shape[0] - half))
    far_copies = [
        pltpu.make_async_remote_copy(
            src_ref=x_ref.at[piece],
            dst_ref=out_ref.at[me, piece],
            send_sem=send_sem.at[1 + k],
            recv_sem=recv_sem.at[1 + k],
            device_id=(dp, far),
            device_id_type=MESH,
        )
        for k, piece in enumerate(pieces)
    ]
    for copy in far_copies:
        copy.start()
    near_copy.start()
    out_ref[me] = x_ref[...]
    relays = []
    for k, piece in enumerate(pieces):
        far_copies[k].wait_recv()
        relay = pltpu.make_async_remote_copy(
            src_ref=out_ref.at[far, piece],
            dst_ref=out_ref.at[far, piece],
            send_sem=send_sem.at[3 + k],
            recv_sem=recv_sem.at[3 + k],
            device_id=(dp, sib),
            device_id_type=MESH,
        )
        relay.start()
        relays.append(relay)
    near_copy.wait_send()
    near_copy.wait_recv()
    for copy in far_copies:
        copy.wait_send()
    for relay in relays:
        relay.wait_send()
        relay.wait_recv()


def gather_rows(values):
    devices = lax.axis_size("tensor")
    if devices != 4:
        return collect(values, "tensor", 0)
    rows, width = values.shape
    parts = pl.pallas_call(
        functools.partial(_gather_kernel, devices),
        out_shape=jax.ShapeDtypeStruct((devices, rows, width), values.dtype),
        in_specs=[pl.BlockSpec(memory_space=pltpu.VMEM)],
        out_specs=pl.BlockSpec(memory_space=pltpu.VMEM),
        scratch_shapes=[
            pltpu.SemaphoreType.DMA((5,)),
            pltpu.SemaphoreType.DMA((5,)),
        ],
        compiler_params=pltpu.CompilerParams(collective_id=0, has_side_effects=True),
    )(values)
    return parts.reshape(devices * rows, width)


def _exchange_kernel(devices, x_ref, out_ref, send_sem, recv_sem):
    me = lax.axis_index("tensor")
    dp = lax.axis_index("dp")
    barrier = pltpu.get_barrier_semaphore()
    for step in range(1, devices):
        pl.semaphore_signal(
            barrier, inc=1, device_id=(dp, lax.rem(me + step, devices)), device_id_type=MESH
        )
    pl.semaphore_wait(barrier, devices - 1)
    copies = []
    for step in range(1, devices):
        peer = lax.rem(me + step, devices)
        copy = pltpu.make_async_remote_copy(
            src_ref=x_ref.at[peer],
            dst_ref=out_ref.at[me],
            send_sem=send_sem.at[step - 1],
            recv_sem=recv_sem.at[step - 1],
            device_id=(dp, peer),
            device_id_type=MESH,
        )
        copy.start()
        copies.append(copy)
    out_ref[me] = x_ref[me]
    for copy in copies:
        copy.wait()


def exchange_rows(parts):
    devices = parts.shape[0]
    return pl.pallas_call(
        functools.partial(_exchange_kernel, devices),
        out_shape=jax.ShapeDtypeStruct(parts.shape, parts.dtype),
        in_specs=[pl.BlockSpec(memory_space=pltpu.VMEM)],
        out_specs=pl.BlockSpec(memory_space=pltpu.VMEM),
        scratch_shapes=[
            pltpu.SemaphoreType.DMA((devices - 1,)),
            pltpu.SemaphoreType.DMA((devices - 1,)),
        ],
        compiler_params=pltpu.CompilerParams(collective_id=1, has_side_effects=True),
    )(parts)


def _reduce_kernel(devices, x_ref, out_ref, held, mate, pre, send_sem, recv_sem):
    me = lax.axis_index("tensor")
    dp = lax.axis_index("dp")
    sib = me + 1 - 2 * lax.rem(me, 2)
    far = lax.rem(me + 2, devices)
    other = lax.rem(sib + 2, devices)
    barrier = pltpu.get_barrier_semaphore()
    for peer in (sib, far):
        pl.semaphore_signal(barrier, inc=1, device_id=(dp, peer), device_id_type=MESH)
    pl.semaphore_wait(barrier, 2)
    own_copy = pltpu.make_async_remote_copy(
        src_ref=x_ref.at[sib],
        dst_ref=held.at[0],
        send_sem=send_sem.at[0],
        recv_sem=recv_sem.at[0],
        device_id=(dp, sib),
        device_id_type=MESH,
    )
    mate_copy = pltpu.make_async_remote_copy(
        src_ref=x_ref.at[other],
        dst_ref=mate,
        send_sem=send_sem.at[1],
        recv_sem=recv_sem.at[1],
        device_id=(dp, sib),
        device_id_type=MESH,
    )
    mate_copy.start()
    own_copy.start()
    mate_copy.wait_recv()
    pre[...] = (x_ref[far].astype(jnp.float32) + mate[...].astype(jnp.float32)).astype(pre.dtype)
    out_ref[...] = x_ref[me].astype(jnp.float32)
    far_copy = pltpu.make_async_remote_copy(
        src_ref=pre,
        dst_ref=held.at[1],
        send_sem=send_sem.at[2],
        recv_sem=recv_sem.at[2],
        device_id=(dp, far),
        device_id_type=MESH,
    )
    far_copy.start()
    own_copy.wait_recv()
    out_ref[...] += held[0].astype(jnp.float32)
    far_copy.wait_recv()
    out_ref[...] += held[1].astype(jnp.float32)
    own_copy.wait_send()
    mate_copy.wait_send()
    far_copy.wait_send()


def summed_over_tensor(value):
    devices = lax.axis_size("tensor")
    parts = split_up(value, 0, devices)
    if devices != 4:
        return jnp.sum(exchange_rows(parts).astype(jnp.float32), axis=0)
    rows, width = parts.shape[1:]
    return pl.pallas_call(
        functools.partial(_reduce_kernel, devices),
        out_shape=jax.ShapeDtypeStruct((rows, width), jnp.float32),
        in_specs=[pl.BlockSpec(memory_space=pltpu.VMEM)],
        out_specs=pl.BlockSpec(memory_space=pltpu.VMEM),
        scratch_shapes=[
            pltpu.VMEM((2, rows, width), parts.dtype),
            pltpu.VMEM((rows, width), parts.dtype),
            pltpu.VMEM((rows, width), parts.dtype),
            pltpu.SemaphoreType.DMA((3,)),
            pltpu.SemaphoreType.DMA((3,)),
        ],
        compiler_params=pltpu.CompilerParams(collective_id=1, has_side_effects=True),
    )(parts)


def gather_forward(values):
    return gather_rows(values)


def gather_backward(values):
    return gather_rows(values)


def sum_forward(product, tok_rows):
    return summed_over_tensor(
        product(jnp.int32(0), tok_rows * lax.axis_size("tensor")).astype(jnp.bfloat16)
    )


def sum_backward(product, tok_rows):
    return summed_over_tensor(
        product(jnp.int32(0), tok_rows * lax.axis_size("tensor")).astype(jnp.bfloat16)
    )


def head_scores(query_head, key_head, allowed):
    raw = lax.dot_general(
        query_head, key_head, (((1,), (1,)), ((), ())), preferred_element_type=jnp.float32
    )
    return jnp.where(allowed, raw * HD ** (-0.5), masked_score)


def split_heads(queries, key_ext):
    heads_here = queries.shape[1] // HD
    query_heads = queries.reshape(queries.shape[0], heads_here, HD)
    key_heads = key_ext[0].reshape(key_ext.shape[1], heads_here, HD)
    value_heads = key_ext[1].reshape(key_ext.shape[1], heads_here, HD)
    return (heads_here, query_heads, key_heads, value_heads)


def merge_heads(per_head):
    return jnp.transpose(per_head, (1, 0, 2)).reshape(
        per_head.shape[1], per_head.shape[0] * per_head.shape[2]
    )


def _mask_from(sq_ref, pq_ref, sk_ref, rk_ref, pk_ref):
    return (sq_ref[...] == sk_ref[...]) & ((rk_ref[...] == 1) | (pq_ref[...] == pk_ref[...]))


def _mask_specs(rows, keys):
    column = pl.BlockSpec((rows, 1), lambda h: (0, 0))
    row = pl.BlockSpec((1, keys), lambda h: (0, 0))
    return [column, column, row, row, row]


def _attend_kernel(q_ref, k_ref, v_ref, sq_ref, pq_ref, sk_ref, rk_ref, pk_ref, o_ref, lse_ref):
    scores = lax.dot_general(
        q_ref[...], k_ref[...], (((1,), (1,)), ((), ())), preferred_element_type=jnp.float32
    )
    allowed = _mask_from(sq_ref, pq_ref, sk_ref, rk_ref, pk_ref)
    scores = jnp.where(allowed, scores * HD ** (-0.5), masked_score)
    row_top = jnp.max(scores, axis=1, keepdims=True)
    exponent = jnp.exp(scores - row_top)
    row_total = jnp.sum(exponent, axis=1, keepdims=True)
    prob_low = (exponent / row_total).astype(jnp.bfloat16)
    o_ref[...] = jnp.dot(prob_low, v_ref[...], preferred_element_type=jnp.float32)
    lse_ref[...] = row_top + jnp.log(row_total)


def attend_forward(queries, key_ext, mask_parts):
    heads_here = queries.shape[1] // HD
    rows, keys = mask_parts[0].shape[0], mask_parts[2].shape[1]
    query_heads = jnp.transpose(queries.reshape(rows, heads_here, HD), (1, 0, 2))
    key_heads = jnp.transpose(key_ext[0].reshape(keys, heads_here, HD), (1, 0, 2))
    value_heads = jnp.transpose(key_ext[1].reshape(keys, heads_here, HD), (1, 0, 2))
    head_outs, log_norm = pl.pallas_call(
        _attend_kernel,
        grid=(heads_here,),
        out_shape=(
            jax.ShapeDtypeStruct((heads_here, rows, HD), jnp.float32),
            jax.ShapeDtypeStruct((heads_here, rows, 1), jnp.float32),
        ),
        in_specs=[
            pl.BlockSpec((None, rows, HD), lambda h: (h, 0, 0)),
            pl.BlockSpec((None, keys, HD), lambda h: (h, 0, 0)),
            pl.BlockSpec((None, keys, HD), lambda h: (h, 0, 0)),
            *_mask_specs(rows, keys),
        ],
        out_specs=(
            pl.BlockSpec((None, rows, HD), lambda h: (h, 0, 0)),
            pl.BlockSpec((None, rows, 1), lambda h: (h, 0, 0)),
        ),
        compiler_params=pltpu.CompilerParams(vmem_limit_bytes=60 * 1024 * 1024),
    )(query_heads, key_heads, value_heads, *mask_parts)
    return (merge_heads(head_outs), log_norm[:, :, 0])


def attend_forward_xla(queries, key_ext, allowed):
    heads_here, query_heads, key_heads, value_heads = split_heads(queries, key_ext)

    def one_head(head_index):
        query_head = lax.dynamic_index_in_dim(query_heads, head_index, 1, keepdims=False)
        key_head = lax.dynamic_index_in_dim(key_heads, head_index, 1, keepdims=False)
        value_head = lax.dynamic_index_in_dim(value_heads, head_index, 1, keepdims=False)
        scores = head_scores(query_head, key_head, allowed)
        row_top = jnp.max(scores, axis=1, keepdims=True)
        exponent = jnp.exp(scores - row_top)
        row_total = jnp.sum(exponent, axis=1, keepdims=True)
        prob_low = (exponent / row_total).astype(jnp.bfloat16)
        head_out = jnp.dot(prob_low, value_head, preferred_element_type=jnp.float32)
        return (head_out, (row_top + jnp.log(row_total))[:, 0])

    head_outs, log_norm = lax.map(one_head, jnp.arange(heads_here, dtype=jnp.int32))
    return (merge_heads(head_outs), log_norm)


def _attend_back_kernel(
    q_ref, k_ref, v_ref, g_ref, lse_ref, sq_ref, pq_ref, sk_ref, rk_ref, pk_ref, dq_ref, dk_ref, dv_ref
):
    query_head, key_head, grad_head = q_ref[...], k_ref[...], g_ref[...]
    scores = lax.dot_general(
        query_head, key_head, (((1,), (1,)), ((), ())), preferred_element_type=jnp.float32
    )
    allowed = _mask_from(sq_ref, pq_ref, sk_ref, rk_ref, pk_ref)
    scores = jnp.where(allowed, scores * HD ** (-0.5), masked_score)
    prob_full = jnp.exp(scores - lse_ref[...])
    prob_low = prob_full.astype(jnp.bfloat16)
    dv_ref[...] = lax.dot_general(
        prob_low, grad_head, (((0,), (0,)), ((), ())), preferred_element_type=jnp.float32
    )
    grad_prob = lax.dot_general(
        grad_head, v_ref[...], (((1,), (1,)), ((), ())), preferred_element_type=jnp.float32
    )
    grad_score = (
        prob_full * (grad_prob - jnp.sum(prob_full * grad_prob, axis=1, keepdims=True))
    ).astype(jnp.bfloat16)
    dq_ref[...] = jnp.dot(grad_score, key_head, preferred_element_type=jnp.float32) * HD ** (-0.5)
    dk_ref[...] = lax.dot_general(
        grad_score, query_head, (((0,), (0,)), ((), ())), preferred_element_type=jnp.float32
    ) * HD ** (-0.5)


def attend_backward(queries, key_ext, mask_parts, log_norm, grad_attended):
    heads_here = queries.shape[1] // HD
    rows, keys = mask_parts[0].shape[0], mask_parts[2].shape[1]

    def by_head(values, count):
        return jnp.transpose(values.reshape(count, heads_here, HD), (1, 0, 2))

    row_spec = pl.BlockSpec((None, rows, HD), lambda h: (h, 0, 0))
    key_spec = pl.BlockSpec((None, keys, HD), lambda h: (h, 0, 0))
    grad_queries, grad_keys, grad_values = pl.pallas_call(
        _attend_back_kernel,
        grid=(heads_here,),
        out_shape=(
            jax.ShapeDtypeStruct((heads_here, rows, HD), jnp.float32),
            jax.ShapeDtypeStruct((heads_here, keys, HD), jnp.float32),
            jax.ShapeDtypeStruct((heads_here, keys, HD), jnp.float32),
        ),
        in_specs=[
            row_spec,
            key_spec,
            key_spec,
            row_spec,
            pl.BlockSpec((None, rows, 1), lambda h: (h, 0, 0)),
            *_mask_specs(rows, keys),
        ],
        out_specs=(row_spec, key_spec, key_spec),
        compiler_params=pltpu.CompilerParams(vmem_limit_bytes=60 * 1024 * 1024),
    )(
        by_head(queries, rows),
        by_head(key_ext[0], keys),
        by_head(key_ext[1], keys),
        by_head(grad_attended, rows),
        log_norm[:, :, None],
        *mask_parts,
    )
    return (merge_heads(grad_queries), merge_heads(grad_keys), merge_heads(grad_values))


def attend_backward_xla(queries, key_ext, allowed, log_norm, grad_attended):
    heads_here, query_heads, key_heads, value_heads = split_heads(queries, key_ext)
    grad_heads = grad_attended.reshape(grad_attended.shape[0], heads_here, HD)

    def one_head(inputs):
        head_index, norm_row = inputs
        query_head = lax.dynamic_index_in_dim(query_heads, head_index, 1, keepdims=False)
        key_head = lax.dynamic_index_in_dim(key_heads, head_index, 1, keepdims=False)
        value_head = lax.dynamic_index_in_dim(value_heads, head_index, 1, keepdims=False)
        grad_head = lax.dynamic_index_in_dim(grad_heads, head_index, 1, keepdims=False)
        prob_full = jnp.exp(head_scores(query_head, key_head, allowed) - norm_row[:, None])
        prob_low = prob_full.astype(jnp.bfloat16)
        grad_value = lax.dot_general(
            prob_low, grad_head, (((0,), (0,)), ((), ())), preferred_element_type=jnp.float32
        )
        grad_prob = lax.dot_general(
            grad_head, value_head, (((1,), (1,)), ((), ())), preferred_element_type=jnp.float32
        )
        grad_score = (
            prob_full * (grad_prob - jnp.sum(prob_full * grad_prob, axis=1, keepdims=True))
        ).astype(jnp.bfloat16)
        grad_query = jnp.dot(grad_score, key_head, preferred_element_type=jnp.float32) * HD ** (
            -0.5
        )
        grad_key = lax.dot_general(
            grad_score, query_head, (((0,), (0,)), ((), ())), preferred_element_type=jnp.float32
        ) * HD ** (-0.5)
        return (grad_query, grad_key, grad_value)

    grad_queries, grad_keys, grad_values = lax.map(
        one_head, (jnp.arange(heads_here, dtype=jnp.int32), log_norm)
    )
    return (merge_heads(grad_queries), merge_heads(grad_keys), merge_heads(grad_values))


def local(
    tokens,
    segment,
    real_token,
    qkv_weight,
    out_weight,
    up_weight,
    down_weight,
    unit_bias,
    norm_gain,
    row_bias,
    cotangent,
):
    tok_rows = tokens.shape[0]
    tensor_size = lax.axis_size("tensor")
    group_rows = tok_rows * tensor_size
    margin = IMG - 1
    cols_here = qkv_weight.shape[3]
    dp_index = lax.axis_index("dp")
    tensor_index = lax.axis_index("tensor")
    group_first = dp_index * group_rows
    own_first = group_first + tensor_index * tok_rows
    segment_pad = jnp.pad(segment, (margin, margin), constant_values=-1)
    real_pad = jnp.pad(real_token, (margin, margin))
    segment_query = lax.dynamic_slice_in_dim(segment, group_first, group_rows, 0)
    segment_key = lax.dynamic_slice_in_dim(segment_pad, group_first, group_rows + 2 * margin, 0)
    real_key = lax.dynamic_slice_in_dim(real_pad, group_first, group_rows + 2 * margin, 0)
    place_query = jnp.arange(group_rows, dtype=jnp.int32)
    place_key = jnp.arange(group_rows + 2 * margin, dtype=jnp.int32) - margin
    allowed = (
        segment_query[:, None],
        place_query[:, None],
        segment_key[None, :],
        real_key[None, :],
        place_key[None, :],
    )
    own_real = lax.dynamic_slice_in_dim(real_token, own_first, tok_rows, 0).astype(jnp.float32)
    stream = tokens.astype(jnp.float32)
    layer_index = 0
    qkv_local = jnp.moveaxis(qkv_weight[layer_index], 1, 0)
    out_local, up_local, down_local = (
        out_weight[layer_index],
        up_weight[layer_index],
        down_weight[layer_index],
    )
    gain_now = norm_gain[layer_index].astype(jnp.float32)
    shift_now = row_bias[layer_index].astype(jnp.float32)
    bias_now = unit_bias[layer_index].astype(jnp.float32)
    normed_full = gather_forward(layer_norm(stream, gain_now[0], shift_now[0]).astype(jnp.bfloat16))
    qkv_full = jnp.moveaxis(collect(qkv_local, "dp", 0), 0, 1)
    projected = jnp.einsum("gd,sde->sge", normed_full, qkv_full, preferred_element_type=jnp.float32)
    queries = (projected[0] + bias_now[0]).astype(jnp.bfloat16)
    queries, out_local, up_local, down_local = lax.optimization_barrier(
        (queries, out_local, up_local, down_local)
    )
    out_full = collect(out_local, "dp", 0)
    up_full = collect(up_local, "dp", 0)
    down_full = collect(down_local, "dp", 0)
    gathered = (qkv_full, out_full, up_full, down_full)
    key_value = jnp.stack([projected[1], projected[2] + bias_now[1]]).astype(jnp.bfloat16)
    key_ext = with_halo(key_value, (("dp", 1),), margin)
    attended, log_norm = attend_forward(queries, key_ext, allowed)
    attended = attended.astype(jnp.bfloat16)

    def attention_term(first_row, row_count):
        return lax.dot_general(
            attended, out_full, (((1,), (1,)), ((), ())), preferred_element_type=jnp.float32
        )

    middle = stream + sum_forward(attention_term, tok_rows) + shift_now[1]
    second_full = gather_forward(layer_norm(middle, gain_now[1], shift_now[2]).astype(jnp.bfloat16))
    hidden = (
        jnp.einsum("gd,dre->gre", second_full, up_full, preferred_element_type=jnp.float32)
        + bias_now[2:][None]
    )
    active = exact_gelu(hidden).astype(jnp.bfloat16)

    def feed_term(first_row, row_count):
        return jnp.einsum("gre,ore->go", active, down_full, preferred_element_type=jnp.float32)

    kept_weights = gathered
    records = [
        (
            stream,
            middle,
            normed_full,
            second_full,
            queries,
            key_ext,
            log_norm,
            attended,
            hidden,
            active,
            kept_weights,
        )
    ]
    stream = middle + sum_forward(feed_term, tok_rows) + shift_now[3]
    gradient = cotangent.astype(jnp.float32) * own_real[:, None]
    local_qkv = [None] * LAYERS
    local_out = [None] * LAYERS
    local_up = [None] * LAYERS
    local_down = [None] * LAYERS
    unit_grads = [None] * LAYERS
    gain_grads = [None] * LAYERS
    shift_grads = [None] * LAYERS
    for layer_index in reversed(range(LAYERS)):
        (
            stream_in,
            middle,
            normed_full,
            second_full,
            queries,
            key_ext,
            log_norm,
            attended,
            hidden,
            active,
            kept_weights,
        ) = records[layer_index]
        qkv_full, out_full, up_full, down_full = kept_weights
        gain_now = norm_gain[layer_index].astype(jnp.float32)
        shift_now = row_bias[layer_index].astype(jnp.float32)
        shift_three = jnp.sum(gradient, axis=0)
        grad_mlp = gather_backward(gradient.astype(jnp.bfloat16))
        down_grad = scatter_rows(
            jnp.einsum("go,gre->ore", grad_mlp, active, preferred_element_type=jnp.float32)
        )
        grad_active = jnp.einsum(
            "go,ore->gre", grad_mlp, down_full, preferred_element_type=jnp.float32
        )
        gelu_again, gelu_pull = jax.vjp(exact_gelu, hidden)
        grad_hidden = gelu_pull(grad_active)[0].astype(jnp.bfloat16)
        up_bias_grad = jnp.sum(grad_hidden.astype(jnp.float32), axis=0)
        up_grad = scatter_rows(
            jnp.einsum("gd,gre->dre", second_full, grad_hidden, preferred_element_type=jnp.float32)
        )

        def second_term(first_row, row_count):
            return jnp.einsum(
                "gre,dre->gd", grad_hidden, up_full, preferred_element_type=jnp.float32
            )

        grad_second = sum_backward(second_term, tok_rows)
        second_again, second_pull = jax.vjp(layer_norm, middle, gain_now[1], shift_now[2])
        grad_mid_norm, gain_one, shift_two = second_pull(grad_second)
        grad_middle = gradient + grad_mid_norm
        shift_one = jnp.sum(grad_middle, axis=0)
        grad_proj = gather_backward(grad_middle.astype(jnp.bfloat16))
        out_grad = scatter_rows(
            lax.dot_general(
                grad_proj, attended, (((0,), (0,)), ((), ())), preferred_element_type=jnp.float32
            )
        )
        grad_attended = jnp.dot(grad_proj, out_full, preferred_element_type=jnp.float32).astype(
            jnp.bfloat16
        )
        grad_query, grad_key_ext, grad_value_ext = attend_backward(
            queries, key_ext, allowed, log_norm, grad_attended
        )
        grad_pair_ext = jnp.stack([grad_key_ext, grad_value_ext])
        from_next = from_behind(grad_pair_ext[:, :margin].astype(jnp.bfloat16), "dp", -1).astype(
            jnp.float32
        )
        from_prev = from_behind(
            grad_pair_ext[:, margin + group_rows :].astype(jnp.bfloat16), "dp", 1
        ).astype(jnp.float32)
        grad_pair = grad_pair_ext[:, margin : margin + group_rows]
        grad_pair = (
            grad_pair.at[:, group_rows - margin :].add(from_next).at[:, :margin].add(from_prev)
        )
        grad_triple = jnp.concatenate(
            [grad_query.astype(jnp.bfloat16)[None], grad_pair.astype(jnp.bfloat16)], axis=0
        )
        qkv_grad = jnp.moveaxis(
            scatter_rows(
                jnp.einsum(
                    "gd,sge->dse", normed_full, grad_triple, preferred_element_type=jnp.float32
                )
            ),
            0,
            1,
        )
        triple_sums = jnp.sum(grad_triple.astype(jnp.float32), axis=1)

        def first_term(first_row, row_count):
            return jnp.einsum(
                "sge,sde->gd", grad_triple, qkv_full, preferred_element_type=jnp.float32
            )

        grad_first = sum_backward(first_term, tok_rows)
        first_again, first_pull = jax.vjp(layer_norm, stream_in, gain_now[0], shift_now[0])
        grad_in_norm, gain_zero, shift_zero = first_pull(grad_first)
        gradient = grad_middle + grad_in_norm
        unit_grads[layer_index] = jnp.concatenate(
            [triple_sums[0][None], triple_sums[2][None], up_bias_grad], axis=0
        )
        gain_grads[layer_index] = jnp.stack([gain_zero, gain_one])
        shift_grads[layer_index] = jnp.stack([shift_zero, shift_one, shift_two, shift_three])
        local_qkv[layer_index] = qkv_grad
        local_out[layer_index] = out_grad
        local_up[layer_index] = up_grad
        local_down[layer_index] = down_grad
    grad_qkv = jnp.stack(local_qkv).astype(jnp.float32)
    grad_out = jnp.stack(local_out).astype(jnp.float32)
    grad_up = jnp.stack(local_up).astype(jnp.float32)
    grad_down = jnp.stack(local_down).astype(jnp.float32)
    unit_local = jnp.stack(unit_grads)
    unit_wide = jnp.zeros((LAYERS, unit_local.shape[1], cols_here * tensor_size), jnp.float32)
    unit_wide = lax.dynamic_update_slice_in_dim(unit_wide, unit_local, tensor_index * cols_here, 2)
    small = jnp.concatenate(
        [jnp.stack(gain_grads), jnp.stack(shift_grads), unit_wide], axis=1
    )
    small_total = jnp.sum(from_everyone(small, "dp"), axis=0)
    small_total = jnp.sum(from_everyone(small_total, "tensor"), axis=0)
    gain_total = small_total[:, :2]
    shift_total = small_total[:, 2:6]
    unit_total = small_total[:, 6:]
    unit_mine = lax.dynamic_slice_in_dim(unit_total, tensor_index * cols_here, cols_here, 2)
    return (
        stream.astype(jnp.bfloat16),
        gradient.astype(jnp.bfloat16),
        grad_qkv,
        grad_out,
        grad_up,
        grad_down,
        unit_mine,
        gain_total,
        shift_total,
    )


def solution(mesh):
    placed = (
        P(("dp", "tensor"), None),
        P(),
        P(),
        P(None, None, "dp", "tensor"),
        P(None, "dp", "tensor"),
        P(None, "dp", None, "tensor"),
        P(None, "dp", None, "tensor"),
        P(None, None, "tensor"),
        P(),
        P(),
        P(("dp", "tensor"), None),
    )
    return jax.shard_map(
        local,
        mesh=mesh,
        in_specs=placed,
        out_specs=(
            P(("dp", "tensor"), None),
            P(("dp", "tensor"), None),
            P(None, None, "dp", "tensor"),
            P(None, "dp", "tensor"),
            P(None, "dp", None, "tensor"),
            P(None, "dp", None, "tensor"),
            P(None, None, "tensor"),
            P(),
            P(),
        ),
        check_vma=False,
    )
```
